128 devices in a mesh: member: 2 (over y_hi), gridy: 8 (over x, core), gridx: 8 (over z, y_lo).
Axes of the slice: x: 4, y: 4 (y_hi: 2, y_lo: 2; y = y_hi * 2 + y_lo), z: 4, core: 2. Of those that a mesh axis runs over, the one named last changes fastest.
Arguments:
- temp: float32 [4, 4, 512, 2048], P('member', None, 'gridy', 'gridx'), may hold values from -6 to 6
- salt: float32 [4, 4, 512, 2048], P('member', None, 'gridy', 'gridx'), may hold values from -6 to 6
- uvel: float32 [4, 4, 512, 2048], P('member', None, 'gridy', 'gridx'), may hold values from -3 to 3
- vvel: float32 [4, 4, 512, 2048], P('member', None, 'gridy', 'gridx'), may hold values from -3 to 3
- eta: float32 [4, 512, 2048], P('member', 'gridy', 'gridx'), may hold values from -6 to 6
- land_mask: int32 [512, 2048], P('gridy', 'gridx'), may hold values 0 or 1
- clone_source: int32 [4], P('member'), may hold values from 0 to 3
Outputs:
- new_temp: float32 [4, 4, 512, 2048], P('member', None, 'gridy', 'gridx')
- new_salt: float32 [4, 4, 512, 2048], P('member', None, 'gridy', 'gridx')
- new_uvel: float32 [4, 4, 512, 2048], P('member', None, 'gridy', 'gridx')
- new_vvel: float32 [4, 4, 512, 2048], P('member', None, 'gridy', 'gridx')
- new_eta: float32 [4, 512, 2048], P('member', 'gridy', 'gridx')
- overturning: float32 [4, 4, 512], P('member', None, 'gridy')
- clone_weight: float32 [4], P('member')
The draws below stay inside these ranges and needn't reach their ends.
All inputs are finite; a program needn't handle non-finite values. No bound on the sum of `land_mask` on one device may be relied on, other than what follows from the above.
Results may differ from the reference program's by a relative error of at most 0.0001.
Values sent between devices are 32-bit elements; how exact they have to be, the bound alone decides.
A program may use at most 128 MiB of HBM per device.

```python
import jax
import jax.numpy as jnp
from jax import lax

LEV = 4
STEPS = 2
ITERS = 3
MEMBERS = 4
NY = 512
NX = 2048


def plant(drawn, rng, least, largest):
    longest = drawn.shape.index(max(drawn.shape))
    spots = []
    for shift in (0, 1):
        where = [jax.random.randint(jax.random.fold_in(rng, axis), (), 0, length) for axis, length in enumerate(drawn.shape)]
        where[longest] = (where[longest] + shift) % drawn.shape[longest]
        spots.append(tuple(where))
    return drawn.at[spots[0]].set(least).at[spots[1]].set(largest)


def block_levels(own_key, dims, cuts, smallest, largest):
    def one(position, shards_of):
        heights = jax.random.uniform(jax.random.fold_in(jax.random.fold_in(own_key, 6), position), (shards_of,), jnp.float32, smallest / len(cuts), largest / len(cuts))
        return jnp.repeat(jnp.exp(heights), dims[position] // shards_of).reshape((-1,) + (1,) * (len(dims) - position - 1))

    factor_of = one(*cuts[0])
    for cut in cuts[1:]:
        factor_of = factor_of * one(*cut)
    return factor_of


def noise(rng, extent, scale, limit, shards=(), held_as=jnp.bfloat16):
    result = scale * jax.random.normal(rng, extent, jnp.float32)
    if shards:
        result = result * block_levels(rng, extent, shards, -0.22, 0.18)
    return jnp.clip(result, -limit, limit).astype(held_as)


def setup_inputs(seed: int = 0) -> dict:
    seeds = jax.random.split(jax.random.key(seed), 8)
    temp = noise(seeds[0], (MEMBERS, LEV, NY, NX), 1.0, 6.0, ((0, 2), (2, 8), (3, 8)), jnp.float32)
    salt = noise(seeds[1], (MEMBERS, LEV, NY, NX), 1.0, 6.0, ((0, 2), (2, 8), (3, 8)), jnp.float32)
    uvel = noise(seeds[2], (MEMBERS, LEV, NY, NX), 0.5, 3.0, ((0, 2), (2, 8), (3, 8)), jnp.float32)
    vvel = noise(seeds[3], (MEMBERS, LEV, NY, NX), 0.5, 3.0, ((0, 2), (2, 8), (3, 8)), jnp.float32)
    eta = noise(seeds[4], (MEMBERS, NY, NX), 1.0, 6.0, ((0, 2), (1, 8), (2, 8)), jnp.float32)
    land_mask = plant((jax.random.randint(seeds[5], (NY, NX), 0, 4) < 3).astype(jnp.int32), jax.random.fold_in(seeds[5], 1), 0, 1)
    clone_source = plant(jax.random.randint(seeds[6], (MEMBERS,), 0, MEMBERS), jax.random.fold_in(seeds[6], 1), 0, MEMBERS - 1).astype(jnp.int32)
    return dict(temp=temp, salt=salt, uvel=uvel, vvel=vvel, eta=eta, land_mask=land_mask, clone_source=clone_source)


ALPHA_T = 0.8
BETA_S = 0.6
PRESS_K = 0.25
STEP_DT = 0.1
KAPPA = 0.1
VISCOSITY = 0.1
DRAG_K = 0.05
CORI_K = 1.0
SURF_C = 4.0
DIV_K = 0.5
GRAV_K = 0.5

def east(field):
    return jnp.roll(field, -1, axis=-1)

def west(field):
    return jnp.roll(field, 1, axis=-1)

def north(field):
    zero_row = jnp.zeros_like(field[..., :1, :])
    return jnp.concatenate([field[..., 1:, :], zero_row], axis=-2)

def south(field):
    zero_row = jnp.zeros_like(field[..., :1, :])
    return jnp.concatenate([zero_row, field[..., :-1, :]], axis=-2)

def laplace(field):
    return east(field) + west(field) + north(field) + south(field) - 4.0 * field

def pressure(temp, salt):
    return PRESS_K * jnp.cumsum(BETA_S * salt - ALPHA_T * temp, axis=0)

def surface_apply(field):
    return (1.0 + 4.0 * SURF_C) * field - SURF_C * (east(field) + west(field) + north(field) + south(field))

def surface_solve(rhs):
    solution = jnp.zeros_like(rhs)
    residual = rhs
    direction = rhs
    norm_now = jnp.sum(residual * residual)
    for count in range(ITERS):
        image = surface_apply(direction)
        alpha = norm_now / jnp.sum(direction * image)
        solution = solution + alpha * direction
        residual = residual - alpha * image
        norm_next = jnp.sum(residual * residual)
        direction = residual + norm_next / norm_now * direction
        norm_now = norm_next
    return solution

def member_window(fields, ocean, coriolis):
    temp, salt, uvel, vvel, eta = fields
    for count in range(STEPS):
        press = pressure(temp, salt)
        temp_next = ocean * (temp - STEP_DT * 0.5 * (uvel * (east(temp) - west(temp)) + vvel * (north(temp) - south(temp))) + KAPPA * laplace(temp))
        salt_next = ocean * (salt - STEP_DT * 0.5 * (uvel * (east(salt) - west(salt)) + vvel * (north(salt) - south(salt))) + KAPPA * laplace(salt))
        ustar = ocean * (uvel + STEP_DT * (coriolis * vvel - 0.5 * (east(press) - west(press)) - DRAG_K * uvel) + VISCOSITY * laplace(uvel))
        vstar = ocean * (vvel + STEP_DT * (-coriolis * uvel - 0.5 * (north(press) - south(press)) - DRAG_K * vvel) + VISCOSITY * laplace(vvel))
        trans_u = lax.optimization_barrier(jnp.sum(ustar, axis=0))
        trans_v = lax.optimization_barrier(jnp.sum(vstar, axis=0))
        rhs = eta - DIV_K * 0.5 * (east(trans_u) - west(trans_u) + (north(trans_v) - south(trans_v)))
        eta = surface_solve(rhs)
        uvel = ocean * (ustar - GRAV_K * 0.5 * (east(eta) - west(eta)))
        vvel = ocean * (vstar - GRAV_K * 0.5 * (north(eta) - south(eta)))
        temp = temp_next
        salt = salt_next
    zonal = lax.optimization_barrier(jnp.sum(vvel, axis=2))
    overturn = jnp.cumsum(zonal, axis=0) / jnp.sqrt(jnp.float32(NX))
    latitude = (jnp.arange(NY).astype(jnp.float32) + 0.5) / NY
    score = jnp.sum(overturn * latitude[None, :]) / jnp.sqrt(jnp.float32(LEV * NY))
    return (temp, salt, uvel, vvel, eta, overturn, score)

def reference(temp, salt, uvel, vvel, eta, land_mask, clone_source):
    ocean = land_mask.astype(jnp.float32)
    rows = jnp.arange(NY).astype(jnp.float32) + 0.5
    coriolis = (CORI_K * (2.0 * rows / NY - 1.0))[:, None]
    results = lax.map(lambda fields: member_window(fields, ocean, coriolis), (temp, salt, uvel, vvel, eta))
    temp_f, salt_f, uvel_f, vvel_f, eta_f, overturn, score = results
    new_temp = jnp.take(temp_f, clone_source, axis=0)
    new_salt = jnp.take(salt_f, clone_source, axis=0)
    new_uvel = jnp.take(uvel_f, clone_source, axis=0)
    new_vvel = jnp.take(vvel_f, clone_source, axis=0)
    new_eta = jnp.take(eta_f, clone_source, axis=0)
    clone_weight = jnp.take(score, clone_source, axis=0) - jnp.mean(score)
    return (new_temp, new_salt, new_uvel, new_vvel, new_eta, overturn, clone_weight)
```

```python
import jax
import jax.numpy as jnp
from jax import lax
from jax.sharding import PartitionSpec as P

STEPS = 2
ITERS = 3


ALPHA_T = 0.8
BETA_S = 0.6
PRESS_K = 0.25
STEP_DT = 0.1
KAPPA = 0.1
VISCOSITY = 0.1
DRAG_K = 0.05
CORI_K = 1.0
SURF_C = 4.0
DIV_K = 0.5
GRAV_K = 0.5


def padded_2(block, sides, width):
    for axis, dim in sides:
        count = lax.axis_size(axis)
        forward = [(i, i + 1) for i in range(count - 1)]
        forward.append((count - 1, 0))
        backward = [(target, source) for source, target in forward]
        low = lax.ppermute(
            lax.slice_in_dim(block, block.shape[dim] - width, None, axis=dim), axis, forward
        )
        high = lax.ppermute(lax.slice_in_dim(block, 0, width, axis=dim), axis, backward)
        block = jnp.concatenate([low, block, high], axis=dim)
    return block


def tree_sum(values, axes):
    for axis in axes:
        count = lax.axis_size(axis)
        step = 1
        while step < count:
            pairs = [(i, i ^ step) for i in range(count)]
            values = values + lax.ppermute(values, axis, pairs)
            step *= 2
    return values


def pressure(temp, salt):
    return PRESS_K * jnp.cumsum(BETA_S * salt - ALPHA_T * temp, axis=-3)


def split_rims(padded, south_keep, north_keep):
    east_side = padded[..., 1:-1, 2:]
    west_side = padded[..., 1:-1, :-2]
    north_side = padded[..., 2:, 1:-1]
    south_side = padded[..., :-2, 1:-1]
    north_side = north_side.at[..., -1, :].multiply(north_keep)
    south_side = south_side.at[..., 0, :].multiply(south_keep)
    return (east_side, west_side, north_side, south_side)


def volume_sides(fields, south_keep, north_keep):
    padded = padded_2(jnp.stack(fields), (("gridy", 3), ("gridx", 4)), 1)
    return split_rims(padded, south_keep, north_keep)


def surface_sides(fields, south_keep, north_keep):
    padded = padded_2(jnp.stack(fields), (("gridy", 2), ("gridx", 3)), 1)
    return split_rims(padded, south_keep, north_keep)


def surface_apply(field, south_keep, north_keep):
    east_side, west_side, north_side, south_side = surface_sides((field,), south_keep, north_keep)
    return (1.0 + 4.0 * SURF_C) * field - SURF_C * (
        east_side[0] + west_side[0] + north_side[0] + south_side[0]
    )


def member_total(values):
    return jnp.sum(values, axis=(1, 2))


def squared_norm(residual):
    return tree_sum(member_total(residual * residual), ("gridy", "gridx"))


def widen(values):
    return values[:, None, None]


def surface_solve(rhs, south_keep, north_keep):
    solution = jnp.zeros_like(rhs)
    residual = rhs
    direction = rhs
    norm_now = squared_norm(residual)
    for count in range(ITERS):
        image = surface_apply(direction, south_keep, north_keep)
        alpha = norm_now / tree_sum(member_total(direction * image), ("gridy", "gridx"))
        solution = solution + widen(alpha) * direction
        residual = residual - widen(alpha) * image
        norm_next = squared_norm(residual)
        direction = residual + widen(norm_next / norm_now) * direction
        norm_now = norm_next
    return solution


def shards(temp, salt, uvel, vvel, eta, land_mask, clone_source):
    levels = temp.shape[1]
    rows = temp.shape[2]
    cols = temp.shape[3]
    ocean = land_mask.astype(jnp.float32)
    tile_row = lax.axis_index("gridy")
    tile_count = lax.axis_size("gridy")
    total_rows = rows * tile_count
    total_cols = cols * lax.axis_size("gridx")
    south_keep = (tile_row > 0).astype(jnp.float32)
    north_keep = (tile_row < tile_count - 1).astype(jnp.float32)
    latitude = (tile_row * rows + jnp.arange(rows, dtype=jnp.int32)).astype(jnp.float32) + 0.5
    coriolis = (CORI_K * (2.0 * latitude / total_rows - 1.0))[:, None]
    for count in range(STEPS):
        press = pressure(temp, salt)
        east_side, west_side, north_side, south_side = volume_sides(
            (temp, salt, uvel, vvel, press), south_keep, north_keep
        )
        lap_temp = east_side[0] + west_side[0] + north_side[0] + south_side[0] - 4.0 * temp
        lap_salt = east_side[1] + west_side[1] + north_side[1] + south_side[1] - 4.0 * salt
        lap_uvel = east_side[2] + west_side[2] + north_side[2] + south_side[2] - 4.0 * uvel
        lap_vvel = east_side[3] + west_side[3] + north_side[3] + south_side[3] - 4.0 * vvel
        temp_next = ocean * (
            temp
            - STEP_DT
            * 0.5
            * (uvel * (east_side[0] - west_side[0]) + vvel * (north_side[0] - south_side[0]))
            + KAPPA * lap_temp
        )
        salt_next = ocean * (
            salt
            - STEP_DT
            * 0.5
            * (uvel * (east_side[1] - west_side[1]) + vvel * (north_side[1] - south_side[1]))
            + KAPPA * lap_salt
        )
        ustar = ocean * (
            uvel
            + STEP_DT * (coriolis * vvel - 0.5 * (east_side[4] - west_side[4]) - DRAG_K * uvel)
            + VISCOSITY * lap_uvel
        )
        vstar = ocean * (
            vvel
            + STEP_DT * (-coriolis * uvel - 0.5 * (north_side[4] - south_side[4]) - DRAG_K * vvel)
            + VISCOSITY * lap_vvel
        )
        trans_u = jnp.sum(ustar, axis=1)
        trans_v = jnp.sum(vstar, axis=1)
        east_t, west_t, north_t, south_t = surface_sides((trans_u, trans_v), south_keep, north_keep)
        rhs = eta - DIV_K * 0.5 * (east_t[0] - west_t[0] + (north_t[1] - south_t[1]))
        eta = surface_solve(rhs, south_keep, north_keep)
        east_e, west_e, north_e, south_e = surface_sides((eta,), south_keep, north_keep)
        uvel = ocean * (ustar - GRAV_K * 0.5 * (east_e[0] - west_e[0])[:, None])
        vvel = ocean * (vstar - GRAV_K * 0.5 * (north_e[0] - south_e[0])[:, None])
        temp = temp_next
        salt = salt_next
    zonal_scale = 1.0 / jnp.sqrt(jnp.float32(total_cols))
    score_scale = 1.0 / jnp.sqrt(jnp.float32(levels * total_rows))
    lat_weight = latitude / total_rows
    zonal_local = jnp.sum(vvel, axis=3)
    zonal_whole = tree_sum(zonal_local, ("gridx",))
    overturn = jnp.cumsum(zonal_whole, axis=1) * zonal_scale
    score = tree_sum(jnp.sum(overturn * lat_weight, axis=(1, 2)) * score_scale, ("gridy",))
    state_stack = jnp.stack((temp, salt, uvel, vvel))
    every_state, every_eta, every_score = (
        lax.all_gather(state_stack, "member", axis=1, tiled=True),
        lax.all_gather(eta, "member", axis=0, tiled=True),
        lax.all_gather(score, "member", axis=0, tiled=True),
    )
    picked = jnp.take(every_state, clone_source, axis=1)
    new_eta = jnp.take(every_eta, clone_source, axis=0)
    clone_weight = jnp.take(every_score, clone_source, axis=0) - jnp.mean(every_score)
    return (picked[0], picked[1], picked[2], picked[3], new_eta, overturn, clone_weight)


def solution(mesh):
    in_specs = (
        P("member", None, "gridy", "gridx"),
        P("member", None, "gridy", "gridx"),
        P("member", None, "gridy", "gridx"),
        P("member", None, "gridy", "gridx"),
        P("member", "gridy", "gridx"),
        P("gridy", "gridx"),
        P("member"),
    )
    out_specs = (
        P("member", None, "gridy", "gridx"),
        P("member", None, "gridy", "gridx"),
        P("member", None, "gridy", "gridx"),
        P("member", None, "gridy", "gridx"),
        P("member", "gridy", "gridx"),
        P("member", None, "gridy"),
        P("member"),
    )
    return jax.shard_map(shards, mesh=mesh, in_specs=in_specs, out_specs=out_specs, check_vma=False)
```

```python
import jax
import jax.numpy as jnp
from jax import lax
from jax.sharding import PartitionSpec as P

STEPS = 2
ITERS = 3


ALPHA_T = 0.8
BETA_S = 0.6
PRESS_K = 0.25
STEP_DT = 0.1
KAPPA = 0.1
VISCOSITY = 0.1
DRAG_K = 0.05
CORI_K = 1.0
SURF_C = 4.0
DIV_K = 0.5
GRAV_K = 0.5


def tree_sum(values, axes):
    for axis in axes:
        count = lax.axis_size(axis)
        step = 1
        while step < count:
            pairs = [(i, i ^ step) for i in range(count)]
            values = values + lax.ppermute(values, axis, pairs)
            step *= 2
    return values


def ring(axis):
    count = lax.axis_size(axis)
    forward = [(i, (i + 1) % count) for i in range(count)]
    backward = [((i + 1) % count, i) for i in range(count)]
    return forward, backward


def exchange(block, ydim, xdim, south_keep, north_keep):
    fwd_y, bwd_y = ring("gridy")
    fwd_x, bwd_x = ring("gridx")
    rows = block.shape[ydim]
    cols = block.shape[xdim]
    north = lax.ppermute(lax.slice_in_dim(block, 0, 1, axis=ydim), "gridy", bwd_y) * north_keep
    south = lax.ppermute(lax.slice_in_dim(block, rows - 1, rows, axis=ydim), "gridy", fwd_y) * south_keep
    east = lax.ppermute(lax.slice_in_dim(block, 0, 1, axis=xdim), "gridx", bwd_x)
    west = lax.ppermute(lax.slice_in_dim(block, cols - 1, cols, axis=xdim), "gridx", fwd_x)
    return (east, west, north, south)


def sides(field, rims, ydim, xdim):
    east, west, north, south = rims
    rows = field.shape[ydim]
    cols = field.shape[xdim]
    east_side = jnp.concatenate([lax.slice_in_dim(field, 1, cols, axis=xdim), east], axis=xdim)
    west_side = jnp.concatenate([west, lax.slice_in_dim(field, 0, cols - 1, axis=xdim)], axis=xdim)
    north_side = jnp.concatenate([lax.slice_in_dim(field, 1, rows, axis=ydim), north], axis=ydim)
    south_side = jnp.concatenate([south, lax.slice_in_dim(field, 0, rows - 1, axis=ydim)], axis=ydim)
    return (east_side, west_side, north_side, south_side)


def pressure(temp, salt):
    return PRESS_K * jnp.cumsum(BETA_S * salt - ALPHA_T * temp, axis=-3)


def surface_apply(field, rims):
    east_side, west_side, north_side, south_side = sides(field, rims, 1, 2)
    return (1.0 + 4.0 * SURF_C) * field - SURF_C * (east_side + west_side + north_side + south_side)


def member_total(values):
    return jnp.sum(values, axis=(1, 2))


def widen(values):
    return values[:, None, None]


def combine(a, fa, b, fb):
    def one(u, v):
        left = u if a is None else widen(a) * u
        return left + (v if b is None else widen(b) * v)

    return one(fa[0], fb[0]), tuple(one(u, v) for u, v in zip(fa[1], fb[1]))


def scaled(a, fa):
    return widen(a) * fa[0], tuple(widen(a) * u for u in fa[1])


def surface_solve(rhs, south_keep, north_keep):
    residual = (rhs, exchange(rhs, 1, 2, south_keep, north_keep))
    direction = None
    image_dir = None
    solution = None
    gamma_prev = None
    alpha_prev = None
    for count in range(ITERS):
        if count > 0:
            residual = (residual[0], exchange(residual[0], 1, 2, south_keep, north_keep))
        image_res = surface_apply(residual[0], residual[1])
        dots = tree_sum(
            jnp.stack(
                [member_total(residual[0] * residual[0]), member_total(residual[0] * image_res)]
            ),
            ("gridy", "gridx"),
        )
        gamma, delta = dots[0], dots[1]
        if count == 0:
            alpha = gamma / delta
            direction = residual
            image_dir = image_res
            solution = scaled(alpha, direction)
        else:
            beta = gamma / gamma_prev
            alpha = gamma / (delta - beta * gamma / alpha_prev)
            direction = combine(None, residual, beta, direction)
            image_dir = image_res + widen(beta) * image_dir
            solution = combine(None, solution, alpha, direction)
        if count < ITERS - 1:
            residual = (residual[0] - widen(alpha) * image_dir, None)
        gamma_prev = gamma
        alpha_prev = alpha
    return solution


def shards(temp, salt, uvel, vvel, eta, land_mask, clone_source):
    levels = temp.shape[1]
    rows = temp.shape[2]
    cols = temp.shape[3]
    ocean = land_mask.astype(jnp.float32)
    tile_row = lax.axis_index("gridy")
    tile_count = lax.axis_size("gridy")
    total_rows = rows * tile_count
    total_cols = cols * lax.axis_size("gridx")
    south_keep = (tile_row > 0).astype(jnp.float32)
    north_keep = (tile_row < tile_count - 1).astype(jnp.float32)
    latitude = (tile_row * rows + jnp.arange(rows, dtype=jnp.int32)).astype(jnp.float32) + 0.5
    coriolis = (CORI_K * (2.0 * latitude / total_rows - 1.0))[:, None]
    for count in range(STEPS):
        press = pressure(temp, salt)
        volume = jnp.stack((temp, salt, uvel, vvel, press))
        east_side, west_side, north_side, south_side = sides(
            volume, exchange(volume, 3, 4, south_keep, north_keep), 3, 4
        )
        lap_temp = east_side[0] + west_side[0] + north_side[0] + south_side[0] - 4.0 * temp
        lap_salt = east_side[1] + west_side[1] + north_side[1] + south_side[1] - 4.0 * salt
        lap_uvel = east_side[2] + west_side[2] + north_side[2] + south_side[2] - 4.0 * uvel
        lap_vvel = east_side[3] + west_side[3] + north_side[3] + south_side[3] - 4.0 * vvel
        temp_next = ocean * (
            temp
            - STEP_DT
            * 0.5
            * (uvel * (east_side[0] - west_side[0]) + vvel * (north_side[0] - south_side[0]))
            + KAPPA * lap_temp
        )
        salt_next = ocean * (
            salt
            - STEP_DT
            * 0.5
            * (uvel * (east_side[1] - west_side[1]) + vvel * (north_side[1] - south_side[1]))
            + KAPPA * lap_salt
        )
        ustar = ocean * (
            uvel
            + STEP_DT * (coriolis * vvel - 0.5 * (east_side[4] - west_side[4]) - DRAG_K * uvel)
            + VISCOSITY * lap_uvel
        )
        vstar = ocean * (
            vvel
            + STEP_DT * (-coriolis * uvel - 0.5 * (north_side[4] - south_side[4]) - DRAG_K * vvel)
            + VISCOSITY * lap_vvel
        )
        trans = jnp.stack((jnp.sum(ustar, axis=1), jnp.sum(vstar, axis=1)))
        east_t, west_t, north_t, south_t = sides(
            trans, exchange(trans, 2, 3, south_keep, north_keep), 2, 3
        )
        rhs = eta - DIV_K * 0.5 * (east_t[0] - west_t[0] + (north_t[1] - south_t[1]))
        eta, eta_rims = surface_solve(rhs, south_keep, north_keep)
        east_e, west_e, north_e, south_e = sides(eta, eta_rims, 1, 2)
        uvel = ocean * (ustar - GRAV_K * 0.5 * (east_e - west_e)[:, None])
        vvel = ocean * (vstar - GRAV_K * 0.5 * (north_e - south_e)[:, None])
        temp = temp_next
        salt = salt_next
    zonal_scale = 1.0 / jnp.sqrt(jnp.float32(total_cols))
    score_scale = 1.0 / jnp.sqrt(jnp.float32(levels * total_rows))
    lat_weight = latitude / total_rows
    zonal_local = jnp.sum(vvel, axis=3)
    zonal_whole = tree_sum(zonal_local, ("gridx",))
    overturn = jnp.cumsum(zonal_whole, axis=1) * zonal_scale
    score = tree_sum(jnp.sum(overturn * lat_weight, axis=(1, 2)) * score_scale, ("gridy",))
    state_stack = jnp.stack((temp, salt, uvel, vvel))
    every_state, every_eta, every_score = (
        lax.all_gather(state_stack, "member", axis=1, tiled=True),
        lax.all_gather(eta, "member", axis=0, tiled=True),
        lax.all_gather(score, "member", axis=0, tiled=True),
    )
    picked = jnp.take(every_state, clone_source, axis=1)
    new_eta = jnp.take(every_eta, clone_source, axis=0)
    clone_weight = jnp.take(every_score, clone_source, axis=0) - jnp.mean(every_score)
    return (picked[0], picked[1], picked[2], picked[3], new_eta, overturn, clone_weight)


def solution(mesh):
    in_specs = (
        P("member", None, "gridy", "gridx"),
        P("member", None, "gridy", "gridx"),
        P("member", None, "gridy", "gridx"),
        P("member", None, "gridy", "gridx"),
        P("member", "gridy", "gridx"),
        P("gridy", "gridx"),
        P("member"),
    )
    out_specs = (
        P("member", None, "gridy", "gridx"),
        P("member", None, "gridy", "gridx"),
        P("member", None, "gridy", "gridx"),
        P("member", None, "gridy", "gridx"),
        P("member", "gridy", "gridx"),
        P("member", None, "gridy"),
        P("member"),
    )
    return jax.shard_map(shards, mesh=mesh, in_specs=in_specs, out_specs=out_specs, check_vma=False)
```

```python
import functools

import jax
import jax.numpy as jnp
from jax import lax
from jax.experimental import pallas as pl
from jax.experimental.pallas import tpu as pltpu
from jax.sharding import PartitionSpec as P

STEPS = 2
ITERS = 3


ALPHA_T = 0.8
BETA_S = 0.6
PRESS_K = 0.25
STEP_DT = 0.1
KAPPA = 0.1
VISCOSITY = 0.1
DRAG_K = 0.05
CORI_K = 1.0
SURF_C = 4.0
DIV_K = 0.5
GRAV_K = 0.5


def tree_sum(values, axes):
    for axis in axes:
        count = lax.axis_size(axis)
        step = 1
        while step < count:
            pairs = [(i, i ^ step) for i in range(count)]
            values = values + lax.ppermute(values, axis, pairs)
            step *= 2
    return values


def gather_sum_kernel(ny, nx, x_ref, o_ref, recv_y, recv_x, part, send_y, rsem_y, send_x, rsem_x):
    mesh_id = pl.DeviceIdType.MESH
    member = lax.axis_index("member")
    my = lax.axis_index("gridy")
    mx = lax.axis_index("gridx")
    barrier = pltpu.get_barrier_semaphore()
    for d in range(1, ny):
        pl.semaphore_signal(barrier, 1, device_id=(member, (my + d) % ny, mx), device_id_type=mesh_id)
    for d in range(1, nx):
        pl.semaphore_signal(barrier, 1, device_id=(member, my, (mx + d) % nx), device_id_type=mesh_id)
    pl.semaphore_wait(barrier, (ny - 1) + (nx - 1))

    def phase(src, recv, send_sem, recv_sem, count, me, device):
        recv[me] = src[...]
        sent = []
        for d in range(1, count):
            peer = (me + d) % count
            copy = pltpu.make_async_remote_copy(
                src_ref=src,
                dst_ref=recv.at[me],
                send_sem=send_sem.at[peer],
                recv_sem=recv_sem.at[me],
                device_id=device(peer),
                device_id_type=mesh_id,
            )
            copy.start()
            sent.append(copy)
        for d in range(1, count):
            peer = (me + d) % count
            pltpu.make_async_remote_copy(
                src_ref=src,
                dst_ref=recv.at[peer],
                send_sem=send_sem.at[peer],
                recv_sem=recv_sem.at[peer],
                device_id=device(peer),
                device_id_type=mesh_id,
            ).wait_recv()
        for copy in sent:
            copy.wait_send()
        total = recv[0]
        for j in range(1, count):
            total = total + recv[j]
        return total

    part[...] = phase(x_ref, recv_y, send_y, rsem_y, ny, my, lambda p: (member, p, mx))
    o_ref[...] = phase(part, recv_x, send_x, rsem_x, nx, mx, lambda p: (member, my, p))


def grid_sum(values):
    ny = lax.axis_size("gridy")
    nx = lax.axis_size("gridx")
    shape = values.shape
    return pl.pallas_call(
        functools.partial(gather_sum_kernel, ny, nx),
        out_shape=jax.ShapeDtypeStruct(shape, values.dtype),
        in_specs=[pl.BlockSpec(memory_space=pltpu.VMEM)],
        out_specs=pl.BlockSpec(memory_space=pltpu.VMEM),
        scratch_shapes=[
            pltpu.VMEM((ny,) + shape, values.dtype),
            pltpu.VMEM((nx,) + shape, values.dtype),
            pltpu.VMEM(shape, values.dtype),
            pltpu.SemaphoreType.DMA((ny,)),
            pltpu.SemaphoreType.DMA((ny,)),
            pltpu.SemaphoreType.DMA((nx,)),
            pltpu.SemaphoreType.DMA((nx,)),
        ],
        compiler_params=pltpu.CompilerParams(collective_id=0, has_side_effects=True),
    )(values)


def ring(axis):
    count = lax.axis_size(axis)
    forward = [(i, (i + 1) % count) for i in range(count)]
    backward = [((i + 1) % count, i) for i in range(count)]
    return forward, backward


def exchange(block, ydim, xdim, south_keep, north_keep):
    fwd_y, bwd_y = ring("gridy")
    fwd_x, bwd_x = ring("gridx")
    rows = block.shape[ydim]
    cols = block.shape[xdim]
    north = lax.ppermute(lax.slice_in_dim(block, 0, 1, axis=ydim), "gridy", bwd_y) * north_keep
    south = lax.ppermute(lax.slice_in_dim(block, rows - 1, rows, axis=ydim), "gridy", fwd_y) * south_keep
    east = lax.ppermute(lax.slice_in_dim(block, 0, 1, axis=xdim), "gridx", bwd_x)
    west = lax.ppermute(lax.slice_in_dim(block, cols - 1, cols, axis=xdim), "gridx", fwd_x)
    return (east, west, north, south)


def sides(field, rims, ydim, xdim):
    east, west, north, south = rims
    rows = field.shape[ydim]
    cols = field.shape[xdim]
    east_side = jnp.concatenate([lax.slice_in_dim(field, 1, cols, axis=xdim), east], axis=xdim)
    west_side = jnp.concatenate([west, lax.slice_in_dim(field, 0, cols - 1, axis=xdim)], axis=xdim)
    north_side = jnp.concatenate([lax.slice_in_dim(field, 1, rows, axis=ydim), north], axis=ydim)
    south_side = jnp.concatenate([south, lax.slice_in_dim(field, 0, rows - 1, axis=ydim)], axis=ydim)
    return (east_side, west_side, north_side, south_side)


def pressure(temp, salt):
    return PRESS_K * jnp.cumsum(BETA_S * salt - ALPHA_T * temp, axis=-3)


def surface_apply(field, rims):
    east_side, west_side, north_side, south_side = sides(field, rims, 1, 2)
    return (1.0 + 4.0 * SURF_C) * field - SURF_C * (east_side + west_side + north_side + south_side)


def member_total(values):
    return jnp.sum(values, axis=(1, 2))


def widen(values):
    return values[:, None, None]


def combine(a, fa, b, fb):
    def one(u, v):
        left = u if a is None else widen(a) * u
        return left + (v if b is None else widen(b) * v)

    return one(fa[0], fb[0]), tuple(one(u, v) for u, v in zip(fa[1], fb[1]))


def scaled(a, fa):
    return widen(a) * fa[0], tuple(widen(a) * u for u in fa[1])


def surface_solve(rhs, south_keep, north_keep):
    residual = (rhs, exchange(rhs, 1, 2, south_keep, north_keep))
    direction = None
    image_dir = None
    solution = None
    gamma_prev = None
    alpha_prev = None
    for count in range(ITERS):
        if count > 0:
            residual = (residual[0], exchange(residual[0], 1, 2, south_keep, north_keep))
        image_res = surface_apply(residual[0], residual[1])
        dots = grid_sum(
            jnp.stack(
                [member_total(residual[0] * residual[0]), member_total(residual[0] * image_res)]
            )
        )
        gamma, delta = dots[0], dots[1]
        if count == 0:
            alpha = gamma / delta
            direction = residual
            image_dir = image_res
            solution = scaled(alpha, direction)
        else:
            beta = gamma / gamma_prev
            alpha = gamma / (delta - beta * gamma / alpha_prev)
            direction = combine(None, residual, beta, direction)
            image_dir = image_res + widen(beta) * image_dir
            solution = combine(None, solution, alpha, direction)
        if count < ITERS - 1:
            residual = (residual[0] - widen(alpha) * image_dir, None)
        gamma_prev = gamma
        alpha_prev = alpha
    return solution


def shards(temp, salt, uvel, vvel, eta, land_mask, clone_source):
    levels = temp.shape[1]
    rows = temp.shape[2]
    cols = temp.shape[3]
    ocean = land_mask.astype(jnp.float32)
    tile_row = lax.axis_index("gridy")
    tile_count = lax.axis_size("gridy")
    total_rows = rows * tile_count
    total_cols = cols * lax.axis_size("gridx")
    south_keep = (tile_row > 0).astype(jnp.float32)
    north_keep = (tile_row < tile_count - 1).astype(jnp.float32)
    latitude = (tile_row * rows + jnp.arange(rows, dtype=jnp.int32)).astype(jnp.float32) + 0.5
    coriolis = (CORI_K * (2.0 * latitude / total_rows - 1.0))[:, None]
    for count in range(STEPS):
        press = pressure(temp, salt)
        volume = jnp.stack((temp, salt, uvel, vvel, press))
        east_side, west_side, north_side, south_side = sides(
            volume, exchange(volume, 3, 4, south_keep, north_keep), 3, 4
        )
        lap_temp = east_side[0] + west_side[0] + north_side[0] + south_side[0] - 4.0 * temp
        lap_salt = east_side[1] + west_side[1] + north_side[1] + south_side[1] - 4.0 * salt
        lap_uvel = east_side[2] + west_side[2] + north_side[2] + south_side[2] - 4.0 * uvel
        lap_vvel = east_side[3] + west_side[3] + north_side[3] + south_side[3] - 4.0 * vvel
        temp_next = ocean * (
            temp
            - STEP_DT
            * 0.5
            * (uvel * (east_side[0] - west_side[0]) + vvel * (north_side[0] - south_side[0]))
            + KAPPA * lap_temp
        )
        salt_next = ocean * (
            salt
            - STEP_DT
            * 0.5
            * (uvel * (east_side[1] - west_side[1]) + vvel * (north_side[1] - south_side[1]))
            + KAPPA * lap_salt
        )
        ustar = ocean * (
            uvel
            + STEP_DT * (coriolis * vvel - 0.5 * (east_side[4] - west_side[4]) - DRAG_K * uvel)
            + VISCOSITY * lap_uvel
        )
        vstar = ocean * (
            vvel
            + STEP_DT * (-coriolis * uvel - 0.5 * (north_side[4] - south_side[4]) - DRAG_K * vvel)
            + VISCOSITY * lap_vvel
        )
        trans = jnp.stack((jnp.sum(ustar, axis=1), jnp.sum(vstar, axis=1)))
        east_t, west_t, north_t, south_t = sides(
            trans, exchange(trans, 2, 3, south_keep, north_keep), 2, 3
        )
        rhs = eta - DIV_K * 0.5 * (east_t[0] - west_t[0] + (north_t[1] - south_t[1]))
        eta, eta_rims = surface_solve(rhs, south_keep, north_keep)
        east_e, west_e, north_e, south_e = sides(eta, eta_rims, 1, 2)
        uvel = ocean * (ustar - GRAV_K * 0.5 * (east_e - west_e)[:, None])
        vvel = ocean * (vstar - GRAV_K * 0.5 * (north_e - south_e)[:, None])
        temp = temp_next
        salt = salt_next
    zonal_scale = 1.0 / jnp.sqrt(jnp.float32(total_cols))
    score_scale = 1.0 / jnp.sqrt(jnp.float32(levels * total_rows))
    lat_weight = latitude / total_rows
    zonal_local = jnp.sum(vvel, axis=3)
    zonal_whole = tree_sum(zonal_local, ("gridx",))
    overturn = jnp.cumsum(zonal_whole, axis=1) * zonal_scale
    score = tree_sum(jnp.sum(overturn * lat_weight, axis=(1, 2)) * score_scale, ("gridy",))
    state_stack = jnp.stack((temp, salt, uvel, vvel))
    every_state, every_eta, every_score = (
        lax.all_gather(state_stack, "member", axis=1, tiled=True),
        lax.all_gather(eta, "member", axis=0, tiled=True),
        lax.all_gather(score, "member", axis=0, tiled=True),
    )
    picked = jnp.take(every_state, clone_source, axis=1)
    new_eta = jnp.take(every_eta, clone_source, axis=0)
    clone_weight = jnp.take(every_score, clone_source, axis=0) - jnp.mean(every_score)
    return (picked[0], picked[1], picked[2], picked[3], new_eta, overturn, clone_weight)


def solution(mesh):
    in_specs = (
        P("member", None, "gridy", "gridx"),
        P("member", None, "gridy", "gridx"),
        P("member", None, "gridy", "gridx"),
        P("member", None, "gridy", "gridx"),
        P("member", "gridy", "gridx"),
        P("gridy", "gridx"),
        P("member"),
    )
    out_specs = (
        P("member", None, "gridy", "gridx"),
        P("member", None, "gridy", "gridx"),
        P("member", None, "gridy", "gridx"),
        P("member", None, "gridy", "gridx"),
        P("member", "gridy", "gridx"),
        P("member", None, "gridy"),
        P("member"),
    )
    return jax.shard_map(shards, mesh=mesh, in_specs=in_specs, out_specs=out_specs, check_vma=False)
```

```python
import functools

import jax
import jax.numpy as jnp
from jax import lax
from jax.experimental import pallas as pl
from jax.experimental.pallas import tpu as pltpu
from jax.sharding import PartitionSpec as P

STEPS = 2
ITERS = 3


ALPHA_T = 0.8
BETA_S = 0.6
PRESS_K = 0.25
STEP_DT = 0.1
KAPPA = 0.1
VISCOSITY = 0.1
DRAG_K = 0.05
CORI_K = 1.0
SURF_C = 4.0
DIV_K = 0.5
GRAV_K = 0.5


def tree_sum(values, axes):
    for axis in axes:
        count = lax.axis_size(axis)
        step = 1
        while step < count:
            pairs = [(i, i ^ step) for i in range(count)]
            values = values + lax.ppermute(values, axis, pairs)
            step *= 2
    return values


def gather_sum_kernel(ny, nx, x_ref, o_ref, recv_y, recv_x, part, send_y, rsem_y, send_x, rsem_x):
    mesh_id = pl.DeviceIdType.MESH
    member = lax.axis_index("member")
    my = lax.axis_index("gridy")
    mx = lax.axis_index("gridx")
    barrier = pltpu.get_barrier_semaphore()
    for d in range(1, ny):
        pl.semaphore_signal(barrier, 1, device_id=(member, (my + d) % ny, mx), device_id_type=mesh_id)
    for d in range(1, nx):
        pl.semaphore_signal(barrier, 1, device_id=(member, my, (mx + d) % nx), device_id_type=mesh_id)
    pl.semaphore_wait(barrier, (ny - 1) + (nx - 1))

    def phase(src, recv, send_sem, recv_sem, count, me, device):
        recv[me] = src[...]
        sent = []
        for d in range(1, count):
            peer = (me + d) % count
            copy = pltpu.make_async_remote_copy(
                src_ref=src,
                dst_ref=recv.at[me],
                send_sem=send_sem.at[peer],
                recv_sem=recv_sem.at[me],
                device_id=device(peer),
                device_id_type=mesh_id,
            )
            copy.start()
            sent.append(copy)
        for d in range(1, count):
            peer = (me + d) % count
            pltpu.make_async_remote_copy(
                src_ref=src,
                dst_ref=recv.at[peer],
                send_sem=send_sem.at[peer],
                recv_sem=recv_sem.at[peer],
                device_id=device(peer),
                device_id_type=mesh_id,
            ).wait_recv()
        for copy in sent:
            copy.wait_send()
        total = recv[0]
        for j in range(1, count):
            total = total + recv[j]
        return total

    part[...] = phase(x_ref, recv_y, send_y, rsem_y, ny, my, lambda p: (member, p, mx))
    o_ref[...] = phase(part, recv_x, send_x, rsem_x, nx, mx, lambda p: (member, my, p))


def grid_sum(values):
    ny = lax.axis_size("gridy")
    nx = lax.axis_size("gridx")
    shape = values.shape
    return pl.pallas_call(
        functools.partial(gather_sum_kernel, ny, nx),
        out_shape=jax.ShapeDtypeStruct(shape, values.dtype),
        in_specs=[pl.BlockSpec(memory_space=pltpu.VMEM)],
        out_specs=pl.BlockSpec(memory_space=pltpu.VMEM),
        scratch_shapes=[
            pltpu.VMEM((ny,) + shape, values.dtype),
            pltpu.VMEM((nx,) + shape, values.dtype),
            pltpu.VMEM(shape, values.dtype),
            pltpu.SemaphoreType.DMA((ny,)),
            pltpu.SemaphoreType.DMA((ny,)),
            pltpu.SemaphoreType.DMA((nx,)),
            pltpu.SemaphoreType.DMA((nx,)),
        ],
        compiler_params=pltpu.CompilerParams(collective_id=0, has_side_effects=True),
    )(values)


def ring(axis):
    count = lax.axis_size(axis)
    forward = [(i, (i + 1) % count) for i in range(count)]
    backward = [((i + 1) % count, i) for i in range(count)]
    return forward, backward


def exchange(block, ydim, xdim, south_keep, north_keep):
    fwd_y, bwd_y = ring("gridy")
    fwd_x, bwd_x = ring("gridx")
    rows = block.shape[ydim]
    cols = block.shape[xdim]
    north = lax.ppermute(lax.slice_in_dim(block, 0, 1, axis=ydim), "gridy", bwd_y) * north_keep
    south = lax.ppermute(lax.slice_in_dim(block, rows - 1, rows, axis=ydim), "gridy", fwd_y) * south_keep
    east = lax.ppermute(lax.slice_in_dim(block, 0, 1, axis=xdim), "gridx", bwd_x)
    west = lax.ppermute(lax.slice_in_dim(block, cols - 1, cols, axis=xdim), "gridx", fwd_x)
    return (east, west, north, south)


def sides(field, rims, ydim, xdim):
    east, west, north, south = rims
    rows = field.shape[ydim]
    cols = field.shape[xdim]
    east_side = jnp.concatenate([lax.slice_in_dim(field, 1, cols, axis=xdim), east], axis=xdim)
    west_side = jnp.concatenate([west, lax.slice_in_dim(field, 0, cols - 1, axis=xdim)], axis=xdim)
    north_side = jnp.concatenate([lax.slice_in_dim(field, 1, rows, axis=ydim), north], axis=ydim)
    south_side = jnp.concatenate([south, lax.slice_in_dim(field, 0, rows - 1, axis=ydim)], axis=ydim)
    return (east_side, west_side, north_side, south_side)


def pressure(temp, salt):
    return PRESS_K * jnp.cumsum(BETA_S * salt - ALPHA_T * temp, axis=-3)


def surface_apply(field, rims):
    east_side, west_side, north_side, south_side = sides(field, rims, 1, 2)
    return (1.0 + 4.0 * SURF_C) * field - SURF_C * (east_side + west_side + north_side + south_side)


def member_total(values):
    return jnp.sum(values, axis=(1, 2))


def widen(values):
    return values[:, None, None]


def combine(a, fa, b, fb):
    def one(u, v):
        left = u if a is None else widen(a) * u
        return left + (v if b is None else widen(b) * v)

    return one(fa[0], fb[0]), tuple(one(u, v) for u, v in zip(fa[1], fb[1]))


def scaled(a, fa):
    return widen(a) * fa[0], tuple(widen(a) * u for u in fa[1])


def padded_2(block, sides_of, width):
    for axis, dim in sides_of:
        count = lax.axis_size(axis)
        forward = [(i, (i + 1) % count) for i in range(count)]
        backward = [((i + 1) % count, i) for i in range(count)]
        size = block.shape[dim]
        low = lax.ppermute(lax.slice_in_dim(block, size - width, size, axis=dim), axis, forward)
        high = lax.ppermute(lax.slice_in_dim(block, 0, width, axis=dim), axis, backward)
        block = jnp.concatenate([low, block, high], axis=dim)
    return block


def crop(field, by):
    if by == 0:
        return field
    return field[..., by:-by, by:-by]


def around(field):
    return (
        field[..., 1:-1, 1:-1],
        field[..., 1:-1, 2:],
        field[..., 1:-1, :-2],
        field[..., 2:, 1:-1],
        field[..., :-2, 1:-1],
    )


def rows_at(inside, full, want):
    cut = full - want
    return inside if cut == 0 else inside[cut:-cut]


def apply_wide(field, inside):
    centre, east, west, north, south = around(field)
    return ((1.0 + 4.0 * SURF_C) * centre - SURF_C * (east + west + north + south)) * inside


def surface_solve(rhs, inside, width, full):
    residual, wide_r = rhs, width
    gamma_prev = None
    alpha_prev = None
    for count in range(ITERS):
        image_res = apply_wide(residual, rows_at(inside, full, wide_r - 1))
        own_res = crop(residual, wide_r)
        own_img = crop(image_res, wide_r - 1)
        dots = grid_sum(jnp.stack([member_total(own_res * own_res), member_total(own_res * own_img)]))
        gamma, delta = dots[0], dots[1]
        if count == 0:
            alpha = gamma / delta
            direction, wide_p = residual, wide_r
            image_dir, wide_s = image_res, wide_r - 1
            solution, wide_x = widen(alpha) * direction, wide_r
        else:
            beta = gamma / gamma_prev
            alpha = gamma / (delta - beta * gamma / alpha_prev)
            direction = residual + widen(beta) * crop(direction, wide_p - wide_r)
            wide_p = wide_r
            image_dir = image_res + widen(beta) * crop(image_dir, wide_s - (wide_r - 1))
            wide_s = wide_r - 1
            solution = crop(solution, wide_x - wide_r) + widen(alpha) * direction
            wide_x = wide_r
        if count < ITERS - 1:
            residual = crop(residual, 1) - widen(alpha) * image_dir
            wide_r -= 1
        gamma_prev = gamma
        alpha_prev = alpha
    return solution


def shards(temp, salt, uvel, vvel, eta, land_mask, clone_source):
    levels = temp.shape[1]
    rows = temp.shape[2]
    cols = temp.shape[3]
    ocean = land_mask.astype(jnp.float32)
    tile_row = lax.axis_index("gridy")
    tile_count = lax.axis_size("gridy")
    total_rows = rows * tile_count
    total_cols = cols * lax.axis_size("gridx")
    south_keep = (tile_row > 0).astype(jnp.float32)
    north_keep = (tile_row < tile_count - 1).astype(jnp.float32)
    latitude = (tile_row * rows + jnp.arange(rows, dtype=jnp.int32)).astype(jnp.float32) + 0.5
    coriolis = (CORI_K * (2.0 * latitude / total_rows - 1.0))[:, None]
    wide_rows = tile_row * rows - (ITERS + 1) + jnp.arange(rows + 2 * (ITERS + 1), dtype=jnp.int32)
    inside = ((wide_rows >= 0) & (wide_rows < total_rows)).astype(jnp.float32)[:, None]
    for count in range(STEPS):
        press = pressure(temp, salt)
        volume = jnp.stack((temp, salt, uvel, vvel, press))
        east_side, west_side, north_side, south_side = sides(
            volume, exchange(volume, 3, 4, south_keep, north_keep), 3, 4
        )
        lap_temp = east_side[0] + west_side[0] + north_side[0] + south_side[0] - 4.0 * temp
        lap_salt = east_side[1] + west_side[1] + north_side[1] + south_side[1] - 4.0 * salt
        lap_uvel = east_side[2] + west_side[2] + north_side[2] + south_side[2] - 4.0 * uvel
        lap_vvel = east_side[3] + west_side[3] + north_side[3] + south_side[3] - 4.0 * vvel
        temp_next = ocean * (
            temp
            - STEP_DT
            * 0.5
            * (uvel * (east_side[0] - west_side[0]) + vvel * (north_side[0] - south_side[0]))
            + KAPPA * lap_temp
        )
        salt_next = ocean * (
            salt
            - STEP_DT
            * 0.5
            * (uvel * (east_side[1] - west_side[1]) + vvel * (north_side[1] - south_side[1]))
            + KAPPA * lap_salt
        )
        ustar = ocean * (
            uvel
            + STEP_DT * (coriolis * vvel - 0.5 * (east_side[4] - west_side[4]) - DRAG_K * uvel)
            + VISCOSITY * lap_uvel
        )
        vstar = ocean * (
            vvel
            + STEP_DT * (-coriolis * uvel - 0.5 * (north_side[4] - south_side[4]) - DRAG_K * vvel)
            + VISCOSITY * lap_vvel
        )
        halo = ITERS + 1
        surface = padded_2(
            jnp.stack((jnp.sum(ustar, axis=1), jnp.sum(vstar, axis=1), eta)),
            (("gridy", 2), ("gridx", 3)),
            halo,
        ) * inside
        centre, east_t, west_t, north_t, south_t = around(surface)
        rhs = (centre[2] - DIV_K * 0.5 * (east_t[0] - west_t[0] + (north_t[1] - south_t[1]))) * rows_at(
            inside, halo, halo - 1
        )
        wide_eta = surface_solve(rhs, inside, halo - 1, halo)
        eta, east_e, west_e, north_e, south_e = around(wide_eta)
        uvel = ocean * (ustar - GRAV_K * 0.5 * (east_e - west_e)[:, None])
        vvel = ocean * (vstar - GRAV_K * 0.5 * (north_e - south_e)[:, None])
        temp = temp_next
        salt = salt_next
    zonal_scale = 1.0 / jnp.sqrt(jnp.float32(total_cols))
    score_scale = 1.0 / jnp.sqrt(jnp.float32(levels * total_rows))
    lat_weight = latitude / total_rows
    zonal_local = jnp.sum(vvel, axis=3)
    zonal_whole = tree_sum(zonal_local, ("gridx",))
    overturn = jnp.cumsum(zonal_whole, axis=1) * zonal_scale
    score = tree_sum(jnp.sum(overturn * lat_weight, axis=(1, 2)) * score_scale, ("gridy",))
    state_stack = jnp.stack((temp, salt, uvel, vvel))
    every_state, every_eta, every_score = (
        lax.all_gather(state_stack, "member", axis=1, tiled=True),
        lax.all_gather(eta, "member", axis=0, tiled=True),
        lax.all_gather(score, "member", axis=0, tiled=True),
    )
    picked = jnp.take(every_state, clone_source, axis=1)
    new_eta = jnp.take(every_eta, clone_source, axis=0)
    clone_weight = jnp.take(every_score, clone_source, axis=0) - jnp.mean(every_score)
    return (picked[0], picked[1], picked[2], picked[3], new_eta, overturn, clone_weight)


def solution(mesh):
    in_specs = (
        P("member", None, "gridy", "gridx"),
        P("member", None, "gridy", "gridx"),
        P("member", None, "gridy", "gridx"),
        P("member", None, "gridy", "gridx"),
        P("member", "gridy", "gridx"),
        P("gridy", "gridx"),
        P("member"),
    )
    out_specs = (
        P("member", None, "gridy", "gridx"),
        P("member", None, "gridy", "gridx"),
        P("member", None, "gridy", "gridx"),
        P("member", None, "gridy", "gridx"),
        P("member", "gridy", "gridx"),
        P("member", None, "gridy"),
        P("member"),
    )
    return jax.shard_map(shards, mesh=mesh, in_specs=in_specs, out_specs=out_specs, check_vma=False)
```

```python
import functools

import jax
import jax.numpy as jnp
from jax import lax
from jax.experimental import pallas as pl
from jax.experimental.pallas import tpu as pltpu
from jax.sharding import PartitionSpec as P

STEPS = 2
ITERS = 3


ALPHA_T = 0.8
BETA_S = 0.6
PRESS_K = 0.25
STEP_DT = 0.1
KAPPA = 0.1
VISCOSITY = 0.1
DRAG_K = 0.05
CORI_K = 1.0
SURF_C = 4.0
DIV_K = 0.5
GRAV_K = 0.5


def tree_sum(values, axes):
    for axis in axes:
        count = lax.axis_size(axis)
        step = 1
        while step < count:
            pairs = [(i, i ^ step) for i in range(count)]
            values = values + lax.ppermute(values, axis, pairs)
            step *= 2
    return values


def gather_sum_kernel(ny, nx, x_ref, o_ref, recv_y, recv_x, part, send_y, rsem_y, send_x, rsem_x):
    mesh_id = pl.DeviceIdType.MESH
    member = lax.axis_index("member")
    my = lax.axis_index("gridy")
    mx = lax.axis_index("gridx")
    barrier = pltpu.get_barrier_semaphore()
    for d in range(1, ny):
        pl.semaphore_signal(barrier, 1, device_id=(member, (my + d) % ny, mx), device_id_type=mesh_id)
    for d in range(1, nx):
        pl.semaphore_signal(barrier, 1, device_id=(member, my, (mx + d) % nx), device_id_type=mesh_id)
    pl.semaphore_wait(barrier, (ny - 1) + (nx - 1))

    def phase(src, recv, send_sem, recv_sem, count, me, device):
        recv[me] = src[...]
        sent = []
        for d in range(1, count):
            peer = (me + d) % count
            copy = pltpu.make_async_remote_copy(
                src_ref=src,
                dst_ref=recv.at[me],
                send_sem=send_sem.at[peer],
                recv_sem=recv_sem.at[me],
                device_id=device(peer),
                device_id_type=mesh_id,
            )
            copy.start()
            sent.append(copy)
        for d in range(1, count):
            peer = (me + d) % count
            pltpu.make_async_remote_copy(
                src_ref=src,
                dst_ref=recv.at[peer],
                send_sem=send_sem.at[peer],
                recv_sem=recv_sem.at[peer],
                device_id=device(peer),
                device_id_type=mesh_id,
            ).wait_recv()
        for copy in sent:
            copy.wait_send()
        total = recv[0]
        for j in range(1, count):
            total = total + recv[j]
        return total

    part[...] = phase(x_ref, recv_y, send_y, rsem_y, ny, my, lambda p: (member, p, mx))
    o_ref[...] = phase(part, recv_x, send_x, rsem_x, nx, mx, lambda p: (member, my, p))


def grid_sum(values):
    ny = lax.axis_size("gridy")
    nx = lax.axis_size("gridx")
    shape = values.shape
    return pl.pallas_call(
        functools.partial(gather_sum_kernel, ny, nx),
        out_shape=jax.ShapeDtypeStruct(shape, values.dtype),
        in_specs=[pl.BlockSpec(memory_space=pltpu.VMEM)],
        out_specs=pl.BlockSpec(memory_space=pltpu.VMEM),
        scratch_shapes=[
            pltpu.VMEM((ny,) + shape, values.dtype),
            pltpu.VMEM((nx,) + shape, values.dtype),
            pltpu.VMEM(shape, values.dtype),
            pltpu.SemaphoreType.DMA((ny,)),
            pltpu.SemaphoreType.DMA((ny,)),
            pltpu.SemaphoreType.DMA((nx,)),
            pltpu.SemaphoreType.DMA((nx,)),
        ],
        compiler_params=pltpu.CompilerParams(collective_id=0, has_side_effects=True),
    )(values)


def exchange_sum(k, vec, ny, nx, bufs, device_ids):
    send_y, recv_y, send_x, recv_x, sy, ry, sx, rx = bufs
    my, mx, along_y, along_x = device_ids
    mesh_id = pl.DeviceIdType.MESH

    def phase(value, send_buf, recv, send_sem, recv_sem, count, me, device):
        send_buf[k] = value
        recv[k, me] = value
        sent = []
        for d in range(1, count):
            peer = (me + d) % count
            copy = pltpu.make_async_remote_copy(
                src_ref=send_buf.at[k],
                dst_ref=recv.at[k, me],
                send_sem=send_sem.at[k, peer],
                recv_sem=recv_sem.at[k, me],
                device_id=device(peer),
                device_id_type=mesh_id,
            )
            copy.start()
            sent.append(copy)
        for d in range(1, count):
            peer = (me + d) % count
            pltpu.make_async_remote_copy(
                src_ref=send_buf.at[k],
                dst_ref=recv.at[k, peer],
                send_sem=send_sem.at[k, peer],
                recv_sem=recv_sem.at[k, peer],
                device_id=device(peer),
                device_id_type=mesh_id,
            ).wait_recv()
        for copy in sent:
            copy.wait_send()
        total = recv[k, 0]
        for j in range(1, count):
            total = total + recv[k, j]
        return total

    partial = phase(vec, send_y, recv_y, sy, ry, ny, my, along_y)
    return phase(partial, send_x, recv_x, sx, rx, nx, mx, along_x)


def solve_kernel(ny, nx, rhs_ref, inside_ref, own_ref, out_ref, *bufs):
    mesh_id = pl.DeviceIdType.MESH
    member = lax.axis_index("member")
    my = lax.axis_index("gridy")
    mx = lax.axis_index("gridx")
    along_y = lambda p: (member, p, mx)
    along_x = lambda p: (member, my, p)
    barrier = pltpu.get_barrier_semaphore()
    for d in range(1, ny):
        pl.semaphore_signal(barrier, 1, device_id=along_y((my + d) % ny), device_id_type=mesh_id)
    for d in range(1, nx):
        pl.semaphore_signal(barrier, 1, device_id=along_x((mx + d) % nx), device_id_type=mesh_id)
    pl.semaphore_wait(barrier, (ny - 1) + (nx - 1))

    members = rhs_ref.shape[0]
    rows, cols = rhs_ref.shape[1], rhs_ref.shape[2]
    inside = inside_ref[...]
    own = own_ref[...] > 0.5

    def east(f):
        return pltpu.roll(f, cols - 1, 1)

    def west(f):
        return pltpu.roll(f, 1, 1)

    def north(f):
        return pltpu.roll(f, rows - 1, 0)

    def south(f):
        return pltpu.roll(f, 1, 0)

    def apply(f):
        return ((1.0 + 4.0 * SURF_C) * f - SURF_C * (east(f) + west(f) + north(f) + south(f))) * inside

    def total(f):
        return jnp.sum(jnp.where(own, f, 0.0), axis=(0, 1), keepdims=True)

    lane = lax.broadcasted_iota(jnp.int32, (8, 128), 1)
    residual = [rhs_ref[m] for m in range(members)]
    direction = [None] * members
    image_dir = [None] * members
    solution = [None] * members
    gamma_prev = [None] * members
    alpha_prev = [None] * members
    for count in range(ITERS):
        image_res = [apply(residual[m]) for m in range(members)]
        vec = jnp.zeros((8, 128), jnp.float32)
        for m in range(members):
            vec = jnp.where(lane == 2 * m, total(residual[m] * residual[m]), vec)
            vec = jnp.where(lane == 2 * m + 1, total(residual[m] * image_res[m]), vec)
        sums = exchange_sum(count, vec, ny, nx, bufs, (my, mx, along_y, along_x))
        for m in range(members):
            gamma = sums[0:1, 2 * m : 2 * m + 1]
            delta = sums[0:1, 2 * m + 1 : 2 * m + 2]
            if count == 0:
                alpha = gamma / delta
                direction[m] = residual[m]
                image_dir[m] = image_res[m]
                solution[m] = alpha * direction[m]
            else:
                beta = gamma / gamma_prev[m]
                alpha = gamma / (delta - beta * gamma / alpha_prev[m])
                direction[m] = residual[m] + beta * direction[m]
                image_dir[m] = image_res[m] + beta * image_dir[m]
                solution[m] = solution[m] + alpha * direction[m]
            if count < ITERS - 1:
                residual[m] = residual[m] - alpha * image_dir[m]
            gamma_prev[m] = gamma
            alpha_prev[m] = alpha
    for m in range(members):
        x = solution[m]
        out_ref[0, m] = x
        out_ref[1, m] = east(x) - west(x)
        out_ref[2, m] = north(x) - south(x)


def surface_kernel_solve(rhs, inside, own):
    ny = lax.axis_size("gridy")
    nx = lax.axis_size("gridx")
    shape = rhs.shape
    return pl.pallas_call(
        functools.partial(solve_kernel, ny, nx),
        out_shape=jax.ShapeDtypeStruct((3,) + shape, jnp.float32),
        in_specs=[pl.BlockSpec(memory_space=pltpu.VMEM)] * 3,
        out_specs=pl.BlockSpec(memory_space=pltpu.VMEM),
        scratch_shapes=[
            pltpu.VMEM((ITERS, 8, 128), jnp.float32),
            pltpu.VMEM((ITERS, ny, 8, 128), jnp.float32),
            pltpu.VMEM((ITERS, 8, 128), jnp.float32),
            pltpu.VMEM((ITERS, nx, 8, 128), jnp.float32),
            pltpu.SemaphoreType.DMA((ITERS, ny)),
            pltpu.SemaphoreType.DMA((ITERS, ny)),
            pltpu.SemaphoreType.DMA((ITERS, nx)),
            pltpu.SemaphoreType.DMA((ITERS, nx)),
        ],
        compiler_params=pltpu.CompilerParams(collective_id=1, has_side_effects=True),
    )(rhs, inside, own)


def ring(axis):
    count = lax.axis_size(axis)
    forward = [(i, (i + 1) % count) for i in range(count)]
    backward = [((i + 1) % count, i) for i in range(count)]
    return forward, backward


def exchange(block, ydim, xdim, south_keep, north_keep):
    fwd_y, bwd_y = ring("gridy")
    fwd_x, bwd_x = ring("gridx")
    rows = block.shape[ydim]
    cols = block.shape[xdim]
    north = lax.ppermute(lax.slice_in_dim(block, 0, 1, axis=ydim), "gridy", bwd_y) * north_keep
    south = lax.ppermute(lax.slice_in_dim(block, rows - 1, rows, axis=ydim), "gridy", fwd_y) * south_keep
    east = lax.ppermute(lax.slice_in_dim(block, 0, 1, axis=xdim), "gridx", bwd_x)
    west = lax.ppermute(lax.slice_in_dim(block, cols - 1, cols, axis=xdim), "gridx", fwd_x)
    return (east, west, north, south)


def sides(field, rims, ydim, xdim):
    east, west, north, south = rims
    rows = field.shape[ydim]
    cols = field.shape[xdim]
    east_side = jnp.concatenate([lax.slice_in_dim(field, 1, cols, axis=xdim), east], axis=xdim)
    west_side = jnp.concatenate([west, lax.slice_in_dim(field, 0, cols - 1, axis=xdim)], axis=xdim)
    north_side = jnp.concatenate([lax.slice_in_dim(field, 1, rows, axis=ydim), north], axis=ydim)
    south_side = jnp.concatenate([south, lax.slice_in_dim(field, 0, rows - 1, axis=ydim)], axis=ydim)
    return (east_side, west_side, north_side, south_side)


def pressure(temp, salt):
    return PRESS_K * jnp.cumsum(BETA_S * salt - ALPHA_T * temp, axis=-3)


def surface_apply(field, rims):
    east_side, west_side, north_side, south_side = sides(field, rims, 1, 2)
    return (1.0 + 4.0 * SURF_C) * field - SURF_C * (east_side + west_side + north_side + south_side)


def member_total(values):
    return jnp.sum(values, axis=(1, 2))


def widen(values):
    return values[:, None, None]


def combine(a, fa, b, fb):
    def one(u, v):
        left = u if a is None else widen(a) * u
        return left + (v if b is None else widen(b) * v)

    return one(fa[0], fb[0]), tuple(one(u, v) for u, v in zip(fa[1], fb[1]))


def scaled(a, fa):
    return widen(a) * fa[0], tuple(widen(a) * u for u in fa[1])


def padded_2(block, sides_of, width):
    for axis, dim in sides_of:
        count = lax.axis_size(axis)
        forward = [(i, (i + 1) % count) for i in range(count)]
        backward = [((i + 1) % count, i) for i in range(count)]
        size = block.shape[dim]
        low = lax.ppermute(lax.slice_in_dim(block, size - width, size, axis=dim), axis, forward)
        high = lax.ppermute(lax.slice_in_dim(block, 0, width, axis=dim), axis, backward)
        block = jnp.concatenate([low, block, high], axis=dim)
    return block


def crop(field, by):
    if by == 0:
        return field
    return field[..., by:-by, by:-by]


def around(field):
    return (
        field[..., 1:-1, 1:-1],
        field[..., 1:-1, 2:],
        field[..., 1:-1, :-2],
        field[..., 2:, 1:-1],
        field[..., :-2, 1:-1],
    )


def rows_at(inside, full, want):
    cut = full - want
    return inside if cut == 0 else inside[cut:-cut]


def apply_wide(field, inside):
    centre, east, west, north, south = around(field)
    return ((1.0 + 4.0 * SURF_C) * centre - SURF_C * (east + west + north + south)) * inside


def surface_solve(rhs, inside, width, full):
    residual, wide_r = rhs, width
    gamma_prev = None
    alpha_prev = None
    for count in range(ITERS):
        image_res = apply_wide(residual, rows_at(inside, full, wide_r - 1))
        own_res = crop(residual, wide_r)
        own_img = crop(image_res, wide_r - 1)
        dots = grid_sum(jnp.stack([member_total(own_res * own_res), member_total(own_res * own_img)]))
        gamma, delta = dots[0], dots[1]
        if count == 0:
            alpha = gamma / delta
            direction, wide_p = residual, wide_r
            image_dir, wide_s = image_res, wide_r - 1
            solution, wide_x = widen(alpha) * direction, wide_r
        else:
            beta = gamma / gamma_prev
            alpha = gamma / (delta - beta * gamma / alpha_prev)
            direction = residual + widen(beta) * crop(direction, wide_p - wide_r)
            wide_p = wide_r
            image_dir = image_res + widen(beta) * crop(image_dir, wide_s - (wide_r - 1))
            wide_s = wide_r - 1
            solution = crop(solution, wide_x - wide_r) + widen(alpha) * direction
            wide_x = wide_r
        if count < ITERS - 1:
            residual = crop(residual, 1) - widen(alpha) * image_dir
            wide_r -= 1
        gamma_prev = gamma
        alpha_prev = alpha
    return solution


def shards(temp, salt, uvel, vvel, eta, land_mask, clone_source):
    levels = temp.shape[1]
    rows = temp.shape[2]
    cols = temp.shape[3]
    ocean = land_mask.astype(jnp.float32)
    tile_row = lax.axis_index("gridy")
    tile_count = lax.axis_size("gridy")
    total_rows = rows * tile_count
    total_cols = cols * lax.axis_size("gridx")
    south_keep = (tile_row > 0).astype(jnp.float32)
    north_keep = (tile_row < tile_count - 1).astype(jnp.float32)
    latitude = (tile_row * rows + jnp.arange(rows, dtype=jnp.int32)).astype(jnp.float32) + 0.5
    coriolis = (CORI_K * (2.0 * latitude / total_rows - 1.0))[:, None]
    wide_rows = tile_row * rows - (ITERS + 1) + jnp.arange(rows + 2 * (ITERS + 1), dtype=jnp.int32)
    inside = ((wide_rows >= 0) & (wide_rows < total_rows)).astype(jnp.float32)[:, None]
    halo = ITERS + 1
    lanes = 128 * ((cols + 2 * halo + 127) // 128)
    wide_inside = jnp.broadcast_to(inside, (rows + 2 * halo, lanes))
    row_at = lax.broadcasted_iota(jnp.int32, (rows + 2 * halo, lanes), 0)
    col_at = lax.broadcasted_iota(jnp.int32, (rows + 2 * halo, lanes), 1)
    own_mask = (
        (row_at >= halo) & (row_at < halo + rows) & (col_at >= halo) & (col_at < halo + cols)
    ).astype(jnp.float32)
    for count in range(STEPS):
        press = pressure(temp, salt)
        volume = jnp.stack((temp, salt, uvel, vvel, press))
        east_side, west_side, north_side, south_side = sides(
            volume, exchange(volume, 3, 4, south_keep, north_keep), 3, 4
        )
        lap_temp = east_side[0] + west_side[0] + north_side[0] + south_side[0] - 4.0 * temp
        lap_salt = east_side[1] + west_side[1] + north_side[1] + south_side[1] - 4.0 * salt
        lap_uvel = east_side[2] + west_side[2] + north_side[2] + south_side[2] - 4.0 * uvel
        lap_vvel = east_side[3] + west_side[3] + north_side[3] + south_side[3] - 4.0 * vvel
        temp_next = ocean * (
            temp
            - STEP_DT
            * 0.5
            * (uvel * (east_side[0] - west_side[0]) + vvel * (north_side[0] - south_side[0]))
            + KAPPA * lap_temp
        )
        salt_next = ocean * (
            salt
            - STEP_DT
            * 0.5
            * (uvel * (east_side[1] - west_side[1]) + vvel * (north_side[1] - south_side[1]))
            + KAPPA * lap_salt
        )
        ustar = ocean * (
            uvel
            + STEP_DT * (coriolis * vvel - 0.5 * (east_side[4] - west_side[4]) - DRAG_K * uvel)
            + VISCOSITY * lap_uvel
        )
        vstar = ocean * (
            vvel
            + STEP_DT * (-coriolis * uvel - 0.5 * (north_side[4] - south_side[4]) - DRAG_K * vvel)
            + VISCOSITY * lap_vvel
        )
        halo = ITERS + 1
        surface = padded_2(
            jnp.stack((jnp.sum(ustar, axis=1), jnp.sum(vstar, axis=1), eta)),
            (("gridy", 2), ("gridx", 3)),
            halo,
        ) * inside
        centre, east_t, west_t, north_t, south_t = around(surface)
        rhs = (centre[2] - DIV_K * 0.5 * (east_t[0] - west_t[0] + (north_t[1] - south_t[1]))) * rows_at(
            inside, halo, halo - 1
        )
        lanes = 128 * ((cols + 2 * halo + 127) // 128)
        rhs_tile = jnp.pad(rhs, ((0, 0), (1, 1), (1, lanes - cols - 2 * halo + 1)))
        solved = surface_kernel_solve(rhs_tile, wide_inside, own_mask)
        eta = solved[0, :, halo : halo + rows, halo : halo + cols]
        east_west = solved[1, :, halo : halo + rows, halo : halo + cols]
        north_south = solved[2, :, halo : halo + rows, halo : halo + cols]
        uvel = ocean * (ustar - GRAV_K * 0.5 * east_west[:, None])
        vvel = ocean * (vstar - GRAV_K * 0.5 * north_south[:, None])
        temp = temp_next
        salt = salt_next
    zonal_scale = 1.0 / jnp.sqrt(jnp.float32(total_cols))
    score_scale = 1.0 / jnp.sqrt(jnp.float32(levels * total_rows))
    lat_weight = latitude / total_rows
    zonal_local = jnp.sum(vvel, axis=3)
    zonal_whole = tree_sum(zonal_local, ("gridx",))
    overturn = jnp.cumsum(zonal_whole, axis=1) * zonal_scale
    score = tree_sum(jnp.sum(overturn * lat_weight, axis=(1, 2)) * score_scale, ("gridy",))
    state_stack = jnp.stack((temp, salt, uvel, vvel))
    every_state, every_eta, every_score = (
        lax.all_gather(state_stack, "member", axis=1, tiled=True),
        lax.all_gather(eta, "member", axis=0, tiled=True),
        lax.all_gather(score, "member", axis=0, tiled=True),
    )
    picked = jnp.take(every_state, clone_source, axis=1)
    new_eta = jnp.take(every_eta, clone_source, axis=0)
    clone_weight = jnp.take(every_score, clone_source, axis=0) - jnp.mean(every_score)
    return (picked[0], picked[1], picked[2], picked[3], new_eta, overturn, clone_weight)


def solution(mesh):
    in_specs = (
        P("member", None, "gridy", "gridx"),
        P("member", None, "gridy", "gridx"),
        P("member", None, "gridy", "gridx"),
        P("member", None, "gridy", "gridx"),
        P("member", "gridy", "gridx"),
        P("gridy", "gridx"),
        P("member"),
    )
    out_specs = (
        P("member", None, "gridy", "gridx"),
        P("member", None, "gridy", "gridx"),
        P("member", None, "gridy", "gridx"),
        P("member", None, "gridy", "gridx"),
        P("member", "gridy", "gridx"),
        P("member", None, "gridy"),
        P("member"),
    )
    return jax.shard_map(shards, mesh=mesh, in_specs=in_specs, out_specs=out_specs, check_vma=False)
```

```python
import functools

import jax
import jax.numpy as jnp
from jax import lax
from jax.experimental import pallas as pl
from jax.experimental.pallas import tpu as pltpu
from jax.sharding import PartitionSpec as P

STEPS = 2
ITERS = 3


ALPHA_T = 0.8
BETA_S = 0.6
PRESS_K = 0.25
STEP_DT = 0.1
KAPPA = 0.1
VISCOSITY = 0.1
DRAG_K = 0.05
CORI_K = 1.0
SURF_C = 4.0
DIV_K = 0.5
GRAV_K = 0.5


def tree_sum(values, axes):
    for axis in axes:
        count = lax.axis_size(axis)
        step = 1
        while step < count:
            pairs = [(i, i ^ step) for i in range(count)]
            values = values + lax.ppermute(values, axis, pairs)
            step *= 2
    return values


def gather_sum_kernel(ny, nx, x_ref, o_ref, recv_y, recv_x, part, send_y, rsem_y, send_x, rsem_x):
    mesh_id = pl.DeviceIdType.MESH
    member = lax.axis_index("member")
    my = lax.axis_index("gridy")
    mx = lax.axis_index("gridx")
    barrier = pltpu.get_barrier_semaphore()
    for d in range(1, ny):
        pl.semaphore_signal(barrier, 1, device_id=(member, (my + d) % ny, mx), device_id_type=mesh_id)
    for d in range(1, nx):
        pl.semaphore_signal(barrier, 1, device_id=(member, my, (mx + d) % nx), device_id_type=mesh_id)
    pl.semaphore_wait(barrier, (ny - 1) + (nx - 1))

    def phase(src, recv, send_sem, recv_sem, count, me, device):
        recv[me] = src[...]
        sent = []
        for d in range(1, count):
            peer = (me + d) % count
            copy = pltpu.make_async_remote_copy(
                src_ref=src,
                dst_ref=recv.at[me],
                send_sem=send_sem.at[peer],
                recv_sem=recv_sem.at[me],
                device_id=device(peer),
                device_id_type=mesh_id,
            )
            copy.start()
            sent.append(copy)
        for d in range(1, count):
            peer = (me + d) % count
            pltpu.make_async_remote_copy(
                src_ref=src,
                dst_ref=recv.at[peer],
                send_sem=send_sem.at[peer],
                recv_sem=recv_sem.at[peer],
                device_id=device(peer),
                device_id_type=mesh_id,
            ).wait_recv()
        for copy in sent:
            copy.wait_send()
        total = recv[0]
        for j in range(1, count):
            total = total + recv[j]
        return total

    part[...] = phase(x_ref, recv_y, send_y, rsem_y, ny, my, lambda p: (member, p, mx))
    o_ref[...] = phase(part, recv_x, send_x, rsem_x, nx, mx, lambda p: (member, my, p))


def grid_sum(values):
    ny = lax.axis_size("gridy")
    nx = lax.axis_size("gridx")
    shape = values.shape
    return pl.pallas_call(
        functools.partial(gather_sum_kernel, ny, nx),
        out_shape=jax.ShapeDtypeStruct(shape, values.dtype),
        in_specs=[pl.BlockSpec(memory_space=pltpu.VMEM)],
        out_specs=pl.BlockSpec(memory_space=pltpu.VMEM),
        scratch_shapes=[
            pltpu.VMEM((ny,) + shape, values.dtype),
            pltpu.VMEM((nx,) + shape, values.dtype),
            pltpu.VMEM(shape, values.dtype),
            pltpu.SemaphoreType.DMA((ny,)),
            pltpu.SemaphoreType.DMA((ny,)),
            pltpu.SemaphoreType.DMA((nx,)),
            pltpu.SemaphoreType.DMA((nx,)),
        ],
        compiler_params=pltpu.CompilerParams(collective_id=0, has_side_effects=True),
    )(values)


def exchange_sum(k, vec, ny, nx, bufs, device_ids):
    send_y, recv_y, send_x, recv_x, sy, ry, sx, rx = bufs
    my, mx, along_y, along_x = device_ids
    mesh_id = pl.DeviceIdType.MESH

    def phase(value, send_buf, recv, send_sem, recv_sem, count, me, device):
        send_buf[k] = value
        recv[k, me] = value
        sent = []
        for d in range(1, count):
            peer = (me + d) % count
            copy = pltpu.make_async_remote_copy(
                src_ref=send_buf.at[k],
                dst_ref=recv.at[k, me],
                send_sem=send_sem.at[k, peer],
                recv_sem=recv_sem.at[k, me],
                device_id=device(peer),
                device_id_type=mesh_id,
            )
            copy.start()
            sent.append(copy)
        for d in range(1, count):
            peer = (me + d) % count
            pltpu.make_async_remote_copy(
                src_ref=send_buf.at[k],
                dst_ref=recv.at[k, peer],
                send_sem=send_sem.at[k, peer],
                recv_sem=recv_sem.at[k, peer],
                device_id=device(peer),
                device_id_type=mesh_id,
            ).wait_recv()
        for copy in sent:
            copy.wait_send()
        total = recv[k, 0]
        for j in range(1, count):
            total = total + recv[k, j]
        return total

    partial = phase(vec, send_y, recv_y, sy, ry, ny, my, along_y)
    return phase(partial, send_x, recv_x, sx, rx, nx, mx, along_x)


def solve_kernel(ny, nx, rhs_ref, inside_ref, own_ref, out_ref, *bufs):
    mesh_id = pl.DeviceIdType.MESH
    member = lax.axis_index("member")
    my = lax.axis_index("gridy")
    mx = lax.axis_index("gridx")
    along_y = lambda p: (member, p, mx)
    along_x = lambda p: (member, my, p)
    barrier = pltpu.get_barrier_semaphore()
    for d in range(1, ny):
        pl.semaphore_signal(barrier, 1, device_id=along_y((my + d) % ny), device_id_type=mesh_id)
    for d in range(1, nx):
        pl.semaphore_signal(barrier, 1, device_id=along_x((mx + d) % nx), device_id_type=mesh_id)
    pl.semaphore_wait(barrier, (ny - 1) + (nx - 1))

    members = rhs_ref.shape[0]
    rows, cols = rhs_ref.shape[1], rhs_ref.shape[2]
    inside = inside_ref[...]
    own = own_ref[...] > 0.5

    def east(f):
        return pltpu.roll(f, cols - 1, 1)

    def west(f):
        return pltpu.roll(f, 1, 1)

    def north(f):
        return pltpu.roll(f, rows - 1, 0)

    def south(f):
        return pltpu.roll(f, 1, 0)

    def apply(f):
        return ((1.0 + 4.0 * SURF_C) * f - SURF_C * (east(f) + west(f) + north(f) + south(f))) * inside

    def total(f):
        return jnp.sum(jnp.where(own, f, 0.0), axis=(0, 1), keepdims=True)

    lane = lax.broadcasted_iota(jnp.int32, (8, 128), 1)
    residual = [rhs_ref[m] for m in range(members)]
    direction = [None] * members
    image_dir = [None] * members
    solution = [None] * members
    gamma_prev = [None] * members
    alpha_prev = [None] * members
    for count in range(ITERS):
        image_res = [apply(residual[m]) for m in range(members)]
        vec = jnp.zeros((8, 128), jnp.float32)
        for m in range(members):
            vec = jnp.where(lane == 2 * m, total(residual[m] * residual[m]), vec)
            vec = jnp.where(lane == 2 * m + 1, total(residual[m] * image_res[m]), vec)
        sums = exchange_sum(count, vec, ny, nx, bufs, (my, mx, along_y, along_x))
        for m in range(members):
            gamma = sums[0:1, 2 * m : 2 * m + 1]
            delta = sums[0:1, 2 * m + 1 : 2 * m + 2]
            if count == 0:
                alpha = gamma / delta
                direction[m] = residual[m]
                image_dir[m] = image_res[m]
                solution[m] = alpha * direction[m]
            else:
                beta = gamma / gamma_prev[m]
                alpha = gamma / (delta - beta * gamma / alpha_prev[m])
                direction[m] = residual[m] + beta * direction[m]
                image_dir[m] = image_res[m] + beta * image_dir[m]
                solution[m] = solution[m] + alpha * direction[m]
            if count < ITERS - 1:
                residual[m] = residual[m] - alpha * image_dir[m]
            gamma_prev[m] = gamma
            alpha_prev[m] = alpha
    for m in range(members):
        x = solution[m]
        out_ref[0, m] = x
        out_ref[1, m] = east(x) - west(x)
        out_ref[2, m] = north(x) - south(x)


def surface_kernel_solve(rhs, inside, own):
    ny = lax.axis_size("gridy")
    nx = lax.axis_size("gridx")
    shape = rhs.shape
    return pl.pallas_call(
        functools.partial(solve_kernel, ny, nx),
        out_shape=jax.ShapeDtypeStruct((3,) + shape, jnp.float32),
        in_specs=[pl.BlockSpec(memory_space=pltpu.VMEM)] * 3,
        out_specs=pl.BlockSpec(memory_space=pltpu.VMEM),
        scratch_shapes=[
            pltpu.VMEM((ITERS, 8, 128), jnp.float32),
            pltpu.VMEM((ITERS, ny, 8, 128), jnp.float32),
            pltpu.VMEM((ITERS, 8, 128), jnp.float32),
            pltpu.VMEM((ITERS, nx, 8, 128), jnp.float32),
            pltpu.SemaphoreType.DMA((ITERS, ny)),
            pltpu.SemaphoreType.DMA((ITERS, ny)),
            pltpu.SemaphoreType.DMA((ITERS, nx)),
            pltpu.SemaphoreType.DMA((ITERS, nx)),
        ],
        compiler_params=pltpu.CompilerParams(collective_id=1, has_side_effects=True),
    )(rhs, inside, own)


def ring(axis):
    count = lax.axis_size(axis)
    forward = [(i, (i + 1) % count) for i in range(count)]
    backward = [((i + 1) % count, i) for i in range(count)]
    return forward, backward


def exchange(block, ydim, xdim, south_keep, north_keep):
    fwd_y, bwd_y = ring("gridy")
    fwd_x, bwd_x = ring("gridx")
    rows = block.shape[ydim]
    cols = block.shape[xdim]
    north = lax.ppermute(lax.slice_in_dim(block, 0, 1, axis=ydim), "gridy", bwd_y) * north_keep
    south = lax.ppermute(lax.slice_in_dim(block, rows - 1, rows, axis=ydim), "gridy", fwd_y) * south_keep
    east = lax.ppermute(lax.slice_in_dim(block, 0, 1, axis=xdim), "gridx", bwd_x)
    west = lax.ppermute(lax.slice_in_dim(block, cols - 1, cols, axis=xdim), "gridx", fwd_x)
    return (east, west, north, south)


def sides(field, rims, ydim, xdim):
    east, west, north, south = rims
    rows = field.shape[ydim]
    cols = field.shape[xdim]
    east_side = jnp.concatenate([lax.slice_in_dim(field, 1, cols, axis=xdim), east], axis=xdim)
    west_side = jnp.concatenate([west, lax.slice_in_dim(field, 0, cols - 1, axis=xdim)], axis=xdim)
    north_side = jnp.concatenate([lax.slice_in_dim(field, 1, rows, axis=ydim), north], axis=ydim)
    south_side = jnp.concatenate([south, lax.slice_in_dim(field, 0, rows - 1, axis=ydim)], axis=ydim)
    return (east_side, west_side, north_side, south_side)


def pressure(temp, salt):
    return PRESS_K * jnp.cumsum(BETA_S * salt - ALPHA_T * temp, axis=-3)


def surface_apply(field, rims):
    east_side, west_side, north_side, south_side = sides(field, rims, 1, 2)
    return (1.0 + 4.0 * SURF_C) * field - SURF_C * (east_side + west_side + north_side + south_side)


def member_total(values):
    return jnp.sum(values, axis=(1, 2))


def widen(values):
    return values[:, None, None]


def combine(a, fa, b, fb):
    def one(u, v):
        left = u if a is None else widen(a) * u
        return left + (v if b is None else widen(b) * v)

    return one(fa[0], fb[0]), tuple(one(u, v) for u, v in zip(fa[1], fb[1]))


def scaled(a, fa):
    return widen(a) * fa[0], tuple(widen(a) * u for u in fa[1])


def padded_2(block, sides_of, width):
    for axis, dim in sides_of:
        count = lax.axis_size(axis)
        forward = [(i, (i + 1) % count) for i in range(count)]
        backward = [((i + 1) % count, i) for i in range(count)]
        size = block.shape[dim]
        low = lax.ppermute(lax.slice_in_dim(block, size - width, size, axis=dim), axis, forward)
        high = lax.ppermute(lax.slice_in_dim(block, 0, width, axis=dim), axis, backward)
        block = jnp.concatenate([low, block, high], axis=dim)
    return block


def crop(field, by):
    if by == 0:
        return field
    return field[..., by:-by, by:-by]


def around(field):
    return (
        field[..., 1:-1, 1:-1],
        field[..., 1:-1, 2:],
        field[..., 1:-1, :-2],
        field[..., 2:, 1:-1],
        field[..., :-2, 1:-1],
    )


def rows_at(inside, full, want):
    cut = full - want
    return inside if cut == 0 else inside[cut:-cut]


def apply_wide(field, inside):
    centre, east, west, north, south = around(field)
    return ((1.0 + 4.0 * SURF_C) * centre - SURF_C * (east + west + north + south)) * inside


def surface_solve(rhs, inside, width, full):
    residual, wide_r = rhs, width
    gamma_prev = None
    alpha_prev = None
    for count in range(ITERS):
        image_res = apply_wide(residual, rows_at(inside, full, wide_r - 1))
        own_res = crop(residual, wide_r)
        own_img = crop(image_res, wide_r - 1)
        dots = grid_sum(jnp.stack([member_total(own_res * own_res), member_total(own_res * own_img)]))
        gamma, delta = dots[0], dots[1]
        if count == 0:
            alpha = gamma / delta
            direction, wide_p = residual, wide_r
            image_dir, wide_s = image_res, wide_r - 1
            solution, wide_x = widen(alpha) * direction, wide_r
        else:
            beta = gamma / gamma_prev
            alpha = gamma / (delta - beta * gamma / alpha_prev)
            direction = residual + widen(beta) * crop(direction, wide_p - wide_r)
            wide_p = wide_r
            image_dir = image_res + widen(beta) * crop(image_dir, wide_s - (wide_r - 1))
            wide_s = wide_r - 1
            solution = crop(solution, wide_x - wide_r) + widen(alpha) * direction
            wide_x = wide_r
        if count < ITERS - 1:
            residual = crop(residual, 1) - widen(alpha) * image_dir
            wide_r -= 1
        gamma_prev = gamma
        alpha_prev = alpha
    return solution


def shards(temp, salt, uvel, vvel, eta, land_mask, clone_source):
    levels = temp.shape[1]
    rows = temp.shape[2]
    cols = temp.shape[3]
    ocean = land_mask.astype(jnp.float32)
    tile_row = lax.axis_index("gridy")
    tile_count = lax.axis_size("gridy")
    total_rows = rows * tile_count
    total_cols = cols * lax.axis_size("gridx")
    south_keep = (tile_row > 0).astype(jnp.float32)
    north_keep = (tile_row < tile_count - 1).astype(jnp.float32)
    latitude = (tile_row * rows + jnp.arange(rows, dtype=jnp.int32)).astype(jnp.float32) + 0.5
    coriolis = (CORI_K * (2.0 * latitude / total_rows - 1.0))[:, None]
    wide_rows = tile_row * rows - (ITERS + 1) + jnp.arange(rows + 2 * (ITERS + 1), dtype=jnp.int32)
    inside = ((wide_rows >= 0) & (wide_rows < total_rows)).astype(jnp.float32)[:, None]
    halo = ITERS + 1
    lanes = 128 * ((cols + 2 * halo + 127) // 128)
    wide_inside = jnp.broadcast_to(inside, (rows + 2 * halo, lanes))
    row_at = lax.broadcasted_iota(jnp.int32, (rows + 2 * halo, lanes), 0)
    col_at = lax.broadcasted_iota(jnp.int32, (rows + 2 * halo, lanes), 1)
    own_mask = (
        (row_at >= halo) & (row_at < halo + rows) & (col_at >= halo) & (col_at < halo + cols)
    ).astype(jnp.float32)
    for count in range(STEPS):
        press = pressure(temp, salt)
        volume = jnp.stack((temp, salt, uvel, vvel, press))
        east_side, west_side, north_side, south_side = sides(
            volume, exchange(volume, 3, 4, south_keep, north_keep), 3, 4
        )
        lap_temp = east_side[0] + west_side[0] + north_side[0] + south_side[0] - 4.0 * temp
        lap_salt = east_side[1] + west_side[1] + north_side[1] + south_side[1] - 4.0 * salt
        lap_uvel = east_side[2] + west_side[2] + north_side[2] + south_side[2] - 4.0 * uvel
        lap_vvel = east_side[3] + west_side[3] + north_side[3] + south_side[3] - 4.0 * vvel
        temp_next = ocean * (
            temp
            - STEP_DT
            * 0.5
            * (uvel * (east_side[0] - west_side[0]) + vvel * (north_side[0] - south_side[0]))
            + KAPPA * lap_temp
        )
        salt_next = ocean * (
            salt
            - STEP_DT
            * 0.5
            * (uvel * (east_side[1] - west_side[1]) + vvel * (north_side[1] - south_side[1]))
            + KAPPA * lap_salt
        )
        ustar = ocean * (
            uvel
            + STEP_DT * (coriolis * vvel - 0.5 * (east_side[4] - west_side[4]) - DRAG_K * uvel)
            + VISCOSITY * lap_uvel
        )
        vstar = ocean * (
            vvel
            + STEP_DT * (-coriolis * uvel - 0.5 * (north_side[4] - south_side[4]) - DRAG_K * vvel)
            + VISCOSITY * lap_vvel
        )
        halo = ITERS + 1
        surface = padded_2(
            jnp.stack((jnp.sum(ustar, axis=1), jnp.sum(vstar, axis=1), eta)),
            (("gridy", 2), ("gridx", 3)),
            halo,
        ) * inside
        centre, east_t, west_t, north_t, south_t = around(surface)
        rhs = (centre[2] - DIV_K * 0.5 * (east_t[0] - west_t[0] + (north_t[1] - south_t[1]))) * rows_at(
            inside, halo, halo - 1
        )
        lanes = 128 * ((cols + 2 * halo + 127) // 128)
        rhs_tile = jnp.pad(rhs, ((0, 0), (1, 1), (1, lanes - cols - 2 * halo + 1)))
        solved = surface_kernel_solve(rhs_tile, wide_inside, own_mask)
        eta = solved[0, :, halo : halo + rows, halo : halo + cols]
        east_west = solved[1, :, halo : halo + rows, halo : halo + cols]
        north_south = solved[2, :, halo : halo + rows, halo : halo + cols]
        uvel = ocean * (ustar - GRAV_K * 0.5 * east_west[:, None])
        vvel = ocean * (vstar - GRAV_K * 0.5 * north_south[:, None])
        if count == STEPS - 1:
            tracers_other = lax.ppermute(jnp.stack((temp_next, salt_next)), "member", [(0, 1), (1, 0)])
        temp = temp_next
        salt = salt_next
    zonal_scale = 1.0 / jnp.sqrt(jnp.float32(total_cols))
    score_scale = 1.0 / jnp.sqrt(jnp.float32(levels * total_rows))
    lat_weight = latitude / total_rows
    members = temp.shape[0]
    zonal_local = jnp.sum(vvel, axis=3)
    depth_weight = (levels - jnp.arange(levels, dtype=jnp.int32)).astype(jnp.float32)
    score_local = jnp.sum(zonal_local * depth_weight[None, :, None] * lat_weight[None, None, :], axis=(1, 2))
    slot = lax.broadcasted_iota(jnp.int32, (tile_count, 1, 1, 1), 0) == tile_row
    zonal_slots = jnp.where(slot, zonal_local[None], 0.0).reshape(-1, 128)
    score_row = jnp.zeros((8, 128), jnp.float32).at[0, :members].set(score_local)
    summed = grid_sum(jnp.concatenate([zonal_slots, score_row], axis=0))
    zonal_whole = summed[: zonal_slots.shape[0]].reshape((tile_count,) + zonal_local.shape)
    zonal_whole = jnp.sum(jnp.where(slot, zonal_whole, 0.0), axis=0)
    overturn = jnp.cumsum(zonal_whole, axis=1) * zonal_scale
    score = summed[zonal_slots.shape[0], :members] * (zonal_scale * score_scale)
    swap = [(0, 1), (1, 0)]
    mine = lax.axis_index("member")
    flows = jnp.concatenate([uvel, vvel, eta[:, None]], axis=1)
    flows_other = lax.ppermute(flows, "member", swap)
    score_other = lax.ppermute(score, "member", swap)
    every_score = jnp.where(
        mine == 0, jnp.concatenate([score, score_other]), jnp.concatenate([score_other, score])
    )
    here = (clone_source // members) == mine
    local_at = clone_source % members

    def pick(local, other):
        chosen_local = jnp.take(local, local_at, axis=0)
        chosen_other = jnp.take(other, local_at, axis=0)
        keep = here.reshape((-1,) + (1,) * (local.ndim - 1))
        return jnp.where(keep, chosen_local, chosen_other)

    new_temp = pick(temp, tracers_other[0])
    new_salt = pick(salt, tracers_other[1])
    new_flows = pick(flows, flows_other)
    clone_weight = jnp.take(every_score, clone_source, axis=0) - jnp.mean(every_score)
    return (
        new_temp,
        new_salt,
        new_flows[:, :levels],
        new_flows[:, levels : 2 * levels],
        new_flows[:, 2 * levels],
        overturn,
        clone_weight,
    )


def solution(mesh):
    in_specs = (
        P("member", None, "gridy", "gridx"),
        P("member", None, "gridy", "gridx"),
        P("member", None, "gridy", "gridx"),
        P("member", None, "gridy", "gridx"),
        P("member", "gridy", "gridx"),
        P("gridy", "gridx"),
        P("member"),
    )
    out_specs = (
        P("member", None, "gridy", "gridx"),
        P("member", None, "gridy", "gridx"),
        P("member", None, "gridy", "gridx"),
        P("member", None, "gridy", "gridx"),
        P("member", "gridy", "gridx"),
        P("member", None, "gridy"),
        P("member"),
    )
    return jax.shard_map(shards, mesh=mesh, in_specs=in_specs, out_specs=out_specs, check_vma=False)
```

```python
import functools

import jax
import jax.numpy as jnp
from jax import lax
from jax.experimental import pallas as pl
from jax.experimental.pallas import tpu as pltpu
from jax.sharding import PartitionSpec as P

STEPS = 2
ITERS = 3


ALPHA_T = 0.8
BETA_S = 0.6
PRESS_K = 0.25
STEP_DT = 0.1
KAPPA = 0.1
VISCOSITY = 0.1
DRAG_K = 0.05
CORI_K = 1.0
SURF_C = 4.0
DIV_K = 0.5
GRAV_K = 0.5


def tree_sum(values, axes):
    for axis in axes:
        count = lax.axis_size(axis)
        step = 1
        while step < count:
            pairs = [(i, i ^ step) for i in range(count)]
            values = values + lax.ppermute(values, axis, pairs)
            step *= 2
    return values


def gather_sum_kernel(ny, nx, x_ref, o_ref, recv_y, recv_x, part, send_y, rsem_y, send_x, rsem_x):
    mesh_id = pl.DeviceIdType.MESH
    member = lax.axis_index("member")
    my = lax.axis_index("gridy")
    mx = lax.axis_index("gridx")
    barrier = pltpu.get_barrier_semaphore()
    for d in range(1, ny):
        pl.semaphore_signal(barrier, 1, device_id=(member, (my + d) % ny, mx), device_id_type=mesh_id)
    for d in range(1, nx):
        pl.semaphore_signal(barrier, 1, device_id=(member, my, (mx + d) % nx), device_id_type=mesh_id)
    pl.semaphore_wait(barrier, (ny - 1) + (nx - 1))

    def phase(src, recv, send_sem, recv_sem, count, me, device):
        recv[me] = src[...]
        sent = []
        for d in range(1, count):
            peer = (me + d) % count
            copy = pltpu.make_async_remote_copy(
                src_ref=src,
                dst_ref=recv.at[me],
                send_sem=send_sem.at[peer],
                recv_sem=recv_sem.at[me],
                device_id=device(peer),
                device_id_type=mesh_id,
            )
            copy.start()
            sent.append(copy)
        for d in range(1, count):
            peer = (me + d) % count
            pltpu.make_async_remote_copy(
                src_ref=src,
                dst_ref=recv.at[peer],
                send_sem=send_sem.at[peer],
                recv_sem=recv_sem.at[peer],
                device_id=device(peer),
                device_id_type=mesh_id,
            ).wait_recv()
        for copy in sent:
            copy.wait_send()
        total = recv[0]
        for j in range(1, count):
            total = total + recv[j]
        return total

    part[...] = phase(x_ref, recv_y, send_y, rsem_y, ny, my, lambda p: (member, p, mx))
    o_ref[...] = phase(part, recv_x, send_x, rsem_x, nx, mx, lambda p: (member, my, p))


def grid_sum(values):
    ny = lax.axis_size("gridy")
    nx = lax.axis_size("gridx")
    shape = values.shape
    return pl.pallas_call(
        functools.partial(gather_sum_kernel, ny, nx),
        out_shape=jax.ShapeDtypeStruct(shape, values.dtype),
        in_specs=[pl.BlockSpec(memory_space=pltpu.VMEM)],
        out_specs=pl.BlockSpec(memory_space=pltpu.VMEM),
        scratch_shapes=[
            pltpu.VMEM((ny,) + shape, values.dtype),
            pltpu.VMEM((nx,) + shape, values.dtype),
            pltpu.VMEM(shape, values.dtype),
            pltpu.SemaphoreType.DMA((ny,)),
            pltpu.SemaphoreType.DMA((ny,)),
            pltpu.SemaphoreType.DMA((nx,)),
            pltpu.SemaphoreType.DMA((nx,)),
        ],
        compiler_params=pltpu.CompilerParams(collective_id=0, has_side_effects=True),
    )(values)


def exchange_sum(k, vec, ny, nx, bufs, device_ids):
    send_y, recv_y, send_x, recv_x, sy, ry, sx, rx = bufs
    my, mx, along_y, along_x = device_ids
    mesh_id = pl.DeviceIdType.MESH

    def phase(value, send_buf, recv, send_sem, recv_sem, count, me, device):
        send_buf[k] = value
        recv[k, me] = value
        sent = []
        for d in range(1, count):
            peer = (me + d) % count
            copy = pltpu.make_async_remote_copy(
                src_ref=send_buf.at[k],
                dst_ref=recv.at[k, me],
                send_sem=send_sem.at[k, peer],
                recv_sem=recv_sem.at[k, me],
                device_id=device(peer),
                device_id_type=mesh_id,
            )
            copy.start()
            sent.append(copy)
        for d in range(1, count):
            peer = (me + d) % count
            pltpu.make_async_remote_copy(
                src_ref=send_buf.at[k],
                dst_ref=recv.at[k, peer],
                send_sem=send_sem.at[k, peer],
                recv_sem=recv_sem.at[k, peer],
                device_id=device(peer),
                device_id_type=mesh_id,
            ).wait_recv()
        for copy in sent:
            copy.wait_send()
        total = recv[k, 0]
        for j in range(1, count):
            total = total + recv[k, j]
        return total

    partial = phase(vec, send_y, recv_y, sy, ry, ny, my, along_y)
    return phase(partial, send_x, recv_x, sx, rx, nx, mx, along_x)


def solve_kernel(ny, nx, rhs_ref, inside_ref, own_ref, out_ref, *bufs):
    mesh_id = pl.DeviceIdType.MESH
    member = lax.axis_index("member")
    my = lax.axis_index("gridy")
    mx = lax.axis_index("gridx")
    along_y = lambda p: (member, p, mx)
    along_x = lambda p: (member, my, p)
    barrier = pltpu.get_barrier_semaphore()
    for d in range(1, ny):
        pl.semaphore_signal(barrier, 1, device_id=along_y((my + d) % ny), device_id_type=mesh_id)
    for d in range(1, nx):
        pl.semaphore_signal(barrier, 1, device_id=along_x((mx + d) % nx), device_id_type=mesh_id)
    pl.semaphore_wait(barrier, (ny - 1) + (nx - 1))

    members = rhs_ref.shape[0]
    rows, cols = rhs_ref.shape[1], rhs_ref.shape[2]
    inside = inside_ref[...]
    own = own_ref[...] > 0.5

    def east(f):
        return pltpu.roll(f, cols - 1, 1)

    def west(f):
        return pltpu.roll(f, 1, 1)

    def north(f):
        return pltpu.roll(f, rows - 1, 0)

    def south(f):
        return pltpu.roll(f, 1, 0)

    def apply(f):
        return ((1.0 + 4.0 * SURF_C) * f - SURF_C * (east(f) + west(f) + north(f) + south(f))) * inside

    def total(f):
        return jnp.sum(jnp.where(own, f, 0.0), axis=(0, 1), keepdims=True)

    lane = lax.broadcasted_iota(jnp.int32, (8, 128), 1)
    residual = [rhs_ref[m] for m in range(members)]
    direction = [None] * members
    image_dir = [None] * members
    solution = [None] * members
    gamma_prev = [None] * members
    alpha_prev = [None] * members
    for count in range(ITERS):
        image_res = [apply(residual[m]) for m in range(members)]
        vec = jnp.zeros((8, 128), jnp.float32)
        for m in range(members):
            vec = jnp.where(lane == 2 * m, total(residual[m] * residual[m]), vec)
            vec = jnp.where(lane == 2 * m + 1, total(residual[m] * image_res[m]), vec)
        sums = exchange_sum(count, vec, ny, nx, bufs, (my, mx, along_y, along_x))
        for m in range(members):
            gamma = sums[0:1, 2 * m : 2 * m + 1]
            delta = sums[0:1, 2 * m + 1 : 2 * m + 2]
            if count == 0:
                alpha = gamma / delta
                direction[m] = residual[m]
                image_dir[m] = image_res[m]
                solution[m] = alpha * direction[m]
            else:
                beta = gamma / gamma_prev[m]
                alpha = gamma / (delta - beta * gamma / alpha_prev[m])
                direction[m] = residual[m] + beta * direction[m]
                image_dir[m] = image_res[m] + beta * image_dir[m]
                solution[m] = solution[m] + alpha * direction[m]
            if count < ITERS - 1:
                residual[m] = residual[m] - alpha * image_dir[m]
            gamma_prev[m] = gamma
            alpha_prev[m] = alpha
    for m in range(members):
        x = solution[m]
        out_ref[0, m] = x
        out_ref[1, m] = east(x) - west(x)
        out_ref[2, m] = north(x) - south(x)


def surface_kernel_solve(rhs, inside, own):
    ny = lax.axis_size("gridy")
    nx = lax.axis_size("gridx")
    shape = rhs.shape
    return pl.pallas_call(
        functools.partial(solve_kernel, ny, nx),
        out_shape=jax.ShapeDtypeStruct((3,) + shape, jnp.float32),
        in_specs=[pl.BlockSpec(memory_space=pltpu.VMEM)] * 3,
        out_specs=pl.BlockSpec(memory_space=pltpu.VMEM),
        scratch_shapes=[
            pltpu.VMEM((ITERS, 8, 128), jnp.float32),
            pltpu.VMEM((ITERS, ny, 8, 128), jnp.float32),
            pltpu.VMEM((ITERS, 8, 128), jnp.float32),
            pltpu.VMEM((ITERS, nx, 8, 128), jnp.float32),
            pltpu.SemaphoreType.DMA((ITERS, ny)),
            pltpu.SemaphoreType.DMA((ITERS, ny)),
            pltpu.SemaphoreType.DMA((ITERS, nx)),
            pltpu.SemaphoreType.DMA((ITERS, nx)),
        ],
        compiler_params=pltpu.CompilerParams(collective_id=1, has_side_effects=True),
    )(rhs, inside, own)


def ring(axis):
    count = lax.axis_size(axis)
    forward = [(i, (i + 1) % count) for i in range(count)]
    backward = [((i + 1) % count, i) for i in range(count)]
    return forward, backward


def exchange(block, ydim, xdim, south_keep, north_keep):
    fwd_y, bwd_y = ring("gridy")
    fwd_x, bwd_x = ring("gridx")
    rows = block.shape[ydim]
    cols = block.shape[xdim]
    north = lax.ppermute(lax.slice_in_dim(block, 0, 1, axis=ydim), "gridy", bwd_y) * north_keep
    south = lax.ppermute(lax.slice_in_dim(block, rows - 1, rows, axis=ydim), "gridy", fwd_y) * south_keep
    east = lax.ppermute(lax.slice_in_dim(block, 0, 1, axis=xdim), "gridx", bwd_x)
    west = lax.ppermute(lax.slice_in_dim(block, cols - 1, cols, axis=xdim), "gridx", fwd_x)
    return (east, west, north, south)


def sides(field, rims, ydim, xdim):
    east, west, north, south = rims
    rows = field.shape[ydim]
    cols = field.shape[xdim]
    east_side = jnp.concatenate([lax.slice_in_dim(field, 1, cols, axis=xdim), east], axis=xdim)
    west_side = jnp.concatenate([west, lax.slice_in_dim(field, 0, cols - 1, axis=xdim)], axis=xdim)
    north_side = jnp.concatenate([lax.slice_in_dim(field, 1, rows, axis=ydim), north], axis=ydim)
    south_side = jnp.concatenate([south, lax.slice_in_dim(field, 0, rows - 1, axis=ydim)], axis=ydim)
    return (east_side, west_side, north_side, south_side)


def pressure(temp, salt):
    return PRESS_K * jnp.cumsum(BETA_S * salt - ALPHA_T * temp, axis=-3)


def surface_apply(field, rims):
    east_side, west_side, north_side, south_side = sides(field, rims, 1, 2)
    return (1.0 + 4.0 * SURF_C) * field - SURF_C * (east_side + west_side + north_side + south_side)


def member_total(values):
    return jnp.sum(values, axis=(1, 2))


def widen(values):
    return values[:, None, None]


def combine(a, fa, b, fb):
    def one(u, v):
        left = u if a is None else widen(a) * u
        return left + (v if b is None else widen(b) * v)

    return one(fa[0], fb[0]), tuple(one(u, v) for u, v in zip(fa[1], fb[1]))


def scaled(a, fa):
    return widen(a) * fa[0], tuple(widen(a) * u for u in fa[1])


def padded_2(block, sides_of, width):
    for axis, dim in sides_of:
        count = lax.axis_size(axis)
        forward = [(i, (i + 1) % count) for i in range(count)]
        backward = [((i + 1) % count, i) for i in range(count)]
        size = block.shape[dim]
        low = lax.ppermute(lax.slice_in_dim(block, size - width, size, axis=dim), axis, forward)
        high = lax.ppermute(lax.slice_in_dim(block, 0, width, axis=dim), axis, backward)
        block = jnp.concatenate([low, block, high], axis=dim)
    return block


def crop(field, by):
    if by == 0:
        return field
    return field[..., by:-by, by:-by]


def around(field):
    return (
        field[..., 1:-1, 1:-1],
        field[..., 1:-1, 2:],
        field[..., 1:-1, :-2],
        field[..., 2:, 1:-1],
        field[..., :-2, 1:-1],
    )


def rows_at(inside, full, want):
    cut = full - want
    return inside if cut == 0 else inside[cut:-cut]


def apply_wide(field, inside):
    centre, east, west, north, south = around(field)
    return ((1.0 + 4.0 * SURF_C) * centre - SURF_C * (east + west + north + south)) * inside


def surface_solve(rhs, inside, width, full):
    residual, wide_r = rhs, width
    gamma_prev = None
    alpha_prev = None
    for count in range(ITERS):
        image_res = apply_wide(residual, rows_at(inside, full, wide_r - 1))
        own_res = crop(residual, wide_r)
        own_img = crop(image_res, wide_r - 1)
        dots = grid_sum(jnp.stack([member_total(own_res * own_res), member_total(own_res * own_img)]))
        gamma, delta = dots[0], dots[1]
        if count == 0:
            alpha = gamma / delta
            direction, wide_p = residual, wide_r
            image_dir, wide_s = image_res, wide_r - 1
            solution, wide_x = widen(alpha) * direction, wide_r
        else:
            beta = gamma / gamma_prev
            alpha = gamma / (delta - beta * gamma / alpha_prev)
            direction = residual + widen(beta) * crop(direction, wide_p - wide_r)
            wide_p = wide_r
            image_dir = image_res + widen(beta) * crop(image_dir, wide_s - (wide_r - 1))
            wide_s = wide_r - 1
            solution = crop(solution, wide_x - wide_r) + widen(alpha) * direction
            wide_x = wide_r
        if count < ITERS - 1:
            residual = crop(residual, 1) - widen(alpha) * image_dir
            wide_r -= 1
        gamma_prev = gamma
        alpha_prev = alpha
    return solution


def shards(temp, salt, uvel, vvel, eta, land_mask, clone_source):
    levels = temp.shape[1]
    rows = temp.shape[2]
    cols = temp.shape[3]
    ocean = land_mask.astype(jnp.float32)
    tile_row = lax.axis_index("gridy")
    tile_count = lax.axis_size("gridy")
    total_rows = rows * tile_count
    total_cols = cols * lax.axis_size("gridx")
    south_keep = (tile_row > 0).astype(jnp.float32)
    north_keep = (tile_row < tile_count - 1).astype(jnp.float32)
    latitude = (tile_row * rows + jnp.arange(rows, dtype=jnp.int32)).astype(jnp.float32) + 0.5
    coriolis = (CORI_K * (2.0 * latitude / total_rows - 1.0))[:, None]
    wide_rows = tile_row * rows - (ITERS + 1) + jnp.arange(rows + 2 * (ITERS + 1), dtype=jnp.int32)
    inside = ((wide_rows >= 0) & (wide_rows < total_rows)).astype(jnp.float32)[:, None]
    halo = ITERS + 1
    lanes = 128 * ((cols + 2 * halo + 127) // 128)
    wide_inside = jnp.broadcast_to(inside, (rows + 2 * halo, lanes))
    row_at = lax.broadcasted_iota(jnp.int32, (rows + 2 * halo, lanes), 0)
    col_at = lax.broadcasted_iota(jnp.int32, (rows + 2 * halo, lanes), 1)
    own_mask = (
        (row_at >= halo) & (row_at < halo + rows) & (col_at >= halo) & (col_at < halo + cols)
    ).astype(jnp.float32)
    for count in range(STEPS):
        press = pressure(temp, salt)
        volume = jnp.stack((temp, salt, uvel, vvel, press))
        east_side, west_side, north_side, south_side = sides(
            volume, exchange(volume, 3, 4, south_keep, north_keep), 3, 4
        )
        lap_temp = east_side[0] + west_side[0] + north_side[0] + south_side[0] - 4.0 * temp
        lap_salt = east_side[1] + west_side[1] + north_side[1] + south_side[1] - 4.0 * salt
        lap_uvel = east_side[2] + west_side[2] + north_side[2] + south_side[2] - 4.0 * uvel
        lap_vvel = east_side[3] + west_side[3] + north_side[3] + south_side[3] - 4.0 * vvel
        temp_next = ocean * (
            temp
            - STEP_DT
            * 0.5
            * (uvel * (east_side[0] - west_side[0]) + vvel * (north_side[0] - south_side[0]))
            + KAPPA * lap_temp
        )
        salt_next = ocean * (
            salt
            - STEP_DT
            * 0.5
            * (uvel * (east_side[1] - west_side[1]) + vvel * (north_side[1] - south_side[1]))
            + KAPPA * lap_salt
        )
        ustar = ocean * (
            uvel
            + STEP_DT * (coriolis * vvel - 0.5 * (east_side[4] - west_side[4]) - DRAG_K * uvel)
            + VISCOSITY * lap_uvel
        )
        vstar = ocean * (
            vvel
            + STEP_DT * (-coriolis * uvel - 0.5 * (north_side[4] - south_side[4]) - DRAG_K * vvel)
            + VISCOSITY * lap_vvel
        )
        halo = ITERS + 1
        surface = padded_2(
            jnp.stack((jnp.sum(ustar, axis=1), jnp.sum(vstar, axis=1), eta)),
            (("gridy", 2), ("gridx", 3)),
            halo,
        ) * inside
        centre, east_t, west_t, north_t, south_t = around(surface)
        rhs = (centre[2] - DIV_K * 0.5 * (east_t[0] - west_t[0] + (north_t[1] - south_t[1]))) * rows_at(
            inside, halo, halo - 1
        )
        lanes = 128 * ((cols + 2 * halo + 127) // 128)
        rhs_tile = jnp.pad(rhs, ((0, 0), (1, 1), (1, lanes - cols - 2 * halo + 1)))
        solved = surface_kernel_solve(rhs_tile, wide_inside, own_mask)
        eta = solved[0, :, halo : halo + rows, halo : halo + cols]
        east_west = solved[1, :, halo : halo + rows, halo : halo + cols]
        north_south = solved[2, :, halo : halo + rows, halo : halo + cols]
        uvel = ocean * (ustar - GRAV_K * 0.5 * east_west[:, None])
        vvel = ocean * (vstar - GRAV_K * 0.5 * north_south[:, None])
        if count == STEPS - 1:
            tracers_other = lax.ppermute(jnp.stack((temp_next, salt_next)), "member", [(0, 1), (1, 0)])
        temp = temp_next
        salt = salt_next
    zonal_scale = 1.0 / jnp.sqrt(jnp.float32(total_cols))
    score_scale = 1.0 / jnp.sqrt(jnp.float32(levels * total_rows))
    lat_weight = latitude / total_rows
    members = temp.shape[0]
    zonal_local = jnp.sum(vvel, axis=3)
    depth_weight = (levels - jnp.arange(levels, dtype=jnp.int32)).astype(jnp.float32)
    score_local = jnp.sum(zonal_local * depth_weight[None, :, None] * lat_weight[None, None, :], axis=(1, 2))
    slot = lax.broadcasted_iota(jnp.int32, (tile_count, 1, 1, 1), 0) == tile_row
    zonal_slots = jnp.where(slot, zonal_local[None], 0.0).reshape(-1, 128)
    score_row = jnp.zeros((8, 128), jnp.float32).at[0, :members].set(score_local)
    summed = grid_sum(jnp.concatenate([zonal_slots, score_row], axis=0))
    zonal_whole = summed[: zonal_slots.shape[0]].reshape((tile_count,) + zonal_local.shape)
    zonal_whole = jnp.sum(jnp.where(slot, zonal_whole, 0.0), axis=0)
    overturn = jnp.cumsum(zonal_whole, axis=1) * zonal_scale
    score = summed[zonal_slots.shape[0], :members] * (zonal_scale * score_scale)
    swap = [(0, 1), (1, 0)]
    mine = lax.axis_index("member")
    score_slab = jnp.zeros((members, 1) + eta.shape[1:], jnp.float32).at[:, 0, 0, 0].set(score)
    flows = jnp.concatenate([uvel, vvel, eta[:, None], score_slab], axis=1)
    flows_other = lax.ppermute(flows, "member", swap)
    score_other = flows_other[:, 2 * levels + 1, 0, 0]
    every_score = jnp.where(
        mine == 0, jnp.concatenate([score, score_other]), jnp.concatenate([score_other, score])
    )
    here = (clone_source // members) == mine
    local_at = clone_source % members

    def pick(local, other):
        chosen = []
        for place in range(members):
            from_here = lax.dynamic_index_in_dim(local, local_at[place], 0, keepdims=False)
            from_other = lax.dynamic_index_in_dim(other, local_at[place], 0, keepdims=False)
            chosen.append(jnp.where(here[place], from_here, from_other))
        return jnp.stack(chosen)

    new_temp = pick(temp, tracers_other[0])
    new_salt = pick(salt, tracers_other[1])
    new_flows = pick(flows[:, : 2 * levels + 1], flows_other[:, : 2 * levels + 1])
    clone_weight = jnp.take(every_score, clone_source, axis=0) - jnp.mean(every_score)
    return (
        new_temp,
        new_salt,
        new_flows[:, :levels],
        new_flows[:, levels : 2 * levels],
        new_flows[:, 2 * levels],
        overturn,
        clone_weight,
    )


def solution(mesh):
    in_specs = (
        P("member", None, "gridy", "gridx"),
        P("member", None, "gridy", "gridx"),
        P("member", None, "gridy", "gridx"),
        P("member", None, "gridy", "gridx"),
        P("member", "gridy", "gridx"),
        P("gridy", "gridx"),
        P("member"),
    )
    out_specs = (
        P("member", None, "gridy", "gridx"),
        P("member", None, "gridy", "gridx"),
        P("member", None, "gridy", "gridx"),
        P("member", None, "gridy", "gridx"),
        P("member", "gridy", "gridx"),
        P("member", None, "gridy"),
        P("member"),
    )
    return jax.shard_map(shards, mesh=mesh, in_specs=in_specs, out_specs=out_specs, check_vma=False)
```

```python
import functools

import jax
import jax.numpy as jnp
from jax import lax
from jax.experimental import pallas as pl
from jax.experimental.pallas import tpu as pltpu
from jax.sharding import PartitionSpec as P

STEPS = 2
ITERS = 3


ALPHA_T = 0.8
BETA_S = 0.6
PRESS_K = 0.25
STEP_DT = 0.1
KAPPA = 0.1
VISCOSITY = 0.1
DRAG_K = 0.05
CORI_K = 1.0
SURF_C = 4.0
DIV_K = 0.5
GRAV_K = 0.5


def tree_sum(values, axes):
    for axis in axes:
        count = lax.axis_size(axis)
        step = 1
        while step < count:
            pairs = [(i, i ^ step) for i in range(count)]
            values = values + lax.ppermute(values, axis, pairs)
            step *= 2
    return values


def gather_sum_kernel(ny, nx, x_ref, o_ref, recv_y, recv_x, part, send_y, rsem_y, send_x, rsem_x):
    mesh_id = pl.DeviceIdType.MESH
    member = lax.axis_index("member")
    my = lax.axis_index("gridy")
    mx = lax.axis_index("gridx")
    barrier = pltpu.get_barrier_semaphore()
    for d in range(1, ny):
        pl.semaphore_signal(barrier, 1, device_id=(member, (my + d) % ny, mx), device_id_type=mesh_id)
    for d in range(1, nx):
        pl.semaphore_signal(barrier, 1, device_id=(member, my, (mx + d) % nx), device_id_type=mesh_id)
    pl.semaphore_wait(barrier, (ny - 1) + (nx - 1))

    def phase(src, recv, send_sem, recv_sem, count, me, device):
        recv[me] = src[...]
        sent = []
        for d in range(1, count):
            peer = (me + d) % count
            copy = pltpu.make_async_remote_copy(
                src_ref=src,
                dst_ref=recv.at[me],
                send_sem=send_sem.at[peer],
                recv_sem=recv_sem.at[me],
                device_id=device(peer),
                device_id_type=mesh_id,
            )
            copy.start()
            sent.append(copy)
        for d in range(1, count):
            peer = (me + d) % count
            pltpu.make_async_remote_copy(
                src_ref=src,
                dst_ref=recv.at[peer],
                send_sem=send_sem.at[peer],
                recv_sem=recv_sem.at[peer],
                device_id=device(peer),
                device_id_type=mesh_id,
            ).wait_recv()
        for copy in sent:
            copy.wait_send()
        total = recv[0]
        for j in range(1, count):
            total = total + recv[j]
        return total

    part[...] = phase(x_ref, recv_y, send_y, rsem_y, ny, my, lambda p: (member, p, mx))
    o_ref[...] = phase(part, recv_x, send_x, rsem_x, nx, mx, lambda p: (member, my, p))


def grid_sum(values):
    ny = lax.axis_size("gridy")
    nx = lax.axis_size("gridx")
    shape = values.shape
    return pl.pallas_call(
        functools.partial(gather_sum_kernel, ny, nx),
        out_shape=jax.ShapeDtypeStruct(shape, values.dtype),
        in_specs=[pl.BlockSpec(memory_space=pltpu.VMEM)],
        out_specs=pl.BlockSpec(memory_space=pltpu.VMEM),
        scratch_shapes=[
            pltpu.VMEM((ny,) + shape, values.dtype),
            pltpu.VMEM((nx,) + shape, values.dtype),
            pltpu.VMEM(shape, values.dtype),
            pltpu.SemaphoreType.DMA((ny,)),
            pltpu.SemaphoreType.DMA((ny,)),
            pltpu.SemaphoreType.DMA((nx,)),
            pltpu.SemaphoreType.DMA((nx,)),
        ],
        compiler_params=pltpu.CompilerParams(collective_id=0, has_side_effects=True),
    )(values)


def exchange_sum(k, vec, ny, nx, bufs, device_ids):
    send_y, recv_y, send_x, recv_x, sy, ry, sx, rx = bufs
    my, mx, along_y, along_x = device_ids
    mesh_id = pl.DeviceIdType.MESH

    def phase(value, send_buf, recv, send_sem, recv_sem, count, me, device):
        send_buf[k] = value
        recv[k, me] = value
        sent = []
        for d in range(1, count):
            peer = (me + d) % count
            copy = pltpu.make_async_remote_copy(
                src_ref=send_buf.at[k],
                dst_ref=recv.at[k, me],
                send_sem=send_sem.at[k, peer],
                recv_sem=recv_sem.at[k, me],
                device_id=device(peer),
                device_id_type=mesh_id,
            )
            copy.start()
            sent.append(copy)
        for d in range(1, count):
            peer = (me + d) % count
            pltpu.make_async_remote_copy(
                src_ref=send_buf.at[k],
                dst_ref=recv.at[k, peer],
                send_sem=send_sem.at[k, peer],
                recv_sem=recv_sem.at[k, peer],
                device_id=device(peer),
                device_id_type=mesh_id,
            ).wait_recv()
        for copy in sent:
            copy.wait_send()
        total = recv[k, 0]
        for j in range(1, count):
            total = total + recv[k, j]
        return total

    partial = phase(vec, send_y, recv_y, sy, ry, ny, my, along_y)
    return phase(partial, send_x, recv_x, sx, rx, nx, mx, along_x)


def solve_kernel(ny, nx, rhs_ref, inside_ref, own_ref, out_ref, *bufs):
    mesh_id = pl.DeviceIdType.MESH
    member = lax.axis_index("member")
    my = lax.axis_index("gridy")
    mx = lax.axis_index("gridx")
    along_y = lambda p: (member, p, mx)
    along_x = lambda p: (member, my, p)
    barrier = pltpu.get_barrier_semaphore()
    for d in range(1, ny):
        pl.semaphore_signal(barrier, 1, device_id=along_y((my + d) % ny), device_id_type=mesh_id)
    for d in range(1, nx):
        pl.semaphore_signal(barrier, 1, device_id=along_x((mx + d) % nx), device_id_type=mesh_id)
    pl.semaphore_wait(barrier, (ny - 1) + (nx - 1))

    members = rhs_ref.shape[0]
    rows, cols = rhs_ref.shape[1], rhs_ref.shape[2]
    inside = inside_ref[...]
    own = own_ref[...] > 0.5

    def east(f):
        return pltpu.roll(f, cols - 1, 1)

    def west(f):
        return pltpu.roll(f, 1, 1)

    def north(f):
        return pltpu.roll(f, rows - 1, 0)

    def south(f):
        return pltpu.roll(f, 1, 0)

    def apply(f):
        return ((1.0 + 4.0 * SURF_C) * f - SURF_C * (east(f) + west(f) + north(f) + south(f))) * inside

    def total(f):
        return jnp.sum(jnp.where(own, f, 0.0), axis=(0, 1), keepdims=True)

    lane = lax.broadcasted_iota(jnp.int32, (8, 128), 1)
    residual = [rhs_ref[m] for m in range(members)]
    direction = [None] * members
    image_dir = [None] * members
    solution = [None] * members
    gamma_prev = [None] * members
    alpha_prev = [None] * members
    for count in range(ITERS):
        image_res = [apply(residual[m]) for m in range(members)]
        vec = jnp.zeros((8, 128), jnp.float32)
        for m in range(members):
            vec = jnp.where(lane == 2 * m, total(residual[m] * residual[m]), vec)
            vec = jnp.where(lane == 2 * m + 1, total(residual[m] * image_res[m]), vec)
        sums = exchange_sum(count, vec, ny, nx, bufs, (my, mx, along_y, along_x))
        for m in range(members):
            gamma = sums[0:1, 2 * m : 2 * m + 1]
            delta = sums[0:1, 2 * m + 1 : 2 * m + 2]
            if count == 0:
                alpha = gamma / delta
                direction[m] = residual[m]
                image_dir[m] = image_res[m]
                solution[m] = alpha * direction[m]
            else:
                beta = gamma / gamma_prev[m]
                alpha = gamma / (delta - beta * gamma / alpha_prev[m])
                direction[m] = residual[m] + beta * direction[m]
                image_dir[m] = image_res[m] + beta * image_dir[m]
                solution[m] = solution[m] + alpha * direction[m]
            if count < ITERS - 1:
                residual[m] = residual[m] - alpha * image_dir[m]
            gamma_prev[m] = gamma
            alpha_prev[m] = alpha
    for m in range(members):
        x = solution[m]
        out_ref[0, m] = x
        out_ref[1, m] = east(x) - west(x)
        out_ref[2, m] = north(x) - south(x)


def surface_kernel_solve(rhs, inside, own):
    ny = lax.axis_size("gridy")
    nx = lax.axis_size("gridx")
    shape = rhs.shape
    return pl.pallas_call(
        functools.partial(solve_kernel, ny, nx),
        out_shape=jax.ShapeDtypeStruct((3,) + shape, jnp.float32),
        in_specs=[pl.BlockSpec(memory_space=pltpu.VMEM)] * 3,
        out_specs=pl.BlockSpec(memory_space=pltpu.VMEM),
        scratch_shapes=[
            pltpu.VMEM((ITERS, 8, 128), jnp.float32),
            pltpu.VMEM((ITERS, ny, 8, 128), jnp.float32),
            pltpu.VMEM((ITERS, 8, 128), jnp.float32),
            pltpu.VMEM((ITERS, nx, 8, 128), jnp.float32),
            pltpu.SemaphoreType.DMA((ITERS, ny)),
            pltpu.SemaphoreType.DMA((ITERS, ny)),
            pltpu.SemaphoreType.DMA((ITERS, nx)),
            pltpu.SemaphoreType.DMA((ITERS, nx)),
        ],
        compiler_params=pltpu.CompilerParams(collective_id=1, has_side_effects=True),
    )(rhs, inside, own)


def volume_kernel(temp_ref, salt_ref, uvel_ref, vvel_ref, ocean_ref, cor_ref, n_ref, s_ref, e_ref, w_ref,
                  tn_ref, sn_ref, us_ref, vs_ref, tu_ref, tv_ref):
    levels, rows, cols = temp_ref.shape[1], temp_ref.shape[2], temp_ref.shape[3]
    row = lax.broadcasted_iota(jnp.int32, (rows, cols), 0)
    col = lax.broadcasted_iota(jnp.int32, (rows, cols), 1)
    top = row == rows - 1
    bottom = row == 0
    right = col == cols - 1
    left = col == 0
    ocean = ocean_ref[...]
    cor = cor_ref[...]

    def around(f, rims):
        n, s, e, w = rims
        return (
            jnp.where(right, e, pltpu.roll(f, cols - 1, 1)),
            jnp.where(left, w, pltpu.roll(f, 1, 1)),
            jnp.where(top, n, pltpu.roll(f, rows - 1, 0)),
            jnp.where(bottom, s, pltpu.roll(f, 1, 0)),
        )

    def rims_of(k, l):
        return (n_ref[k, 0, l], s_ref[k, 0, l], e_ref[k, 0, l], w_ref[k, 0, l])

    running = None
    running_rims = None
    tu = None
    tv = None
    for l in range(levels):
        t = temp_ref[0, l]
        s = salt_ref[0, l]
        u = uvel_ref[0, l]
        v = vvel_ref[0, l]
        rt, rs, ru, rv = rims_of(0, l), rims_of(1, l), rims_of(2, l), rims_of(3, l)
        layer = BETA_S * s - ALPHA_T * t
        layer_rims = tuple(BETA_S * b - ALPHA_T * a for a, b in zip(rt, rs))
        if running is None:
            running, running_rims = layer, layer_rims
        else:
            running = running + layer
            running_rims = tuple(a + b for a, b in zip(running_rims, layer_rims))
        press = PRESS_K * running
        press_rims = tuple(PRESS_K * a for a in running_rims)
        te, tw, tn, ts = around(t, rt)
        se, sw, sn, ss = around(s, rs)
        ue, uw, un, us = around(u, ru)
        ve, vw, vn, vs = around(v, rv)
        pe, pw, pn, ps = around(press, press_rims)
        tn_ref[0, l] = ocean * (
            t - STEP_DT * 0.5 * (u * (te - tw) + v * (tn - ts)) + KAPPA * (te + tw + tn + ts - 4.0 * t)
        )
        sn_ref[0, l] = ocean * (
            s - STEP_DT * 0.5 * (u * (se - sw) + v * (sn - ss)) + KAPPA * (se + sw + sn + ss - 4.0 * s)
        )
        ustar = ocean * (
            u + STEP_DT * (cor * v - 0.5 * (pe - pw) - DRAG_K * u) + VISCOSITY * (ue + uw + un + us - 4.0 * u)
        )
        vstar = ocean * (
            v + STEP_DT * (-cor * u - 0.5 * (pn - ps) - DRAG_K * v) + VISCOSITY * (ve + vw + vn + vs - 4.0 * v)
        )
        us_ref[0, l] = ustar
        vs_ref[0, l] = vstar
        tu = ustar if tu is None else tu + ustar
        tv = vstar if tv is None else tv + vstar
    tu_ref[0] = tu
    tv_ref[0] = tv


def volume_step(temp, salt, uvel, vvel, ocean, cor_tile, rims):
    members, levels, rows, cols = temp.shape
    field = pl.BlockSpec((1, levels, rows, cols), lambda m: (m, 0, 0, 0))
    plane = pl.BlockSpec((rows, cols), lambda m: (0, 0))
    north, south, east, west = rims
    row_rim = pl.BlockSpec((4, 1, levels, 1, cols), lambda m: (0, m, 0, 0, 0))
    col_rim = pl.BlockSpec((4, 1, levels, rows, 1), lambda m: (0, m, 0, 0, 0))
    surface = pl.BlockSpec((1, rows, cols), lambda m: (m, 0, 0))
    volume_shape = jax.ShapeDtypeStruct(temp.shape, jnp.float32)
    surface_shape = jax.ShapeDtypeStruct((members, rows, cols), jnp.float32)
    return pl.pallas_call(
        volume_kernel,
        grid=(members,),
        in_specs=[field] * 4 + [plane, plane, row_rim, row_rim, col_rim, col_rim],
        out_specs=[field] * 4 + [surface] * 2,
        out_shape=[volume_shape] * 4 + [surface_shape] * 2,
    )(temp, salt, uvel, vvel, ocean, cor_tile, north, south, east, west)


def ring(axis):
    count = lax.axis_size(axis)
    forward = [(i, (i + 1) % count) for i in range(count)]
    backward = [((i + 1) % count, i) for i in range(count)]
    return forward, backward


def exchange(block, ydim, xdim, south_keep, north_keep):
    fwd_y, bwd_y = ring("gridy")
    fwd_x, bwd_x = ring("gridx")
    rows = block.shape[ydim]
    cols = block.shape[xdim]
    north = lax.ppermute(lax.slice_in_dim(block, 0, 1, axis=ydim), "gridy", bwd_y) * north_keep
    south = lax.ppermute(lax.slice_in_dim(block, rows - 1, rows, axis=ydim), "gridy", fwd_y) * south_keep
    east = lax.ppermute(lax.slice_in_dim(block, 0, 1, axis=xdim), "gridx", bwd_x)
    west = lax.ppermute(lax.slice_in_dim(block, cols - 1, cols, axis=xdim), "gridx", fwd_x)
    return (east, west, north, south)


def exchange_fields(fields, south_keep, north_keep):
    fwd_y, bwd_y = ring("gridy")
    fwd_x, bwd_x = ring("gridx")
    north = lax.ppermute(jnp.stack([f[..., :1, :] for f in fields]), "gridy", bwd_y) * north_keep
    south = lax.ppermute(jnp.stack([f[..., -1:, :] for f in fields]), "gridy", fwd_y) * south_keep
    east = lax.ppermute(jnp.stack([f[..., :, :1] for f in fields]), "gridx", bwd_x)
    west = lax.ppermute(jnp.stack([f[..., :, -1:] for f in fields]), "gridx", fwd_x)
    return (north, south, east, west)


def sides(field, rims, ydim, xdim):
    east, west, north, south = rims
    rows = field.shape[ydim]
    cols = field.shape[xdim]
    east_side = jnp.concatenate([lax.slice_in_dim(field, 1, cols, axis=xdim), east], axis=xdim)
    west_side = jnp.concatenate([west, lax.slice_in_dim(field, 0, cols - 1, axis=xdim)], axis=xdim)
    north_side = jnp.concatenate([lax.slice_in_dim(field, 1, rows, axis=ydim), north], axis=ydim)
    south_side = jnp.concatenate([south, lax.slice_in_dim(field, 0, rows - 1, axis=ydim)], axis=ydim)
    return (east_side, west_side, north_side, south_side)


def pressure(temp, salt):
    return PRESS_K * jnp.cumsum(BETA_S * salt - ALPHA_T * temp, axis=-3)


def surface_apply(field, rims):
    east_side, west_side, north_side, south_side = sides(field, rims, 1, 2)
    return (1.0 + 4.0 * SURF_C) * field - SURF_C * (east_side + west_side + north_side + south_side)


def member_total(values):
    return jnp.sum(values, axis=(1, 2))


def widen(values):
    return values[:, None, None]


def combine(a, fa, b, fb):
    def one(u, v):
        left = u if a is None else widen(a) * u
        return left + (v if b is None else widen(b) * v)

    return one(fa[0], fb[0]), tuple(one(u, v) for u, v in zip(fa[1], fb[1]))


def scaled(a, fa):
    return widen(a) * fa[0], tuple(widen(a) * u for u in fa[1])


def padded_2(block, sides_of, width):
    for axis, dim in sides_of:
        count = lax.axis_size(axis)
        forward = [(i, (i + 1) % count) for i in range(count)]
        backward = [((i + 1) % count, i) for i in range(count)]
        size = block.shape[dim]
        low = lax.ppermute(lax.slice_in_dim(block, size - width, size, axis=dim), axis, forward)
        high = lax.ppermute(lax.slice_in_dim(block, 0, width, axis=dim), axis, backward)
        block = jnp.concatenate([low, block, high], axis=dim)
    return block


def crop(field, by):
    if by == 0:
        return field
    return field[..., by:-by, by:-by]


def around(field):
    return (
        field[..., 1:-1, 1:-1],
        field[..., 1:-1, 2:],
        field[..., 1:-1, :-2],
        field[..., 2:, 1:-1],
        field[..., :-2, 1:-1],
    )


def rows_at(inside, full, want):
    cut = full - want
    return inside if cut == 0 else inside[cut:-cut]


def apply_wide(field, inside):
    centre, east, west, north, south = around(field)
    return ((1.0 + 4.0 * SURF_C) * centre - SURF_C * (east + west + north + south)) * inside


def surface_solve(rhs, inside, width, full):
    residual, wide_r = rhs, width
    gamma_prev = None
    alpha_prev = None
    for count in range(ITERS):
        image_res = apply_wide(residual, rows_at(inside, full, wide_r - 1))
        own_res = crop(residual, wide_r)
        own_img = crop(image_res, wide_r - 1)
        dots = grid_sum(jnp.stack([member_total(own_res * own_res), member_total(own_res * own_img)]))
        gamma, delta = dots[0], dots[1]
        if count == 0:
            alpha = gamma / delta
            direction, wide_p = residual, wide_r
            image_dir, wide_s = image_res, wide_r - 1
            solution, wide_x = widen(alpha) * direction, wide_r
        else:
            beta = gamma / gamma_prev
            alpha = gamma / (delta - beta * gamma / alpha_prev)
            direction = residual + widen(beta) * crop(direction, wide_p - wide_r)
            wide_p = wide_r
            image_dir = image_res + widen(beta) * crop(image_dir, wide_s - (wide_r - 1))
            wide_s = wide_r - 1
            solution = crop(solution, wide_x - wide_r) + widen(alpha) * direction
            wide_x = wide_r
        if count < ITERS - 1:
            residual = crop(residual, 1) - widen(alpha) * image_dir
            wide_r -= 1
        gamma_prev = gamma
        alpha_prev = alpha
    return solution


def shards(temp, salt, uvel, vvel, eta, land_mask, clone_source):
    levels = temp.shape[1]
    rows = temp.shape[2]
    cols = temp.shape[3]
    ocean = land_mask.astype(jnp.float32)
    tile_row = lax.axis_index("gridy")
    tile_count = lax.axis_size("gridy")
    total_rows = rows * tile_count
    total_cols = cols * lax.axis_size("gridx")
    south_keep = (tile_row > 0).astype(jnp.float32)
    north_keep = (tile_row < tile_count - 1).astype(jnp.float32)
    latitude = (tile_row * rows + jnp.arange(rows, dtype=jnp.int32)).astype(jnp.float32) + 0.5
    coriolis = (CORI_K * (2.0 * latitude / total_rows - 1.0))[:, None]
    cor_tile = jnp.broadcast_to(coriolis, (rows, cols))
    wide_rows = tile_row * rows - (ITERS + 1) + jnp.arange(rows + 2 * (ITERS + 1), dtype=jnp.int32)
    inside = ((wide_rows >= 0) & (wide_rows < total_rows)).astype(jnp.float32)[:, None]
    halo = ITERS + 1
    lanes = 128 * ((cols + 2 * halo + 127) // 128)
    wide_inside = jnp.broadcast_to(inside, (rows + 2 * halo, lanes))
    row_at = lax.broadcasted_iota(jnp.int32, (rows + 2 * halo, lanes), 0)
    col_at = lax.broadcasted_iota(jnp.int32, (rows + 2 * halo, lanes), 1)
    own_mask = (
        (row_at >= halo) & (row_at < halo + rows) & (col_at >= halo) & (col_at < halo + cols)
    ).astype(jnp.float32)
    for count in range(STEPS):
        fields = (temp, salt, uvel, vvel)
        rims = exchange_fields(fields, south_keep, north_keep)
        temp_next, salt_next, ustar, vstar, trans_u, trans_v = volume_step(
            temp, salt, uvel, vvel, ocean, cor_tile, rims
        )
        halo = ITERS + 1
        surface = padded_2(
            jnp.stack((trans_u, trans_v, eta)),
            (("gridy", 2), ("gridx", 3)),
            halo,
        ) * inside
        centre, east_t, west_t, north_t, south_t = around(surface)
        rhs = (centre[2] - DIV_K * 0.5 * (east_t[0] - west_t[0] + (north_t[1] - south_t[1]))) * rows_at(
            inside, halo, halo - 1
        )
        lanes = 128 * ((cols + 2 * halo + 127) // 128)
        rhs_tile = jnp.pad(rhs, ((0, 0), (1, 1), (1, lanes - cols - 2 * halo + 1)))
        solved = surface_kernel_solve(rhs_tile, wide_inside, own_mask)
        eta = solved[0, :, halo : halo + rows, halo : halo + cols]
        east_west = solved[1, :, halo : halo + rows, halo : halo + cols]
        north_south = solved[2, :, halo : halo + rows, halo : halo + cols]
        uvel = ocean * (ustar - GRAV_K * 0.5 * east_west[:, None])
        vvel = ocean * (vstar - GRAV_K * 0.5 * north_south[:, None])
        if count == STEPS - 1:
            tracers_other = lax.ppermute(jnp.stack((temp_next, salt_next)), "member", [(0, 1), (1, 0)])
        temp = temp_next
        salt = salt_next
    zonal_scale = 1.0 / jnp.sqrt(jnp.float32(total_cols))
    score_scale = 1.0 / jnp.sqrt(jnp.float32(levels * total_rows))
    lat_weight = latitude / total_rows
    members = temp.shape[0]
    zonal_local = jnp.sum(vvel, axis=3)
    depth_weight = (levels - jnp.arange(levels, dtype=jnp.int32)).astype(jnp.float32)
    score_local = jnp.sum(zonal_local * depth_weight[None, :, None] * lat_weight[None, None, :], axis=(1, 2))
    slot = lax.broadcasted_iota(jnp.int32, (tile_count, 1, 1, 1), 0) == tile_row
    zonal_slots = jnp.where(slot, zonal_local[None], 0.0).reshape(-1, 128)
    score_row = jnp.zeros((8, 128), jnp.float32).at[0, :members].set(score_local)
    summed = grid_sum(jnp.concatenate([zonal_slots, score_row], axis=0))
    zonal_whole = summed[: zonal_slots.shape[0]].reshape((tile_count,) + zonal_local.shape)
    zonal_whole = jnp.sum(jnp.where(slot, zonal_whole, 0.0), axis=0)
    overturn = jnp.cumsum(zonal_whole, axis=1) * zonal_scale
    score = summed[zonal_slots.shape[0], :members] * (zonal_scale * score_scale)
    swap = [(0, 1), (1, 0)]
    mine = lax.axis_index("member")
    score_slab = jnp.zeros((members, 1) + eta.shape[1:], jnp.float32).at[:, 0, 0, 0].set(score)
    flows = jnp.concatenate([uvel, vvel, eta[:, None], score_slab], axis=1)
    flows_other = lax.ppermute(flows, "member", swap)
    score_other = flows_other[:, 2 * levels + 1, 0, 0]
    every_score = jnp.where(
        mine == 0, jnp.concatenate([score, score_other]), jnp.concatenate([score_other, score])
    )
    here = (clone_source // members) == mine
    local_at = clone_source % members

    def pick(local, other):
        chosen = []
        for place in range(members):
            from_here = lax.dynamic_index_in_dim(local, local_at[place], 0, keepdims=False)
            from_other = lax.dynamic_index_in_dim(other, local_at[place], 0, keepdims=False)
            chosen.append(jnp.where(here[place], from_here, from_other))
        return jnp.stack(chosen)

    new_temp = pick(temp, tracers_other[0])
    new_salt = pick(salt, tracers_other[1])
    new_flows = pick(flows[:, : 2 * levels + 1], flows_other[:, : 2 * levels + 1])
    clone_weight = jnp.take(every_score, clone_source, axis=0) - jnp.mean(every_score)
    return (
        new_temp,
        new_salt,
        new_flows[:, :levels],
        new_flows[:, levels : 2 * levels],
        new_flows[:, 2 * levels],
        overturn,
        clone_weight,
    )


def solution(mesh):
    in_specs = (
        P("member", None, "gridy", "gridx"),
        P("member", None, "gridy", "gridx"),
        P("member", None, "gridy", "gridx"),
        P("member", None, "gridy", "gridx"),
        P("member", "gridy", "gridx"),
        P("gridy", "gridx"),
        P("member"),
    )
    out_specs = (
        P("member", None, "gridy", "gridx"),
        P("member", None, "gridy", "gridx"),
        P("member", None, "gridy", "gridx"),
        P("member", None, "gridy", "gridx"),
        P("member", "gridy", "gridx"),
        P("member", None, "gridy"),
        P("member"),
    )
    return jax.shard_map(shards, mesh=mesh, in_specs=in_specs, out_specs=out_specs, check_vma=False)
```

```python
import functools

import jax
import jax.numpy as jnp
from jax import lax
from jax.experimental import pallas as pl
from jax.experimental.pallas import tpu as pltpu
from jax.sharding import PartitionSpec as P

STEPS = 2
ITERS = 3


ALPHA_T = 0.8
BETA_S = 0.6
PRESS_K = 0.25
STEP_DT = 0.1
KAPPA = 0.1
VISCOSITY = 0.1
DRAG_K = 0.05
CORI_K = 1.0
SURF_C = 4.0
DIV_K = 0.5
GRAV_K = 0.5


def tree_sum(values, axes):
    for axis in axes:
        count = lax.axis_size(axis)
        step = 1
        while step < count:
            pairs = [(i, i ^ step) for i in range(count)]
            values = values + lax.ppermute(values, axis, pairs)
            step *= 2
    return values


def gather_sum_kernel(ny, nx, x_ref, o_ref, recv_y, recv_x, part, send_y, rsem_y, send_x, rsem_x):
    mesh_id = pl.DeviceIdType.MESH
    member = lax.axis_index("member")
    my = lax.axis_index("gridy")
    mx = lax.axis_index("gridx")
    barrier = pltpu.get_barrier_semaphore()
    for d in range(1, ny):
        pl.semaphore_signal(barrier, 1, device_id=(member, (my + d) % ny, mx), device_id_type=mesh_id)
    for d in range(1, nx):
        pl.semaphore_signal(barrier, 1, device_id=(member, my, (mx + d) % nx), device_id_type=mesh_id)
    pl.semaphore_wait(barrier, (ny - 1) + (nx - 1))

    def phase(src, recv, send_sem, recv_sem, count, me, device):
        recv[me] = src[...]
        sent = []
        for d in range(1, count):
            peer = (me + d) % count
            copy = pltpu.make_async_remote_copy(
                src_ref=src,
                dst_ref=recv.at[me],
                send_sem=send_sem.at[peer],
                recv_sem=recv_sem.at[me],
                device_id=device(peer),
                device_id_type=mesh_id,
            )
            copy.start()
            sent.append(copy)
        for d in range(1, count):
            peer = (me + d) % count
            pltpu.make_async_remote_copy(
                src_ref=src,
                dst_ref=recv.at[peer],
                send_sem=send_sem.at[peer],
                recv_sem=recv_sem.at[peer],
                device_id=device(peer),
                device_id_type=mesh_id,
            ).wait_recv()
        for copy in sent:
            copy.wait_send()
        total = recv[0]
        for j in range(1, count):
            total = total + recv[j]
        return total

    part[...] = phase(x_ref, recv_y, send_y, rsem_y, ny, my, lambda p: (member, p, mx))
    o_ref[...] = phase(part, recv_x, send_x, rsem_x, nx, mx, lambda p: (member, my, p))


def grid_sum(values):
    ny = lax.axis_size("gridy")
    nx = lax.axis_size("gridx")
    shape = values.shape
    return pl.pallas_call(
        functools.partial(gather_sum_kernel, ny, nx),
        out_shape=jax.ShapeDtypeStruct(shape, values.dtype),
        in_specs=[pl.BlockSpec(memory_space=pltpu.VMEM)],
        out_specs=pl.BlockSpec(memory_space=pltpu.VMEM),
        scratch_shapes=[
            pltpu.VMEM((ny,) + shape, values.dtype),
            pltpu.VMEM((nx,) + shape, values.dtype),
            pltpu.VMEM(shape, values.dtype),
            pltpu.SemaphoreType.DMA((ny,)),
            pltpu.SemaphoreType.DMA((ny,)),
            pltpu.SemaphoreType.DMA((nx,)),
            pltpu.SemaphoreType.DMA((nx,)),
        ],
        compiler_params=pltpu.CompilerParams(collective_id=0, has_side_effects=True),
    )(values)


def exchange_sum(k, vec, ny, nx, bufs, device_ids):
    send_y, recv_y, send_x, recv_x, sy, ry, sx, rx = bufs
    my, mx, along_y, along_x = device_ids
    mesh_id = pl.DeviceIdType.MESH

    def phase(value, send_buf, recv, send_sem, recv_sem, count, me, device):
        send_buf[k] = value
        recv[k, me] = value
        sent = []
        for d in range(1, count):
            peer = (me + d) % count
            copy = pltpu.make_async_remote_copy(
                src_ref=send_buf.at[k],
                dst_ref=recv.at[k, me],
                send_sem=send_sem.at[k, peer],
                recv_sem=recv_sem.at[k, me],
                device_id=device(peer),
                device_id_type=mesh_id,
            )
            copy.start()
            sent.append(copy)
        for d in range(1, count):
            peer = (me + d) % count
            pltpu.make_async_remote_copy(
                src_ref=send_buf.at[k],
                dst_ref=recv.at[k, peer],
                send_sem=send_sem.at[k, peer],
                recv_sem=recv_sem.at[k, peer],
                device_id=device(peer),
                device_id_type=mesh_id,
            ).wait_recv()
        for copy in sent:
            copy.wait_send()
        total = recv[k, 0]
        for j in range(1, count):
            total = total + recv[k, j]
        return total

    partial = phase(vec, send_y, recv_y, sy, ry, ny, my, along_y)
    return phase(partial, send_x, recv_x, sx, rx, nx, mx, along_x)


def solve_kernel(ny, nx, surf_ref, inside_ref, own_ref, out_ref, frame, hsend, hrecv, *bufs):
    mesh_id = pl.DeviceIdType.MESH
    member = lax.axis_index("member")
    my = lax.axis_index("gridy")
    mx = lax.axis_index("gridx")
    along_y = lambda p: (member, p, mx)
    along_x = lambda p: (member, my, p)
    barrier = pltpu.get_barrier_semaphore()
    for d in range(1, ny):
        pl.semaphore_signal(barrier, 1, device_id=along_y((my + d) % ny), device_id_type=mesh_id)
    for d in range(1, nx):
        pl.semaphore_signal(barrier, 1, device_id=along_x((mx + d) % nx), device_id_type=mesh_id)
    rows, cols = surf_ref.shape[2], surf_ref.shape[3]
    wide_rows, wide_cols = frame.shape[2], frame.shape[3]
    band = (wide_rows - rows) // 2
    block = (wide_cols - cols) // 2
    frame[:, :, 0:rows, 0:cols] = surf_ref[...]
    pl.semaphore_wait(barrier, (ny - 1) + (nx - 1))

    def halo_copies(first, moves):
        started = []
        for slot, (src, dst, device) in enumerate(moves, start=first):
            copy = pltpu.make_async_remote_copy(
                src_ref=src, dst_ref=dst, send_sem=hsend.at[slot], recv_sem=hrecv.at[slot],
                device_id=device, device_id_type=mesh_id,
            )
            copy.start()
            started.append(copy)
        for copy in started:
            copy.wait()

    halo_copies(0, [
        (frame.at[:, :, 0:band, 0:cols], frame.at[:, :, rows : rows + band, 0:cols], along_y((my + ny - 1) % ny)),
        (frame.at[:, :, rows - band : rows, 0:cols], frame.at[:, :, rows + band : wide_rows, 0:cols],
         along_y((my + 1) % ny)),
    ])
    halo_copies(2, [
        (frame.at[:, :, :, 0:block], frame.at[:, :, :, cols : cols + block], along_x((mx + nx - 1) % nx)),
        (frame.at[:, :, :, cols - block : cols], frame.at[:, :, :, cols + block : wide_cols],
         along_x((mx + 1) % nx)),
    ])

    members = surf_ref.shape[1]
    inside = inside_ref[...]
    own = own_ref[...] > 0.5

    def east(f):
        return pltpu.roll(f, wide_cols - 1, 1)

    def west(f):
        return pltpu.roll(f, 1, 1)

    def north(f):
        return pltpu.roll(f, wide_rows - 1, 0)

    def south(f):
        return pltpu.roll(f, 1, 0)

    def apply(f):
        return ((1.0 + 4.0 * SURF_C) * f - SURF_C * (east(f) + west(f) + north(f) + south(f))) * inside

    def total(f):
        return jnp.sum(jnp.where(own, f, 0.0), axis=(0, 1), keepdims=True)

    residual = []
    for m in range(members):
        trans_u = frame[0, m] * inside
        trans_v = frame[1, m] * inside
        level = frame[2, m] * inside
        residual.append(
            (level - DIV_K * 0.5 * (east(trans_u) - west(trans_u) + (north(trans_v) - south(trans_v)))) * inside
        )
    lane = lax.broadcasted_iota(jnp.int32, (8, 128), 1)
    direction = [None] * members
    image_dir = [None] * members
    solution = [None] * members
    gamma_prev = [None] * members
    alpha_prev = [None] * members
    for count in range(ITERS):
        image_res = [apply(residual[m]) for m in range(members)]
        vec = jnp.zeros((8, 128), jnp.float32)
        for m in range(members):
            vec = jnp.where(lane == 2 * m, total(residual[m] * residual[m]), vec)
            vec = jnp.where(lane == 2 * m + 1, total(residual[m] * image_res[m]), vec)
        sums = exchange_sum(count, vec, ny, nx, bufs, (my, mx, along_y, along_x))
        for m in range(members):
            gamma = sums[0:1, 2 * m : 2 * m + 1]
            delta = sums[0:1, 2 * m + 1 : 2 * m + 2]
            if count == 0:
                alpha = gamma / delta
                direction[m] = residual[m]
                image_dir[m] = image_res[m]
                solution[m] = alpha * direction[m]
            else:
                beta = gamma / gamma_prev[m]
                alpha = gamma / (delta - beta * gamma / alpha_prev[m])
                direction[m] = residual[m] + beta * direction[m]
                image_dir[m] = image_res[m] + beta * image_dir[m]
                solution[m] = solution[m] + alpha * direction[m]
            if count < ITERS - 1:
                residual[m] = residual[m] - alpha * image_dir[m]
            gamma_prev[m] = gamma
            alpha_prev[m] = alpha
    for m in range(members):
        x = solution[m]
        out_ref[0, m] = x[0:rows, 0:cols]
        out_ref[1, m] = (east(x) - west(x))[0:rows, 0:cols]
        out_ref[2, m] = (north(x) - south(x))[0:rows, 0:cols]


def surface_kernel_solve(surf, inside, own):
    ny = lax.axis_size("gridy")
    nx = lax.axis_size("gridx")
    fields, members, rows, cols = surf.shape
    return pl.pallas_call(
        functools.partial(solve_kernel, ny, nx),
        out_shape=jax.ShapeDtypeStruct((3, members, rows, cols), jnp.float32),
        in_specs=[pl.BlockSpec(memory_space=pltpu.VMEM)] * 3,
        out_specs=pl.BlockSpec(memory_space=pltpu.VMEM),
        scratch_shapes=[
            pltpu.VMEM((fields, members) + inside.shape, jnp.float32),
            pltpu.SemaphoreType.DMA((4,)),
            pltpu.SemaphoreType.DMA((4,)),
            pltpu.VMEM((ITERS, 8, 128), jnp.float32),
            pltpu.VMEM((ITERS, ny, 8, 128), jnp.float32),
            pltpu.VMEM((ITERS, 8, 128), jnp.float32),
            pltpu.VMEM((ITERS, nx, 8, 128), jnp.float32),
            pltpu.SemaphoreType.DMA((ITERS, ny)),
            pltpu.SemaphoreType.DMA((ITERS, ny)),
            pltpu.SemaphoreType.DMA((ITERS, nx)),
            pltpu.SemaphoreType.DMA((ITERS, nx)),
        ],
        compiler_params=pltpu.CompilerParams(collective_id=1, has_side_effects=True),
    )(surf, inside, own)


def volume_kernel(temp_ref, salt_ref, uvel_ref, vvel_ref, ocean_ref, cor_ref, n_ref, s_ref, e_ref, w_ref,
                  tn_ref, sn_ref, us_ref, vs_ref, tu_ref, tv_ref):
    levels, rows, cols = temp_ref.shape[1], temp_ref.shape[2], temp_ref.shape[3]
    row = lax.broadcasted_iota(jnp.int32, (rows, cols), 0)
    col = lax.broadcasted_iota(jnp.int32, (rows, cols), 1)
    top = row == rows - 1
    bottom = row == 0
    right = col == cols - 1
    left = col == 0
    ocean = ocean_ref[...]
    cor = cor_ref[...]

    def around(f, rims):
        n, s, e, w = rims
        return (
            jnp.where(right, e, pltpu.roll(f, cols - 1, 1)),
            jnp.where(left, w, pltpu.roll(f, 1, 1)),
            jnp.where(top, n, pltpu.roll(f, rows - 1, 0)),
            jnp.where(bottom, s, pltpu.roll(f, 1, 0)),
        )

    def rims_of(k, l):
        return (n_ref[k, 0, l], s_ref[k, 0, l], e_ref[k, 0, l], w_ref[k, 0, l])

    running = None
    running_rims = None
    tu = None
    tv = None
    for l in range(levels):
        t = temp_ref[0, l]
        s = salt_ref[0, l]
        u = uvel_ref[0, l]
        v = vvel_ref[0, l]
        rt, rs, ru, rv = rims_of(0, l), rims_of(1, l), rims_of(2, l), rims_of(3, l)
        layer = BETA_S * s - ALPHA_T * t
        layer_rims = tuple(BETA_S * b - ALPHA_T * a for a, b in zip(rt, rs))
        if running is None:
            running, running_rims = layer, layer_rims
        else:
            running = running + layer
            running_rims = tuple(a + b for a, b in zip(running_rims, layer_rims))
        press = PRESS_K * running
        press_rims = tuple(PRESS_K * a for a in running_rims)
        te, tw, tn, ts = around(t, rt)
        se, sw, sn, ss = around(s, rs)
        ue, uw, un, us = around(u, ru)
        ve, vw, vn, vs = around(v, rv)
        pe, pw, pn, ps = around(press, press_rims)
        tn_ref[0, l] = ocean * (
            t - STEP_DT * 0.5 * (u * (te - tw) + v * (tn - ts)) + KAPPA * (te + tw + tn + ts - 4.0 * t)
        )
        sn_ref[0, l] = ocean * (
            s - STEP_DT * 0.5 * (u * (se - sw) + v * (sn - ss)) + KAPPA * (se + sw + sn + ss - 4.0 * s)
        )
        ustar = ocean * (
            u + STEP_DT * (cor * v - 0.5 * (pe - pw) - DRAG_K * u) + VISCOSITY * (ue + uw + un + us - 4.0 * u)
        )
        vstar = ocean * (
            v + STEP_DT * (-cor * u - 0.5 * (pn - ps) - DRAG_K * v) + VISCOSITY * (ve + vw + vn + vs - 4.0 * v)
        )
        us_ref[0, l] = ustar
        vs_ref[0, l] = vstar
        tu = ustar if tu is None else tu + ustar
        tv = vstar if tv is None else tv + vstar
    tu_ref[0] = tu
    tv_ref[0] = tv


def volume_step(temp, salt, uvel, vvel, ocean, cor_tile, rims):
    members, levels, rows, cols = temp.shape
    field = pl.BlockSpec((1, levels, rows, cols), lambda m: (m, 0, 0, 0))
    plane = pl.BlockSpec((rows, cols), lambda m: (0, 0))
    north, south, east, west = rims
    row_rim = pl.BlockSpec((4, 1, levels, 1, cols), lambda m: (0, m, 0, 0, 0))
    col_rim = pl.BlockSpec((4, 1, levels, rows, 1), lambda m: (0, m, 0, 0, 0))
    surface = pl.BlockSpec((1, rows, cols), lambda m: (m, 0, 0))
    volume_shape = jax.ShapeDtypeStruct(temp.shape, jnp.float32)
    surface_shape = jax.ShapeDtypeStruct((members, rows, cols), jnp.float32)
    return pl.pallas_call(
        volume_kernel,
        grid=(members,),
        in_specs=[field] * 4 + [plane, plane, row_rim, row_rim, col_rim, col_rim],
        out_specs=[field] * 4 + [surface] * 2,
        out_shape=[volume_shape] * 4 + [surface_shape] * 2,
    )(temp, salt, uvel, vvel, ocean, cor_tile, north, south, east, west)


def ring(axis):
    count = lax.axis_size(axis)
    forward = [(i, (i + 1) % count) for i in range(count)]
    backward = [((i + 1) % count, i) for i in range(count)]
    return forward, backward


def exchange(block, ydim, xdim, south_keep, north_keep):
    fwd_y, bwd_y = ring("gridy")
    fwd_x, bwd_x = ring("gridx")
    rows = block.shape[ydim]
    cols = block.shape[xdim]
    north = lax.ppermute(lax.slice_in_dim(block, 0, 1, axis=ydim), "gridy", bwd_y) * north_keep
    south = lax.ppermute(lax.slice_in_dim(block, rows - 1, rows, axis=ydim), "gridy", fwd_y) * south_keep
    east = lax.ppermute(lax.slice_in_dim(block, 0, 1, axis=xdim), "gridx", bwd_x)
    west = lax.ppermute(lax.slice_in_dim(block, cols - 1, cols, axis=xdim), "gridx", fwd_x)
    return (east, west, north, south)


def exchange_fields(fields, south_keep, north_keep):
    fwd_y, bwd_y = ring("gridy")
    fwd_x, bwd_x = ring("gridx")
    north = lax.ppermute(jnp.stack([f[..., :1, :] for f in fields]), "gridy", bwd_y) * north_keep
    south = lax.ppermute(jnp.stack([f[..., -1:, :] for f in fields]), "gridy", fwd_y) * south_keep
    east = lax.ppermute(jnp.stack([f[..., :, :1] for f in fields]), "gridx", bwd_x)
    west = lax.ppermute(jnp.stack([f[..., :, -1:] for f in fields]), "gridx", fwd_x)
    return (north, south, east, west)


def sides(field, rims, ydim, xdim):
    east, west, north, south = rims
    rows = field.shape[ydim]
    cols = field.shape[xdim]
    east_side = jnp.concatenate([lax.slice_in_dim(field, 1, cols, axis=xdim), east], axis=xdim)
    west_side = jnp.concatenate([west, lax.slice_in_dim(field, 0, cols - 1, axis=xdim)], axis=xdim)
    north_side = jnp.concatenate([lax.slice_in_dim(field, 1, rows, axis=ydim), north], axis=ydim)
    south_side = jnp.concatenate([south, lax.slice_in_dim(field, 0, rows - 1, axis=ydim)], axis=ydim)
    return (east_side, west_side, north_side, south_side)


def pressure(temp, salt):
    return PRESS_K * jnp.cumsum(BETA_S * salt - ALPHA_T * temp, axis=-3)


def surface_apply(field, rims):
    east_side, west_side, north_side, south_side = sides(field, rims, 1, 2)
    return (1.0 + 4.0 * SURF_C) * field - SURF_C * (east_side + west_side + north_side + south_side)


def member_total(values):
    return jnp.sum(values, axis=(1, 2))


def widen(values):
    return values[:, None, None]


def combine(a, fa, b, fb):
    def one(u, v):
        left = u if a is None else widen(a) * u
        return left + (v if b is None else widen(b) * v)

    return one(fa[0], fb[0]), tuple(one(u, v) for u, v in zip(fa[1], fb[1]))


def scaled(a, fa):
    return widen(a) * fa[0], tuple(widen(a) * u for u in fa[1])


def padded_2(block, sides_of, width):
    for axis, dim in sides_of:
        count = lax.axis_size(axis)
        forward = [(i, (i + 1) % count) for i in range(count)]
        backward = [((i + 1) % count, i) for i in range(count)]
        size = block.shape[dim]
        low = lax.ppermute(lax.slice_in_dim(block, size - width, size, axis=dim), axis, forward)
        high = lax.ppermute(lax.slice_in_dim(block, 0, width, axis=dim), axis, backward)
        block = jnp.concatenate([low, block, high], axis=dim)
    return block


def crop(field, by):
    if by == 0:
        return field
    return field[..., by:-by, by:-by]


def around(field):
    return (
        field[..., 1:-1, 1:-1],
        field[..., 1:-1, 2:],
        field[..., 1:-1, :-2],
        field[..., 2:, 1:-1],
        field[..., :-2, 1:-1],
    )


def rows_at(inside, full, want):
    cut = full - want
    return inside if cut == 0 else inside[cut:-cut]


def apply_wide(field, inside):
    centre, east, west, north, south = around(field)
    return ((1.0 + 4.0 * SURF_C) * centre - SURF_C * (east + west + north + south)) * inside


def surface_solve(rhs, inside, width, full):
    residual, wide_r = rhs, width
    gamma_prev = None
    alpha_prev = None
    for count in range(ITERS):
        image_res = apply_wide(residual, rows_at(inside, full, wide_r - 1))
        own_res = crop(residual, wide_r)
        own_img = crop(image_res, wide_r - 1)
        dots = grid_sum(jnp.stack([member_total(own_res * own_res), member_total(own_res * own_img)]))
        gamma, delta = dots[0], dots[1]
        if count == 0:
            alpha = gamma / delta
            direction, wide_p = residual, wide_r
            image_dir, wide_s = image_res, wide_r - 1
            solution, wide_x = widen(alpha) * direction, wide_r
        else:
            beta = gamma / gamma_prev
            alpha = gamma / (delta - beta * gamma / alpha_prev)
            direction = residual + widen(beta) * crop(direction, wide_p - wide_r)
            wide_p = wide_r
            image_dir = image_res + widen(beta) * crop(image_dir, wide_s - (wide_r - 1))
            wide_s = wide_r - 1
            solution = crop(solution, wide_x - wide_r) + widen(alpha) * direction
            wide_x = wide_r
        if count < ITERS - 1:
            residual = crop(residual, 1) - widen(alpha) * image_dir
            wide_r -= 1
        gamma_prev = gamma
        alpha_prev = alpha
    return solution


def shards(temp, salt, uvel, vvel, eta, land_mask, clone_source):
    levels = temp.shape[1]
    rows = temp.shape[2]
    cols = temp.shape[3]
    ocean = land_mask.astype(jnp.float32)
    tile_row = lax.axis_index("gridy")
    tile_count = lax.axis_size("gridy")
    total_rows = rows * tile_count
    total_cols = cols * lax.axis_size("gridx")
    south_keep = (tile_row > 0).astype(jnp.float32)
    north_keep = (tile_row < tile_count - 1).astype(jnp.float32)
    latitude = (tile_row * rows + jnp.arange(rows, dtype=jnp.int32)).astype(jnp.float32) + 0.5
    coriolis = (CORI_K * (2.0 * latitude / total_rows - 1.0))[:, None]
    cor_tile = jnp.broadcast_to(coriolis, (rows, cols))
    band = 8
    block = 128
    frame_rows = rows + 2 * band
    frame_cols = cols + 2 * block
    row_at = lax.broadcasted_iota(jnp.int32, (frame_rows, frame_cols), 0)
    col_at = lax.broadcasted_iota(jnp.int32, (frame_rows, frame_cols), 1)
    global_row = tile_row * rows + jnp.where(row_at < rows + band, row_at, row_at - frame_rows)
    wide_inside = ((global_row >= 0) & (global_row < total_rows)).astype(jnp.float32)
    own_mask = ((row_at < rows) & (col_at < cols)).astype(jnp.float32)
    for count in range(STEPS):
        fields = (temp, salt, uvel, vvel)
        rims = exchange_fields(fields, south_keep, north_keep)
        temp_next, salt_next, ustar, vstar, trans_u, trans_v = volume_step(
            temp, salt, uvel, vvel, ocean, cor_tile, rims
        )
        solved = surface_kernel_solve(jnp.stack((trans_u, trans_v, eta)), wide_inside, own_mask)
        eta = solved[0]
        east_west = solved[1]
        north_south = solved[2]
        uvel = ocean * (ustar - GRAV_K * 0.5 * east_west[:, None])
        vvel = ocean * (vstar - GRAV_K * 0.5 * north_south[:, None])
        if count == STEPS - 1:
            tracers_other = lax.ppermute(jnp.stack((temp_next, salt_next)), "member", [(0, 1), (1, 0)])
        temp = temp_next
        salt = salt_next
    zonal_scale = 1.0 / jnp.sqrt(jnp.float32(total_cols))
    score_scale = 1.0 / jnp.sqrt(jnp.float32(levels * total_rows))
    lat_weight = latitude / total_rows
    members = temp.shape[0]
    zonal_local = jnp.sum(vvel, axis=3)
    depth_weight = (levels - jnp.arange(levels, dtype=jnp.int32)).astype(jnp.float32)
    score_local = jnp.sum(zonal_local * depth_weight[None, :, None] * lat_weight[None, None, :], axis=(1, 2))
    slot = lax.broadcasted_iota(jnp.int32, (tile_count, 1, 1, 1), 0) == tile_row
    zonal_slots = jnp.where(slot, zonal_local[None], 0.0).reshape(-1, 128)
    score_row = jnp.zeros((8, 128), jnp.float32).at[0, :members].set(score_local)
    summed = grid_sum(jnp.concatenate([zonal_slots, score_row], axis=0))
    zonal_whole = summed[: zonal_slots.shape[0]].reshape((tile_count,) + zonal_local.shape)
    zonal_whole = jnp.sum(jnp.where(slot, zonal_whole, 0.0), axis=0)
    overturn = jnp.cumsum(zonal_whole, axis=1) * zonal_scale
    score = summed[zonal_slots.shape[0], :members] * (zonal_scale * score_scale)
    swap = [(0, 1), (1, 0)]
    mine = lax.axis_index("member")
    score_slab = jnp.zeros((members, 1) + eta.shape[1:], jnp.float32).at[:, 0, 0, 0].set(score)
    flows = jnp.concatenate([uvel, vvel, eta[:, None], score_slab], axis=1)
    flows_other = lax.ppermute(flows, "member", swap)
    score_other = flows_other[:, 2 * levels + 1, 0, 0]
    every_score = jnp.where(
        mine == 0, jnp.concatenate([score, score_other]), jnp.concatenate([score_other, score])
    )
    here = (clone_source // members) == mine
    local_at = clone_source % members

    def pick(local, other):
        chosen = []
        for place in range(members):
            from_here = lax.dynamic_index_in_dim(local, local_at[place], 0, keepdims=False)
            from_other = lax.dynamic_index_in_dim(other, local_at[place], 0, keepdims=False)
            chosen.append(jnp.where(here[place], from_here, from_other))
        return jnp.stack(chosen)

    new_temp = pick(temp, tracers_other[0])
    new_salt = pick(salt, tracers_other[1])
    new_flows = pick(flows[:, : 2 * levels + 1], flows_other[:, : 2 * levels + 1])
    clone_weight = jnp.take(every_score, clone_source, axis=0) - jnp.mean(every_score)
    return (
        new_temp,
        new_salt,
        new_flows[:, :levels],
        new_flows[:, levels : 2 * levels],
        new_flows[:, 2 * levels],
        overturn,
        clone_weight,
    )


def solution(mesh):
    in_specs = (
        P("member", None, "gridy", "gridx"),
        P("member", None, "gridy", "gridx"),
        P("member", None, "gridy", "gridx"),
        P("member", None, "gridy", "gridx"),
        P("member", "gridy", "gridx"),
        P("gridy", "gridx"),
        P("member"),
    )
    out_specs = (
        P("member", None, "gridy", "gridx"),
        P("member", None, "gridy", "gridx"),
        P("member", None, "gridy", "gridx"),
        P("member", None, "gridy", "gridx"),
        P("member", "gridy", "gridx"),
        P("member", None, "gridy"),
        P("member"),
    )
    return jax.shard_map(shards, mesh=mesh, in_specs=in_specs, out_specs=out_specs, check_vma=False)
```

```python
import functools

import jax
import jax.numpy as jnp
from jax import lax
from jax.experimental import pallas as pl
from jax.experimental.pallas import tpu as pltpu
from jax.sharding import PartitionSpec as P

STEPS = 2
ITERS = 3


ALPHA_T = 0.8
BETA_S = 0.6
PRESS_K = 0.25
STEP_DT = 0.1
KAPPA = 0.1
VISCOSITY = 0.1
DRAG_K = 0.05
CORI_K = 1.0
SURF_C = 4.0
DIV_K = 0.5
GRAV_K = 0.5


def tree_sum(values, axes):
    for axis in axes:
        count = lax.axis_size(axis)
        step = 1
        while step < count:
            pairs = [(i, i ^ step) for i in range(count)]
            values = values + lax.ppermute(values, axis, pairs)
            step *= 2
    return values


def gather_sum_kernel(ny, nx, x_ref, o_ref, recv_y, recv_x, part, send_y, rsem_y, send_x, rsem_x):
    mesh_id = pl.DeviceIdType.MESH
    member = lax.axis_index("member")
    my = lax.axis_index("gridy")
    mx = lax.axis_index("gridx")
    barrier = pltpu.get_barrier_semaphore()
    for d in range(1, ny):
        pl.semaphore_signal(barrier, 1, device_id=(member, (my + d) % ny, mx), device_id_type=mesh_id)
    for d in range(1, nx):
        pl.semaphore_signal(barrier, 1, device_id=(member, my, (mx + d) % nx), device_id_type=mesh_id)
    pl.semaphore_wait(barrier, (ny - 1) + (nx - 1))

    def phase(src, recv, send_sem, recv_sem, count, me, device):
        recv[me] = src[...]
        sent = []
        for d in range(1, count):
            peer = (me + d) % count
            copy = pltpu.make_async_remote_copy(
                src_ref=src,
                dst_ref=recv.at[me],
                send_sem=send_sem.at[peer],
                recv_sem=recv_sem.at[me],
                device_id=device(peer),
                device_id_type=mesh_id,
            )
            copy.start()
            sent.append(copy)
        for d in range(1, count):
            peer = (me + d) % count
            pltpu.make_async_remote_copy(
                src_ref=src,
                dst_ref=recv.at[peer],
                send_sem=send_sem.at[peer],
                recv_sem=recv_sem.at[peer],
                device_id=device(peer),
                device_id_type=mesh_id,
            ).wait_recv()
        for copy in sent:
            copy.wait_send()
        total = recv[0]
        for j in range(1, count):
            total = total + recv[j]
        return total

    part[...] = phase(x_ref, recv_y, send_y, rsem_y, ny, my, lambda p: (member, p, mx))
    o_ref[...] = phase(part, recv_x, send_x, rsem_x, nx, mx, lambda p: (member, my, p))


def grid_sum(values):
    ny = lax.axis_size("gridy")
    nx = lax.axis_size("gridx")
    shape = values.shape
    return pl.pallas_call(
        functools.partial(gather_sum_kernel, ny, nx),
        out_shape=jax.ShapeDtypeStruct(shape, values.dtype),
        in_specs=[pl.BlockSpec(memory_space=pltpu.VMEM)],
        out_specs=pl.BlockSpec(memory_space=pltpu.VMEM),
        scratch_shapes=[
            pltpu.VMEM((ny,) + shape, values.dtype),
            pltpu.VMEM((nx,) + shape, values.dtype),
            pltpu.VMEM(shape, values.dtype),
            pltpu.SemaphoreType.DMA((ny,)),
            pltpu.SemaphoreType.DMA((ny,)),
            pltpu.SemaphoreType.DMA((nx,)),
            pltpu.SemaphoreType.DMA((nx,)),
        ],
        compiler_params=pltpu.CompilerParams(collective_id=0, has_side_effects=True),
    )(values)


def exchange_sum(k, vec, ny, nx, bufs, device_ids):
    send_y, recv_y, send_x, recv_x, sy, ry, sx, rx = bufs
    my, mx, along_y, along_x = device_ids
    mesh_id = pl.DeviceIdType.MESH

    def phase(value, send_buf, recv, send_sem, recv_sem, count, me, device):
        send_buf[k] = value
        recv[k, me] = value
        sent = []
        for d in range(1, count):
            peer = (me + d) % count
            copy = pltpu.make_async_remote_copy(
                src_ref=send_buf.at[k],
                dst_ref=recv.at[k, me],
                send_sem=send_sem.at[k, peer],
                recv_sem=recv_sem.at[k, me],
                device_id=device(peer),
                device_id_type=mesh_id,
            )
            copy.start()
            sent.append(copy)
        for d in range(1, count):
            peer = (me + d) % count
            pltpu.make_async_remote_copy(
                src_ref=send_buf.at[k],
                dst_ref=recv.at[k, peer],
                send_sem=send_sem.at[k, peer],
                recv_sem=recv_sem.at[k, peer],
                device_id=device(peer),
                device_id_type=mesh_id,
            ).wait_recv()
        for copy in sent:
            copy.wait_send()
        total = recv[k, 0]
        for j in range(1, count):
            total = total + recv[k, j]
        return total

    partial = phase(vec, send_y, recv_y, sy, ry, ny, my, along_y)
    return phase(partial, send_x, recv_x, sx, rx, nx, mx, along_x)


def solve_kernel(ny, nx, surf_ref, inside_ref, own_ref, out_ref, frame, hsend, hrecv, *bufs):
    mesh_id = pl.DeviceIdType.MESH
    member = lax.axis_index("member")
    my = lax.axis_index("gridy")
    mx = lax.axis_index("gridx")
    along_y = lambda p: (member, p, mx)
    along_x = lambda p: (member, my, p)
    barrier = pltpu.get_barrier_semaphore()
    for d in range(1, ny):
        pl.semaphore_signal(barrier, 1, device_id=along_y((my + d) % ny), device_id_type=mesh_id)
    for d in range(1, nx):
        pl.semaphore_signal(barrier, 1, device_id=along_x((mx + d) % nx), device_id_type=mesh_id)
    for dy in (1, ny - 1):
        for dx in (1, nx - 1):
            pl.semaphore_signal(
                barrier, 1, device_id=(member, (my + dy) % ny, (mx + dx) % nx), device_id_type=mesh_id
            )
    rows, cols = surf_ref.shape[2], surf_ref.shape[3]
    wide_rows, wide_cols = frame.shape[2], frame.shape[3]
    band = (wide_rows - rows) // 2
    block = (wide_cols - cols) // 2
    frame[:, :, 0:rows, 0:cols] = surf_ref[...]
    pl.semaphore_wait(barrier, (ny - 1) + (nx - 1) + 4)

    def halo_copies(first, moves):
        started = []
        for slot, (src, dst, device) in enumerate(moves, start=first):
            copy = pltpu.make_async_remote_copy(
                src_ref=src, dst_ref=dst, send_sem=hsend.at[slot], recv_sem=hrecv.at[slot],
                device_id=device, device_id_type=mesh_id,
            )
            copy.start()
            started.append(copy)
        for copy in started:
            copy.wait()

    up, down = (my + 1) % ny, (my + ny - 1) % ny
    right, left = (mx + 1) % nx, (mx + nx - 1) % nx
    top_rows = slice(0, band)
    low_rows = slice(rows - band, rows)
    own_rows = slice(0, rows)
    west_part = slice(0, block)
    east_part = slice(cols - block, cols)
    own_cols = slice(0, cols)
    north_halo = slice(rows, rows + band)
    south_halo = slice(rows + band, wide_rows)
    east_halo = slice(cols, cols + block)
    west_halo = slice(cols + block, wide_cols)
    halo_copies(0, [
        (frame.at[:, :, top_rows, own_cols], frame.at[:, :, north_halo, own_cols], (member, down, mx)),
        (frame.at[:, :, low_rows, own_cols], frame.at[:, :, south_halo, own_cols], (member, up, mx)),
        (frame.at[:, :, own_rows, west_part], frame.at[:, :, own_rows, east_halo], (member, my, left)),
        (frame.at[:, :, own_rows, east_part], frame.at[:, :, own_rows, west_halo], (member, my, right)),
        (frame.at[:, :, top_rows, west_part], frame.at[:, :, north_halo, east_halo], (member, down, left)),
        (frame.at[:, :, top_rows, east_part], frame.at[:, :, north_halo, west_halo], (member, down, right)),
        (frame.at[:, :, low_rows, west_part], frame.at[:, :, south_halo, east_halo], (member, up, left)),
        (frame.at[:, :, low_rows, east_part], frame.at[:, :, south_halo, west_halo], (member, up, right)),
    ])

    members = surf_ref.shape[1]
    inside = inside_ref[...]
    own = own_ref[...] > 0.5

    def east(f):
        return pltpu.roll(f, wide_cols - 1, 1)

    def west(f):
        return pltpu.roll(f, 1, 1)

    def north(f):
        return pltpu.roll(f, wide_rows - 1, 0)

    def south(f):
        return pltpu.roll(f, 1, 0)

    def apply(f):
        return ((1.0 + 4.0 * SURF_C) * f - SURF_C * (east(f) + west(f) + north(f) + south(f))) * inside

    def total(f):
        return jnp.sum(jnp.where(own, f, 0.0), axis=(0, 1), keepdims=True)

    residual = []
    for m in range(members):
        trans_u = frame[0, m] * inside
        trans_v = frame[1, m] * inside
        level = frame[2, m] * inside
        residual.append(
            (level - DIV_K * 0.5 * (east(trans_u) - west(trans_u) + (north(trans_v) - south(trans_v)))) * inside
        )
    lane = lax.broadcasted_iota(jnp.int32, (8, 128), 1)
    direction = [None] * members
    image_dir = [None] * members
    solution = [None] * members
    gamma_prev = [None] * members
    alpha_prev = [None] * members
    for count in range(ITERS):
        image_res = [apply(residual[m]) for m in range(members)]
        vec = jnp.zeros((8, 128), jnp.float32)
        for m in range(members):
            vec = jnp.where(lane == 2 * m, total(residual[m] * residual[m]), vec)
            vec = jnp.where(lane == 2 * m + 1, total(residual[m] * image_res[m]), vec)
        sums = exchange_sum(count, vec, ny, nx, bufs, (my, mx, along_y, along_x))
        for m in range(members):
            gamma = sums[0:1, 2 * m : 2 * m + 1]
            delta = sums[0:1, 2 * m + 1 : 2 * m + 2]
            if count == 0:
                alpha = gamma / delta
                direction[m] = residual[m]
                image_dir[m] = image_res[m]
                solution[m] = alpha * direction[m]
            else:
                beta = gamma / gamma_prev[m]
                alpha = gamma / (delta - beta * gamma / alpha_prev[m])
                direction[m] = residual[m] + beta * direction[m]
                image_dir[m] = image_res[m] + beta * image_dir[m]
                solution[m] = solution[m] + alpha * direction[m]
            if count < ITERS - 1:
                residual[m] = residual[m] - alpha * image_dir[m]
            gamma_prev[m] = gamma
            alpha_prev[m] = alpha
    for m in range(members):
        x = solution[m]
        out_ref[0, m] = x[0:rows, 0:cols]
        out_ref[1, m] = (east(x) - west(x))[0:rows, 0:cols]
        out_ref[2, m] = (north(x) - south(x))[0:rows, 0:cols]


def surface_kernel_solve(surf, inside, own):
    ny = lax.axis_size("gridy")
    nx = lax.axis_size("gridx")
    fields, members, rows, cols = surf.shape
    return pl.pallas_call(
        functools.partial(solve_kernel, ny, nx),
        out_shape=jax.ShapeDtypeStruct((3, members, rows, cols), jnp.float32),
        in_specs=[pl.BlockSpec(memory_space=pltpu.VMEM)] * 3,
        out_specs=pl.BlockSpec(memory_space=pltpu.VMEM),
        scratch_shapes=[
            pltpu.VMEM((fields, members) + inside.shape, jnp.float32),
            pltpu.SemaphoreType.DMA((8,)),
            pltpu.SemaphoreType.DMA((8,)),
            pltpu.VMEM((ITERS, 8, 128), jnp.float32),
            pltpu.VMEM((ITERS, ny, 8, 128), jnp.float32),
            pltpu.VMEM((ITERS, 8, 128), jnp.float32),
            pltpu.VMEM((ITERS, nx, 8, 128), jnp.float32),
            pltpu.SemaphoreType.DMA((ITERS, ny)),
            pltpu.SemaphoreType.DMA((ITERS, ny)),
            pltpu.SemaphoreType.DMA((ITERS, nx)),
            pltpu.SemaphoreType.DMA((ITERS, nx)),
        ],
        compiler_params=pltpu.CompilerParams(collective_id=1, has_side_effects=True),
    )(surf, inside, own)


def volume_kernel(temp_ref, salt_ref, uvel_ref, vvel_ref, ocean_ref, cor_ref, n_ref, s_ref, e_ref, w_ref,
                  tn_ref, sn_ref, us_ref, vs_ref, tu_ref, tv_ref):
    levels, rows, cols = temp_ref.shape[1], temp_ref.shape[2], temp_ref.shape[3]
    row = lax.broadcasted_iota(jnp.int32, (rows, cols), 0)
    col = lax.broadcasted_iota(jnp.int32, (rows, cols), 1)
    top = row == rows - 1
    bottom = row == 0
    right = col == cols - 1
    left = col == 0
    ocean = ocean_ref[...]
    cor = cor_ref[...]

    def around(f, rims):
        n, s, e, w = rims
        return (
            jnp.where(right, e, pltpu.roll(f, cols - 1, 1)),
            jnp.where(left, w, pltpu.roll(f, 1, 1)),
            jnp.where(top, n, pltpu.roll(f, rows - 1, 0)),
            jnp.where(bottom, s, pltpu.roll(f, 1, 0)),
        )

    def rims_of(k, l):
        return (n_ref[k, 0, l], s_ref[k, 0, l], e_ref[k, 0, l], w_ref[k, 0, l])

    running = None
    running_rims = None
    tu = None
    tv = None
    for l in range(levels):
        t = temp_ref[0, l]
        s = salt_ref[0, l]
        u = uvel_ref[0, l]
        v = vvel_ref[0, l]
        rt, rs, ru, rv = rims_of(0, l), rims_of(1, l), rims_of(2, l), rims_of(3, l)
        layer = BETA_S * s - ALPHA_T * t
        layer_rims = tuple(BETA_S * b - ALPHA_T * a for a, b in zip(rt, rs))
        if running is None:
            running, running_rims = layer, layer_rims
        else:
            running = running + layer
            running_rims = tuple(a + b for a, b in zip(running_rims, layer_rims))
        press = PRESS_K * running
        press_rims = tuple(PRESS_K * a for a in running_rims)
        te, tw, tn, ts = around(t, rt)
        se, sw, sn, ss = around(s, rs)
        ue, uw, un, us = around(u, ru)
        ve, vw, vn, vs = around(v, rv)
        pe, pw, pn, ps = around(press, press_rims)
        tn_ref[0, l] = ocean * (
            t - STEP_DT * 0.5 * (u * (te - tw) + v * (tn - ts)) + KAPPA * (te + tw + tn + ts - 4.0 * t)
        )
        sn_ref[0, l] = ocean * (
            s - STEP_DT * 0.5 * (u * (se - sw) + v * (sn - ss)) + KAPPA * (se + sw + sn + ss - 4.0 * s)
        )
        ustar = ocean * (
            u + STEP_DT * (cor * v - 0.5 * (pe - pw) - DRAG_K * u) + VISCOSITY * (ue + uw + un + us - 4.0 * u)
        )
        vstar = ocean * (
            v + STEP_DT * (-cor * u - 0.5 * (pn - ps) - DRAG_K * v) + VISCOSITY * (ve + vw + vn + vs - 4.0 * v)
        )
        us_ref[0, l] = ustar
        vs_ref[0, l] = vstar
        tu = ustar if tu is None else tu + ustar
        tv = vstar if tv is None else tv + vstar
    tu_ref[0] = tu
    tv_ref[0] = tv


def volume_step(temp, salt, uvel, vvel, ocean, cor_tile, rims):
    members, levels, rows, cols = temp.shape
    field = pl.BlockSpec((1, levels, rows, cols), lambda m: (m, 0, 0, 0))
    plane = pl.BlockSpec((rows, cols), lambda m: (0, 0))
    north, south, east, west = rims
    row_rim = pl.BlockSpec((4, 1, levels, 1, cols), lambda m: (0, m, 0, 0, 0))
    col_rim = pl.BlockSpec((4, 1, levels, rows, 1), lambda m: (0, m, 0, 0, 0))
    surface = pl.BlockSpec((1, rows, cols), lambda m: (m, 0, 0))
    volume_shape = jax.ShapeDtypeStruct(temp.shape, jnp.float32)
    surface_shape = jax.ShapeDtypeStruct((members, rows, cols), jnp.float32)
    return pl.pallas_call(
        volume_kernel,
        grid=(members,),
        in_specs=[field] * 4 + [plane, plane, row_rim, row_rim, col_rim, col_rim],
        out_specs=[field] * 4 + [surface] * 2,
        out_shape=[volume_shape] * 4 + [surface_shape] * 2,
    )(temp, salt, uvel, vvel, ocean, cor_tile, north, south, east, west)


def ring(axis):
    count = lax.axis_size(axis)
    forward = [(i, (i + 1) % count) for i in range(count)]
    backward = [((i + 1) % count, i) for i in range(count)]
    return forward, backward


def exchange(block, ydim, xdim, south_keep, north_keep):
    fwd_y, bwd_y = ring("gridy")
    fwd_x, bwd_x = ring("gridx")
    rows = block.shape[ydim]
    cols = block.shape[xdim]
    north = lax.ppermute(lax.slice_in_dim(block, 0, 1, axis=ydim), "gridy", bwd_y) * north_keep
    south = lax.ppermute(lax.slice_in_dim(block, rows - 1, rows, axis=ydim), "gridy", fwd_y) * south_keep
    east = lax.ppermute(lax.slice_in_dim(block, 0, 1, axis=xdim), "gridx", bwd_x)
    west = lax.ppermute(lax.slice_in_dim(block, cols - 1, cols, axis=xdim), "gridx", fwd_x)
    return (east, west, north, south)


def exchange_fields(fields, south_keep, north_keep):
    fwd_y, bwd_y = ring("gridy")
    fwd_x, bwd_x = ring("gridx")
    north = lax.ppermute(jnp.stack([f[..., :1, :] for f in fields]), "gridy", bwd_y) * north_keep
    south = lax.ppermute(jnp.stack([f[..., -1:, :] for f in fields]), "gridy", fwd_y) * south_keep
    east = lax.ppermute(jnp.stack([f[..., :, :1] for f in fields]), "gridx", bwd_x)
    west = lax.ppermute(jnp.stack([f[..., :, -1:] for f in fields]), "gridx", fwd_x)
    return (north, south, east, west)


def sides(field, rims, ydim, xdim):
    east, west, north, south = rims
    rows = field.shape[ydim]
    cols = field.shape[xdim]
    east_side = jnp.concatenate([lax.slice_in_dim(field, 1, cols, axis=xdim), east], axis=xdim)
    west_side = jnp.concatenate([west, lax.slice_in_dim(field, 0, cols - 1, axis=xdim)], axis=xdim)
    north_side = jnp.concatenate([lax.slice_in_dim(field, 1, rows, axis=ydim), north], axis=ydim)
    south_side = jnp.concatenate([south, lax.slice_in_dim(field, 0, rows - 1, axis=ydim)], axis=ydim)
    return (east_side, west_side, north_side, south_side)


def pressure(temp, salt):
    return PRESS_K * jnp.cumsum(BETA_S * salt - ALPHA_T * temp, axis=-3)


def surface_apply(field, rims):
    east_side, west_side, north_side, south_side = sides(field, rims, 1, 2)
    return (1.0 + 4.0 * SURF_C) * field - SURF_C * (east_side + west_side + north_side + south_side)


def member_total(values):
    return jnp.sum(values, axis=(1, 2))


def widen(values):
    return values[:, None, None]


def combine(a, fa, b, fb):
    def one(u, v):
        left = u if a is None else widen(a) * u
        return left + (v if b is None else widen(b) * v)

    return one(fa[0], fb[0]), tuple(one(u, v) for u, v in zip(fa[1], fb[1]))


def scaled(a, fa):
    return widen(a) * fa[0], tuple(widen(a) * u for u in fa[1])


def padded_2(block, sides_of, width):
    for axis, dim in sides_of:
        count = lax.axis_size(axis)
        forward = [(i, (i + 1) % count) for i in range(count)]
        backward = [((i + 1) % count, i) for i in range(count)]
        size = block.shape[dim]
        low = lax.ppermute(lax.slice_in_dim(block, size - width, size, axis=dim), axis, forward)
        high = lax.ppermute(lax.slice_in_dim(block, 0, width, axis=dim), axis, backward)
        block = jnp.concatenate([low, block, high], axis=dim)
    return block


def crop(field, by):
    if by == 0:
        return field
    return field[..., by:-by, by:-by]


def around(field):
    return (
        field[..., 1:-1, 1:-1],
        field[..., 1:-1, 2:],
        field[..., 1:-1, :-2],
        field[..., 2:, 1:-1],
        field[..., :-2, 1:-1],
    )


def rows_at(inside, full, want):
    cut = full - want
    return inside if cut == 0 else inside[cut:-cut]


def apply_wide(field, inside):
    centre, east, west, north, south = around(field)
    return ((1.0 + 4.0 * SURF_C) * centre - SURF_C * (east + west + north + south)) * inside


def surface_solve(rhs, inside, width, full):
    residual, wide_r = rhs, width
    gamma_prev = None
    alpha_prev = None
    for count in range(ITERS):
        image_res = apply_wide(residual, rows_at(inside, full, wide_r - 1))
        own_res = crop(residual, wide_r)
        own_img = crop(image_res, wide_r - 1)
        dots = grid_sum(jnp.stack([member_total(own_res * own_res), member_total(own_res * own_img)]))
        gamma, delta = dots[0], dots[1]
        if count == 0:
            alpha = gamma / delta
            direction, wide_p = residual, wide_r
            image_dir, wide_s = image_res, wide_r - 1
            solution, wide_x = widen(alpha) * direction, wide_r
        else:
            beta = gamma / gamma_prev
            alpha = gamma / (delta - beta * gamma / alpha_prev)
            direction = residual + widen(beta) * crop(direction, wide_p - wide_r)
            wide_p = wide_r
            image_dir = image_res + widen(beta) * crop(image_dir, wide_s - (wide_r - 1))
            wide_s = wide_r - 1
            solution = crop(solution, wide_x - wide_r) + widen(alpha) * direction
            wide_x = wide_r
        if count < ITERS - 1:
            residual = crop(residual, 1) - widen(alpha) * image_dir
            wide_r -= 1
        gamma_prev = gamma
        alpha_prev = alpha
    return solution


def shards(temp, salt, uvel, vvel, eta, land_mask, clone_source):
    levels = temp.shape[1]
    rows = temp.shape[2]
    cols = temp.shape[3]
    ocean = land_mask.astype(jnp.float32)
    tile_row = lax.axis_index("gridy")
    tile_count = lax.axis_size("gridy")
    total_rows = rows * tile_count
    total_cols = cols * lax.axis_size("gridx")
    south_keep = (tile_row > 0).astype(jnp.float32)
    north_keep = (tile_row < tile_count - 1).astype(jnp.float32)
    latitude = (tile_row * rows + jnp.arange(rows, dtype=jnp.int32)).astype(jnp.float32) + 0.5
    coriolis = (CORI_K * (2.0 * latitude / total_rows - 1.0))[:, None]
    cor_tile = jnp.broadcast_to(coriolis, (rows, cols))
    band = 8
    block = 128
    frame_rows = rows + 2 * band
    frame_cols = cols + 2 * block
    row_at = lax.broadcasted_iota(jnp.int32, (frame_rows, frame_cols), 0)
    col_at = lax.broadcasted_iota(jnp.int32, (frame_rows, frame_cols), 1)
    global_row = tile_row * rows + jnp.where(row_at < rows + band, row_at, row_at - frame_rows)
    wide_inside = ((global_row >= 0) & (global_row < total_rows)).astype(jnp.float32)
    own_mask = ((row_at < rows) & (col_at < cols)).astype(jnp.float32)
    for count in range(STEPS):
        fields = (temp, salt, uvel, vvel)
        rims = exchange_fields(fields, south_keep, north_keep)
        temp_next, salt_next, ustar, vstar, trans_u, trans_v = volume_step(
            temp, salt, uvel, vvel, ocean, cor_tile, rims
        )
        solved = surface_kernel_solve(jnp.stack((trans_u, trans_v, eta)), wide_inside, own_mask)
        eta = solved[0]
        east_west = solved[1]
        north_south = solved[2]
        uvel = ocean * (ustar - GRAV_K * 0.5 * east_west[:, None])
        vvel = ocean * (vstar - GRAV_K * 0.5 * north_south[:, None])
        if count == STEPS - 1:
            tracers_other = lax.ppermute(jnp.stack((temp_next, salt_next)), "member", [(0, 1), (1, 0)])
        temp = temp_next
        salt = salt_next
    zonal_scale = 1.0 / jnp.sqrt(jnp.float32(total_cols))
    score_scale = 1.0 / jnp.sqrt(jnp.float32(levels * total_rows))
    lat_weight = latitude / total_rows
    members = temp.shape[0]
    zonal_local = jnp.sum(vvel, axis=3)
    depth_weight = (levels - jnp.arange(levels, dtype=jnp.int32)).astype(jnp.float32)
    score_local = jnp.sum(zonal_local * depth_weight[None, :, None] * lat_weight[None, None, :], axis=(1, 2))
    slot = lax.broadcasted_iota(jnp.int32, (tile_count, 1, 1, 1), 0) == tile_row
    zonal_slots = jnp.where(slot, zonal_local[None], 0.0).reshape(-1, 128)
    score_row = jnp.zeros((8, 128), jnp.float32).at[0, :members].set(score_local)
    summed = grid_sum(jnp.concatenate([zonal_slots, score_row], axis=0))
    zonal_whole = summed[: zonal_slots.shape[0]].reshape((tile_count,) + zonal_local.shape)
    zonal_whole = jnp.sum(jnp.where(slot, zonal_whole, 0.0), axis=0)
    overturn = jnp.cumsum(zonal_whole, axis=1) * zonal_scale
    score = summed[zonal_slots.shape[0], :members] * (zonal_scale * score_scale)
    swap = [(0, 1), (1, 0)]
    mine = lax.axis_index("member")
    score_slab = jnp.zeros((members, 1) + eta.shape[1:], jnp.float32).at[:, 0, 0, 0].set(score)
    flows = jnp.concatenate([uvel, vvel, eta[:, None], score_slab], axis=1)
    flows_other = lax.ppermute(flows, "member", swap)
    score_other = flows_other[:, 2 * levels + 1, 0, 0]
    every_score = jnp.where(
        mine == 0, jnp.concatenate([score, score_other]), jnp.concatenate([score_other, score])
    )
    here = (clone_source // members) == mine
    local_at = clone_source % members

    def pick(local, other):
        chosen = []
        for place in range(members):
            from_here = lax.dynamic_index_in_dim(local, local_at[place], 0, keepdims=False)
            from_other = lax.dynamic_index_in_dim(other, local_at[place], 0, keepdims=False)
            chosen.append(jnp.where(here[place], from_here, from_other))
        return jnp.stack(chosen)

    new_temp = pick(temp, tracers_other[0])
    new_salt = pick(salt, tracers_other[1])
    new_flows = pick(flows[:, : 2 * levels + 1], flows_other[:, : 2 * levels + 1])
    clone_weight = jnp.take(every_score, clone_source, axis=0) - jnp.mean(every_score)
    return (
        new_temp,
        new_salt,
        new_flows[:, :levels],
        new_flows[:, levels : 2 * levels],
        new_flows[:, 2 * levels],
        overturn,
        clone_weight,
    )


def solution(mesh):
    in_specs = (
        P("member", None, "gridy", "gridx"),
        P("member", None, "gridy", "gridx"),
        P("member", None, "gridy", "gridx"),
        P("member", None, "gridy", "gridx"),
        P("member", "gridy", "gridx"),
        P("gridy", "gridx"),
        P("member"),
    )
    out_specs = (
        P("member", None, "gridy", "gridx"),
        P("member", None, "gridy", "gridx"),
        P("member", None, "gridy", "gridx"),
        P("member", None, "gridy", "gridx"),
        P("member", "gridy", "gridx"),
        P("member", None, "gridy"),
        P("member"),
    )
    return jax.shard_map(shards, mesh=mesh, in_specs=in_specs, out_specs=out_specs, check_vma=False)
```

```python
import functools

import jax
import jax.numpy as jnp
from jax import lax
from jax.experimental import pallas as pl
from jax.experimental.pallas import tpu as pltpu
from jax.sharding import PartitionSpec as P

STEPS = 2
ITERS = 3


ALPHA_T = 0.8
BETA_S = 0.6
PRESS_K = 0.25
STEP_DT = 0.1
KAPPA = 0.1
VISCOSITY = 0.1
DRAG_K = 0.05
CORI_K = 1.0
SURF_C = 4.0
DIV_K = 0.5
GRAV_K = 0.5


def tree_sum(values, axes):
    for axis in axes:
        count = lax.axis_size(axis)
        step = 1
        while step < count:
            pairs = [(i, i ^ step) for i in range(count)]
            values = values + lax.ppermute(values, axis, pairs)
            step *= 2
    return values


def gather_sum_kernel(ny, nx, x_ref, o_ref, recv_y, recv_x, part, send_y, rsem_y, send_x, rsem_x):
    mesh_id = pl.DeviceIdType.MESH
    member = lax.axis_index("member")
    my = lax.axis_index("gridy")
    mx = lax.axis_index("gridx")
    barrier = pltpu.get_barrier_semaphore()
    for d in range(1, ny):
        pl.semaphore_signal(barrier, 1, device_id=(member, (my + d) % ny, mx), device_id_type=mesh_id)
    for d in range(1, nx):
        pl.semaphore_signal(barrier, 1, device_id=(member, my, (mx + d) % nx), device_id_type=mesh_id)
    pl.semaphore_wait(barrier, (ny - 1) + (nx - 1))

    def phase(src, recv, send_sem, recv_sem, count, me, device):
        recv[me] = src[...]
        sent = []
        for d in range(1, count):
            peer = (me + d) % count
            copy = pltpu.make_async_remote_copy(
                src_ref=src,
                dst_ref=recv.at[me],
                send_sem=send_sem.at[peer],
                recv_sem=recv_sem.at[me],
                device_id=device(peer),
                device_id_type=mesh_id,
            )
            copy.start()
            sent.append(copy)
        for d in range(1, count):
            peer = (me + d) % count
            pltpu.make_async_remote_copy(
                src_ref=src,
                dst_ref=recv.at[peer],
                send_sem=send_sem.at[peer],
                recv_sem=recv_sem.at[peer],
                device_id=device(peer),
                device_id_type=mesh_id,
            ).wait_recv()
        for copy in sent:
            copy.wait_send()
        total = recv[0]
        for j in range(1, count):
            total = total + recv[j]
        return total

    part[...] = phase(x_ref, recv_y, send_y, rsem_y, ny, my, lambda p: (member, p, mx))
    o_ref[...] = phase(part, recv_x, send_x, rsem_x, nx, mx, lambda p: (member, my, p))


def grid_sum(values):
    ny = lax.axis_size("gridy")
    nx = lax.axis_size("gridx")
    shape = values.shape
    return pl.pallas_call(
        functools.partial(gather_sum_kernel, ny, nx),
        out_shape=jax.ShapeDtypeStruct(shape, values.dtype),
        in_specs=[pl.BlockSpec(memory_space=pltpu.VMEM)],
        out_specs=pl.BlockSpec(memory_space=pltpu.VMEM),
        scratch_shapes=[
            pltpu.VMEM((ny,) + shape, values.dtype),
            pltpu.VMEM((nx,) + shape, values.dtype),
            pltpu.VMEM(shape, values.dtype),
            pltpu.SemaphoreType.DMA((ny,)),
            pltpu.SemaphoreType.DMA((ny,)),
            pltpu.SemaphoreType.DMA((nx,)),
            pltpu.SemaphoreType.DMA((nx,)),
        ],
        compiler_params=pltpu.CompilerParams(collective_id=0, has_side_effects=True),
    )(values)


def exchange_sum(k, vec, ny, nx, bufs, device_ids):
    send_y, recv_y, send_x, recv_x, sy, ry, sx, rx = bufs
    my, mx, along_y, along_x = device_ids
    mesh_id = pl.DeviceIdType.MESH

    def phase(value, send_buf, recv, send_sem, recv_sem, count, me, device):
        send_buf[k] = value
        recv[k, me] = value
        sent = []
        for d in range(1, count):
            peer = (me + d) % count
            copy = pltpu.make_async_remote_copy(
                src_ref=send_buf.at[k],
                dst_ref=recv.at[k, me],
                send_sem=send_sem.at[k, peer],
                recv_sem=recv_sem.at[k, me],
                device_id=device(peer),
                device_id_type=mesh_id,
            )
            copy.start()
            sent.append(copy)
        for d in range(1, count):
            peer = (me + d) % count
            pltpu.make_async_remote_copy(
                src_ref=send_buf.at[k],
                dst_ref=recv.at[k, peer],
                send_sem=send_sem.at[k, peer],
                recv_sem=recv_sem.at[k, peer],
                device_id=device(peer),
                device_id_type=mesh_id,
            ).wait_recv()
        for copy in sent:
            copy.wait_send()
        total = recv[k, 0]
        for j in range(1, count):
            total = total + recv[k, j]
        return total

    partial = phase(vec, send_y, recv_y, sy, ry, ny, my, along_y)
    return phase(partial, send_x, recv_x, sx, rx, nx, mx, along_x)


def solve_kernel(ny, nx, carry, *refs):
    if carry:
        surf_ref, inside_ref, own_ref, cargo_ref, out_ref, cargo_out, frame, hsend, hrecv, csem = refs[:10]
        bufs = refs[10:]
    else:
        surf_ref, inside_ref, own_ref, out_ref, frame, hsend, hrecv = refs[:7]
        bufs = refs[7:]
    mesh_id = pl.DeviceIdType.MESH
    member = lax.axis_index("member")
    my = lax.axis_index("gridy")
    mx = lax.axis_index("gridx")
    along_y = lambda p: (member, p, mx)
    along_x = lambda p: (member, my, p)
    barrier = pltpu.get_barrier_semaphore()
    for d in range(1, ny):
        pl.semaphore_signal(barrier, 1, device_id=along_y((my + d) % ny), device_id_type=mesh_id)
    for d in range(1, nx):
        pl.semaphore_signal(barrier, 1, device_id=along_x((mx + d) % nx), device_id_type=mesh_id)
    for dy in (1, ny - 1):
        for dx in (1, nx - 1):
            pl.semaphore_signal(
                barrier, 1, device_id=(member, (my + dy) % ny, (mx + dx) % nx), device_id_type=mesh_id
            )
    rows, cols = surf_ref.shape[2], surf_ref.shape[3]
    wide_rows, wide_cols = frame.shape[2], frame.shape[3]
    band = (wide_rows - rows) // 2
    block = (wide_cols - cols) // 2
    frame[:, :, 0:rows, 0:cols] = surf_ref[...]
    if carry:
        partner = (lax.axis_index("member") + 1) % 2
        pl.semaphore_signal(barrier, 1, device_id=(partner, my, mx), device_id_type=mesh_id)
    pl.semaphore_wait(barrier, (ny - 1) + (nx - 1) + 4 + (1 if carry else 0))
    if carry:
        cargo_copy = pltpu.make_async_remote_copy(
            src_ref=cargo_ref, dst_ref=cargo_out, send_sem=csem.at[0], recv_sem=csem.at[1],
            device_id=(partner, my, mx), device_id_type=mesh_id,
        )
        cargo_copy.start()

    def halo_copies(first, moves):
        started = []
        for slot, (src, dst, device) in enumerate(moves, start=first):
            copy = pltpu.make_async_remote_copy(
                src_ref=src, dst_ref=dst, send_sem=hsend.at[slot], recv_sem=hrecv.at[slot],
                device_id=device, device_id_type=mesh_id,
            )
            copy.start()
            started.append(copy)
        for copy in started:
            copy.wait()

    up, down = (my + 1) % ny, (my + ny - 1) % ny
    right, left = (mx + 1) % nx, (mx + nx - 1) % nx
    top_rows = slice(0, band)
    low_rows = slice(rows - band, rows)
    own_rows = slice(0, rows)
    west_part = slice(0, block)
    east_part = slice(cols - block, cols)
    own_cols = slice(0, cols)
    north_halo = slice(rows, rows + band)
    south_halo = slice(rows + band, wide_rows)
    east_halo = slice(cols, cols + block)
    west_halo = slice(cols + block, wide_cols)
    halo_copies(0, [
        (frame.at[:, :, top_rows, own_cols], frame.at[:, :, north_halo, own_cols], (member, down, mx)),
        (frame.at[:, :, low_rows, own_cols], frame.at[:, :, south_halo, own_cols], (member, up, mx)),
        (frame.at[:, :, own_rows, west_part], frame.at[:, :, own_rows, east_halo], (member, my, left)),
        (frame.at[:, :, own_rows, east_part], frame.at[:, :, own_rows, west_halo], (member, my, right)),
        (frame.at[:, :, top_rows, west_part], frame.at[:, :, north_halo, east_halo], (member, down, left)),
        (frame.at[:, :, top_rows, east_part], frame.at[:, :, north_halo, west_halo], (member, down, right)),
        (frame.at[:, :, low_rows, west_part], frame.at[:, :, south_halo, east_halo], (member, up, left)),
        (frame.at[:, :, low_rows, east_part], frame.at[:, :, south_halo, west_halo], (member, up, right)),
    ])

    members = surf_ref.shape[1]
    inside = inside_ref[...]
    own = own_ref[...] > 0.5

    def east(f):
        return pltpu.roll(f, wide_cols - 1, 1)

    def west(f):
        return pltpu.roll(f, 1, 1)

    def north(f):
        return pltpu.roll(f, wide_rows - 1, 0)

    def south(f):
        return pltpu.roll(f, 1, 0)

    def apply(f):
        return ((1.0 + 4.0 * SURF_C) * f - SURF_C * (east(f) + west(f) + north(f) + south(f))) * inside

    def total(f):
        return jnp.sum(jnp.where(own, f, 0.0), axis=(0, 1), keepdims=True)

    residual = []
    for m in range(members):
        trans_u = frame[0, m] * inside
        trans_v = frame[1, m] * inside
        level = frame[2, m] * inside
        residual.append(
            (level - DIV_K * 0.5 * (east(trans_u) - west(trans_u) + (north(trans_v) - south(trans_v)))) * inside
        )
    lane = lax.broadcasted_iota(jnp.int32, (8, 128), 1)
    direction = [None] * members
    image_dir = [None] * members
    solution = [None] * members
    gamma_prev = [None] * members
    alpha_prev = [None] * members
    for count in range(ITERS):
        image_res = [apply(residual[m]) for m in range(members)]
        vec = jnp.zeros((8, 128), jnp.float32)
        for m in range(members):
            vec = jnp.where(lane == 2 * m, total(residual[m] * residual[m]), vec)
            vec = jnp.where(lane == 2 * m + 1, total(residual[m] * image_res[m]), vec)
        sums = exchange_sum(count, vec, ny, nx, bufs, (my, mx, along_y, along_x))
        for m in range(members):
            gamma = sums[0:1, 2 * m : 2 * m + 1]
            delta = sums[0:1, 2 * m + 1 : 2 * m + 2]
            if count == 0:
                alpha = gamma / delta
                direction[m] = residual[m]
                image_dir[m] = image_res[m]
                solution[m] = alpha * direction[m]
            else:
                beta = gamma / gamma_prev[m]
                alpha = gamma / (delta - beta * gamma / alpha_prev[m])
                direction[m] = residual[m] + beta * direction[m]
                image_dir[m] = image_res[m] + beta * image_dir[m]
                solution[m] = solution[m] + alpha * direction[m]
            if count < ITERS - 1:
                residual[m] = residual[m] - alpha * image_dir[m]
            gamma_prev[m] = gamma
            alpha_prev[m] = alpha
    for m in range(members):
        x = solution[m]
        out_ref[0, m] = x[0:rows, 0:cols]
        out_ref[1, m] = (east(x) - west(x))[0:rows, 0:cols]
        out_ref[2, m] = (north(x) - south(x))[0:rows, 0:cols]
    if carry:
        cargo_copy.wait()


def surface_kernel_solve(surf, inside, own, cargo=None):
    ny = lax.axis_size("gridy")
    nx = lax.axis_size("gridx")
    fields, members, rows, cols = surf.shape
    carry = cargo is not None
    vmem = pl.BlockSpec(memory_space=pltpu.VMEM)
    anywhere = pl.BlockSpec(memory_space=pl.ANY)
    solved_shape = jax.ShapeDtypeStruct((3, members, rows, cols), jnp.float32)
    operands = (surf, inside, own) + ((cargo,) if carry else ())
    results = pl.pallas_call(
        functools.partial(solve_kernel, ny, nx, carry),
        out_shape=[solved_shape] + ([jax.ShapeDtypeStruct(cargo.shape, cargo.dtype)] if carry else []),
        in_specs=[vmem] * 3 + ([anywhere] if carry else []),
        out_specs=[vmem] + ([anywhere] if carry else []),
        scratch_shapes=[
            pltpu.VMEM((fields, members) + inside.shape, jnp.float32),
            pltpu.SemaphoreType.DMA((8,)),
            pltpu.SemaphoreType.DMA((8,)),
        ]
        + ([pltpu.SemaphoreType.DMA((2,))] if carry else [])
        + [
            pltpu.VMEM((ITERS, 8, 128), jnp.float32),
            pltpu.VMEM((ITERS, ny, 8, 128), jnp.float32),
            pltpu.VMEM((ITERS, 8, 128), jnp.float32),
            pltpu.VMEM((ITERS, nx, 8, 128), jnp.float32),
            pltpu.SemaphoreType.DMA((ITERS, ny)),
            pltpu.SemaphoreType.DMA((ITERS, ny)),
            pltpu.SemaphoreType.DMA((ITERS, nx)),
            pltpu.SemaphoreType.DMA((ITERS, nx)),
        ],
        compiler_params=pltpu.CompilerParams(collective_id=2 if carry else 1, has_side_effects=True),
    )(*operands)
    return results if carry else (results[0], None)


def volume_kernel(temp_ref, salt_ref, uvel_ref, vvel_ref, ocean_ref, cor_ref, n_ref, s_ref, e_ref, w_ref,
                  tn_ref, sn_ref, us_ref, vs_ref, tu_ref, tv_ref):
    levels, rows, cols = temp_ref.shape[1], temp_ref.shape[2], temp_ref.shape[3]
    row = lax.broadcasted_iota(jnp.int32, (rows, cols), 0)
    col = lax.broadcasted_iota(jnp.int32, (rows, cols), 1)
    top = row == rows - 1
    bottom = row == 0
    right = col == cols - 1
    left = col == 0
    ocean = ocean_ref[...]
    cor = cor_ref[...]

    def around(f, rims):
        n, s, e, w = rims
        return (
            jnp.where(right, e, pltpu.roll(f, cols - 1, 1)),
            jnp.where(left, w, pltpu.roll(f, 1, 1)),
            jnp.where(top, n, pltpu.roll(f, rows - 1, 0)),
            jnp.where(bottom, s, pltpu.roll(f, 1, 0)),
        )

    def rims_of(k, l):
        return (n_ref[k, 0, l], s_ref[k, 0, l], e_ref[k, 0, l], w_ref[k, 0, l])

    running = None
    running_rims = None
    tu = None
    tv = None
    for l in range(levels):
        t = temp_ref[0, l]
        s = salt_ref[0, l]
        u = uvel_ref[0, l]
        v = vvel_ref[0, l]
        rt, rs, ru, rv = rims_of(0, l), rims_of(1, l), rims_of(2, l), rims_of(3, l)
        layer = BETA_S * s - ALPHA_T * t
        layer_rims = tuple(BETA_S * b - ALPHA_T * a for a, b in zip(rt, rs))
        if running is None:
            running, running_rims = layer, layer_rims
        else:
            running = running + layer
            running_rims = tuple(a + b for a, b in zip(running_rims, layer_rims))
        press = PRESS_K * running
        press_rims = tuple(PRESS_K * a for a in running_rims)
        te, tw, tn, ts = around(t, rt)
        se, sw, sn, ss = around(s, rs)
        ue, uw, un, us = around(u, ru)
        ve, vw, vn, vs = around(v, rv)
        pe, pw, pn, ps = around(press, press_rims)
        tn_ref[0, l] = ocean * (
            t - STEP_DT * 0.5 * (u * (te - tw) + v * (tn - ts)) + KAPPA * (te + tw + tn + ts - 4.0 * t)
        )
        sn_ref[0, l] = ocean * (
            s - STEP_DT * 0.5 * (u * (se - sw) + v * (sn - ss)) + KAPPA * (se + sw + sn + ss - 4.0 * s)
        )
        ustar = ocean * (
            u + STEP_DT * (cor * v - 0.5 * (pe - pw) - DRAG_K * u) + VISCOSITY * (ue + uw + un + us - 4.0 * u)
        )
        vstar = ocean * (
            v + STEP_DT * (-cor * u - 0.5 * (pn - ps) - DRAG_K * v) + VISCOSITY * (ve + vw + vn + vs - 4.0 * v)
        )
        us_ref[0, l] = ustar
        vs_ref[0, l] = vstar
        tu = ustar if tu is None else tu + ustar
        tv = vstar if tv is None else tv + vstar
    tu_ref[0] = tu
    tv_ref[0] = tv


def volume_step(temp, salt, uvel, vvel, ocean, cor_tile, rims):
    members, levels, rows, cols = temp.shape
    field = pl.BlockSpec((1, levels, rows, cols), lambda m: (m, 0, 0, 0))
    plane = pl.BlockSpec((rows, cols), lambda m: (0, 0))
    north, south, east, west = rims
    row_rim = pl.BlockSpec((4, 1, levels, 1, cols), lambda m: (0, m, 0, 0, 0))
    col_rim = pl.BlockSpec((4, 1, levels, rows, 1), lambda m: (0, m, 0, 0, 0))
    surface = pl.BlockSpec((1, rows, cols), lambda m: (m, 0, 0))
    volume_shape = jax.ShapeDtypeStruct(temp.shape, jnp.float32)
    surface_shape = jax.ShapeDtypeStruct((members, rows, cols), jnp.float32)
    return pl.pallas_call(
        volume_kernel,
        grid=(members,),
        in_specs=[field] * 4 + [plane, plane, row_rim, row_rim, col_rim, col_rim],
        out_specs=[field] * 4 + [surface] * 2,
        out_shape=[volume_shape] * 4 + [surface_shape] * 2,
    )(temp, salt, uvel, vvel, ocean, cor_tile, north, south, east, west)


def ring(axis):
    count = lax.axis_size(axis)
    forward = [(i, (i + 1) % count) for i in range(count)]
    backward = [((i + 1) % count, i) for i in range(count)]
    return forward, backward


def exchange(block, ydim, xdim, south_keep, north_keep):
    fwd_y, bwd_y = ring("gridy")
    fwd_x, bwd_x = ring("gridx")
    rows = block.shape[ydim]
    cols = block.shape[xdim]
    north = lax.ppermute(lax.slice_in_dim(block, 0, 1, axis=ydim), "gridy", bwd_y) * north_keep
    south = lax.ppermute(lax.slice_in_dim(block, rows - 1, rows, axis=ydim), "gridy", fwd_y) * south_keep
    east = lax.ppermute(lax.slice_in_dim(block, 0, 1, axis=xdim), "gridx", bwd_x)
    west = lax.ppermute(lax.slice_in_dim(block, cols - 1, cols, axis=xdim), "gridx", fwd_x)
    return (east, west, north, south)


def exchange_fields(fields, south_keep, north_keep):
    fwd_y, bwd_y = ring("gridy")
    fwd_x, bwd_x = ring("gridx")
    north = lax.ppermute(jnp.stack([f[..., :1, :] for f in fields]), "gridy", bwd_y) * north_keep
    south = lax.ppermute(jnp.stack([f[..., -1:, :] for f in fields]), "gridy", fwd_y) * south_keep
    east = lax.ppermute(jnp.stack([f[..., :, :1] for f in fields]), "gridx", bwd_x)
    west = lax.ppermute(jnp.stack([f[..., :, -1:] for f in fields]), "gridx", fwd_x)
    return (north, south, east, west)


def sides(field, rims, ydim, xdim):
    east, west, north, south = rims
    rows = field.shape[ydim]
    cols = field.shape[xdim]
    east_side = jnp.concatenate([lax.slice_in_dim(field, 1, cols, axis=xdim), east], axis=xdim)
    west_side = jnp.concatenate([west, lax.slice_in_dim(field, 0, cols - 1, axis=xdim)], axis=xdim)
    north_side = jnp.concatenate([lax.slice_in_dim(field, 1, rows, axis=ydim), north], axis=ydim)
    south_side = jnp.concatenate([south, lax.slice_in_dim(field, 0, rows - 1, axis=ydim)], axis=ydim)
    return (east_side, west_side, north_side, south_side)


def pressure(temp, salt):
    return PRESS_K * jnp.cumsum(BETA_S * salt - ALPHA_T * temp, axis=-3)


def surface_apply(field, rims):
    east_side, west_side, north_side, south_side = sides(field, rims, 1, 2)
    return (1.0 + 4.0 * SURF_C) * field - SURF_C * (east_side + west_side + north_side + south_side)


def member_total(values):
    return jnp.sum(values, axis=(1, 2))


def widen(values):
    return values[:, None, None]


def combine(a, fa, b, fb):
    def one(u, v):
        left = u if a is None else widen(a) * u
        return left + (v if b is None else widen(b) * v)

    return one(fa[0], fb[0]), tuple(one(u, v) for u, v in zip(fa[1], fb[1]))


def scaled(a, fa):
    return widen(a) * fa[0], tuple(widen(a) * u for u in fa[1])


def padded_2(block, sides_of, width):
    for axis, dim in sides_of:
        count = lax.axis_size(axis)
        forward = [(i, (i + 1) % count) for i in range(count)]
        backward = [((i + 1) % count, i) for i in range(count)]
        size = block.shape[dim]
        low = lax.ppermute(lax.slice_in_dim(block, size - width, size, axis=dim), axis, forward)
        high = lax.ppermute(lax.slice_in_dim(block, 0, width, axis=dim), axis, backward)
        block = jnp.concatenate([low, block, high], axis=dim)
    return block


def crop(field, by):
    if by == 0:
        return field
    return field[..., by:-by, by:-by]


def around(field):
    return (
        field[..., 1:-1, 1:-1],
        field[..., 1:-1, 2:],
        field[..., 1:-1, :-2],
        field[..., 2:, 1:-1],
        field[..., :-2, 1:-1],
    )


def rows_at(inside, full, want):
    cut = full - want
    return inside if cut == 0 else inside[cut:-cut]


def apply_wide(field, inside):
    centre, east, west, north, south = around(field)
    return ((1.0 + 4.0 * SURF_C) * centre - SURF_C * (east + west + north + south)) * inside


def surface_solve(rhs, inside, width, full):
    residual, wide_r = rhs, width
    gamma_prev = None
    alpha_prev = None
    for count in range(ITERS):
        image_res = apply_wide(residual, rows_at(inside, full, wide_r - 1))
        own_res = crop(residual, wide_r)
        own_img = crop(image_res, wide_r - 1)
        dots = grid_sum(jnp.stack([member_total(own_res * own_res), member_total(own_res * own_img)]))
        gamma, delta = dots[0], dots[1]
        if count == 0:
            alpha = gamma / delta
            direction, wide_p = residual, wide_r
            image_dir, wide_s = image_res, wide_r - 1
            solution, wide_x = widen(alpha) * direction, wide_r
        else:
            beta = gamma / gamma_prev
            alpha = gamma / (delta - beta * gamma / alpha_prev)
            direction = residual + widen(beta) * crop(direction, wide_p - wide_r)
            wide_p = wide_r
            image_dir = image_res + widen(beta) * crop(image_dir, wide_s - (wide_r - 1))
            wide_s = wide_r - 1
            solution = crop(solution, wide_x - wide_r) + widen(alpha) * direction
            wide_x = wide_r
        if count < ITERS - 1:
            residual = crop(residual, 1) - widen(alpha) * image_dir
            wide_r -= 1
        gamma_prev = gamma
        alpha_prev = alpha
    return solution


def shards(temp, salt, uvel, vvel, eta, land_mask, clone_source):
    levels = temp.shape[1]
    rows = temp.shape[2]
    cols = temp.shape[3]
    ocean = land_mask.astype(jnp.float32)
    tile_row = lax.axis_index("gridy")
    tile_count = lax.axis_size("gridy")
    total_rows = rows * tile_count
    total_cols = cols * lax.axis_size("gridx")
    south_keep = (tile_row > 0).astype(jnp.float32)
    north_keep = (tile_row < tile_count - 1).astype(jnp.float32)
    latitude = (tile_row * rows + jnp.arange(rows, dtype=jnp.int32)).astype(jnp.float32) + 0.5
    coriolis = (CORI_K * (2.0 * latitude / total_rows - 1.0))[:, None]
    cor_tile = jnp.broadcast_to(coriolis, (rows, cols))
    band = 8
    block = 128
    frame_rows = rows + 2 * band
    frame_cols = cols + 2 * block
    row_at = lax.broadcasted_iota(jnp.int32, (frame_rows, frame_cols), 0)
    col_at = lax.broadcasted_iota(jnp.int32, (frame_rows, frame_cols), 1)
    global_row = tile_row * rows + jnp.where(row_at < rows + band, row_at, row_at - frame_rows)
    wide_inside = ((global_row >= 0) & (global_row < total_rows)).astype(jnp.float32)
    own_mask = ((row_at < rows) & (col_at < cols)).astype(jnp.float32)
    for count in range(STEPS):
        fields = (temp, salt, uvel, vvel)
        rims = exchange_fields(fields, south_keep, north_keep)
        temp_next, salt_next, ustar, vstar, trans_u, trans_v = volume_step(
            temp, salt, uvel, vvel, ocean, cor_tile, rims
        )
        last = count == STEPS - 1
        cargo = jnp.stack((temp_next, salt_next, ustar, vstar)) if last else None
        solved, cargo_other = surface_kernel_solve(
            jnp.stack((trans_u, trans_v, eta)), wide_inside, own_mask, cargo
        )
        eta = solved[0]
        east_west = solved[1]
        north_south = solved[2]
        uvel = ocean * (ustar - GRAV_K * 0.5 * east_west[:, None])
        vvel = ocean * (vstar - GRAV_K * 0.5 * north_south[:, None])
        temp = temp_next
        salt = salt_next
    zonal_scale = 1.0 / jnp.sqrt(jnp.float32(total_cols))
    score_scale = 1.0 / jnp.sqrt(jnp.float32(levels * total_rows))
    lat_weight = latitude / total_rows
    members = temp.shape[0]
    zonal_local = jnp.sum(vvel, axis=3)
    depth_weight = (levels - jnp.arange(levels, dtype=jnp.int32)).astype(jnp.float32)
    score_local = jnp.sum(zonal_local * depth_weight[None, :, None] * lat_weight[None, None, :], axis=(1, 2))
    slot = lax.broadcasted_iota(jnp.int32, (tile_count, 1, 1, 1), 0) == tile_row
    zonal_slots = jnp.where(slot, zonal_local[None], 0.0).reshape(-1, 128)
    score_row = jnp.zeros((8, 128), jnp.float32).at[0, :members].set(score_local)
    summed = grid_sum(jnp.concatenate([zonal_slots, score_row], axis=0))
    zonal_whole = summed[: zonal_slots.shape[0]].reshape((tile_count,) + zonal_local.shape)
    zonal_whole = jnp.sum(jnp.where(slot, zonal_whole, 0.0), axis=0)
    overturn = jnp.cumsum(zonal_whole, axis=1) * zonal_scale
    score = summed[zonal_slots.shape[0], :members] * (zonal_scale * score_scale)
    swap = [(0, 1), (1, 0)]
    mine = lax.axis_index("member")
    score_slab = jnp.zeros((members, 1) + eta.shape[1:], jnp.float32).at[:, 0, 0, 0].set(score)
    surface_last = jnp.concatenate([solved.transpose(1, 0, 2, 3), score_slab], axis=1)
    surface_other = lax.ppermute(surface_last, "member", swap)
    score_other = surface_other[:, 3, 0, 0]
    every_score = jnp.where(
        mine == 0, jnp.concatenate([score, score_other]), jnp.concatenate([score_other, score])
    )
    here = (clone_source // members) == mine
    local_at = clone_source % members

    def pick(local, other):
        chosen = []
        for place in range(members):
            from_here = lax.dynamic_index_in_dim(local, local_at[place], 0, keepdims=False)
            from_other = lax.dynamic_index_in_dim(other, local_at[place], 0, keepdims=False)
            chosen.append(jnp.where(here[place], from_here, from_other))
        return jnp.stack(chosen)

    uvel_other = ocean * (cargo_other[2] - GRAV_K * 0.5 * surface_other[:, 1][:, None])
    vvel_other = ocean * (cargo_other[3] - GRAV_K * 0.5 * surface_other[:, 2][:, None])
    new_temp = pick(temp, cargo_other[0])
    new_salt = pick(salt, cargo_other[1])
    new_uvel = pick(uvel, uvel_other)
    new_vvel = pick(vvel, vvel_other)
    new_eta = pick(eta, surface_other[:, 0])
    clone_weight = jnp.take(every_score, clone_source, axis=0) - jnp.mean(every_score)
    return (new_temp, new_salt, new_uvel, new_vvel, new_eta, overturn, clone_weight)


def solution(mesh):
    in_specs = (
        P("member", None, "gridy", "gridx"),
        P("member", None, "gridy", "gridx"),
        P("member", None, "gridy", "gridx"),
        P("member", None, "gridy", "gridx"),
        P("member", "gridy", "gridx"),
        P("gridy", "gridx"),
        P("member"),
    )
    out_specs = (
        P("member", None, "gridy", "gridx"),
        P("member", None, "gridy", "gridx"),
        P("member", None, "gridy", "gridx"),
        P("member", None, "gridy", "gridx"),
        P("member", "gridy", "gridx"),
        P("member", None, "gridy"),
        P("member"),
    )
    return jax.shard_map(shards, mesh=mesh, in_specs=in_specs, out_specs=out_specs, check_vma=False)
```

```python
import functools

import jax
import jax.numpy as jnp
from jax import lax
from jax.experimental import pallas as pl
from jax.experimental.pallas import tpu as pltpu
from jax.sharding import PartitionSpec as P

STEPS = 2
ITERS = 3


ALPHA_T = 0.8
BETA_S = 0.6
PRESS_K = 0.25
STEP_DT = 0.1
KAPPA = 0.1
VISCOSITY = 0.1
DRAG_K = 0.05
CORI_K = 1.0
SURF_C = 4.0
DIV_K = 0.5
GRAV_K = 0.5


def tree_sum(values, axes):
    for axis in axes:
        count = lax.axis_size(axis)
        step = 1
        while step < count:
            pairs = [(i, i ^ step) for i in range(count)]
            values = values + lax.ppermute(values, axis, pairs)
            step *= 2
    return values


def gather_sum_kernel(ny, nx, x_ref, o_ref, recv_y, recv_x, part, send_y, rsem_y, send_x, rsem_x):
    mesh_id = pl.DeviceIdType.MESH
    member = lax.axis_index("member")
    my = lax.axis_index("gridy")
    mx = lax.axis_index("gridx")
    barrier = pltpu.get_barrier_semaphore()
    for d in range(1, ny):
        pl.semaphore_signal(barrier, 1, device_id=(member, (my + d) % ny, mx), device_id_type=mesh_id)
    for d in range(1, nx):
        pl.semaphore_signal(barrier, 1, device_id=(member, my, (mx + d) % nx), device_id_type=mesh_id)
    pl.semaphore_wait(barrier, (ny - 1) + (nx - 1))

    def phase(src, recv, send_sem, recv_sem, count, me, device):
        recv[me] = src[...]
        sent = []
        for d in range(1, count):
            peer = (me + d) % count
            copy = pltpu.make_async_remote_copy(
                src_ref=src,
                dst_ref=recv.at[me],
                send_sem=send_sem.at[peer],
                recv_sem=recv_sem.at[me],
                device_id=device(peer),
                device_id_type=mesh_id,
            )
            copy.start()
            sent.append(copy)
        for d in range(1, count):
            peer = (me + d) % count
            pltpu.make_async_remote_copy(
                src_ref=src,
                dst_ref=recv.at[peer],
                send_sem=send_sem.at[peer],
                recv_sem=recv_sem.at[peer],
                device_id=device(peer),
                device_id_type=mesh_id,
            ).wait_recv()
        for copy in sent:
            copy.wait_send()
        total = recv[0]
        for j in range(1, count):
            total = total + recv[j]
        return total

    part[...] = phase(x_ref, recv_y, send_y, rsem_y, ny, my, lambda p: (member, p, mx))
    o_ref[...] = phase(part, recv_x, send_x, rsem_x, nx, mx, lambda p: (member, my, p))


def grid_sum(values):
    ny = lax.axis_size("gridy")
    nx = lax.axis_size("gridx")
    shape = values.shape
    return pl.pallas_call(
        functools.partial(gather_sum_kernel, ny, nx),
        out_shape=jax.ShapeDtypeStruct(shape, values.dtype),
        in_specs=[pl.BlockSpec(memory_space=pltpu.VMEM)],
        out_specs=pl.BlockSpec(memory_space=pltpu.VMEM),
        scratch_shapes=[
            pltpu.VMEM((ny,) + shape, values.dtype),
            pltpu.VMEM((nx,) + shape, values.dtype),
            pltpu.VMEM(shape, values.dtype),
            pltpu.SemaphoreType.DMA((ny,)),
            pltpu.SemaphoreType.DMA((ny,)),
            pltpu.SemaphoreType.DMA((nx,)),
            pltpu.SemaphoreType.DMA((nx,)),
        ],
        compiler_params=pltpu.CompilerParams(collective_id=0, has_side_effects=True),
    )(values)


def exchange_sum(k, vec, ny, nx, bufs, device_ids):
    send_y, recv_y, send_x, recv_x, sy, ry, sx, rx = bufs
    my, mx, along_y, along_x = device_ids
    mesh_id = pl.DeviceIdType.MESH

    def phase(value, send_buf, recv, send_sem, recv_sem, count, me, device):
        send_buf[k] = value
        recv[k, me] = value
        sent = []
        for d in range(1, count):
            peer = (me + d) % count
            copy = pltpu.make_async_remote_copy(
                src_ref=send_buf.at[k],
                dst_ref=recv.at[k, me],
                send_sem=send_sem.at[k, peer],
                recv_sem=recv_sem.at[k, me],
                device_id=device(peer),
                device_id_type=mesh_id,
            )
            copy.start()
            sent.append(copy)
        for d in range(1, count):
            peer = (me + d) % count
            pltpu.make_async_remote_copy(
                src_ref=send_buf.at[k],
                dst_ref=recv.at[k, peer],
                send_sem=send_sem.at[k, peer],
                recv_sem=recv_sem.at[k, peer],
                device_id=device(peer),
                device_id_type=mesh_id,
            ).wait_recv()
        for copy in sent:
            copy.wait_send()
        total = recv[k, 0]
        for j in range(1, count):
            total = total + recv[k, j]
        return total

    partial = phase(vec, send_y, recv_y, sy, ry, ny, my, along_y)
    return phase(partial, send_x, recv_x, sx, rx, nx, mx, along_x)


def solve_kernel(ny, nx, carry, *refs):
    if carry:
        surf_ref, inside_ref, own_ref, cargo_ref, out_ref, cargo_out, frame, hsend, hrecv, csem = refs[:10]
        bufs = refs[10:]
    else:
        surf_ref, inside_ref, own_ref, out_ref, frame, hsend, hrecv = refs[:7]
        bufs = refs[7:]
    mesh_id = pl.DeviceIdType.MESH
    member = lax.axis_index("member")
    my = lax.axis_index("gridy")
    mx = lax.axis_index("gridx")
    along_y = lambda p: (member, p, mx)
    along_x = lambda p: (member, my, p)
    barrier = pltpu.get_barrier_semaphore()
    for d in range(1, ny):
        pl.semaphore_signal(barrier, 1, device_id=along_y((my + d) % ny), device_id_type=mesh_id)
    for d in range(1, nx):
        pl.semaphore_signal(barrier, 1, device_id=along_x((mx + d) % nx), device_id_type=mesh_id)
    for dy in (1, ny - 1):
        for dx in (1, nx - 1):
            pl.semaphore_signal(
                barrier, 1, device_id=(member, (my + dy) % ny, (mx + dx) % nx), device_id_type=mesh_id
            )
    rows, cols = surf_ref.shape[2], surf_ref.shape[3]
    wide_rows, wide_cols = frame.shape[2], frame.shape[3]
    band = (wide_rows - rows) // 2
    block = (wide_cols - cols) // 2
    frame[:, :, 0:rows, 0:cols] = surf_ref[...]
    if carry:
        partner = (lax.axis_index("member") + 1) % 2
        pl.semaphore_signal(barrier, 1, device_id=(partner, my, mx), device_id_type=mesh_id)
    pl.semaphore_wait(barrier, (ny - 1) + (nx - 1) + 4 + (1 if carry else 0))
    cargo_copies = []
    if carry:
        for part in range(cargo_ref.shape[0]):
            for half in range(cargo_ref.shape[1]):
                piece = part * cargo_ref.shape[1] + half
                copy = pltpu.make_async_remote_copy(
                    src_ref=cargo_ref.at[part, half], dst_ref=cargo_out.at[part, half],
                    send_sem=csem.at[0, piece], recv_sem=csem.at[1, piece],
                    device_id=(partner, my, mx), device_id_type=mesh_id,
                )
                copy.start()
                cargo_copies.append(copy)

    def halo_copies(first, moves):
        started = []
        for slot, (src, dst, device) in enumerate(moves, start=first):
            copy = pltpu.make_async_remote_copy(
                src_ref=src, dst_ref=dst, send_sem=hsend.at[slot], recv_sem=hrecv.at[slot],
                device_id=device, device_id_type=mesh_id,
            )
            copy.start()
            started.append(copy)
        for copy in started:
            copy.wait()

    up, down = (my + 1) % ny, (my + ny - 1) % ny
    right, left = (mx + 1) % nx, (mx + nx - 1) % nx
    top_rows = slice(0, band)
    low_rows = slice(rows - band, rows)
    own_rows = slice(0, rows)
    west_part = slice(0, block)
    east_part = slice(cols - block, cols)
    own_cols = slice(0, cols)
    north_halo = slice(rows, rows + band)
    south_halo = slice(rows + band, wide_rows)
    east_halo = slice(cols, cols + block)
    west_halo = slice(cols + block, wide_cols)
    halo_copies(0, [
        (frame.at[:, :, top_rows, own_cols], frame.at[:, :, north_halo, own_cols], (member, down, mx)),
        (frame.at[:, :, low_rows, own_cols], frame.at[:, :, south_halo, own_cols], (member, up, mx)),
        (frame.at[:, :, own_rows, west_part], frame.at[:, :, own_rows, east_halo], (member, my, left)),
        (frame.at[:, :, own_rows, east_part], frame.at[:, :, own_rows, west_halo], (member, my, right)),
        (frame.at[:, :, top_rows, west_part], frame.at[:, :, north_halo, east_halo], (member, down, left)),
        (frame.at[:, :, top_rows, east_part], frame.at[:, :, north_halo, west_halo], (member, down, right)),
        (frame.at[:, :, low_rows, west_part], frame.at[:, :, south_halo, east_halo], (member, up, left)),
        (frame.at[:, :, low_rows, east_part], frame.at[:, :, south_halo, west_halo], (member, up, right)),
    ])

    members = surf_ref.shape[1]
    inside = inside_ref[...]
    own = own_ref[...] > 0.5

    def east(f):
        return pltpu.roll(f, wide_cols - 1, 1)

    def west(f):
        return pltpu.roll(f, 1, 1)

    def north(f):
        return pltpu.roll(f, wide_rows - 1, 0)

    def south(f):
        return pltpu.roll(f, 1, 0)

    def apply(f):
        return ((1.0 + 4.0 * SURF_C) * f - SURF_C * (east(f) + west(f) + north(f) + south(f))) * inside

    def total(f):
        return jnp.sum(jnp.where(own, f, 0.0), axis=(0, 1), keepdims=True)

    residual = []
    for m in range(members):
        trans_u = frame[0, m] * inside
        trans_v = frame[1, m] * inside
        level = frame[2, m] * inside
        residual.append(
            (level - DIV_K * 0.5 * (east(trans_u) - west(trans_u) + (north(trans_v) - south(trans_v)))) * inside
        )
    lane = lax.broadcasted_iota(jnp.int32, (8, 128), 1)
    direction = [None] * members
    image_dir = [None] * members
    solution = [None] * members
    gamma_prev = [None] * members
    alpha_prev = [None] * members
    for count in range(ITERS):
        image_res = [apply(residual[m]) for m in range(members)]
        vec = jnp.zeros((8, 128), jnp.float32)
        for m in range(members):
            vec = jnp.where(lane == 2 * m, total(residual[m] * residual[m]), vec)
            vec = jnp.where(lane == 2 * m + 1, total(residual[m] * image_res[m]), vec)
        sums = exchange_sum(count, vec, ny, nx, bufs, (my, mx, along_y, along_x))
        for m in range(members):
            gamma = sums[0:1, 2 * m : 2 * m + 1]
            delta = sums[0:1, 2 * m + 1 : 2 * m + 2]
            if count == 0:
                alpha = gamma / delta
                direction[m] = residual[m]
                image_dir[m] = image_res[m]
                solution[m] = alpha * direction[m]
            else:
                beta = gamma / gamma_prev[m]
                alpha = gamma / (delta - beta * gamma / alpha_prev[m])
                direction[m] = residual[m] + beta * direction[m]
                image_dir[m] = image_res[m] + beta * image_dir[m]
                solution[m] = solution[m] + alpha * direction[m]
            if count < ITERS - 1:
                residual[m] = residual[m] - alpha * image_dir[m]
            gamma_prev[m] = gamma
            alpha_prev[m] = alpha
    for m in range(members):
        x = solution[m]
        out_ref[0, m] = x[0:rows, 0:cols]
        out_ref[1, m] = (east(x) - west(x))[0:rows, 0:cols]
        out_ref[2, m] = (north(x) - south(x))[0:rows, 0:cols]
    for copy in cargo_copies:
        copy.wait()


def surface_kernel_solve(surf, inside, own, cargo=None):
    ny = lax.axis_size("gridy")
    nx = lax.axis_size("gridx")
    fields, members, rows, cols = surf.shape
    carry = cargo is not None
    vmem = pl.BlockSpec(memory_space=pltpu.VMEM)
    anywhere = pl.BlockSpec(memory_space=pl.ANY)
    solved_shape = jax.ShapeDtypeStruct((3, members, rows, cols), jnp.float32)
    operands = (surf, inside, own) + ((cargo,) if carry else ())
    results = pl.pallas_call(
        functools.partial(solve_kernel, ny, nx, carry),
        out_shape=[solved_shape] + ([jax.ShapeDtypeStruct(cargo.shape, cargo.dtype)] if carry else []),
        in_specs=[vmem] * 3 + ([anywhere] if carry else []),
        out_specs=[vmem] + ([anywhere] if carry else []),
        scratch_shapes=[
            pltpu.VMEM((fields, members) + inside.shape, jnp.float32),
            pltpu.SemaphoreType.DMA((8,)),
            pltpu.SemaphoreType.DMA((8,)),
        ]
        + ([pltpu.SemaphoreType.DMA((2, cargo.shape[0] * cargo.shape[1]))] if carry else [])
        + [
            pltpu.VMEM((ITERS, 8, 128), jnp.float32),
            pltpu.VMEM((ITERS, ny, 8, 128), jnp.float32),
            pltpu.VMEM((ITERS, 8, 128), jnp.float32),
            pltpu.VMEM((ITERS, nx, 8, 128), jnp.float32),
            pltpu.SemaphoreType.DMA((ITERS, ny)),
            pltpu.SemaphoreType.DMA((ITERS, ny)),
            pltpu.SemaphoreType.DMA((ITERS, nx)),
            pltpu.SemaphoreType.DMA((ITERS, nx)),
        ],
        compiler_params=pltpu.CompilerParams(collective_id=2 if carry else 1, has_side_effects=True),
    )(*operands)
    return results if carry else (results[0], None)


def volume_kernel(temp_ref, salt_ref, uvel_ref, vvel_ref, ocean_ref, cor_ref, n_ref, s_ref, e_ref, w_ref,
                  tn_ref, sn_ref, us_ref, vs_ref, tu_ref, tv_ref):
    levels, rows, cols = temp_ref.shape[1], temp_ref.shape[2], temp_ref.shape[3]
    row = lax.broadcasted_iota(jnp.int32, (rows, cols), 0)
    col = lax.broadcasted_iota(jnp.int32, (rows, cols), 1)
    top = row == rows - 1
    bottom = row == 0
    right = col == cols - 1
    left = col == 0
    ocean = ocean_ref[...]
    cor = cor_ref[...]

    def around(f, rims):
        n, s, e, w = rims
        return (
            jnp.where(right, e, pltpu.roll(f, cols - 1, 1)),
            jnp.where(left, w, pltpu.roll(f, 1, 1)),
            jnp.where(top, n, pltpu.roll(f, rows - 1, 0)),
            jnp.where(bottom, s, pltpu.roll(f, 1, 0)),
        )

    def rims_of(k, l):
        return (n_ref[k, 0, l], s_ref[k, 0, l], e_ref[k, 0, l], w_ref[k, 0, l])

    running = None
    running_rims = None
    tu = None
    tv = None
    for l in range(levels):
        t = temp_ref[0, l]
        s = salt_ref[0, l]
        u = uvel_ref[0, l]
        v = vvel_ref[0, l]
        rt, rs, ru, rv = rims_of(0, l), rims_of(1, l), rims_of(2, l), rims_of(3, l)
        layer = BETA_S * s - ALPHA_T * t
        layer_rims = tuple(BETA_S * b - ALPHA_T * a for a, b in zip(rt, rs))
        if running is None:
            running, running_rims = layer, layer_rims
        else:
            running = running + layer
            running_rims = tuple(a + b for a, b in zip(running_rims, layer_rims))
        press = PRESS_K * running
        press_rims = tuple(PRESS_K * a for a in running_rims)
        te, tw, tn, ts = around(t, rt)
        se, sw, sn, ss = around(s, rs)
        ue, uw, un, us = around(u, ru)
        ve, vw, vn, vs = around(v, rv)
        pe, pw, pn, ps = around(press, press_rims)
        tn_ref[0, l] = ocean * (
            t - STEP_DT * 0.5 * (u * (te - tw) + v * (tn - ts)) + KAPPA * (te + tw + tn + ts - 4.0 * t)
        )
        sn_ref[0, l] = ocean * (
            s - STEP_DT * 0.5 * (u * (se - sw) + v * (sn - ss)) + KAPPA * (se + sw + sn + ss - 4.0 * s)
        )
        ustar = ocean * (
            u + STEP_DT * (cor * v - 0.5 * (pe - pw) - DRAG_K * u) + VISCOSITY * (ue + uw + un + us - 4.0 * u)
        )
        vstar = ocean * (
            v + STEP_DT * (-cor * u - 0.5 * (pn - ps) - DRAG_K * v) + VISCOSITY * (ve + vw + vn + vs - 4.0 * v)
        )
        us_ref[0, l] = ustar
        vs_ref[0, l] = vstar
        tu = ustar if tu is None else tu + ustar
        tv = vstar if tv is None else tv + vstar
    tu_ref[0] = tu
    tv_ref[0] = tv


def volume_step(temp, salt, uvel, vvel, ocean, cor_tile, rims):
    members, levels, rows, cols = temp.shape
    field = pl.BlockSpec((1, levels, rows, cols), lambda m: (m, 0, 0, 0))
    plane = pl.BlockSpec((rows, cols), lambda m: (0, 0))
    north, south, east, west = rims
    row_rim = pl.BlockSpec((4, 1, levels, 1, cols), lambda m: (0, m, 0, 0, 0))
    col_rim = pl.BlockSpec((4, 1, levels, rows, 1), lambda m: (0, m, 0, 0, 0))
    surface = pl.BlockSpec((1, rows, cols), lambda m: (m, 0, 0))
    volume_shape = jax.ShapeDtypeStruct(temp.shape, jnp.float32)
    surface_shape = jax.ShapeDtypeStruct((members, rows, cols), jnp.float32)
    return pl.pallas_call(
        volume_kernel,
        grid=(members,),
        in_specs=[field] * 4 + [plane, plane, row_rim, row_rim, col_rim, col_rim],
        out_specs=[field] * 4 + [surface] * 2,
        out_shape=[volume_shape] * 4 + [surface_shape] * 2,
    )(temp, salt, uvel, vvel, ocean, cor_tile, north, south, east, west)


def ring(axis):
    count = lax.axis_size(axis)
    forward = [(i, (i + 1) % count) for i in range(count)]
    backward = [((i + 1) % count, i) for i in range(count)]
    return forward, backward


def exchange(block, ydim, xdim, south_keep, north_keep):
    fwd_y, bwd_y = ring("gridy")
    fwd_x, bwd_x = ring("gridx")
    rows = block.shape[ydim]
    cols = block.shape[xdim]
    north = lax.ppermute(lax.slice_in_dim(block, 0, 1, axis=ydim), "gridy", bwd_y) * north_keep
    south = lax.ppermute(lax.slice_in_dim(block, rows - 1, rows, axis=ydim), "gridy", fwd_y) * south_keep
    east = lax.ppermute(lax.slice_in_dim(block, 0, 1, axis=xdim), "gridx", bwd_x)
    west = lax.ppermute(lax.slice_in_dim(block, cols - 1, cols, axis=xdim), "gridx", fwd_x)
    return (east, west, north, south)


def exchange_fields(fields, south_keep, north_keep):
    fwd_y, bwd_y = ring("gridy")
    fwd_x, bwd_x = ring("gridx")
    north = lax.ppermute(jnp.stack([f[..., :1, :] for f in fields]), "gridy", bwd_y) * north_keep
    south = lax.ppermute(jnp.stack([f[..., -1:, :] for f in fields]), "gridy", fwd_y) * south_keep
    east = lax.ppermute(jnp.stack([f[..., :, :1] for f in fields]), "gridx", bwd_x)
    west = lax.ppermute(jnp.stack([f[..., :, -1:] for f in fields]), "gridx", fwd_x)
    return (north, south, east, west)


def sides(field, rims, ydim, xdim):
    east, west, north, south = rims
    rows = field.shape[ydim]
    cols = field.shape[xdim]
    east_side = jnp.concatenate([lax.slice_in_dim(field, 1, cols, axis=xdim), east], axis=xdim)
    west_side = jnp.concatenate([west, lax.slice_in_dim(field, 0, cols - 1, axis=xdim)], axis=xdim)
    north_side = jnp.concatenate([lax.slice_in_dim(field, 1, rows, axis=ydim), north], axis=ydim)
    south_side = jnp.concatenate([south, lax.slice_in_dim(field, 0, rows - 1, axis=ydim)], axis=ydim)
    return (east_side, west_side, north_side, south_side)


def pressure(temp, salt):
    return PRESS_K * jnp.cumsum(BETA_S * salt - ALPHA_T * temp, axis=-3)


def surface_apply(field, rims):
    east_side, west_side, north_side, south_side = sides(field, rims, 1, 2)
    return (1.0 + 4.0 * SURF_C) * field - SURF_C * (east_side + west_side + north_side + south_side)


def member_total(values):
    return jnp.sum(values, axis=(1, 2))


def widen(values):
    return values[:, None, None]


def combine(a, fa, b, fb):
    def one(u, v):
        left = u if a is None else widen(a) * u
        return left + (v if b is None else widen(b) * v)

    return one(fa[0], fb[0]), tuple(one(u, v) for u, v in zip(fa[1], fb[1]))


def scaled(a, fa):
    return widen(a) * fa[0], tuple(widen(a) * u for u in fa[1])


def padded_2(block, sides_of, width):
    for axis, dim in sides_of:
        count = lax.axis_size(axis)
        forward = [(i, (i + 1) % count) for i in range(count)]
        backward = [((i + 1) % count, i) for i in range(count)]
        size = block.shape[dim]
        low = lax.ppermute(lax.slice_in_dim(block, size - width, size, axis=dim), axis, forward)
        high = lax.ppermute(lax.slice_in_dim(block, 0, width, axis=dim), axis, backward)
        block = jnp.concatenate([low, block, high], axis=dim)
    return block


def crop(field, by):
    if by == 0:
        return field
    return field[..., by:-by, by:-by]


def around(field):
    return (
        field[..., 1:-1, 1:-1],
        field[..., 1:-1, 2:],
        field[..., 1:-1, :-2],
        field[..., 2:, 1:-1],
        field[..., :-2, 1:-1],
    )


def rows_at(inside, full, want):
    cut = full - want
    return inside if cut == 0 else inside[cut:-cut]


def apply_wide(field, inside):
    centre, east, west, north, south = around(field)
    return ((1.0 + 4.0 * SURF_C) * centre - SURF_C * (east + west + north + south)) * inside


def surface_solve(rhs, inside, width, full):
    residual, wide_r = rhs, width
    gamma_prev = None
    alpha_prev = None
    for count in range(ITERS):
        image_res = apply_wide(residual, rows_at(inside, full, wide_r - 1))
        own_res = crop(residual, wide_r)
        own_img = crop(image_res, wide_r - 1)
        dots = grid_sum(jnp.stack([member_total(own_res * own_res), member_total(own_res * own_img)]))
        gamma, delta = dots[0], dots[1]
        if count == 0:
            alpha = gamma / delta
            direction, wide_p = residual, wide_r
            image_dir, wide_s = image_res, wide_r - 1
            solution, wide_x = widen(alpha) * direction, wide_r
        else:
            beta = gamma / gamma_prev
            alpha = gamma / (delta - beta * gamma / alpha_prev)
            direction = residual + widen(beta) * crop(direction, wide_p - wide_r)
            wide_p = wide_r
            image_dir = image_res + widen(beta) * crop(image_dir, wide_s - (wide_r - 1))
            wide_s = wide_r - 1
            solution = crop(solution, wide_x - wide_r) + widen(alpha) * direction
            wide_x = wide_r
        if count < ITERS - 1:
            residual = crop(residual, 1) - widen(alpha) * image_dir
            wide_r -= 1
        gamma_prev = gamma
        alpha_prev = alpha
    return solution


def shards(temp, salt, uvel, vvel, eta, land_mask, clone_source):
    levels = temp.shape[1]
    rows = temp.shape[2]
    cols = temp.shape[3]
    ocean = land_mask.astype(jnp.float32)
    tile_row = lax.axis_index("gridy")
    tile_count = lax.axis_size("gridy")
    total_rows = rows * tile_count
    total_cols = cols * lax.axis_size("gridx")
    south_keep = (tile_row > 0).astype(jnp.float32)
    north_keep = (tile_row < tile_count - 1).astype(jnp.float32)
    latitude = (tile_row * rows + jnp.arange(rows, dtype=jnp.int32)).astype(jnp.float32) + 0.5
    coriolis = (CORI_K * (2.0 * latitude / total_rows - 1.0))[:, None]
    cor_tile = jnp.broadcast_to(coriolis, (rows, cols))
    band = 8
    block = 128
    frame_rows = rows + 2 * band
    frame_cols = cols + 2 * block
    row_at = lax.broadcasted_iota(jnp.int32, (frame_rows, frame_cols), 0)
    col_at = lax.broadcasted_iota(jnp.int32, (frame_rows, frame_cols), 1)
    global_row = tile_row * rows + jnp.where(row_at < rows + band, row_at, row_at - frame_rows)
    wide_inside = ((global_row >= 0) & (global_row < total_rows)).astype(jnp.float32)
    own_mask = ((row_at < rows) & (col_at < cols)).astype(jnp.float32)
    for count in range(STEPS):
        fields = (temp, salt, uvel, vvel)
        rims = exchange_fields(fields, south_keep, north_keep)
        temp_next, salt_next, ustar, vstar, trans_u, trans_v = volume_step(
            temp, salt, uvel, vvel, ocean, cor_tile, rims
        )
        last = count == STEPS - 1
        cargo = jnp.stack((temp_next, salt_next, ustar, vstar)) if last else None
        solved, cargo_other = surface_kernel_solve(
            jnp.stack((trans_u, trans_v, eta)), wide_inside, own_mask, cargo
        )
        eta = solved[0]
        east_west = solved[1]
        north_south = solved[2]
        uvel = ocean * (ustar - GRAV_K * 0.5 * east_west[:, None])
        vvel = ocean * (vstar - GRAV_K * 0.5 * north_south[:, None])
        temp = temp_next
        salt = salt_next
    zonal_scale = 1.0 / jnp.sqrt(jnp.float32(total_cols))
    score_scale = 1.0 / jnp.sqrt(jnp.float32(levels * total_rows))
    lat_weight = latitude / total_rows
    members = temp.shape[0]
    zonal_local = jnp.sum(vvel, axis=3)
    depth_weight = (levels - jnp.arange(levels, dtype=jnp.int32)).astype(jnp.float32)
    score_local = jnp.sum(zonal_local * depth_weight[None, :, None] * lat_weight[None, None, :], axis=(1, 2))
    slot = lax.broadcasted_iota(jnp.int32, (tile_count, 1, 1, 1), 0) == tile_row
    zonal_slots = jnp.where(slot, zonal_local[None], 0.0).reshape(-1, 128)
    score_row = jnp.zeros((8, 128), jnp.float32).at[0, :members].set(score_local)
    summed = grid_sum(jnp.concatenate([zonal_slots, score_row], axis=0))
    zonal_whole = summed[: zonal_slots.shape[0]].reshape((tile_count,) + zonal_local.shape)
    zonal_whole = jnp.sum(jnp.where(slot, zonal_whole, 0.0), axis=0)
    overturn = jnp.cumsum(zonal_whole, axis=1) * zonal_scale
    score = summed[zonal_slots.shape[0], :members] * (zonal_scale * score_scale)
    swap = [(0, 1), (1, 0)]
    mine = lax.axis_index("member")
    score_slab = jnp.zeros((members, 1) + eta.shape[1:], jnp.float32).at[:, 0, 0, 0].set(score)
    surface_last = jnp.concatenate([solved.transpose(1, 0, 2, 3), score_slab], axis=1)
    surface_other = lax.ppermute(surface_last, "member", swap)
    score_other = surface_other[:, 3, 0, 0]
    every_score = jnp.where(
        mine == 0, jnp.concatenate([score, score_other]), jnp.concatenate([score_other, score])
    )
    here = (clone_source // members) == mine
    local_at = clone_source % members

    def pick(local, other):
        chosen = []
        for place in range(members):
            from_here = lax.dynamic_index_in_dim(local, local_at[place], 0, keepdims=False)
            from_other = lax.dynamic_index_in_dim(other, local_at[place], 0, keepdims=False)
            chosen.append(jnp.where(here[place], from_here, from_other))
        return jnp.stack(chosen)

    uvel_other = ocean * (cargo_other[2] - GRAV_K * 0.5 * surface_other[:, 1][:, None])
    vvel_other = ocean * (cargo_other[3] - GRAV_K * 0.5 * surface_other[:, 2][:, None])
    new_temp = pick(temp, cargo_other[0])
    new_salt = pick(salt, cargo_other[1])
    new_uvel = pick(uvel, uvel_other)
    new_vvel = pick(vvel, vvel_other)
    new_eta = pick(eta, surface_other[:, 0])
    clone_weight = jnp.take(every_score, clone_source, axis=0) - jnp.mean(every_score)
    return (new_temp, new_salt, new_uvel, new_vvel, new_eta, overturn, clone_weight)


def solution(mesh):
    in_specs = (
        P("member", None, "gridy", "gridx"),
        P("member", None, "gridy", "gridx"),
        P("member", None, "gridy", "gridx"),
        P("member", None, "gridy", "gridx"),
        P("member", "gridy", "gridx"),
        P("gridy", "gridx"),
        P("member"),
    )
    out_specs = (
        P("member", None, "gridy", "gridx"),
        P("member", None, "gridy", "gridx"),
        P("member", None, "gridy", "gridx"),
        P("member", None, "gridy", "gridx"),
        P("member", "gridy", "gridx"),
        P("member", None, "gridy"),
        P("member"),
    )
    return jax.shard_map(shards, mesh=mesh, in_specs=in_specs, out_specs=out_specs, check_vma=False)
```

```python
import functools

import jax
import jax.numpy as jnp
from jax import lax
from jax.experimental import pallas as pl
from jax.experimental.pallas import tpu as pltpu
from jax.sharding import PartitionSpec as P

STEPS = 2
ITERS = 3


ALPHA_T = 0.8
BETA_S = 0.6
PRESS_K = 0.25
STEP_DT = 0.1
KAPPA = 0.1
VISCOSITY = 0.1
DRAG_K = 0.05
CORI_K = 1.0
SURF_C = 4.0
DIV_K = 0.5
GRAV_K = 0.5


def tree_sum(values, axes):
    for axis in axes:
        count = lax.axis_size(axis)
        step = 1
        while step < count:
            pairs = [(i, i ^ step) for i in range(count)]
            values = values + lax.ppermute(values, axis, pairs)
            step *= 2
    return values


def gather_sum_kernel(ny, nx, x_ref, o_ref, recv_y, recv_x, part, send_y, rsem_y, send_x, rsem_x):
    mesh_id = pl.DeviceIdType.MESH
    member = lax.axis_index("member")
    my = lax.axis_index("gridy")
    mx = lax.axis_index("gridx")
    barrier = pltpu.get_barrier_semaphore()
    for d in range(1, ny):
        pl.semaphore_signal(barrier, 1, device_id=(member, (my + d) % ny, mx), device_id_type=mesh_id)
    for d in range(1, nx):
        pl.semaphore_signal(barrier, 1, device_id=(member, my, (mx + d) % nx), device_id_type=mesh_id)
    pl.semaphore_wait(barrier, (ny - 1) + (nx - 1))

    def phase(src, recv, send_sem, recv_sem, count, me, device):
        recv[me] = src[...]
        sent = []
        for d in range(1, count):
            peer = (me + d) % count
            copy = pltpu.make_async_remote_copy(
                src_ref=src,
                dst_ref=recv.at[me],
                send_sem=send_sem.at[peer],
                recv_sem=recv_sem.at[me],
                device_id=device(peer),
                device_id_type=mesh_id,
            )
            copy.start()
            sent.append(copy)
        for d in range(1, count):
            peer = (me + d) % count
            pltpu.make_async_remote_copy(
                src_ref=src,
                dst_ref=recv.at[peer],
                send_sem=send_sem.at[peer],
                recv_sem=recv_sem.at[peer],
                device_id=device(peer),
                device_id_type=mesh_id,
            ).wait_recv()
        for copy in sent:
            copy.wait_send()
        total = recv[0]
        for j in range(1, count):
            total = total + recv[j]
        return total

    part[...] = phase(x_ref, recv_y, send_y, rsem_y, ny, my, lambda p: (member, p, mx))
    o_ref[...] = phase(part, recv_x, send_x, rsem_x, nx, mx, lambda p: (member, my, p))


def grid_sum(values):
    ny = lax.axis_size("gridy")
    nx = lax.axis_size("gridx")
    shape = values.shape
    return pl.pallas_call(
        functools.partial(gather_sum_kernel, ny, nx),
        out_shape=jax.ShapeDtypeStruct(shape, values.dtype),
        in_specs=[pl.BlockSpec(memory_space=pltpu.VMEM)],
        out_specs=pl.BlockSpec(memory_space=pltpu.VMEM),
        scratch_shapes=[
            pltpu.VMEM((ny,) + shape, values.dtype),
            pltpu.VMEM((nx,) + shape, values.dtype),
            pltpu.VMEM(shape, values.dtype),
            pltpu.SemaphoreType.DMA((ny,)),
            pltpu.SemaphoreType.DMA((ny,)),
            pltpu.SemaphoreType.DMA((nx,)),
            pltpu.SemaphoreType.DMA((nx,)),
        ],
        compiler_params=pltpu.CompilerParams(collective_id=0, has_side_effects=True),
    )(values)


def exchange_sum(k, vec, ny, nx, bufs, device_ids):
    send_buf, recv, send_sem, recv_sem = bufs
    me, device = device_ids
    count = ny * nx
    mesh_id = pl.DeviceIdType.MESH
    send_buf[k] = vec
    recv[k, me] = vec
    sent = []
    for d in range(1, count):
        peer = (me + d) % count
        copy = pltpu.make_async_remote_copy(
            src_ref=send_buf.at[k],
            dst_ref=recv.at[k, me],
            send_sem=send_sem.at[k, peer],
            recv_sem=recv_sem.at[k, me],
            device_id=device(peer),
            device_id_type=mesh_id,
        )
        copy.start()
        sent.append(copy)
    for d in range(1, count):
        peer = (me + d) % count
        pltpu.make_async_remote_copy(
            src_ref=send_buf.at[k],
            dst_ref=recv.at[k, peer],
            send_sem=send_sem.at[k, peer],
            recv_sem=recv_sem.at[k, peer],
            device_id=device(peer),
            device_id_type=mesh_id,
        ).wait_recv()
    for copy in sent:
        copy.wait_send()
    total = recv[k, 0]
    for j in range(1, count):
        total = total + recv[k, j]
    return total


def solve_kernel(ny, nx, surf_ref, inside_ref, own_ref, out_ref, frame, hsend, hrecv, *bufs):
    mesh_id = pl.DeviceIdType.MESH
    member = lax.axis_index("member")
    my = lax.axis_index("gridy")
    mx = lax.axis_index("gridx")
    along_y = lambda p: (member, p, mx)
    along_x = lambda p: (member, my, p)
    group_size = ny * nx
    me = my * nx + mx
    group = lambda q: (member, q // nx, q % nx)
    barrier = pltpu.get_barrier_semaphore()
    for d in range(1, group_size):
        pl.semaphore_signal(barrier, 1, device_id=group((me + d) % group_size), device_id_type=mesh_id)
    rows, cols = surf_ref.shape[2], surf_ref.shape[3]
    wide_rows, wide_cols = frame.shape[2], frame.shape[3]
    band = (wide_rows - rows) // 2
    block = (wide_cols - cols) // 2
    frame[:, :, 0:rows, 0:cols] = surf_ref[...]
    pl.semaphore_wait(barrier, group_size - 1)

    def halo_copies(first, moves):
        started = []
        for slot, (src, dst, device) in enumerate(moves, start=first):
            copy = pltpu.make_async_remote_copy(
                src_ref=src, dst_ref=dst, send_sem=hsend.at[slot], recv_sem=hrecv.at[slot],
                device_id=device, device_id_type=mesh_id,
            )
            copy.start()
            started.append(copy)
        for copy in started:
            copy.wait()

    up, down = (my + 1) % ny, (my + ny - 1) % ny
    right, left = (mx + 1) % nx, (mx + nx - 1) % nx
    top_rows = slice(0, band)
    low_rows = slice(rows - band, rows)
    own_rows = slice(0, rows)
    west_part = slice(0, block)
    east_part = slice(cols - block, cols)
    own_cols = slice(0, cols)
    north_halo = slice(rows, rows + band)
    south_halo = slice(rows + band, wide_rows)
    east_halo = slice(cols, cols + block)
    west_halo = slice(cols + block, wide_cols)
    halo_copies(0, [
        (frame.at[:, :, top_rows, own_cols], frame.at[:, :, north_halo, own_cols], (member, down, mx)),
        (frame.at[:, :, low_rows, own_cols], frame.at[:, :, south_halo, own_cols], (member, up, mx)),
        (frame.at[:, :, own_rows, west_part], frame.at[:, :, own_rows, east_halo], (member, my, left)),
        (frame.at[:, :, own_rows, east_part], frame.at[:, :, own_rows, west_halo], (member, my, right)),
        (frame.at[:, :, top_rows, west_part], frame.at[:, :, north_halo, east_halo], (member, down, left)),
        (frame.at[:, :, top_rows, east_part], frame.at[:, :, north_halo, west_halo], (member, down, right)),
        (frame.at[:, :, low_rows, west_part], frame.at[:, :, south_halo, east_halo], (member, up, left)),
        (frame.at[:, :, low_rows, east_part], frame.at[:, :, south_halo, west_halo], (member, up, right)),
    ])

    members = surf_ref.shape[1]
    inside = inside_ref[...]
    own = own_ref[...] > 0.5

    def east(f):
        return pltpu.roll(f, wide_cols - 1, 1)

    def west(f):
        return pltpu.roll(f, 1, 1)

    def north(f):
        return pltpu.roll(f, wide_rows - 1, 0)

    def south(f):
        return pltpu.roll(f, 1, 0)

    def apply(f):
        return ((1.0 + 4.0 * SURF_C) * f - SURF_C * (east(f) + west(f) + north(f) + south(f))) * inside

    def total(f):
        return jnp.sum(jnp.where(own, f, 0.0), axis=(0, 1), keepdims=True)

    residual = []
    for m in range(members):
        trans_u = frame[0, m] * inside
        trans_v = frame[1, m] * inside
        level = frame[2, m] * inside
        residual.append(
            (level - DIV_K * 0.5 * (east(trans_u) - west(trans_u) + (north(trans_v) - south(trans_v)))) * inside
        )
    lane = lax.broadcasted_iota(jnp.int32, (8, 128), 1)
    direction = [None] * members
    image_dir = [None] * members
    solution = [None] * members
    gamma_prev = [None] * members
    alpha_prev = [None] * members
    for count in range(ITERS):
        image_res = [apply(residual[m]) for m in range(members)]
        vec = jnp.zeros((8, 128), jnp.float32)
        for m in range(members):
            vec = jnp.where(lane == 2 * m, total(residual[m] * residual[m]), vec)
            vec = jnp.where(lane == 2 * m + 1, total(residual[m] * image_res[m]), vec)
        sums = exchange_sum(count, vec, ny, nx, bufs, (me, group))
        for m in range(members):
            gamma = sums[0:1, 2 * m : 2 * m + 1]
            delta = sums[0:1, 2 * m + 1 : 2 * m + 2]
            if count == 0:
                alpha = gamma / delta
                direction[m] = residual[m]
                image_dir[m] = image_res[m]
                solution[m] = alpha * direction[m]
            else:
                beta = gamma / gamma_prev[m]
                alpha = gamma / (delta - beta * gamma / alpha_prev[m])
                direction[m] = residual[m] + beta * direction[m]
                image_dir[m] = image_res[m] + beta * image_dir[m]
                solution[m] = solution[m] + alpha * direction[m]
            if count < ITERS - 1:
                residual[m] = residual[m] - alpha * image_dir[m]
            gamma_prev[m] = gamma
            alpha_prev[m] = alpha
    for m in range(members):
        x = solution[m]
        out_ref[0, m] = x[0:rows, 0:cols]
        out_ref[1, m] = (east(x) - west(x))[0:rows, 0:cols]
        out_ref[2, m] = (north(x) - south(x))[0:rows, 0:cols]


def surface_kernel_solve(surf, inside, own):
    ny = lax.axis_size("gridy")
    nx = lax.axis_size("gridx")
    fields, members, rows, cols = surf.shape
    return pl.pallas_call(
        functools.partial(solve_kernel, ny, nx),
        out_shape=jax.ShapeDtypeStruct((3, members, rows, cols), jnp.float32),
        in_specs=[pl.BlockSpec(memory_space=pltpu.VMEM)] * 3,
        out_specs=pl.BlockSpec(memory_space=pltpu.VMEM),
        scratch_shapes=[
            pltpu.VMEM((fields, members) + inside.shape, jnp.float32),
            pltpu.SemaphoreType.DMA((8,)),
            pltpu.SemaphoreType.DMA((8,)),
            pltpu.VMEM((ITERS, 8, 128), jnp.float32),
            pltpu.VMEM((ITERS, ny * nx, 8, 128), jnp.float32),
            pltpu.SemaphoreType.DMA((ITERS, ny * nx)),
            pltpu.SemaphoreType.DMA((ITERS, ny * nx)),
        ],
        compiler_params=pltpu.CompilerParams(collective_id=1, has_side_effects=True),
    )(surf, inside, own)


def volume_kernel(temp_ref, salt_ref, uvel_ref, vvel_ref, ocean_ref, cor_ref, n_ref, s_ref, e_ref, w_ref,
                  tn_ref, sn_ref, us_ref, vs_ref, tu_ref, tv_ref):
    levels, rows, cols = temp_ref.shape[1], temp_ref.shape[2], temp_ref.shape[3]
    row = lax.broadcasted_iota(jnp.int32, (rows, cols), 0)
    col = lax.broadcasted_iota(jnp.int32, (rows, cols), 1)
    top = row == rows - 1
    bottom = row == 0
    right = col == cols - 1
    left = col == 0
    ocean = ocean_ref[...]
    cor = cor_ref[...]

    def around(f, rims):
        n, s, e, w = rims
        return (
            jnp.where(right, e, pltpu.roll(f, cols - 1, 1)),
            jnp.where(left, w, pltpu.roll(f, 1, 1)),
            jnp.where(top, n, pltpu.roll(f, rows - 1, 0)),
            jnp.where(bottom, s, pltpu.roll(f, 1, 0)),
        )

    def rims_of(k, l):
        return (n_ref[k, 0, l], s_ref[k, 0, l], e_ref[k, 0, l], w_ref[k, 0, l])

    running = None
    running_rims = None
    tu = None
    tv = None
    for l in range(levels):
        t = temp_ref[0, l]
        s = salt_ref[0, l]
        u = uvel_ref[0, l]
        v = vvel_ref[0, l]
        rt, rs, ru, rv = rims_of(0, l), rims_of(1, l), rims_of(2, l), rims_of(3, l)
        layer = BETA_S * s - ALPHA_T * t
        layer_rims = tuple(BETA_S * b - ALPHA_T * a for a, b in zip(rt, rs))
        if running is None:
            running, running_rims = layer, layer_rims
        else:
            running = running + layer
            running_rims = tuple(a + b for a, b in zip(running_rims, layer_rims))
        press = PRESS_K * running
        press_rims = tuple(PRESS_K * a for a in running_rims)
        te, tw, tn, ts = around(t, rt)
        se, sw, sn, ss = around(s, rs)
        ue, uw, un, us = around(u, ru)
        ve, vw, vn, vs = around(v, rv)
        pe, pw, pn, ps = around(press, press_rims)
        tn_ref[0, l] = ocean * (
            t - STEP_DT * 0.5 * (u * (te - tw) + v * (tn - ts)) + KAPPA * (te + tw + tn + ts - 4.0 * t)
        )
        sn_ref[0, l] = ocean * (
            s - STEP_DT * 0.5 * (u * (se - sw) + v * (sn - ss)) + KAPPA * (se + sw + sn + ss - 4.0 * s)
        )
        ustar = ocean * (
            u + STEP_DT * (cor * v - 0.5 * (pe - pw) - DRAG_K * u) + VISCOSITY * (ue + uw + un + us - 4.0 * u)
        )
        vstar = ocean * (
            v + STEP_DT * (-cor * u - 0.5 * (pn - ps) - DRAG_K * v) + VISCOSITY * (ve + vw + vn + vs - 4.0 * v)
        )
        us_ref[0, l] = ustar
        vs_ref[0, l] = vstar
        tu = ustar if tu is None else tu + ustar
        tv = vstar if tv is None else tv + vstar
    tu_ref[0] = tu
    tv_ref[0] = tv


def volume_step(temp, salt, uvel, vvel, ocean, cor_tile, rims):
    members, levels, rows, cols = temp.shape
    field = pl.BlockSpec((1, levels, rows, cols), lambda m: (m, 0, 0, 0))
    plane = pl.BlockSpec((rows, cols), lambda m: (0, 0))
    north, south, east, west = rims
    row_rim = pl.BlockSpec((4, 1, levels, 1, cols), lambda m: (0, m, 0, 0, 0))
    col_rim = pl.BlockSpec((4, 1, levels, rows, 1), lambda m: (0, m, 0, 0, 0))
    surface = pl.BlockSpec((1, rows, cols), lambda m: (m, 0, 0))
    volume_shape = jax.ShapeDtypeStruct(temp.shape, jnp.float32)
    surface_shape = jax.ShapeDtypeStruct((members, rows, cols), jnp.float32)
    return pl.pallas_call(
        volume_kernel,
        grid=(members,),
        in_specs=[field] * 4 + [plane, plane, row_rim, row_rim, col_rim, col_rim],
        out_specs=[field] * 4 + [surface] * 2,
        out_shape=[volume_shape] * 4 + [surface_shape] * 2,
    )(temp, salt, uvel, vvel, ocean, cor_tile, north, south, east, west)


def ring(axis):
    count = lax.axis_size(axis)
    forward = [(i, (i + 1) % count) for i in range(count)]
    backward = [((i + 1) % count, i) for i in range(count)]
    return forward, backward


def exchange(block, ydim, xdim, south_keep, north_keep):
    fwd_y, bwd_y = ring("gridy")
    fwd_x, bwd_x = ring("gridx")
    rows = block.shape[ydim]
    cols = block.shape[xdim]
    north = lax.ppermute(lax.slice_in_dim(block, 0, 1, axis=ydim), "gridy", bwd_y) * north_keep
    south = lax.ppermute(lax.slice_in_dim(block, rows - 1, rows, axis=ydim), "gridy", fwd_y) * south_keep
    east = lax.ppermute(lax.slice_in_dim(block, 0, 1, axis=xdim), "gridx", bwd_x)
    west = lax.ppermute(lax.slice_in_dim(block, cols - 1, cols, axis=xdim), "gridx", fwd_x)
    return (east, west, north, south)


def exchange_fields(fields, south_keep, north_keep):
    fwd_y, bwd_y = ring("gridy")
    fwd_x, bwd_x = ring("gridx")
    north = lax.ppermute(jnp.stack([f[..., :1, :] for f in fields]), "gridy", bwd_y) * north_keep
    south = lax.ppermute(jnp.stack([f[..., -1:, :] for f in fields]), "gridy", fwd_y) * south_keep
    east = lax.ppermute(jnp.stack([f[..., :, :1] for f in fields]), "gridx", bwd_x)
    west = lax.ppermute(jnp.stack([f[..., :, -1:] for f in fields]), "gridx", fwd_x)
    return (north, south, east, west)


def sides(field, rims, ydim, xdim):
    east, west, north, south = rims
    rows = field.shape[ydim]
    cols = field.shape[xdim]
    east_side = jnp.concatenate([lax.slice_in_dim(field, 1, cols, axis=xdim), east], axis=xdim)
    west_side = jnp.concatenate([west, lax.slice_in_dim(field, 0, cols - 1, axis=xdim)], axis=xdim)
    north_side = jnp.concatenate([lax.slice_in_dim(field, 1, rows, axis=ydim), north], axis=ydim)
    south_side = jnp.concatenate([south, lax.slice_in_dim(field, 0, rows - 1, axis=ydim)], axis=ydim)
    return (east_side, west_side, north_side, south_side)


def pressure(temp, salt):
    return PRESS_K * jnp.cumsum(BETA_S * salt - ALPHA_T * temp, axis=-3)


def surface_apply(field, rims):
    east_side, west_side, north_side, south_side = sides(field, rims, 1, 2)
    return (1.0 + 4.0 * SURF_C) * field - SURF_C * (east_side + west_side + north_side + south_side)


def member_total(values):
    return jnp.sum(values, axis=(1, 2))


def widen(values):
    return values[:, None, None]


def combine(a, fa, b, fb):
    def one(u, v):
        left = u if a is None else widen(a) * u
        return left + (v if b is None else widen(b) * v)

    return one(fa[0], fb[0]), tuple(one(u, v) for u, v in zip(fa[1], fb[1]))


def scaled(a, fa):
    return widen(a) * fa[0], tuple(widen(a) * u for u in fa[1])


def padded_2(block, sides_of, width):
    for axis, dim in sides_of:
        count = lax.axis_size(axis)
        forward = [(i, (i + 1) % count) for i in range(count)]
        backward = [((i + 1) % count, i) for i in range(count)]
        size = block.shape[dim]
        low = lax.ppermute(lax.slice_in_dim(block, size - width, size, axis=dim), axis, forward)
        high = lax.ppermute(lax.slice_in_dim(block, 0, width, axis=dim), axis, backward)
        block = jnp.concatenate([low, block, high], axis=dim)
    return block


def crop(field, by):
    if by == 0:
        return field
    return field[..., by:-by, by:-by]


def around(field):
    return (
        field[..., 1:-1, 1:-1],
        field[..., 1:-1, 2:],
        field[..., 1:-1, :-2],
        field[..., 2:, 1:-1],
        field[..., :-2, 1:-1],
    )


def rows_at(inside, full, want):
    cut = full - want
    return inside if cut == 0 else inside[cut:-cut]


def apply_wide(field, inside):
    centre, east, west, north, south = around(field)
    return ((1.0 + 4.0 * SURF_C) * centre - SURF_C * (east + west + north + south)) * inside


def surface_solve(rhs, inside, width, full):
    residual, wide_r = rhs, width
    gamma_prev = None
    alpha_prev = None
    for count in range(ITERS):
        image_res = apply_wide(residual, rows_at(inside, full, wide_r - 1))
        own_res = crop(residual, wide_r)
        own_img = crop(image_res, wide_r - 1)
        dots = grid_sum(jnp.stack([member_total(own_res * own_res), member_total(own_res * own_img)]))
        gamma, delta = dots[0], dots[1]
        if count == 0:
            alpha = gamma / delta
            direction, wide_p = residual, wide_r
            image_dir, wide_s = image_res, wide_r - 1
            solution, wide_x = widen(alpha) * direction, wide_r
        else:
            beta = gamma / gamma_prev
            alpha = gamma / (delta - beta * gamma / alpha_prev)
            direction = residual + widen(beta) * crop(direction, wide_p - wide_r)
            wide_p = wide_r
            image_dir = image_res + widen(beta) * crop(image_dir, wide_s - (wide_r - 1))
            wide_s = wide_r - 1
            solution = crop(solution, wide_x - wide_r) + widen(alpha) * direction
            wide_x = wide_r
        if count < ITERS - 1:
            residual = crop(residual, 1) - widen(alpha) * image_dir
            wide_r -= 1
        gamma_prev = gamma
        alpha_prev = alpha
    return solution


def shards(temp, salt, uvel, vvel, eta, land_mask, clone_source):
    levels = temp.shape[1]
    rows = temp.shape[2]
    cols = temp.shape[3]
    ocean = land_mask.astype(jnp.float32)
    tile_row = lax.axis_index("gridy")
    tile_count = lax.axis_size("gridy")
    total_rows = rows * tile_count
    total_cols = cols * lax.axis_size("gridx")
    south_keep = (tile_row > 0).astype(jnp.float32)
    north_keep = (tile_row < tile_count - 1).astype(jnp.float32)
    latitude = (tile_row * rows + jnp.arange(rows, dtype=jnp.int32)).astype(jnp.float32) + 0.5
    coriolis = (CORI_K * (2.0 * latitude / total_rows - 1.0))[:, None]
    cor_tile = jnp.broadcast_to(coriolis, (rows, cols))
    band = 8
    block = 128
    frame_rows = rows + 2 * band
    frame_cols = cols + 2 * block
    row_at = lax.broadcasted_iota(jnp.int32, (frame_rows, frame_cols), 0)
    col_at = lax.broadcasted_iota(jnp.int32, (frame_rows, frame_cols), 1)
    global_row = tile_row * rows + jnp.where(row_at < rows + band, row_at, row_at - frame_rows)
    wide_inside = ((global_row >= 0) & (global_row < total_rows)).astype(jnp.float32)
    own_mask = ((row_at < rows) & (col_at < cols)).astype(jnp.float32)
    for count in range(STEPS):
        fields = (temp, salt, uvel, vvel)
        rims = exchange_fields(fields, south_keep, north_keep)
        temp_next, salt_next, ustar, vstar, trans_u, trans_v = volume_step(
            temp, salt, uvel, vvel, ocean, cor_tile, rims
        )
        solved = surface_kernel_solve(jnp.stack((trans_u, trans_v, eta)), wide_inside, own_mask)
        eta = solved[0]
        east_west = solved[1]
        north_south = solved[2]
        uvel = ocean * (ustar - GRAV_K * 0.5 * east_west[:, None])
        vvel = ocean * (vstar - GRAV_K * 0.5 * north_south[:, None])
        if count == STEPS - 1:
            tracers_other = lax.ppermute(jnp.stack((temp_next, salt_next)), "member", [(0, 1), (1, 0)])
        temp = temp_next
        salt = salt_next
    zonal_scale = 1.0 / jnp.sqrt(jnp.float32(total_cols))
    score_scale = 1.0 / jnp.sqrt(jnp.float32(levels * total_rows))
    lat_weight = latitude / total_rows
    members = temp.shape[0]
    zonal_local = jnp.sum(vvel, axis=3)
    depth_weight = (levels - jnp.arange(levels, dtype=jnp.int32)).astype(jnp.float32)
    score_local = jnp.sum(zonal_local * depth_weight[None, :, None] * lat_weight[None, None, :], axis=(1, 2))
    slot = lax.broadcasted_iota(jnp.int32, (tile_count, 1, 1, 1), 0) == tile_row
    zonal_slots = jnp.where(slot, zonal_local[None], 0.0).reshape(-1, 128)
    score_row = jnp.zeros((8, 128), jnp.float32).at[0, :members].set(score_local)
    summed = grid_sum(jnp.concatenate([zonal_slots, score_row], axis=0))
    zonal_whole = summed[: zonal_slots.shape[0]].reshape((tile_count,) + zonal_local.shape)
    zonal_whole = jnp.sum(jnp.where(slot, zonal_whole, 0.0), axis=0)
    overturn = jnp.cumsum(zonal_whole, axis=1) * zonal_scale
    score = summed[zonal_slots.shape[0], :members] * (zonal_scale * score_scale)
    swap = [(0, 1), (1, 0)]
    mine = lax.axis_index("member")
    score_slab = jnp.zeros((members, 1) + eta.shape[1:], jnp.float32).at[:, 0, 0, 0].set(score)
    flows = jnp.concatenate([uvel, vvel, eta[:, None], score_slab], axis=1)
    flows_other = lax.ppermute(flows, "member", swap)
    score_other = flows_other[:, 2 * levels + 1, 0, 0]
    every_score = jnp.where(
        mine == 0, jnp.concatenate([score, score_other]), jnp.concatenate([score_other, score])
    )
    here = (clone_source // members) == mine
    local_at = clone_source % members

    def pick(local, other):
        chosen = []
        for place in range(members):
            from_here = lax.dynamic_index_in_dim(local, local_at[place], 0, keepdims=False)
            from_other = lax.dynamic_index_in_dim(other, local_at[place], 0, keepdims=False)
            chosen.append(jnp.where(here[place], from_here, from_other))
        return jnp.stack(chosen)

    new_temp = pick(temp, tracers_other[0])
    new_salt = pick(salt, tracers_other[1])
    new_flows = pick(flows[:, : 2 * levels + 1], flows_other[:, : 2 * levels + 1])
    clone_weight = jnp.take(every_score, clone_source, axis=0) - jnp.mean(every_score)
    return (
        new_temp,
        new_salt,
        new_flows[:, :levels],
        new_flows[:, levels : 2 * levels],
        new_flows[:, 2 * levels],
        overturn,
        clone_weight,
    )


def solution(mesh):
    in_specs = (
        P("member", None, "gridy", "gridx"),
        P("member", None, "gridy", "gridx"),
        P("member", None, "gridy", "gridx"),
        P("member", None, "gridy", "gridx"),
        P("member", "gridy", "gridx"),
        P("gridy", "gridx"),
        P("member"),
    )
    out_specs = (
        P("member", None, "gridy", "gridx"),
        P("member", None, "gridy", "gridx"),
        P("member", None, "gridy", "gridx"),
        P("member", None, "gridy", "gridx"),
        P("member", "gridy", "gridx"),
        P("member", None, "gridy"),
        P("member"),
    )
    return jax.shard_map(shards, mesh=mesh, in_specs=in_specs, out_specs=out_specs, check_vma=False)
```

```python
import functools

import jax
import jax.numpy as jnp
from jax import lax
from jax.experimental import pallas as pl
from jax.experimental.pallas import tpu as pltpu
from jax.sharding import PartitionSpec as P

STEPS = 2
ITERS = 3


ALPHA_T = 0.8
BETA_S = 0.6
PRESS_K = 0.25
STEP_DT = 0.1
KAPPA = 0.1
VISCOSITY = 0.1
DRAG_K = 0.05
CORI_K = 1.0
SURF_C = 4.0
DIV_K = 0.5
GRAV_K = 0.5


def tree_sum(values, axes):
    for axis in axes:
        count = lax.axis_size(axis)
        step = 1
        while step < count:
            pairs = [(i, i ^ step) for i in range(count)]
            values = values + lax.ppermute(values, axis, pairs)
            step *= 2
    return values


def gather_sum_kernel(ny, nx, x_ref, o_ref, recv_y, recv_x, part, send_y, rsem_y, send_x, rsem_x):
    mesh_id = pl.DeviceIdType.MESH
    member = lax.axis_index("member")
    my = lax.axis_index("gridy")
    mx = lax.axis_index("gridx")
    barrier = pltpu.get_barrier_semaphore()
    for d in range(1, ny):
        pl.semaphore_signal(barrier, 1, device_id=(member, (my + d) % ny, mx), device_id_type=mesh_id)
    for d in range(1, nx):
        pl.semaphore_signal(barrier, 1, device_id=(member, my, (mx + d) % nx), device_id_type=mesh_id)
    pl.semaphore_wait(barrier, (ny - 1) + (nx - 1))

    def phase(src, recv, send_sem, recv_sem, count, me, device):
        recv[me] = src[...]
        sent = []
        for d in range(1, count):
            peer = (me + d) % count
            copy = pltpu.make_async_remote_copy(
                src_ref=src,
                dst_ref=recv.at[me],
                send_sem=send_sem.at[peer],
                recv_sem=recv_sem.at[me],
                device_id=device(peer),
                device_id_type=mesh_id,
            )
            copy.start()
            sent.append(copy)
        for d in range(1, count):
            peer = (me + d) % count
            pltpu.make_async_remote_copy(
                src_ref=src,
                dst_ref=recv.at[peer],
                send_sem=send_sem.at[peer],
                recv_sem=recv_sem.at[peer],
                device_id=device(peer),
                device_id_type=mesh_id,
            ).wait_recv()
        for copy in sent:
            copy.wait_send()
        total = recv[0]
        for j in range(1, count):
            total = total + recv[j]
        return total

    part[...] = phase(x_ref, recv_y, send_y, rsem_y, ny, my, lambda p: (member, p, mx))
    o_ref[...] = phase(part, recv_x, send_x, rsem_x, nx, mx, lambda p: (member, my, p))


def grid_sum(values):
    ny = lax.axis_size("gridy")
    nx = lax.axis_size("gridx")
    shape = values.shape
    return pl.pallas_call(
        functools.partial(gather_sum_kernel, ny, nx),
        out_shape=jax.ShapeDtypeStruct(shape, values.dtype),
        in_specs=[pl.BlockSpec(memory_space=pltpu.VMEM)],
        out_specs=pl.BlockSpec(memory_space=pltpu.VMEM),
        scratch_shapes=[
            pltpu.VMEM((ny,) + shape, values.dtype),
            pltpu.VMEM((nx,) + shape, values.dtype),
            pltpu.VMEM(shape, values.dtype),
            pltpu.SemaphoreType.DMA((ny,)),
            pltpu.SemaphoreType.DMA((ny,)),
            pltpu.SemaphoreType.DMA((nx,)),
            pltpu.SemaphoreType.DMA((nx,)),
        ],
        compiler_params=pltpu.CompilerParams(collective_id=0, has_side_effects=True),
    )(values)


def exchange_sum(k, vec, ny, nx, bufs, device_ids):
    send_y, recv_y, send_x, recv_x, sy, ry, sx, rx = bufs
    my, mx, along_y, along_x = device_ids
    mesh_id = pl.DeviceIdType.MESH

    def phase(value, send_buf, recv, send_sem, recv_sem, count, me, device):
        send_buf[k] = value
        recv[k, me] = value
        sent = []
        for d in range(1, count):
            peer = (me + d) % count
            copy = pltpu.make_async_remote_copy(
                src_ref=send_buf.at[k],
                dst_ref=recv.at[k, me],
                send_sem=send_sem.at[k, peer],
                recv_sem=recv_sem.at[k, me],
                device_id=device(peer),
                device_id_type=mesh_id,
            )
            copy.start()
            sent.append(copy)
        for d in range(1, count):
            peer = (me + d) % count
            pltpu.make_async_remote_copy(
                src_ref=send_buf.at[k],
                dst_ref=recv.at[k, peer],
                send_sem=send_sem.at[k, peer],
                recv_sem=recv_sem.at[k, peer],
                device_id=device(peer),
                device_id_type=mesh_id,
            ).wait_recv()
        for copy in sent:
            copy.wait_send()
        total = recv[k, 0]
        for j in range(1, count):
            total = total + recv[k, j]
        return total

    partial = phase(vec, send_y, recv_y, sy, ry, ny, my, along_y)
    return phase(partial, send_x, recv_x, sx, rx, nx, mx, along_x)


def solve_kernel(ny, nx, carry, *refs):
    if carry:
        surf_ref, inside_ref, own_ref, cargo_ref, out_ref, cargo_out, frame, hsend, hrecv, csem = refs[:10]
        bufs = refs[10:]
    else:
        surf_ref, inside_ref, own_ref, out_ref, frame, hsend, hrecv = refs[:7]
        bufs = refs[7:]
    mesh_id = pl.DeviceIdType.MESH
    member = lax.axis_index("member")
    my = lax.axis_index("gridy")
    mx = lax.axis_index("gridx")
    along_y = lambda p: (member, p, mx)
    along_x = lambda p: (member, my, p)
    barrier = pltpu.get_barrier_semaphore()
    for d in range(1, ny):
        pl.semaphore_signal(barrier, 1, device_id=along_y((my + d) % ny), device_id_type=mesh_id)
    for d in range(1, nx):
        pl.semaphore_signal(barrier, 1, device_id=along_x((mx + d) % nx), device_id_type=mesh_id)
    for dy in (1, ny - 1):
        for dx in (1, nx - 1):
            pl.semaphore_signal(
                barrier, 1, device_id=(member, (my + dy) % ny, (mx + dx) % nx), device_id_type=mesh_id
            )
    rows, cols = surf_ref.shape[2], surf_ref.shape[3]
    wide_rows, wide_cols = frame.shape[2], frame.shape[3]
    band = (wide_rows - rows) // 2
    block = (wide_cols - cols) // 2
    frame[:, :, 0:rows, 0:cols] = surf_ref[...]
    if carry:
        partner = (lax.axis_index("member") + 1) % 2
        pl.semaphore_signal(barrier, 1, device_id=(partner, my, mx), device_id_type=mesh_id)
    pl.semaphore_wait(barrier, (ny - 1) + (nx - 1) + 4 + (1 if carry else 0))
    cargo_copies = []
    if carry:
        for part in range(cargo_ref.shape[0]):
            for half in range(cargo_ref.shape[1]):
                piece = part * cargo_ref.shape[1] + half
                copy = pltpu.make_async_remote_copy(
                    src_ref=cargo_ref.at[part, half], dst_ref=cargo_out.at[part, half],
                    send_sem=csem.at[0, piece], recv_sem=csem.at[1, piece],
                    device_id=(partner, my, mx), device_id_type=mesh_id,
                )
                copy.start()
                cargo_copies.append(copy)

    def halo_copies(first, moves):
        started = []
        for slot, (src, dst, device) in enumerate(moves, start=first):
            copy = pltpu.make_async_remote_copy(
                src_ref=src, dst_ref=dst, send_sem=hsend.at[slot], recv_sem=hrecv.at[slot],
                device_id=device, device_id_type=mesh_id,
            )
            copy.start()
            started.append(copy)
        for copy in started:
            copy.wait()

    up, down = (my + 1) % ny, (my + ny - 1) % ny
    right, left = (mx + 1) % nx, (mx + nx - 1) % nx
    top_rows = slice(0, band)
    low_rows = slice(rows - band, rows)
    own_rows = slice(0, rows)
    west_part = slice(0, block)
    east_part = slice(cols - block, cols)
    own_cols = slice(0, cols)
    north_halo = slice(rows, rows + band)
    south_halo = slice(rows + band, wide_rows)
    east_halo = slice(cols, cols + block)
    west_halo = slice(cols + block, wide_cols)
    halo_copies(0, [
        (frame.at[:, :, top_rows, own_cols], frame.at[:, :, north_halo, own_cols], (member, down, mx)),
        (frame.at[:, :, low_rows, own_cols], frame.at[:, :, south_halo, own_cols], (member, up, mx)),
        (frame.at[:, :, own_rows, west_part], frame.at[:, :, own_rows, east_halo], (member, my, left)),
        (frame.at[:, :, own_rows, east_part], frame.at[:, :, own_rows, west_halo], (member, my, right)),
        (frame.at[:, :, top_rows, west_part], frame.at[:, :, north_halo, east_halo], (member, down, left)),
        (frame.at[:, :, top_rows, east_part], frame.at[:, :, north_halo, west_halo], (member, down, right)),
        (frame.at[:, :, low_rows, west_part], frame.at[:, :, south_halo, east_halo], (member, up, left)),
        (frame.at[:, :, low_rows, east_part], frame.at[:, :, south_halo, west_halo], (member, up, right)),
    ])

    members = surf_ref.shape[1]
    inside = inside_ref[...]
    own = own_ref[...] > 0.5

    def east(f):
        return pltpu.roll(f, wide_cols - 1, 1)

    def west(f):
        return pltpu.roll(f, 1, 1)

    def north(f):
        return pltpu.roll(f, wide_rows - 1, 0)

    def south(f):
        return pltpu.roll(f, 1, 0)

    def apply(f):
        return ((1.0 + 4.0 * SURF_C) * f - SURF_C * (east(f) + west(f) + north(f) + south(f))) * inside

    def total(f):
        return jnp.sum(jnp.where(own, f, 0.0), axis=(0, 1), keepdims=True)

    residual = []
    for m in range(members):
        trans_u = frame[0, m] * inside
        trans_v = frame[1, m] * inside
        level = frame[2, m] * inside
        residual.append(
            (level - DIV_K * 0.5 * (east(trans_u) - west(trans_u) + (north(trans_v) - south(trans_v)))) * inside
        )
    lane = lax.broadcasted_iota(jnp.int32, (8, 128), 1)
    direction = [None] * members
    image_dir = [None] * members
    solution = [None] * members
    gamma_prev = [None] * members
    alpha_prev = [None] * members
    for count in range(ITERS):
        image_res = [apply(residual[m]) for m in range(members)]
        vec = jnp.zeros((8, 128), jnp.float32)
        for m in range(members):
            vec = jnp.where(lane == 2 * m, total(residual[m] * residual[m]), vec)
            vec = jnp.where(lane == 2 * m + 1, total(residual[m] * image_res[m]), vec)
        sums = exchange_sum(count, vec, ny, nx, bufs, (my, mx, along_y, along_x))
        for m in range(members):
            gamma = sums[0:1, 2 * m : 2 * m + 1]
            delta = sums[0:1, 2 * m + 1 : 2 * m + 2]
            if count == 0:
                alpha = gamma / delta
                direction[m] = residual[m]
                image_dir[m] = image_res[m]
                solution[m] = alpha * direction[m]
            else:
                beta = gamma / gamma_prev[m]
                alpha = gamma / (delta - beta * gamma / alpha_prev[m])
                direction[m] = residual[m] + beta * direction[m]
                image_dir[m] = image_res[m] + beta * image_dir[m]
                solution[m] = solution[m] + alpha * direction[m]
            if count < ITERS - 1:
                residual[m] = residual[m] - alpha * image_dir[m]
            gamma_prev[m] = gamma
            alpha_prev[m] = alpha
    for m in range(members):
        x = solution[m]
        out_ref[0, m] = x[0:rows, 0:cols]
        out_ref[1, m] = (east(x) - west(x))[0:rows, 0:cols]
        out_ref[2, m] = (north(x) - south(x))[0:rows, 0:cols]
    for copy in cargo_copies:
        copy.wait()


def surface_kernel_solve(surf, inside, own, cargo=None):
    ny = lax.axis_size("gridy")
    nx = lax.axis_size("gridx")
    fields, members, rows, cols = surf.shape
    carry = cargo is not None
    vmem = pl.BlockSpec(memory_space=pltpu.VMEM)
    solved_shape = jax.ShapeDtypeStruct((3, members, rows, cols), jnp.float32)
    operands = (surf, inside, own) + ((cargo,) if carry else ())
    results = pl.pallas_call(
        functools.partial(solve_kernel, ny, nx, carry),
        out_shape=[solved_shape] + ([jax.ShapeDtypeStruct(cargo.shape, cargo.dtype)] if carry else []),
        in_specs=[vmem] * 3 + ([vmem] if carry else []),
        out_specs=[vmem] + ([vmem] if carry else []),
        scratch_shapes=[
            pltpu.VMEM((fields, members) + inside.shape, jnp.float32),
            pltpu.SemaphoreType.DMA((8,)),
            pltpu.SemaphoreType.DMA((8,)),
        ]
        + ([pltpu.SemaphoreType.DMA((2, cargo.shape[0] * cargo.shape[1]))] if carry else [])
        + [
            pltpu.VMEM((ITERS, 8, 128), jnp.float32),
            pltpu.VMEM((ITERS, ny, 8, 128), jnp.float32),
            pltpu.VMEM((ITERS, 8, 128), jnp.float32),
            pltpu.VMEM((ITERS, nx, 8, 128), jnp.float32),
            pltpu.SemaphoreType.DMA((ITERS, ny)),
            pltpu.SemaphoreType.DMA((ITERS, ny)),
            pltpu.SemaphoreType.DMA((ITERS, nx)),
            pltpu.SemaphoreType.DMA((ITERS, nx)),
        ],
        compiler_params=pltpu.CompilerParams(collective_id=2 if carry else 1, has_side_effects=True),
    )(*operands)
    return results if carry else (results[0], None)


def volume_kernel(temp_ref, salt_ref, uvel_ref, vvel_ref, ocean_ref, cor_ref, n_ref, s_ref, e_ref, w_ref,
                  tn_ref, sn_ref, us_ref, vs_ref, tu_ref, tv_ref):
    levels, rows, cols = temp_ref.shape[1], temp_ref.shape[2], temp_ref.shape[3]
    row = lax.broadcasted_iota(jnp.int32, (rows, cols), 0)
    col = lax.broadcasted_iota(jnp.int32, (rows, cols), 1)
    top = row == rows - 1
    bottom = row == 0
    right = col == cols - 1
    left = col == 0
    ocean = ocean_ref[...]
    cor = cor_ref[...]

    def around(f, rims):
        n, s, e, w = rims
        return (
            jnp.where(right, e, pltpu.roll(f, cols - 1, 1)),
            jnp.where(left, w, pltpu.roll(f, 1, 1)),
            jnp.where(top, n, pltpu.roll(f, rows - 1, 0)),
            jnp.where(bottom, s, pltpu.roll(f, 1, 0)),
        )

    def rims_of(k, l):
        return (n_ref[k, 0, l], s_ref[k, 0, l], e_ref[k, 0, l], w_ref[k, 0, l])

    running = None
    running_rims = None
    tu = None
    tv = None
    for l in range(levels):
        t = temp_ref[0, l]
        s = salt_ref[0, l]
        u = uvel_ref[0, l]
        v = vvel_ref[0, l]
        rt, rs, ru, rv = rims_of(0, l), rims_of(1, l), rims_of(2, l), rims_of(3, l)
        layer = BETA_S * s - ALPHA_T * t
        layer_rims = tuple(BETA_S * b - ALPHA_T * a for a, b in zip(rt, rs))
        if running is None:
            running, running_rims = layer, layer_rims
        else:
            running = running + layer
            running_rims = tuple(a + b for a, b in zip(running_rims, layer_rims))
        press = PRESS_K * running
        press_rims = tuple(PRESS_K * a for a in running_rims)
        te, tw, tn, ts = around(t, rt)
        se, sw, sn, ss = around(s, rs)
        ue, uw, un, us = around(u, ru)
        ve, vw, vn, vs = around(v, rv)
        pe, pw, pn, ps = around(press, press_rims)
        tn_ref[0, l] = ocean * (
            t - STEP_DT * 0.5 * (u * (te - tw) + v * (tn - ts)) + KAPPA * (te + tw + tn + ts - 4.0 * t)
        )
        sn_ref[0, l] = ocean * (
            s - STEP_DT * 0.5 * (u * (se - sw) + v * (sn - ss)) + KAPPA * (se + sw + sn + ss - 4.0 * s)
        )
        ustar = ocean * (
            u + STEP_DT * (cor * v - 0.5 * (pe - pw) - DRAG_K * u) + VISCOSITY * (ue + uw + un + us - 4.0 * u)
        )
        vstar = ocean * (
            v + STEP_DT * (-cor * u - 0.5 * (pn - ps) - DRAG_K * v) + VISCOSITY * (ve + vw + vn + vs - 4.0 * v)
        )
        us_ref[0, l] = ustar
        vs_ref[0, l] = vstar
        tu = ustar if tu is None else tu + ustar
        tv = vstar if tv is None else tv + vstar
    tu_ref[0] = tu
    tv_ref[0] = tv


def volume_step(temp, salt, uvel, vvel, ocean, cor_tile, rims):
    members, levels, rows, cols = temp.shape
    field = pl.BlockSpec((1, levels, rows, cols), lambda m: (m, 0, 0, 0))
    plane = pl.BlockSpec((rows, cols), lambda m: (0, 0))
    north, south, east, west = rims
    row_rim = pl.BlockSpec((4, 1, levels, 1, cols), lambda m: (0, m, 0, 0, 0))
    col_rim = pl.BlockSpec((4, 1, levels, rows, 1), lambda m: (0, m, 0, 0, 0))
    surface = pl.BlockSpec((1, rows, cols), lambda m: (m, 0, 0))
    volume_shape = jax.ShapeDtypeStruct(temp.shape, jnp.float32)
    surface_shape = jax.ShapeDtypeStruct((members, rows, cols), jnp.float32)
    return pl.pallas_call(
        volume_kernel,
        grid=(members,),
        in_specs=[field] * 4 + [plane, plane, row_rim, row_rim, col_rim, col_rim],
        out_specs=[field] * 4 + [surface] * 2,
        out_shape=[volume_shape] * 4 + [surface_shape] * 2,
    )(temp, salt, uvel, vvel, ocean, cor_tile, north, south, east, west)


def ring(axis):
    count = lax.axis_size(axis)
    forward = [(i, (i + 1) % count) for i in range(count)]
    backward = [((i + 1) % count, i) for i in range(count)]
    return forward, backward


def exchange(block, ydim, xdim, south_keep, north_keep):
    fwd_y, bwd_y = ring("gridy")
    fwd_x, bwd_x = ring("gridx")
    rows = block.shape[ydim]
    cols = block.shape[xdim]
    north = lax.ppermute(lax.slice_in_dim(block, 0, 1, axis=ydim), "gridy", bwd_y) * north_keep
    south = lax.ppermute(lax.slice_in_dim(block, rows - 1, rows, axis=ydim), "gridy", fwd_y) * south_keep
    east = lax.ppermute(lax.slice_in_dim(block, 0, 1, axis=xdim), "gridx", bwd_x)
    west = lax.ppermute(lax.slice_in_dim(block, cols - 1, cols, axis=xdim), "gridx", fwd_x)
    return (east, west, north, south)


def exchange_fields(fields, south_keep, north_keep):
    fwd_y, bwd_y = ring("gridy")
    fwd_x, bwd_x = ring("gridx")
    north = lax.ppermute(jnp.stack([f[..., :1, :] for f in fields]), "gridy", bwd_y) * north_keep
    south = lax.ppermute(jnp.stack([f[..., -1:, :] for f in fields]), "gridy", fwd_y) * south_keep
    east = lax.ppermute(jnp.stack([f[..., :, :1] for f in fields]), "gridx", bwd_x)
    west = lax.ppermute(jnp.stack([f[..., :, -1:] for f in fields]), "gridx", fwd_x)
    return (north, south, east, west)


def sides(field, rims, ydim, xdim):
    east, west, north, south = rims
    rows = field.shape[ydim]
    cols = field.shape[xdim]
    east_side = jnp.concatenate([lax.slice_in_dim(field, 1, cols, axis=xdim), east], axis=xdim)
    west_side = jnp.concatenate([west, lax.slice_in_dim(field, 0, cols - 1, axis=xdim)], axis=xdim)
    north_side = jnp.concatenate([lax.slice_in_dim(field, 1, rows, axis=ydim), north], axis=ydim)
    south_side = jnp.concatenate([south, lax.slice_in_dim(field, 0, rows - 1, axis=ydim)], axis=ydim)
    return (east_side, west_side, north_side, south_side)


def pressure(temp, salt):
    return PRESS_K * jnp.cumsum(BETA_S * salt - ALPHA_T * temp, axis=-3)


def surface_apply(field, rims):
    east_side, west_side, north_side, south_side = sides(field, rims, 1, 2)
    return (1.0 + 4.0 * SURF_C) * field - SURF_C * (east_side + west_side + north_side + south_side)


def member_total(values):
    return jnp.sum(values, axis=(1, 2))


def widen(values):
    return values[:, None, None]


def combine(a, fa, b, fb):
    def one(u, v):
        left = u if a is None else widen(a) * u
        return left + (v if b is None else widen(b) * v)

    return one(fa[0], fb[0]), tuple(one(u, v) for u, v in zip(fa[1], fb[1]))


def scaled(a, fa):
    return widen(a) * fa[0], tuple(widen(a) * u for u in fa[1])


def padded_2(block, sides_of, width):
    for axis, dim in sides_of:
        count = lax.axis_size(axis)
        forward = [(i, (i + 1) % count) for i in range(count)]
        backward = [((i + 1) % count, i) for i in range(count)]
        size = block.shape[dim]
        low = lax.ppermute(lax.slice_in_dim(block, size - width, size, axis=dim), axis, forward)
        high = lax.ppermute(lax.slice_in_dim(block, 0, width, axis=dim), axis, backward)
        block = jnp.concatenate([low, block, high], axis=dim)
    return block


def crop(field, by):
    if by == 0:
        return field
    return field[..., by:-by, by:-by]


def around(field):
    return (
        field[..., 1:-1, 1:-1],
        field[..., 1:-1, 2:],
        field[..., 1:-1, :-2],
        field[..., 2:, 1:-1],
        field[..., :-2, 1:-1],
    )


def rows_at(inside, full, want):
    cut = full - want
    return inside if cut == 0 else inside[cut:-cut]


def apply_wide(field, inside):
    centre, east, west, north, south = around(field)
    return ((1.0 + 4.0 * SURF_C) * centre - SURF_C * (east + west + north + south)) * inside


def surface_solve(rhs, inside, width, full):
    residual, wide_r = rhs, width
    gamma_prev = None
    alpha_prev = None
    for count in range(ITERS):
        image_res = apply_wide(residual, rows_at(inside, full, wide_r - 1))
        own_res = crop(residual, wide_r)
        own_img = crop(image_res, wide_r - 1)
        dots = grid_sum(jnp.stack([member_total(own_res * own_res), member_total(own_res * own_img)]))
        gamma, delta = dots[0], dots[1]
        if count == 0:
            alpha = gamma / delta
            direction, wide_p = residual, wide_r
            image_dir, wide_s = image_res, wide_r - 1
            solution, wide_x = widen(alpha) * direction, wide_r
        else:
            beta = gamma / gamma_prev
            alpha = gamma / (delta - beta * gamma / alpha_prev)
            direction = residual + widen(beta) * crop(direction, wide_p - wide_r)
            wide_p = wide_r
            image_dir = image_res + widen(beta) * crop(image_dir, wide_s - (wide_r - 1))
            wide_s = wide_r - 1
            solution = crop(solution, wide_x - wide_r) + widen(alpha) * direction
            wide_x = wide_r
        if count < ITERS - 1:
            residual = crop(residual, 1) - widen(alpha) * image_dir
            wide_r -= 1
        gamma_prev = gamma
        alpha_prev = alpha
    return solution


def shards(temp, salt, uvel, vvel, eta, land_mask, clone_source):
    levels = temp.shape[1]
    rows = temp.shape[2]
    cols = temp.shape[3]
    ocean = land_mask.astype(jnp.float32)
    tile_row = lax.axis_index("gridy")
    tile_count = lax.axis_size("gridy")
    total_rows = rows * tile_count
    total_cols = cols * lax.axis_size("gridx")
    south_keep = (tile_row > 0).astype(jnp.float32)
    north_keep = (tile_row < tile_count - 1).astype(jnp.float32)
    latitude = (tile_row * rows + jnp.arange(rows, dtype=jnp.int32)).astype(jnp.float32) + 0.5
    coriolis = (CORI_K * (2.0 * latitude / total_rows - 1.0))[:, None]
    cor_tile = jnp.broadcast_to(coriolis, (rows, cols))
    band = 8
    block = 128
    frame_rows = rows + 2 * band
    frame_cols = cols + 2 * block
    row_at = lax.broadcasted_iota(jnp.int32, (frame_rows, frame_cols), 0)
    col_at = lax.broadcasted_iota(jnp.int32, (frame_rows, frame_cols), 1)
    global_row = tile_row * rows + jnp.where(row_at < rows + band, row_at, row_at - frame_rows)
    wide_inside = ((global_row >= 0) & (global_row < total_rows)).astype(jnp.float32)
    own_mask = ((row_at < rows) & (col_at < cols)).astype(jnp.float32)
    for count in range(STEPS):
        fields = (temp, salt, uvel, vvel)
        rims = exchange_fields(fields, south_keep, north_keep)
        temp_next, salt_next, ustar, vstar, trans_u, trans_v = volume_step(
            temp, salt, uvel, vvel, ocean, cor_tile, rims
        )
        last = count == STEPS - 1
        cargo = jnp.stack((temp_next, salt_next, ustar, vstar)) if last else None
        solved, cargo_other = surface_kernel_solve(
            jnp.stack((trans_u, trans_v, eta)), wide_inside, own_mask, cargo
        )
        eta = solved[0]
        east_west = solved[1]
        north_south = solved[2]
        uvel = ocean * (ustar - GRAV_K * 0.5 * east_west[:, None])
        vvel = ocean * (vstar - GRAV_K * 0.5 * north_south[:, None])
        temp = temp_next
        salt = salt_next
    zonal_scale = 1.0 / jnp.sqrt(jnp.float32(total_cols))
    score_scale = 1.0 / jnp.sqrt(jnp.float32(levels * total_rows))
    lat_weight = latitude / total_rows
    members = temp.shape[0]
    zonal_local = jnp.sum(vvel, axis=3)
    depth_weight = (levels - jnp.arange(levels, dtype=jnp.int32)).astype(jnp.float32)
    score_local = jnp.sum(zonal_local * depth_weight[None, :, None] * lat_weight[None, None, :], axis=(1, 2))
    slot = lax.broadcasted_iota(jnp.int32, (tile_count, 1, 1, 1), 0) == tile_row
    zonal_slots = jnp.where(slot, zonal_local[None], 0.0).reshape(-1, 128)
    score_row = jnp.zeros((8, 128), jnp.float32).at[0, :members].set(score_local)
    summed = grid_sum(jnp.concatenate([zonal_slots, score_row], axis=0))
    zonal_whole = summed[: zonal_slots.shape[0]].reshape((tile_count,) + zonal_local.shape)
    zonal_whole = jnp.sum(jnp.where(slot, zonal_whole, 0.0), axis=0)
    overturn = jnp.cumsum(zonal_whole, axis=1) * zonal_scale
    score = summed[zonal_slots.shape[0], :members] * (zonal_scale * score_scale)
    swap = [(0, 1), (1, 0)]
    mine = lax.axis_index("member")
    score_slab = jnp.zeros((members, 1) + eta.shape[1:], jnp.float32).at[:, 0, 0, 0].set(score)
    surface_last = jnp.concatenate([solved.transpose(1, 0, 2, 3), score_slab], axis=1)
    surface_other = lax.ppermute(surface_last, "member", swap)
    score_other = surface_other[:, 3, 0, 0]
    every_score = jnp.where(
        mine == 0, jnp.concatenate([score, score_other]), jnp.concatenate([score_other, score])
    )
    here = (clone_source // members) == mine
    local_at = clone_source % members

    def pick(local, other):
        chosen = []
        for place in range(members):
            from_here = lax.dynamic_index_in_dim(local, local_at[place], 0, keepdims=False)
            from_other = lax.dynamic_index_in_dim(other, local_at[place], 0, keepdims=False)
            chosen.append(jnp.where(here[place], from_here, from_other))
        return jnp.stack(chosen)

    uvel_other = ocean * (cargo_other[2] - GRAV_K * 0.5 * surface_other[:, 1][:, None])
    vvel_other = ocean * (cargo_other[3] - GRAV_K * 0.5 * surface_other[:, 2][:, None])
    new_temp = pick(temp, cargo_other[0])
    new_salt = pick(salt, cargo_other[1])
    new_uvel = pick(uvel, uvel_other)
    new_vvel = pick(vvel, vvel_other)
    new_eta = pick(eta, surface_other[:, 0])
    clone_weight = jnp.take(every_score, clone_source, axis=0) - jnp.mean(every_score)
    return (new_temp, new_salt, new_uvel, new_vvel, new_eta, overturn, clone_weight)


def solution(mesh):
    in_specs = (
        P("member", None, "gridy", "gridx"),
        P("member", None, "gridy", "gridx"),
        P("member", None, "gridy", "gridx"),
        P("member", None, "gridy", "gridx"),
        P("member", "gridy", "gridx"),
        P("gridy", "gridx"),
        P("member"),
    )
    out_specs = (
        P("member", None, "gridy", "gridx"),
        P("member", None, "gridy", "gridx"),
        P("member", None, "gridy", "gridx"),
        P("member", None, "gridy", "gridx"),
        P("member", "gridy", "gridx"),
        P("member", None, "gridy"),
        P("member"),
    )
    return jax.shard_map(shards, mesh=mesh, in_specs=in_specs, out_specs=out_specs, check_vma=False)
```

```python
import functools

import jax
import jax.numpy as jnp
from jax import lax
from jax.experimental import pallas as pl
from jax.experimental.pallas import tpu as pltpu
from jax.sharding import PartitionSpec as P

STEPS = 2
ITERS = 3


ALPHA_T = 0.8
BETA_S = 0.6
PRESS_K = 0.25
STEP_DT = 0.1
KAPPA = 0.1
VISCOSITY = 0.1
DRAG_K = 0.05
CORI_K = 1.0
SURF_C = 4.0
DIV_K = 0.5
GRAV_K = 0.5


def tree_sum(values, axes):
    for axis in axes:
        count = lax.axis_size(axis)
        step = 1
        while step < count:
            pairs = [(i, i ^ step) for i in range(count)]
            values = values + lax.ppermute(values, axis, pairs)
            step *= 2
    return values


def gather_sum_kernel(ny, nx, x_ref, o_ref, recv_y, recv_x, part, send_y, rsem_y, send_x, rsem_x):
    mesh_id = pl.DeviceIdType.MESH
    member = lax.axis_index("member")
    my = lax.axis_index("gridy")
    mx = lax.axis_index("gridx")
    barrier = pltpu.get_barrier_semaphore()
    for d in range(1, ny):
        pl.semaphore_signal(barrier, 1, device_id=(member, (my + d) % ny, mx), device_id_type=mesh_id)
    for d in range(1, nx):
        pl.semaphore_signal(barrier, 1, device_id=(member, my, (mx + d) % nx), device_id_type=mesh_id)
    pl.semaphore_wait(barrier, (ny - 1) + (nx - 1))

    def phase(src, recv, send_sem, recv_sem, count, me, device):
        recv[me] = src[...]
        sent = []
        for d in range(1, count):
            peer = (me + d) % count
            copy = pltpu.make_async_remote_copy(
                src_ref=src,
                dst_ref=recv.at[me],
                send_sem=send_sem.at[peer],
                recv_sem=recv_sem.at[me],
                device_id=device(peer),
                device_id_type=mesh_id,
            )
            copy.start()
            sent.append(copy)
        for d in range(1, count):
            peer = (me + d) % count
            pltpu.make_async_remote_copy(
                src_ref=src,
                dst_ref=recv.at[peer],
                send_sem=send_sem.at[peer],
                recv_sem=recv_sem.at[peer],
                device_id=device(peer),
                device_id_type=mesh_id,
            ).wait_recv()
        for copy in sent:
            copy.wait_send()
        total = recv[0]
        for j in range(1, count):
            total = total + recv[j]
        return total

    part[...] = phase(x_ref, recv_y, send_y, rsem_y, ny, my, lambda p: (member, p, mx))
    o_ref[...] = phase(part, recv_x, send_x, rsem_x, nx, mx, lambda p: (member, my, p))


def grid_sum(values):
    ny = lax.axis_size("gridy")
    nx = lax.axis_size("gridx")
    shape = values.shape
    return pl.pallas_call(
        functools.partial(gather_sum_kernel, ny, nx),
        out_shape=jax.ShapeDtypeStruct(shape, values.dtype),
        in_specs=[pl.BlockSpec(memory_space=pltpu.VMEM)],
        out_specs=pl.BlockSpec(memory_space=pltpu.VMEM),
        scratch_shapes=[
            pltpu.VMEM((ny,) + shape, values.dtype),
            pltpu.VMEM((nx,) + shape, values.dtype),
            pltpu.VMEM(shape, values.dtype),
            pltpu.SemaphoreType.DMA((ny,)),
            pltpu.SemaphoreType.DMA((ny,)),
            pltpu.SemaphoreType.DMA((nx,)),
            pltpu.SemaphoreType.DMA((nx,)),
        ],
        compiler_params=pltpu.CompilerParams(collective_id=0, has_side_effects=True),
    )(values)


def exchange_sum(k, vec, ny, nx, bufs, device_ids):
    send_y, recv_y, send_x, recv_x, sy, ry, sx, rx = bufs
    my, mx, along_y, along_x = device_ids
    mesh_id = pl.DeviceIdType.MESH

    def phase(value, send_buf, recv, send_sem, recv_sem, count, me, device):
        send_buf[k] = value
        recv[k, me] = value
        sent = []
        for d in range(1, count):
            peer = (me + d) % count
            copy = pltpu.make_async_remote_copy(
                src_ref=send_buf.at[k],
                dst_ref=recv.at[k, me],
                send_sem=send_sem.at[k, peer],
                recv_sem=recv_sem.at[k, me],
                device_id=device(peer),
                device_id_type=mesh_id,
            )
            copy.start()
            sent.append(copy)
        for d in range(1, count):
            peer = (me + d) % count
            pltpu.make_async_remote_copy(
                src_ref=send_buf.at[k],
                dst_ref=recv.at[k, peer],
                send_sem=send_sem.at[k, peer],
                recv_sem=recv_sem.at[k, peer],
                device_id=device(peer),
                device_id_type=mesh_id,
            ).wait_recv()
        for copy in sent:
            copy.wait_send()
        total = recv[k, 0]
        for j in range(1, count):
            total = total + recv[k, j]
        return total

    partial = phase(vec, send_y, recv_y, sy, ry, ny, my, along_y)
    return phase(partial, send_x, recv_x, sx, rx, nx, mx, along_x)


def solve_kernel(ny, nx, surf_ref, inside_ref, own_ref, out_ref, frame, hsend, hrecv, *bufs):
    mesh_id = pl.DeviceIdType.MESH
    member = lax.axis_index("member")
    my = lax.axis_index("gridy")
    mx = lax.axis_index("gridx")
    along_y = lambda p: (member, p, mx)
    along_x = lambda p: (member, my, p)
    barrier = pltpu.get_barrier_semaphore()
    for d in range(1, ny):
        pl.semaphore_signal(barrier, 1, device_id=along_y((my + d) % ny), device_id_type=mesh_id)
    for d in range(1, nx):
        pl.semaphore_signal(barrier, 1, device_id=along_x((mx + d) % nx), device_id_type=mesh_id)
    for dy in (1, ny - 1):
        for dx in (1, nx - 1):
            pl.semaphore_signal(
                barrier, 1, device_id=(member, (my + dy) % ny, (mx + dx) % nx), device_id_type=mesh_id
            )
    rows, cols = surf_ref.shape[2], surf_ref.shape[3]
    wide_rows, wide_cols = frame.shape[2], frame.shape[3]
    band = (wide_rows - rows) // 2
    block = (wide_cols - cols) // 2
    frame[:, :, 0:rows, 0:cols] = surf_ref[...]
    pl.semaphore_wait(barrier, (ny - 1) + (nx - 1) + 4)

    def halo_copies(first, moves):
        started = []
        for slot, (src, dst, device) in enumerate(moves, start=first):
            copy = pltpu.make_async_remote_copy(
                src_ref=src, dst_ref=dst, send_sem=hsend.at[slot], recv_sem=hrecv.at[slot],
                device_id=device, device_id_type=mesh_id,
            )
            copy.start()
            started.append(copy)
        for copy in started:
            copy.wait()

    up, down = (my + 1) % ny, (my + ny - 1) % ny
    right, left = (mx + 1) % nx, (mx + nx - 1) % nx
    top_rows = slice(0, band)
    low_rows = slice(rows - band, rows)
    own_rows = slice(0, rows)
    west_part = slice(0, block)
    east_part = slice(cols - block, cols)
    own_cols = slice(0, cols)
    north_halo = slice(rows, rows + band)
    south_halo = slice(rows + band, wide_rows)
    east_halo = slice(cols, cols + block)
    west_halo = slice(cols + block, wide_cols)
    halo_copies(0, [
        (frame.at[:, :, top_rows, own_cols], frame.at[:, :, north_halo, own_cols], (member, down, mx)),
        (frame.at[:, :, low_rows, own_cols], frame.at[:, :, south_halo, own_cols], (member, up, mx)),
        (frame.at[:, :, own_rows, west_part], frame.at[:, :, own_rows, east_halo], (member, my, left)),
        (frame.at[:, :, own_rows, east_part], frame.at[:, :, own_rows, west_halo], (member, my, right)),
        (frame.at[:, :, top_rows, west_part], frame.at[:, :, north_halo, east_halo], (member, down, left)),
        (frame.at[:, :, top_rows, east_part], frame.at[:, :, north_halo, west_halo], (member, down, right)),
        (frame.at[:, :, low_rows, west_part], frame.at[:, :, south_halo, east_halo], (member, up, left)),
        (frame.at[:, :, low_rows, east_part], frame.at[:, :, south_halo, west_halo], (member, up, right)),
    ])

    members = surf_ref.shape[1]
    inside = inside_ref[...]
    own = own_ref[...] > 0.5

    def east(f):
        return pltpu.roll(f, wide_cols - 1, 1)

    def west(f):
        return pltpu.roll(f, 1, 1)

    def north(f):
        return pltpu.roll(f, wide_rows - 1, 0)

    def south(f):
        return pltpu.roll(f, 1, 0)

    def apply(f):
        return ((1.0 + 4.0 * SURF_C) * f - SURF_C * (east(f) + west(f) + north(f) + south(f))) * inside

    def total(f):
        return jnp.sum(f[0:rows, 0:cols], axis=(0, 1), keepdims=True)

    residual = []
    for m in range(members):
        trans_u = frame[0, m] * inside
        trans_v = frame[1, m] * inside
        level = frame[2, m] * inside
        residual.append(
            (level - DIV_K * 0.5 * (east(trans_u) - west(trans_u) + (north(trans_v) - south(trans_v)))) * inside
        )
    lane = lax.broadcasted_iota(jnp.int32, (8, 128), 1)
    direction = [None] * members
    image_dir = [None] * members
    solution = [None] * members
    gamma_prev = [None] * members
    alpha_prev = [None] * members
    for count in range(ITERS):
        image_res = [apply(residual[m]) for m in range(members)]
        vec = jnp.zeros((8, 128), jnp.float32)
        for m in range(members):
            vec = jnp.where(lane == 2 * m, total(residual[m] * residual[m]), vec)
            vec = jnp.where(lane == 2 * m + 1, total(residual[m] * image_res[m]), vec)
        sums = exchange_sum(count, vec, ny, nx, bufs, (my, mx, along_y, along_x))
        for m in range(members):
            gamma = sums[0:1, 2 * m : 2 * m + 1]
            delta = sums[0:1, 2 * m + 1 : 2 * m + 2]
            if count == 0:
                alpha = gamma / delta
                direction[m] = residual[m]
                image_dir[m] = image_res[m]
                solution[m] = alpha * direction[m]
            else:
                beta = gamma / gamma_prev[m]
                alpha = gamma / (delta - beta * gamma / alpha_prev[m])
                direction[m] = residual[m] + beta * direction[m]
                image_dir[m] = image_res[m] + beta * image_dir[m]
                solution[m] = solution[m] + alpha * direction[m]
            if count < ITERS - 1:
                residual[m] = residual[m] - alpha * image_dir[m]
            gamma_prev[m] = gamma
            alpha_prev[m] = alpha
    for m in range(members):
        x = solution[m]
        out_ref[0, m] = x[0:rows, 0:cols]
        out_ref[1, m] = (east(x) - west(x))[0:rows, 0:cols]
        out_ref[2, m] = (north(x) - south(x))[0:rows, 0:cols]


def surface_kernel_solve(surf, inside, own):
    ny = lax.axis_size("gridy")
    nx = lax.axis_size("gridx")
    fields, members, rows, cols = surf.shape
    return pl.pallas_call(
        functools.partial(solve_kernel, ny, nx),
        out_shape=jax.ShapeDtypeStruct((3, members, rows, cols), jnp.float32),
        in_specs=[pl.BlockSpec(memory_space=pltpu.VMEM)] * 3,
        out_specs=pl.BlockSpec(memory_space=pltpu.VMEM),
        scratch_shapes=[
            pltpu.VMEM((fields, members) + inside.shape, jnp.float32),
            pltpu.SemaphoreType.DMA((8,)),
            pltpu.SemaphoreType.DMA((8,)),
            pltpu.VMEM((ITERS, 8, 128), jnp.float32),
            pltpu.VMEM((ITERS, ny, 8, 128), jnp.float32),
            pltpu.VMEM((ITERS, 8, 128), jnp.float32),
            pltpu.VMEM((ITERS, nx, 8, 128), jnp.float32),
            pltpu.SemaphoreType.DMA((ITERS, ny)),
            pltpu.SemaphoreType.DMA((ITERS, ny)),
            pltpu.SemaphoreType.DMA((ITERS, nx)),
            pltpu.SemaphoreType.DMA((ITERS, nx)),
        ],
        compiler_params=pltpu.CompilerParams(collective_id=1, has_side_effects=True),
    )(surf, inside, own)


def volume_kernel(temp_ref, salt_ref, uvel_ref, vvel_ref, ocean_ref, cor_ref, n_ref, s_ref, e_ref, w_ref,
                  tn_ref, sn_ref, us_ref, vs_ref, tu_ref, tv_ref):
    levels, rows, cols = temp_ref.shape[1], temp_ref.shape[2], temp_ref.shape[3]
    row = lax.broadcasted_iota(jnp.int32, (rows, cols), 0)
    col = lax.broadcasted_iota(jnp.int32, (rows, cols), 1)
    top = row == rows - 1
    bottom = row == 0
    right = col == cols - 1
    left = col == 0
    ocean = ocean_ref[...]
    cor = cor_ref[...]

    def around(f, rims):
        n, s, e, w = rims
        return (
            jnp.where(right, e, pltpu.roll(f, cols - 1, 1)),
            jnp.where(left, w, pltpu.roll(f, 1, 1)),
            jnp.where(top, n, pltpu.roll(f, rows - 1, 0)),
            jnp.where(bottom, s, pltpu.roll(f, 1, 0)),
        )

    def rims_of(k, l):
        return (n_ref[k, 0, l], s_ref[k, 0, l], e_ref[k, 0, l], w_ref[k, 0, l])

    running = None
    running_rims = None
    tu = None
    tv = None
    for l in range(levels):
        t = temp_ref[0, l]
        s = salt_ref[0, l]
        u = uvel_ref[0, l]
        v = vvel_ref[0, l]
        rt, rs, ru, rv = rims_of(0, l), rims_of(1, l), rims_of(2, l), rims_of(3, l)
        layer = BETA_S * s - ALPHA_T * t
        layer_rims = tuple(BETA_S * b - ALPHA_T * a for a, b in zip(rt, rs))
        if running is None:
            running, running_rims = layer, layer_rims
        else:
            running = running + layer
            running_rims = tuple(a + b for a, b in zip(running_rims, layer_rims))
        press = PRESS_K * running
        press_rims = tuple(PRESS_K * a for a in running_rims)
        te, tw, tn, ts = around(t, rt)
        se, sw, sn, ss = around(s, rs)
        ue, uw, un, us = around(u, ru)
        ve, vw, vn, vs = around(v, rv)
        pe, pw, pn, ps = around(press, press_rims)
        tn_ref[0, l] = ocean * (
            t - STEP_DT * 0.5 * (u * (te - tw) + v * (tn - ts)) + KAPPA * (te + tw + tn + ts - 4.0 * t)
        )
        sn_ref[0, l] = ocean * (
            s - STEP_DT * 0.5 * (u * (se - sw) + v * (sn - ss)) + KAPPA * (se + sw + sn + ss - 4.0 * s)
        )
        ustar = ocean * (
            u + STEP_DT * (cor * v - 0.5 * (pe - pw) - DRAG_K * u) + VISCOSITY * (ue + uw + un + us - 4.0 * u)
        )
        vstar = ocean * (
            v + STEP_DT * (-cor * u - 0.5 * (pn - ps) - DRAG_K * v) + VISCOSITY * (ve + vw + vn + vs - 4.0 * v)
        )
        us_ref[0, l] = ustar
        vs_ref[0, l] = vstar
        tu = ustar if tu is None else tu + ustar
        tv = vstar if tv is None else tv + vstar
    tu_ref[0] = tu
    tv_ref[0] = tv


def volume_step(temp, salt, uvel, vvel, ocean, cor_tile, rims):
    members, levels, rows, cols = temp.shape
    field = pl.BlockSpec((1, levels, rows, cols), lambda m: (m, 0, 0, 0))
    plane = pl.BlockSpec((rows, cols), lambda m: (0, 0))
    north, south, east, west = rims
    row_rim = pl.BlockSpec((4, 1, levels, 1, cols), lambda m: (0, m, 0, 0, 0))
    col_rim = pl.BlockSpec((4, 1, levels, rows, 1), lambda m: (0, m, 0, 0, 0))
    surface = pl.BlockSpec((1, rows, cols), lambda m: (m, 0, 0))
    volume_shape = jax.ShapeDtypeStruct(temp.shape, jnp.float32)
    surface_shape = jax.ShapeDtypeStruct((members, rows, cols), jnp.float32)
    return pl.pallas_call(
        volume_kernel,
        grid=(members,),
        in_specs=[field] * 4 + [plane, plane, row_rim, row_rim, col_rim, col_rim],
        out_specs=[field] * 4 + [surface] * 2,
        out_shape=[volume_shape] * 4 + [surface_shape] * 2,
    )(temp, salt, uvel, vvel, ocean, cor_tile, north, south, east, west)


def ring(axis):
    count = lax.axis_size(axis)
    forward = [(i, (i + 1) % count) for i in range(count)]
    backward = [((i + 1) % count, i) for i in range(count)]
    return forward, backward


def exchange(block, ydim, xdim, south_keep, north_keep):
    fwd_y, bwd_y = ring("gridy")
    fwd_x, bwd_x = ring("gridx")
    rows = block.shape[ydim]
    cols = block.shape[xdim]
    north = lax.ppermute(lax.slice_in_dim(block, 0, 1, axis=ydim), "gridy", bwd_y) * north_keep
    south = lax.ppermute(lax.slice_in_dim(block, rows - 1, rows, axis=ydim), "gridy", fwd_y) * south_keep
    east = lax.ppermute(lax.slice_in_dim(block, 0, 1, axis=xdim), "gridx", bwd_x)
    west = lax.ppermute(lax.slice_in_dim(block, cols - 1, cols, axis=xdim), "gridx", fwd_x)
    return (east, west, north, south)


def exchange_fields(fields, south_keep, north_keep):
    fwd_y, bwd_y = ring("gridy")
    fwd_x, bwd_x = ring("gridx")
    north = lax.ppermute(jnp.stack([f[..., :1, :] for f in fields]), "gridy", bwd_y) * north_keep
    south = lax.ppermute(jnp.stack([f[..., -1:, :] for f in fields]), "gridy", fwd_y) * south_keep
    east = lax.ppermute(jnp.stack([f[..., :, :1] for f in fields]), "gridx", bwd_x)
    west = lax.ppermute(jnp.stack([f[..., :, -1:] for f in fields]), "gridx", fwd_x)
    return (north, south, east, west)


def sides(field, rims, ydim, xdim):
    east, west, north, south = rims
    rows = field.shape[ydim]
    cols = field.shape[xdim]
    east_side = jnp.concatenate([lax.slice_in_dim(field, 1, cols, axis=xdim), east], axis=xdim)
    west_side = jnp.concatenate([west, lax.slice_in_dim(field, 0, cols - 1, axis=xdim)], axis=xdim)
    north_side = jnp.concatenate([lax.slice_in_dim(field, 1, rows, axis=ydim), north], axis=ydim)
    south_side = jnp.concatenate([south, lax.slice_in_dim(field, 0, rows - 1, axis=ydim)], axis=ydim)
    return (east_side, west_side, north_side, south_side)


def pressure(temp, salt):
    return PRESS_K * jnp.cumsum(BETA_S * salt - ALPHA_T * temp, axis=-3)


def surface_apply(field, rims):
    east_side, west_side, north_side, south_side = sides(field, rims, 1, 2)
    return (1.0 + 4.0 * SURF_C) * field - SURF_C * (east_side + west_side + north_side + south_side)


def member_total(values):
    return jnp.sum(values, axis=(1, 2))


def widen(values):
    return values[:, None, None]


def combine(a, fa, b, fb):
    def one(u, v):
        left = u if a is None else widen(a) * u
        return left + (v if b is None else widen(b) * v)

    return one(fa[0], fb[0]), tuple(one(u, v) for u, v in zip(fa[1], fb[1]))


def scaled(a, fa):
    return widen(a) * fa[0], tuple(widen(a) * u for u in fa[1])


def padded_2(block, sides_of, width):
    for axis, dim in sides_of:
        count = lax.axis_size(axis)
        forward = [(i, (i + 1) % count) for i in range(count)]
        backward = [((i + 1) % count, i) for i in range(count)]
        size = block.shape[dim]
        low = lax.ppermute(lax.slice_in_dim(block, size - width, size, axis=dim), axis, forward)
        high = lax.ppermute(lax.slice_in_dim(block, 0, width, axis=dim), axis, backward)
        block = jnp.concatenate([low, block, high], axis=dim)
    return block


def crop(field, by):
    if by == 0:
        return field
    return field[..., by:-by, by:-by]


def around(field):
    return (
        field[..., 1:-1, 1:-1],
        field[..., 1:-1, 2:],
        field[..., 1:-1, :-2],
        field[..., 2:, 1:-1],
        field[..., :-2, 1:-1],
    )


def rows_at(inside, full, want):
    cut = full - want
    return inside if cut == 0 else inside[cut:-cut]


def apply_wide(field, inside):
    centre, east, west, north, south = around(field)
    return ((1.0 + 4.0 * SURF_C) * centre - SURF_C * (east + west + north + south)) * inside


def surface_solve(rhs, inside, width, full):
    residual, wide_r = rhs, width
    gamma_prev = None
    alpha_prev = None
    for count in range(ITERS):
        image_res = apply_wide(residual, rows_at(inside, full, wide_r - 1))
        own_res = crop(residual, wide_r)
        own_img = crop(image_res, wide_r - 1)
        dots = grid_sum(jnp.stack([member_total(own_res * own_res), member_total(own_res * own_img)]))
        gamma, delta = dots[0], dots[1]
        if count == 0:
            alpha = gamma / delta
            direction, wide_p = residual, wide_r
            image_dir, wide_s = image_res, wide_r - 1
            solution, wide_x = widen(alpha) * direction, wide_r
        else:
            beta = gamma / gamma_prev
            alpha = gamma / (delta - beta * gamma / alpha_prev)
            direction = residual + widen(beta) * crop(direction, wide_p - wide_r)
            wide_p = wide_r
            image_dir = image_res + widen(beta) * crop(image_dir, wide_s - (wide_r - 1))
            wide_s = wide_r - 1
            solution = crop(solution, wide_x - wide_r) + widen(alpha) * direction
            wide_x = wide_r
        if count < ITERS - 1:
            residual = crop(residual, 1) - widen(alpha) * image_dir
            wide_r -= 1
        gamma_prev = gamma
        alpha_prev = alpha
    return solution


def shards(temp, salt, uvel, vvel, eta, land_mask, clone_source):
    levels = temp.shape[1]
    rows = temp.shape[2]
    cols = temp.shape[3]
    ocean = land_mask.astype(jnp.float32)
    tile_row = lax.axis_index("gridy")
    tile_count = lax.axis_size("gridy")
    total_rows = rows * tile_count
    total_cols = cols * lax.axis_size("gridx")
    south_keep = (tile_row > 0).astype(jnp.float32)
    north_keep = (tile_row < tile_count - 1).astype(jnp.float32)
    latitude = (tile_row * rows + jnp.arange(rows, dtype=jnp.int32)).astype(jnp.float32) + 0.5
    coriolis = (CORI_K * (2.0 * latitude / total_rows - 1.0))[:, None]
    cor_tile = jnp.broadcast_to(coriolis, (rows, cols))
    band = 8
    block = 128
    frame_rows = rows + 2 * band
    frame_cols = cols + 2 * block
    row_at = lax.broadcasted_iota(jnp.int32, (frame_rows, frame_cols), 0)
    col_at = lax.broadcasted_iota(jnp.int32, (frame_rows, frame_cols), 1)
    global_row = tile_row * rows + jnp.where(row_at < rows + band, row_at, row_at - frame_rows)
    wide_inside = ((global_row >= 0) & (global_row < total_rows)).astype(jnp.float32)
    own_mask = ((row_at < rows) & (col_at < cols)).astype(jnp.float32)
    for count in range(STEPS):
        fields = (temp, salt, uvel, vvel)
        rims = exchange_fields(fields, south_keep, north_keep)
        temp_next, salt_next, ustar, vstar, trans_u, trans_v = volume_step(
            temp, salt, uvel, vvel, ocean, cor_tile, rims
        )
        solved = surface_kernel_solve(jnp.stack((trans_u, trans_v, eta)), wide_inside, own_mask)
        eta = solved[0]
        east_west = solved[1]
        north_south = solved[2]
        uvel = ocean * (ustar - GRAV_K * 0.5 * east_west[:, None])
        vvel = ocean * (vstar - GRAV_K * 0.5 * north_south[:, None])
        if count == STEPS - 1:
            tracers_other = lax.ppermute(jnp.stack((temp_next, salt_next)), "member", [(0, 1), (1, 0)])
        temp = temp_next
        salt = salt_next
    zonal_scale = 1.0 / jnp.sqrt(jnp.float32(total_cols))
    score_scale = 1.0 / jnp.sqrt(jnp.float32(levels * total_rows))
    lat_weight = latitude / total_rows
    members = temp.shape[0]
    zonal_local = jnp.sum(vvel, axis=3)
    depth_weight = (levels - jnp.arange(levels, dtype=jnp.int32)).astype(jnp.float32)
    score_local = jnp.sum(zonal_local * depth_weight[None, :, None] * lat_weight[None, None, :], axis=(1, 2))
    slot = lax.broadcasted_iota(jnp.int32, (tile_count, 1, 1, 1), 0) == tile_row
    zonal_slots = jnp.where(slot, zonal_local[None], 0.0).reshape(-1, 128)
    score_row = jnp.zeros((8, 128), jnp.float32).at[0, :members].set(score_local)
    summed = grid_sum(jnp.concatenate([zonal_slots, score_row], axis=0))
    zonal_whole = summed[: zonal_slots.shape[0]].reshape((tile_count,) + zonal_local.shape)
    zonal_whole = jnp.sum(jnp.where(slot, zonal_whole, 0.0), axis=0)
    overturn = jnp.cumsum(zonal_whole, axis=1) * zonal_scale
    score = summed[zonal_slots.shape[0], :members] * (zonal_scale * score_scale)
    swap = [(0, 1), (1, 0)]
    mine = lax.axis_index("member")
    score_slab = jnp.zeros((members, 1) + eta.shape[1:], jnp.float32).at[:, 0, 0, 0].set(score)
    flows = jnp.concatenate([uvel, vvel, eta[:, None], score_slab], axis=1)
    flows_other = lax.ppermute(flows, "member", swap)
    score_other = flows_other[:, 2 * levels + 1, 0, 0]
    every_score = jnp.where(
        mine == 0, jnp.concatenate([score, score_other]), jnp.concatenate([score_other, score])
    )
    here = (clone_source // members) == mine
    local_at = clone_source % members

    def pick(local, other):
        chosen = []
        for place in range(members):
            from_here = lax.dynamic_index_in_dim(local, local_at[place], 0, keepdims=False)
            from_other = lax.dynamic_index_in_dim(other, local_at[place], 0, keepdims=False)
            chosen.append(jnp.where(here[place], from_here, from_other))
        return jnp.stack(chosen)

    new_temp = pick(temp, tracers_other[0])
    new_salt = pick(salt, tracers_other[1])
    new_flows = pick(flows[:, : 2 * levels + 1], flows_other[:, : 2 * levels + 1])
    clone_weight = jnp.take(every_score, clone_source, axis=0) - jnp.mean(every_score)
    return (
        new_temp,
        new_salt,
        new_flows[:, :levels],
        new_flows[:, levels : 2 * levels],
        new_flows[:, 2 * levels],
        overturn,
        clone_weight,
    )


def solution(mesh):
    in_specs = (
        P("member", None, "gridy", "gridx"),
        P("member", None, "gridy", "gridx"),
        P("member", None, "gridy", "gridx"),
        P("member", None, "gridy", "gridx"),
        P("member", "gridy", "gridx"),
        P("gridy", "gridx"),
        P("member"),
    )
    out_specs = (
        P("member", None, "gridy", "gridx"),
        P("member", None, "gridy", "gridx"),
        P("member", None, "gridy", "gridx"),
        P("member", None, "gridy", "gridx"),
        P("member", "gridy", "gridx"),
        P("member", None, "gridy"),
        P("member"),
    )
    return jax.shard_map(shards, mesh=mesh, in_specs=in_specs, out_specs=out_specs, check_vma=False)
```

```python
import functools

import jax
import jax.numpy as jnp
from jax import lax
from jax.experimental import pallas as pl
from jax.experimental.pallas import tpu as pltpu
from jax.sharding import PartitionSpec as P

STEPS = 2
ITERS = 3


ALPHA_T = 0.8
BETA_S = 0.6
PRESS_K = 0.25
STEP_DT = 0.1
KAPPA = 0.1
VISCOSITY = 0.1
DRAG_K = 0.05
CORI_K = 1.0
SURF_C = 4.0
DIV_K = 0.5
GRAV_K = 0.5


def tree_sum(values, axes):
    for axis in axes:
        count = lax.axis_size(axis)
        step = 1
        while step < count:
            pairs = [(i, i ^ step) for i in range(count)]
            values = values + lax.ppermute(values, axis, pairs)
            step *= 2
    return values


def gather_sum_kernel(ny, nx, x_ref, o_ref, recv_y, recv_x, part, send_y, rsem_y, send_x, rsem_x):
    mesh_id = pl.DeviceIdType.MESH
    member = lax.axis_index("member")
    my = lax.axis_index("gridy")
    mx = lax.axis_index("gridx")
    barrier = pltpu.get_barrier_semaphore()
    for d in range(1, ny):
        pl.semaphore_signal(barrier, 1, device_id=(member, (my + d) % ny, mx), device_id_type=mesh_id)
    for d in range(1, nx):
        pl.semaphore_signal(barrier, 1, device_id=(member, my, (mx + d) % nx), device_id_type=mesh_id)
    pl.semaphore_wait(barrier, (ny - 1) + (nx - 1))

    def phase(src, recv, send_sem, recv_sem, count, me, device):
        recv[me] = src[...]
        sent = []
        for d in range(1, count):
            peer = (me + d) % count
            copy = pltpu.make_async_remote_copy(
                src_ref=src,
                dst_ref=recv.at[me],
                send_sem=send_sem.at[peer],
                recv_sem=recv_sem.at[me],
                device_id=device(peer),
                device_id_type=mesh_id,
            )
            copy.start()
            sent.append(copy)
        for d in range(1, count):
            peer = (me + d) % count
            pltpu.make_async_remote_copy(
                src_ref=src,
                dst_ref=recv.at[peer],
                send_sem=send_sem.at[peer],
                recv_sem=recv_sem.at[peer],
                device_id=device(peer),
                device_id_type=mesh_id,
            ).wait_recv()
        for copy in sent:
            copy.wait_send()
        total = recv[0]
        for j in range(1, count):
            total = total + recv[j]
        return total

    part[...] = phase(x_ref, recv_y, send_y, rsem_y, ny, my, lambda p: (member, p, mx))
    o_ref[...] = phase(part, recv_x, send_x, rsem_x, nx, mx, lambda p: (member, my, p))


def grid_sum(values):
    ny = lax.axis_size("gridy")
    nx = lax.axis_size("gridx")
    shape = values.shape
    return pl.pallas_call(
        functools.partial(gather_sum_kernel, ny, nx),
        out_shape=jax.ShapeDtypeStruct(shape, values.dtype),
        in_specs=[pl.BlockSpec(memory_space=pltpu.VMEM)],
        out_specs=pl.BlockSpec(memory_space=pltpu.VMEM),
        scratch_shapes=[
            pltpu.VMEM((ny,) + shape, values.dtype),
            pltpu.VMEM((nx,) + shape, values.dtype),
            pltpu.VMEM(shape, values.dtype),
            pltpu.SemaphoreType.DMA((ny,)),
            pltpu.SemaphoreType.DMA((ny,)),
            pltpu.SemaphoreType.DMA((nx,)),
            pltpu.SemaphoreType.DMA((nx,)),
        ],
        compiler_params=pltpu.CompilerParams(collective_id=0, has_side_effects=True),
    )(values)


def exchange_sum(k, vec, ny, nx, bufs, device_ids):
    send_y, recv_y, send_x, recv_x, sy, ry, sx, rx = bufs
    my, mx, along_y, along_x = device_ids
    mesh_id = pl.DeviceIdType.MESH

    def phase(value, send_buf, recv, send_sem, recv_sem, count, me, device):
        send_buf[k] = value
        recv[k, me] = value
        sent = []
        for d in range(1, count):
            peer = (me + d) % count
            copy = pltpu.make_async_remote_copy(
                src_ref=send_buf.at[k],
                dst_ref=recv.at[k, me],
                send_sem=send_sem.at[k, peer],
                recv_sem=recv_sem.at[k, me],
                device_id=device(peer),
                device_id_type=mesh_id,
            )
            copy.start()
            sent.append(copy)
        for d in range(1, count):
            peer = (me + d) % count
            pltpu.make_async_remote_copy(
                src_ref=send_buf.at[k],
                dst_ref=recv.at[k, peer],
                send_sem=send_sem.at[k, peer],
                recv_sem=recv_sem.at[k, peer],
                device_id=device(peer),
                device_id_type=mesh_id,
            ).wait_recv()
        for copy in sent:
            copy.wait_send()
        total = recv[k, 0]
        for j in range(1, count):
            total = total + recv[k, j]
        return total

    partial = phase(vec, send_y, recv_y, sy, ry, ny, my, along_y)
    return phase(partial, send_x, recv_x, sx, rx, nx, mx, along_x)


def solve_kernel(ny, nx, tu_ref, tv_ref, eta_ref, inside_ref, own_ref, out_ref, frame, hsend, hrecv, *bufs):
    mesh_id = pl.DeviceIdType.MESH
    member = lax.axis_index("member")
    my = lax.axis_index("gridy")
    mx = lax.axis_index("gridx")
    along_y = lambda p: (member, p, mx)
    along_x = lambda p: (member, my, p)
    barrier = pltpu.get_barrier_semaphore()
    for d in range(1, ny):
        pl.semaphore_signal(barrier, 1, device_id=along_y((my + d) % ny), device_id_type=mesh_id)
    for d in range(1, nx):
        pl.semaphore_signal(barrier, 1, device_id=along_x((mx + d) % nx), device_id_type=mesh_id)
    for dy in (1, ny - 1):
        for dx in (1, nx - 1):
            pl.semaphore_signal(
                barrier, 1, device_id=(member, (my + dy) % ny, (mx + dx) % nx), device_id_type=mesh_id
            )
    rows, cols = eta_ref.shape[1], eta_ref.shape[2]
    wide_rows, wide_cols = frame.shape[2], frame.shape[3]
    band = (wide_rows - rows) // 2
    block = (wide_cols - cols) // 2
    frame[0, :, 0:rows, 0:cols] = tu_ref[...]
    frame[1, :, 0:rows, 0:cols] = tv_ref[...]
    frame[2, :, 0:rows, 0:cols] = eta_ref[...]
    pl.semaphore_wait(barrier, (ny - 1) + (nx - 1) + 4)

    def halo_copies(first, moves):
        started = []
        for slot, (src, dst, device) in enumerate(moves, start=first):
            copy = pltpu.make_async_remote_copy(
                src_ref=src, dst_ref=dst, send_sem=hsend.at[slot], recv_sem=hrecv.at[slot],
                device_id=device, device_id_type=mesh_id,
            )
            copy.start()
            started.append(copy)
        for copy in started:
            copy.wait()

    up, down = (my + 1) % ny, (my + ny - 1) % ny
    right, left = (mx + 1) % nx, (mx + nx - 1) % nx
    top_rows = slice(0, band)
    low_rows = slice(rows - band, rows)
    own_rows = slice(0, rows)
    west_part = slice(0, block)
    east_part = slice(cols - block, cols)
    own_cols = slice(0, cols)
    north_halo = slice(rows, rows + band)
    south_halo = slice(rows + band, wide_rows)
    east_halo = slice(cols, cols + block)
    west_halo = slice(cols + block, wide_cols)
    halo_copies(0, [
        (frame.at[:, :, top_rows, own_cols], frame.at[:, :, north_halo, own_cols], (member, down, mx)),
        (frame.at[:, :, low_rows, own_cols], frame.at[:, :, south_halo, own_cols], (member, up, mx)),
        (frame.at[:, :, own_rows, west_part], frame.at[:, :, own_rows, east_halo], (member, my, left)),
        (frame.at[:, :, own_rows, east_part], frame.at[:, :, own_rows, west_halo], (member, my, right)),
        (frame.at[:, :, top_rows, west_part], frame.at[:, :, north_halo, east_halo], (member, down, left)),
        (frame.at[:, :, top_rows, east_part], frame.at[:, :, north_halo, west_halo], (member, down, right)),
        (frame.at[:, :, low_rows, west_part], frame.at[:, :, south_halo, east_halo], (member, up, left)),
        (frame.at[:, :, low_rows, east_part], frame.at[:, :, south_halo, west_halo], (member, up, right)),
    ])

    members = eta_ref.shape[0]
    inside = inside_ref[...]
    own = own_ref[...] > 0.5

    def east(f):
        return pltpu.roll(f, wide_cols - 1, 1)

    def west(f):
        return pltpu.roll(f, 1, 1)

    def north(f):
        return pltpu.roll(f, wide_rows - 1, 0)

    def south(f):
        return pltpu.roll(f, 1, 0)

    def apply(f):
        return ((1.0 + 4.0 * SURF_C) * f - SURF_C * (east(f) + west(f) + north(f) + south(f))) * inside

    def total(f):
        return jnp.sum(f[0:rows, 0:cols], axis=(0, 1), keepdims=True)

    residual = []
    for m in range(members):
        trans_u = frame[0, m] * inside
        trans_v = frame[1, m] * inside
        level = frame[2, m] * inside
        residual.append(
            (level - DIV_K * 0.5 * (east(trans_u) - west(trans_u) + (north(trans_v) - south(trans_v)))) * inside
        )
    lane = lax.broadcasted_iota(jnp.int32, (8, 128), 1)
    direction = [None] * members
    image_dir = [None] * members
    solution = [None] * members
    gamma_prev = [None] * members
    alpha_prev = [None] * members
    for count in range(ITERS):
        image_res = [apply(residual[m]) for m in range(members)]
        vec = jnp.zeros((8, 128), jnp.float32)
        for m in range(members):
            vec = jnp.where(lane == 2 * m, total(residual[m] * residual[m]), vec)
            vec = jnp.where(lane == 2 * m + 1, total(residual[m] * image_res[m]), vec)
        sums = exchange_sum(count, vec, ny, nx, bufs, (my, mx, along_y, along_x))
        for m in range(members):
            gamma = sums[0:1, 2 * m : 2 * m + 1]
            delta = sums[0:1, 2 * m + 1 : 2 * m + 2]
            if count == 0:
                alpha = gamma / delta
                direction[m] = residual[m]
                image_dir[m] = image_res[m]
                solution[m] = alpha * direction[m]
            else:
                beta = gamma / gamma_prev[m]
                alpha = gamma / (delta - beta * gamma / alpha_prev[m])
                direction[m] = residual[m] + beta * direction[m]
                image_dir[m] = image_res[m] + beta * image_dir[m]
                solution[m] = solution[m] + alpha * direction[m]
            if count < ITERS - 1:
                residual[m] = residual[m] - alpha * image_dir[m]
            gamma_prev[m] = gamma
            alpha_prev[m] = alpha
    for m in range(members):
        x = solution[m]
        out_ref[0, m] = x[0:rows, 0:cols]
        out_ref[1, m] = (east(x) - west(x))[0:rows, 0:cols]
        out_ref[2, m] = (north(x) - south(x))[0:rows, 0:cols]


def surface_kernel_solve(trans_u, trans_v, eta, inside, own):
    ny = lax.axis_size("gridy")
    nx = lax.axis_size("gridx")
    members, rows, cols = eta.shape
    fields = 3
    return pl.pallas_call(
        functools.partial(solve_kernel, ny, nx),
        out_shape=jax.ShapeDtypeStruct((3, members, rows, cols), jnp.float32),
        in_specs=[pl.BlockSpec(memory_space=pltpu.VMEM)] * 5,
        out_specs=pl.BlockSpec(memory_space=pltpu.VMEM),
        scratch_shapes=[
            pltpu.VMEM((fields, members) + inside.shape, jnp.float32),
            pltpu.SemaphoreType.DMA((8,)),
            pltpu.SemaphoreType.DMA((8,)),
            pltpu.VMEM((ITERS, 8, 128), jnp.float32),
            pltpu.VMEM((ITERS, ny, 8, 128), jnp.float32),
            pltpu.VMEM((ITERS, 8, 128), jnp.float32),
            pltpu.VMEM((ITERS, nx, 8, 128), jnp.float32),
            pltpu.SemaphoreType.DMA((ITERS, ny)),
            pltpu.SemaphoreType.DMA((ITERS, ny)),
            pltpu.SemaphoreType.DMA((ITERS, nx)),
            pltpu.SemaphoreType.DMA((ITERS, nx)),
        ],
        compiler_params=pltpu.CompilerParams(collective_id=1, has_side_effects=True),
    )(trans_u, trans_v, eta, inside, own)


def volume_kernel(temp_ref, salt_ref, uvel_ref, vvel_ref, ocean_ref, cor_ref, n_ref, s_ref, e_ref, w_ref,
                  tn_ref, sn_ref, us_ref, vs_ref, tu_ref, tv_ref):
    levels, rows, cols = temp_ref.shape[1], temp_ref.shape[2], temp_ref.shape[3]
    row = lax.broadcasted_iota(jnp.int32, (rows, cols), 0)
    col = lax.broadcasted_iota(jnp.int32, (rows, cols), 1)
    top = row == rows - 1
    bottom = row == 0
    right = col == cols - 1
    left = col == 0
    ocean = ocean_ref[...]
    cor = cor_ref[...]

    def around(f, rims):
        n, s, e, w = rims
        return (
            jnp.where(right, e, pltpu.roll(f, cols - 1, 1)),
            jnp.where(left, w, pltpu.roll(f, 1, 1)),
            jnp.where(top, n, pltpu.roll(f, rows - 1, 0)),
            jnp.where(bottom, s, pltpu.roll(f, 1, 0)),
        )

    def rims_of(k, l):
        return (n_ref[k, 0, l], s_ref[k, 0, l], e_ref[k, 0, l], w_ref[k, 0, l])

    running = None
    running_rims = None
    tu = None
    tv = None
    for l in range(levels):
        t = temp_ref[0, l]
        s = salt_ref[0, l]
        u = uvel_ref[0, l]
        v = vvel_ref[0, l]
        rt, rs, ru, rv = rims_of(0, l), rims_of(1, l), rims_of(2, l), rims_of(3, l)
        layer = BETA_S * s - ALPHA_T * t
        layer_rims = tuple(BETA_S * b - ALPHA_T * a for a, b in zip(rt, rs))
        if running is None:
            running, running_rims = layer, layer_rims
        else:
            running = running + layer
            running_rims = tuple(a + b for a, b in zip(running_rims, layer_rims))
        press = PRESS_K * running
        press_rims = tuple(PRESS_K * a for a in running_rims)
        te, tw, tn, ts = around(t, rt)
        se, sw, sn, ss = around(s, rs)
        ue, uw, un, us = around(u, ru)
        ve, vw, vn, vs = around(v, rv)
        pe, pw, pn, ps = around(press, press_rims)
        tn_ref[0, l] = ocean * (
            t - STEP_DT * 0.5 * (u * (te - tw) + v * (tn - ts)) + KAPPA * (te + tw + tn + ts - 4.0 * t)
        )
        sn_ref[0, l] = ocean * (
            s - STEP_DT * 0.5 * (u * (se - sw) + v * (sn - ss)) + KAPPA * (se + sw + sn + ss - 4.0 * s)
        )
        ustar = ocean * (
            u + STEP_DT * (cor * v - 0.5 * (pe - pw) - DRAG_K * u) + VISCOSITY * (ue + uw + un + us - 4.0 * u)
        )
        vstar = ocean * (
            v + STEP_DT * (-cor * u - 0.5 * (pn - ps) - DRAG_K * v) + VISCOSITY * (ve + vw + vn + vs - 4.0 * v)
        )
        us_ref[0, l] = ustar
        vs_ref[0, l] = vstar
        tu = ustar if tu is None else tu + ustar
        tv = vstar if tv is None else tv + vstar
    tu_ref[0] = tu
    tv_ref[0] = tv


def volume_step(temp, salt, uvel, vvel, ocean, cor_tile, rims):
    members, levels, rows, cols = temp.shape
    field = pl.BlockSpec((1, levels, rows, cols), lambda m: (m, 0, 0, 0))
    plane = pl.BlockSpec((rows, cols), lambda m: (0, 0))
    north, south, east, west = rims
    row_rim = pl.BlockSpec((4, 1, levels, 1, cols), lambda m: (0, m, 0, 0, 0))
    col_rim = pl.BlockSpec((4, 1, levels, rows, 1), lambda m: (0, m, 0, 0, 0))
    surface = pl.BlockSpec((1, rows, cols), lambda m: (m, 0, 0))
    volume_shape = jax.ShapeDtypeStruct(temp.shape, jnp.float32)
    surface_shape = jax.ShapeDtypeStruct((members, rows, cols), jnp.float32)
    return pl.pallas_call(
        volume_kernel,
        grid=(members,),
        in_specs=[field] * 4 + [plane, plane, row_rim, row_rim, col_rim, col_rim],
        out_specs=[field] * 4 + [surface] * 2,
        out_shape=[volume_shape] * 4 + [surface_shape] * 2,
    )(temp, salt, uvel, vvel, ocean, cor_tile, north, south, east, west)


def ring(axis):
    count = lax.axis_size(axis)
    forward = [(i, (i + 1) % count) for i in range(count)]
    backward = [((i + 1) % count, i) for i in range(count)]
    return forward, backward


def exchange(block, ydim, xdim, south_keep, north_keep):
    fwd_y, bwd_y = ring("gridy")
    fwd_x, bwd_x = ring("gridx")
    rows = block.shape[ydim]
    cols = block.shape[xdim]
    north = lax.ppermute(lax.slice_in_dim(block, 0, 1, axis=ydim), "gridy", bwd_y) * north_keep
    south = lax.ppermute(lax.slice_in_dim(block, rows - 1, rows, axis=ydim), "gridy", fwd_y) * south_keep
    east = lax.ppermute(lax.slice_in_dim(block, 0, 1, axis=xdim), "gridx", bwd_x)
    west = lax.ppermute(lax.slice_in_dim(block, cols - 1, cols, axis=xdim), "gridx", fwd_x)
    return (east, west, north, south)


def exchange_fields(fields, south_keep, north_keep):
    fwd_y, bwd_y = ring("gridy")
    fwd_x, bwd_x = ring("gridx")
    north = lax.ppermute(jnp.stack([f[..., :1, :] for f in fields]), "gridy", bwd_y) * north_keep
    south = lax.ppermute(jnp.stack([f[..., -1:, :] for f in fields]), "gridy", fwd_y) * south_keep
    east = lax.ppermute(jnp.stack([f[..., :, :1] for f in fields]), "gridx", bwd_x)
    west = lax.ppermute(jnp.stack([f[..., :, -1:] for f in fields]), "gridx", fwd_x)
    return (north, south, east, west)


def sides(field, rims, ydim, xdim):
    east, west, north, south = rims
    rows = field.shape[ydim]
    cols = field.shape[xdim]
    east_side = jnp.concatenate([lax.slice_in_dim(field, 1, cols, axis=xdim), east], axis=xdim)
    west_side = jnp.concatenate([west, lax.slice_in_dim(field, 0, cols - 1, axis=xdim)], axis=xdim)
    north_side = jnp.concatenate([lax.slice_in_dim(field, 1, rows, axis=ydim), north], axis=ydim)
    south_side = jnp.concatenate([south, lax.slice_in_dim(field, 0, rows - 1, axis=ydim)], axis=ydim)
    return (east_side, west_side, north_side, south_side)


def pressure(temp, salt):
    return PRESS_K * jnp.cumsum(BETA_S * salt - ALPHA_T * temp, axis=-3)


def surface_apply(field, rims):
    east_side, west_side, north_side, south_side = sides(field, rims, 1, 2)
    return (1.0 + 4.0 * SURF_C) * field - SURF_C * (east_side + west_side + north_side + south_side)


def member_total(values):
    return jnp.sum(values, axis=(1, 2))


def widen(values):
    return values[:, None, None]


def combine(a, fa, b, fb):
    def one(u, v):
        left = u if a is None else widen(a) * u
        return left + (v if b is None else widen(b) * v)

    return one(fa[0], fb[0]), tuple(one(u, v) for u, v in zip(fa[1], fb[1]))


def scaled(a, fa):
    return widen(a) * fa[0], tuple(widen(a) * u for u in fa[1])


def padded_2(block, sides_of, width):
    for axis, dim in sides_of:
        count = lax.axis_size(axis)
        forward = [(i, (i + 1) % count) for i in range(count)]
        backward = [((i + 1) % count, i) for i in range(count)]
        size = block.shape[dim]
        low = lax.ppermute(lax.slice_in_dim(block, size - width, size, axis=dim), axis, forward)
        high = lax.ppermute(lax.slice_in_dim(block, 0, width, axis=dim), axis, backward)
        block = jnp.concatenate([low, block, high], axis=dim)
    return block


def crop(field, by):
    if by == 0:
        return field
    return field[..., by:-by, by:-by]


def around(field):
    return (
        field[..., 1:-1, 1:-1],
        field[..., 1:-1, 2:],
        field[..., 1:-1, :-2],
        field[..., 2:, 1:-1],
        field[..., :-2, 1:-1],
    )


def rows_at(inside, full, want):
    cut = full - want
    return inside if cut == 0 else inside[cut:-cut]


def apply_wide(field, inside):
    centre, east, west, north, south = around(field)
    return ((1.0 + 4.0 * SURF_C) * centre - SURF_C * (east + west + north + south)) * inside


def surface_solve(rhs, inside, width, full):
    residual, wide_r = rhs, width
    gamma_prev = None
    alpha_prev = None
    for count in range(ITERS):
        image_res = apply_wide(residual, rows_at(inside, full, wide_r - 1))
        own_res = crop(residual, wide_r)
        own_img = crop(image_res, wide_r - 1)
        dots = grid_sum(jnp.stack([member_total(own_res * own_res), member_total(own_res * own_img)]))
        gamma, delta = dots[0], dots[1]
        if count == 0:
            alpha = gamma / delta
            direction, wide_p = residual, wide_r
            image_dir, wide_s = image_res, wide_r - 1
            solution, wide_x = widen(alpha) * direction, wide_r
        else:
            beta = gamma / gamma_prev
            alpha = gamma / (delta - beta * gamma / alpha_prev)
            direction = residual + widen(beta) * crop(direction, wide_p - wide_r)
            wide_p = wide_r
            image_dir = image_res + widen(beta) * crop(image_dir, wide_s - (wide_r - 1))
            wide_s = wide_r - 1
            solution = crop(solution, wide_x - wide_r) + widen(alpha) * direction
            wide_x = wide_r
        if count < ITERS - 1:
            residual = crop(residual, 1) - widen(alpha) * image_dir
            wide_r -= 1
        gamma_prev = gamma
        alpha_prev = alpha
    return solution


def shards(temp, salt, uvel, vvel, eta, land_mask, clone_source):
    levels = temp.shape[1]
    rows = temp.shape[2]
    cols = temp.shape[3]
    ocean = land_mask.astype(jnp.float32)
    tile_row = lax.axis_index("gridy")
    tile_count = lax.axis_size("gridy")
    total_rows = rows * tile_count
    total_cols = cols * lax.axis_size("gridx")
    south_keep = (tile_row > 0).astype(jnp.float32)
    north_keep = (tile_row < tile_count - 1).astype(jnp.float32)
    latitude = (tile_row * rows + jnp.arange(rows, dtype=jnp.int32)).astype(jnp.float32) + 0.5
    coriolis = (CORI_K * (2.0 * latitude / total_rows - 1.0))[:, None]
    cor_tile = jnp.broadcast_to(coriolis, (rows, cols))
    band = 8
    block = 128
    frame_rows = rows + 2 * band
    frame_cols = cols + 2 * block
    row_at = lax.broadcasted_iota(jnp.int32, (frame_rows, frame_cols), 0)
    col_at = lax.broadcasted_iota(jnp.int32, (frame_rows, frame_cols), 1)
    global_row = tile_row * rows + jnp.where(row_at < rows + band, row_at, row_at - frame_rows)
    wide_inside = ((global_row >= 0) & (global_row < total_rows)).astype(jnp.float32)
    own_mask = ((row_at < rows) & (col_at < cols)).astype(jnp.float32)
    for count in range(STEPS):
        fields = (temp, salt, uvel, vvel)
        rims = exchange_fields(fields, south_keep, north_keep)
        temp_next, salt_next, ustar, vstar, trans_u, trans_v = volume_step(
            temp, salt, uvel, vvel, ocean, cor_tile, rims
        )
        solved = surface_kernel_solve(trans_u, trans_v, eta, wide_inside, own_mask)
        eta = solved[0]
        east_west = solved[1]
        north_south = solved[2]
        uvel = ocean * (ustar - GRAV_K * 0.5 * east_west[:, None])
        vvel = ocean * (vstar - GRAV_K * 0.5 * north_south[:, None])
        if count == STEPS - 1:
            tracers_other = lax.ppermute(jnp.stack((temp_next, salt_next)), "member", [(0, 1), (1, 0)])
        temp = temp_next
        salt = salt_next
    zonal_scale = 1.0 / jnp.sqrt(jnp.float32(total_cols))
    score_scale = 1.0 / jnp.sqrt(jnp.float32(levels * total_rows))
    lat_weight = latitude / total_rows
    members = temp.shape[0]
    zonal_local = jnp.sum(vvel, axis=3)
    depth_weight = (levels - jnp.arange(levels, dtype=jnp.int32)).astype(jnp.float32)
    score_local = jnp.sum(zonal_local * depth_weight[None, :, None] * lat_weight[None, None, :], axis=(1, 2))
    slot = lax.broadcasted_iota(jnp.int32, (tile_count, 1, 1, 1), 0) == tile_row
    zonal_slots = jnp.where(slot, zonal_local[None], 0.0).reshape(-1, 128)
    score_row = jnp.zeros((8, 128), jnp.float32).at[0, :members].set(score_local)
    summed = grid_sum(jnp.concatenate([zonal_slots, score_row], axis=0))
    zonal_whole = summed[: zonal_slots.shape[0]].reshape((tile_count,) + zonal_local.shape)
    zonal_whole = jnp.sum(jnp.where(slot, zonal_whole, 0.0), axis=0)
    overturn = jnp.cumsum(zonal_whole, axis=1) * zonal_scale
    score = summed[zonal_slots.shape[0], :members] * (zonal_scale * score_scale)
    swap = [(0, 1), (1, 0)]
    mine = lax.axis_index("member")
    score_slab = jnp.zeros((members, 1) + eta.shape[1:], jnp.float32).at[:, 0, 0, 0].set(score)
    flows = jnp.concatenate([uvel, vvel, eta[:, None], score_slab], axis=1)
    flows_other = lax.ppermute(flows, "member", swap)
    score_other = flows_other[:, 2 * levels + 1, 0, 0]
    every_score = jnp.where(
        mine == 0, jnp.concatenate([score, score_other]), jnp.concatenate([score_other, score])
    )
    here = (clone_source // members) == mine
    local_at = clone_source % members

    def pick(local, other):
        chosen = []
        for place in range(members):
            from_here = lax.dynamic_index_in_dim(local, local_at[place], 0, keepdims=False)
            from_other = lax.dynamic_index_in_dim(other, local_at[place], 0, keepdims=False)
            chosen.append(jnp.where(here[place], from_here, from_other))
        return jnp.stack(chosen)

    new_temp = pick(temp, tracers_other[0])
    new_salt = pick(salt, tracers_other[1])
    new_flows = pick(flows[:, : 2 * levels + 1], flows_other[:, : 2 * levels + 1])
    clone_weight = jnp.take(every_score, clone_source, axis=0) - jnp.mean(every_score)
    return (
        new_temp,
        new_salt,
        new_flows[:, :levels],
        new_flows[:, levels : 2 * levels],
        new_flows[:, 2 * levels],
        overturn,
        clone_weight,
    )


def solution(mesh):
    in_specs = (
        P("member", None, "gridy", "gridx"),
        P("member", None, "gridy", "gridx"),
        P("member", None, "gridy", "gridx"),
        P("member", None, "gridy", "gridx"),
        P("member", "gridy", "gridx"),
        P("gridy", "gridx"),
        P("member"),
    )
    out_specs = (
        P("member", None, "gridy", "gridx"),
        P("member", None, "gridy", "gridx"),
        P("member", None, "gridy", "gridx"),
        P("member", None, "gridy", "gridx"),
        P("member", "gridy", "gridx"),
        P("member", None, "gridy"),
        P("member"),
    )
    return jax.shard_map(shards, mesh=mesh, in_specs=in_specs, out_specs=out_specs, check_vma=False)
```

```python
import functools

import jax
import jax.numpy as jnp
from jax import lax
from jax.experimental import pallas as pl
from jax.experimental.pallas import tpu as pltpu
from jax.sharding import PartitionSpec as P

STEPS = 2
ITERS = 3


ALPHA_T = 0.8
BETA_S = 0.6
PRESS_K = 0.25
STEP_DT = 0.1
KAPPA = 0.1
VISCOSITY = 0.1
DRAG_K = 0.05
CORI_K = 1.0
SURF_C = 4.0
DIV_K = 0.5
GRAV_K = 0.5


def tree_sum(values, axes):
    for axis in axes:
        count = lax.axis_size(axis)
        step = 1
        while step < count:
            pairs = [(i, i ^ step) for i in range(count)]
            values = values + lax.ppermute(values, axis, pairs)
            step *= 2
    return values


def gather_sum_kernel(ny, nx, x_ref, o_ref, recv_y, recv_x, part, send_y, rsem_y, send_x, rsem_x):
    mesh_id = pl.DeviceIdType.MESH
    member = lax.axis_index("member")
    my = lax.axis_index("gridy")
    mx = lax.axis_index("gridx")
    barrier = pltpu.get_barrier_semaphore()
    for d in range(1, ny):
        pl.semaphore_signal(barrier, 1, device_id=(member, (my + d) % ny, mx), device_id_type=mesh_id)
    for d in range(1, nx):
        pl.semaphore_signal(barrier, 1, device_id=(member, my, (mx + d) % nx), device_id_type=mesh_id)
    pl.semaphore_wait(barrier, (ny - 1) + (nx - 1))

    def phase(src, recv, send_sem, recv_sem, count, me, device):
        recv[me] = src[...]
        sent = []
        for d in range(1, count):
            peer = (me + d) % count
            copy = pltpu.make_async_remote_copy(
                src_ref=src,
                dst_ref=recv.at[me],
                send_sem=send_sem.at[peer],
                recv_sem=recv_sem.at[me],
                device_id=device(peer),
                device_id_type=mesh_id,
            )
            copy.start()
            sent.append(copy)
        for d in range(1, count):
            peer = (me + d) % count
            pltpu.make_async_remote_copy(
                src_ref=src,
                dst_ref=recv.at[peer],
                send_sem=send_sem.at[peer],
                recv_sem=recv_sem.at[peer],
                device_id=device(peer),
                device_id_type=mesh_id,
            ).wait_recv()
        for copy in sent:
            copy.wait_send()
        total = recv[0]
        for j in range(1, count):
            total = total + recv[j]
        return total

    part[...] = phase(x_ref, recv_y, send_y, rsem_y, ny, my, lambda p: (member, p, mx))
    o_ref[...] = phase(part, recv_x, send_x, rsem_x, nx, mx, lambda p: (member, my, p))


def grid_sum(values):
    ny = lax.axis_size("gridy")
    nx = lax.axis_size("gridx")
    shape = values.shape
    return pl.pallas_call(
        functools.partial(gather_sum_kernel, ny, nx),
        out_shape=jax.ShapeDtypeStruct(shape, values.dtype),
        in_specs=[pl.BlockSpec(memory_space=pltpu.VMEM)],
        out_specs=pl.BlockSpec(memory_space=pltpu.VMEM),
        scratch_shapes=[
            pltpu.VMEM((ny,) + shape, values.dtype),
            pltpu.VMEM((nx,) + shape, values.dtype),
            pltpu.VMEM(shape, values.dtype),
            pltpu.SemaphoreType.DMA((ny,)),
            pltpu.SemaphoreType.DMA((ny,)),
            pltpu.SemaphoreType.DMA((nx,)),
            pltpu.SemaphoreType.DMA((nx,)),
        ],
        compiler_params=pltpu.CompilerParams(collective_id=0, has_side_effects=True),
    )(values)


def exchange_sum(k, vec, ny, nx, bufs, device_ids):
    send_y, recv_y, send_x, recv_x, sy, ry, sx, rx = bufs
    my, mx, along_y, along_x = device_ids
    mesh_id = pl.DeviceIdType.MESH

    def phase(value, send_buf, recv, send_sem, recv_sem, count, me, device):
        send_buf[k] = value
        recv[k, me] = value
        sent = []
        for d in range(1, count):
            peer = (me + d) % count
            copy = pltpu.make_async_remote_copy(
                src_ref=send_buf.at[k],
                dst_ref=recv.at[k, me],
                send_sem=send_sem.at[k, peer],
                recv_sem=recv_sem.at[k, me],
                device_id=device(peer),
                device_id_type=mesh_id,
            )
            copy.start()
            sent.append(copy)
        for d in range(1, count):
            peer = (me + d) % count
            pltpu.make_async_remote_copy(
                src_ref=send_buf.at[k],
                dst_ref=recv.at[k, peer],
                send_sem=send_sem.at[k, peer],
                recv_sem=recv_sem.at[k, peer],
                device_id=device(peer),
                device_id_type=mesh_id,
            ).wait_recv()
        for copy in sent:
            copy.wait_send()
        total = recv[k, 0]
        for j in range(1, count):
            total = total + recv[k, j]
        return total

    partial = phase(vec, send_y, recv_y, sy, ry, ny, my, along_y)
    return phase(partial, send_x, recv_x, sx, rx, nx, mx, along_x)


def solve_kernel(ny, nx, tu_ref, tv_ref, eta_ref, inside_ref, own_ref, out_ref, frame, hsend, hrecv, *bufs):
    mesh_id = pl.DeviceIdType.MESH
    member = lax.axis_index("member")
    my = lax.axis_index("gridy")
    mx = lax.axis_index("gridx")
    along_y = lambda p: (member, p, mx)
    along_x = lambda p: (member, my, p)
    barrier = pltpu.get_barrier_semaphore()
    for d in range(1, ny):
        pl.semaphore_signal(barrier, 1, device_id=along_y((my + d) % ny), device_id_type=mesh_id)
    for d in range(1, nx):
        pl.semaphore_signal(barrier, 1, device_id=along_x((mx + d) % nx), device_id_type=mesh_id)
    for dy in (1, ny - 1):
        for dx in (1, nx - 1):
            pl.semaphore_signal(
                barrier, 1, device_id=(member, (my + dy) % ny, (mx + dx) % nx), device_id_type=mesh_id
            )
    rows, cols = eta_ref.shape[1], eta_ref.shape[2]
    wide_rows, wide_cols = frame.shape[2], frame.shape[3]
    band = (wide_rows - rows) // 2
    block = (wide_cols - cols) // 2
    frame[0, :, 0:rows, 0:cols] = tu_ref[...]
    frame[1, :, 0:rows, 0:cols] = tv_ref[...]
    frame[2, :, 0:rows, 0:cols] = eta_ref[...]
    pl.semaphore_wait(barrier, (ny - 1) + (nx - 1) + 4)

    def halo_copies(first, moves):
        started = []
        for slot, (src, dst, device) in enumerate(moves, start=first):
            copy = pltpu.make_async_remote_copy(
                src_ref=src, dst_ref=dst, send_sem=hsend.at[slot], recv_sem=hrecv.at[slot],
                device_id=device, device_id_type=mesh_id,
            )
            copy.start()
            started.append(copy)
        for copy in started:
            copy.wait()

    up, down = (my + 1) % ny, (my + ny - 1) % ny
    right, left = (mx + 1) % nx, (mx + nx - 1) % nx
    top_rows = slice(0, band)
    low_rows = slice(rows - band, rows)
    own_rows = slice(0, rows)
    west_part = slice(0, block)
    east_part = slice(cols - block, cols)
    own_cols = slice(0, cols)
    north_halo = slice(rows, rows + band)
    south_halo = slice(rows + band, wide_rows)
    east_halo = slice(cols, cols + block)
    west_halo = slice(cols + block, wide_cols)
    halo_copies(0, [
        (frame.at[:, :, top_rows, own_cols], frame.at[:, :, north_halo, own_cols], (member, down, mx)),
        (frame.at[:, :, low_rows, own_cols], frame.at[:, :, south_halo, own_cols], (member, up, mx)),
        (frame.at[:, :, own_rows, west_part], frame.at[:, :, own_rows, east_halo], (member, my, left)),
        (frame.at[:, :, own_rows, east_part], frame.at[:, :, own_rows, west_halo], (member, my, right)),
        (frame.at[:, :, top_rows, west_part], frame.at[:, :, north_halo, east_halo], (member, down, left)),
        (frame.at[:, :, top_rows, east_part], frame.at[:, :, north_halo, west_halo], (member, down, right)),
        (frame.at[:, :, low_rows, west_part], frame.at[:, :, south_halo, east_halo], (member, up, left)),
        (frame.at[:, :, low_rows, east_part], frame.at[:, :, south_halo, west_halo], (member, up, right)),
    ])

    members = eta_ref.shape[0]
    inside = inside_ref[...]
    own = own_ref[...] > 0.5

    def east(f):
        return pltpu.roll(f, wide_cols - 1, 1)

    def west(f):
        return pltpu.roll(f, 1, 1)

    def north(f):
        return pltpu.roll(f, wide_rows - 1, 0)

    def south(f):
        return pltpu.roll(f, 1, 0)

    def apply(f):
        return ((1.0 + 4.0 * SURF_C) * f - SURF_C * (east(f) + west(f) + north(f) + south(f))) * inside

    def total(f):
        return jnp.sum(f[0:rows, 0:cols], axis=(0, 1), keepdims=True)

    residual = []
    for m in range(members):
        trans_u = frame[0, m] * inside
        trans_v = frame[1, m] * inside
        level = frame[2, m] * inside
        residual.append(
            (level - DIV_K * 0.5 * (east(trans_u) - west(trans_u) + (north(trans_v) - south(trans_v)))) * inside
        )
    lane = lax.broadcasted_iota(jnp.int32, (8, 128), 1)
    direction = [None] * members
    image_dir = [None] * members
    solution = [None] * members
    gamma_prev = [None] * members
    alpha_prev = [None] * members
    for count in range(ITERS):
        image_res = [apply(residual[m]) for m in range(members)]
        vec = jnp.zeros((8, 128), jnp.float32)
        for m in range(members):
            vec = jnp.where(lane == 2 * m, total(residual[m] * residual[m]), vec)
            vec = jnp.where(lane == 2 * m + 1, total(residual[m] * image_res[m]), vec)
        sums = exchange_sum(count, vec, ny, nx, bufs, (my, mx, along_y, along_x))
        for m in range(members):
            gamma = sums[0:1, 2 * m : 2 * m + 1]
            delta = sums[0:1, 2 * m + 1 : 2 * m + 2]
            if count == 0:
                alpha = gamma / delta
                direction[m] = residual[m]
                image_dir[m] = image_res[m]
                solution[m] = alpha * direction[m]
            else:
                beta = gamma / gamma_prev[m]
                alpha = gamma / (delta - beta * gamma / alpha_prev[m])
                direction[m] = residual[m] + beta * direction[m]
                image_dir[m] = image_res[m] + beta * image_dir[m]
                solution[m] = solution[m] + alpha * direction[m]
            if count < ITERS - 1:
                residual[m] = residual[m] - alpha * image_dir[m]
            gamma_prev[m] = gamma
            alpha_prev[m] = alpha
    for m in range(members):
        x = solution[m]
        out_ref[0, m] = x[0:rows, 0:cols]
        out_ref[1, m] = (east(x) - west(x))[0:rows, 0:cols]
        out_ref[2, m] = (north(x) - south(x))[0:rows, 0:cols]


def surface_kernel_solve(trans_u, trans_v, eta, inside, own):
    ny = lax.axis_size("gridy")
    nx = lax.axis_size("gridx")
    members, rows, cols = eta.shape
    fields = 3
    return pl.pallas_call(
        functools.partial(solve_kernel, ny, nx),
        out_shape=jax.ShapeDtypeStruct((3, members, rows, cols), jnp.float32),
        in_specs=[pl.BlockSpec(memory_space=pltpu.VMEM)] * 5,
        out_specs=pl.BlockSpec(memory_space=pltpu.VMEM),
        scratch_shapes=[
            pltpu.VMEM((fields, members) + inside.shape, jnp.float32),
            pltpu.SemaphoreType.DMA((8,)),
            pltpu.SemaphoreType.DMA((8,)),
            pltpu.VMEM((ITERS, 8, 128), jnp.float32),
            pltpu.VMEM((ITERS, ny, 8, 128), jnp.float32),
            pltpu.VMEM((ITERS, 8, 128), jnp.float32),
            pltpu.VMEM((ITERS, nx, 8, 128), jnp.float32),
            pltpu.SemaphoreType.DMA((ITERS, ny)),
            pltpu.SemaphoreType.DMA((ITERS, ny)),
            pltpu.SemaphoreType.DMA((ITERS, nx)),
            pltpu.SemaphoreType.DMA((ITERS, nx)),
        ],
        compiler_params=pltpu.CompilerParams(collective_id=1, has_side_effects=True),
    )(trans_u, trans_v, eta, inside, own)


def volume_kernel(ny, temp_ref, salt_ref, uvel_ref, vvel_ref, land_ref, n_ref, s_ref, e_ref, w_ref,
                  tn_ref, sn_ref, us_ref, vs_ref, tu_ref, tv_ref):
    levels, rows, cols = temp_ref.shape[1], temp_ref.shape[2], temp_ref.shape[3]
    row = lax.broadcasted_iota(jnp.int32, (rows, cols), 0)
    col = lax.broadcasted_iota(jnp.int32, (rows, cols), 1)
    tile_row = lax.axis_index("gridy")
    north_keep = jnp.where(tile_row < ny - 1, 1.0, 0.0)
    south_keep = jnp.where(tile_row > 0, 1.0, 0.0)
    latitude = (tile_row * rows + row).astype(jnp.float32) + 0.5
    top = row == rows - 1
    bottom = row == 0
    right = col == cols - 1
    left = col == 0
    ocean = land_ref[...].astype(jnp.float32)
    cor = CORI_K * (2.0 * latitude / (rows * ny) - 1.0)

    def around(f, rims):
        n, s, e, w = rims
        return (
            jnp.where(right, e, pltpu.roll(f, cols - 1, 1)),
            jnp.where(left, w, pltpu.roll(f, 1, 1)),
            jnp.where(top, n, pltpu.roll(f, rows - 1, 0)),
            jnp.where(bottom, s, pltpu.roll(f, 1, 0)),
        )

    def rims_of(k, l):
        return (n_ref[k, 0, l] * north_keep, s_ref[k, 0, l] * south_keep, e_ref[k, 0, l], w_ref[k, 0, l])

    running = None
    running_rims = None
    tu = None
    tv = None
    for l in range(levels):
        t = temp_ref[0, l]
        s = salt_ref[0, l]
        u = uvel_ref[0, l]
        v = vvel_ref[0, l]
        rt, rs, ru, rv = rims_of(0, l), rims_of(1, l), rims_of(2, l), rims_of(3, l)
        layer = BETA_S * s - ALPHA_T * t
        layer_rims = tuple(BETA_S * b - ALPHA_T * a for a, b in zip(rt, rs))
        if running is None:
            running, running_rims = layer, layer_rims
        else:
            running = running + layer
            running_rims = tuple(a + b for a, b in zip(running_rims, layer_rims))
        press = PRESS_K * running
        press_rims = tuple(PRESS_K * a for a in running_rims)
        te, tw, tn, ts = around(t, rt)
        se, sw, sn, ss = around(s, rs)
        ue, uw, un, us = around(u, ru)
        ve, vw, vn, vs = around(v, rv)
        pe, pw, pn, ps = around(press, press_rims)
        tn_ref[0, l] = ocean * (
            t - STEP_DT * 0.5 * (u * (te - tw) + v * (tn - ts)) + KAPPA * (te + tw + tn + ts - 4.0 * t)
        )
        sn_ref[0, l] = ocean * (
            s - STEP_DT * 0.5 * (u * (se - sw) + v * (sn - ss)) + KAPPA * (se + sw + sn + ss - 4.0 * s)
        )
        ustar = ocean * (
            u + STEP_DT * (cor * v - 0.5 * (pe - pw) - DRAG_K * u) + VISCOSITY * (ue + uw + un + us - 4.0 * u)
        )
        vstar = ocean * (
            v + STEP_DT * (-cor * u - 0.5 * (pn - ps) - DRAG_K * v) + VISCOSITY * (ve + vw + vn + vs - 4.0 * v)
        )
        us_ref[0, l] = ustar
        vs_ref[0, l] = vstar
        tu = ustar if tu is None else tu + ustar
        tv = vstar if tv is None else tv + vstar
    tu_ref[0] = tu
    tv_ref[0] = tv


def volume_step(temp, salt, uvel, vvel, land_mask, rims):
    members, levels, rows, cols = temp.shape
    field = pl.BlockSpec((1, levels, rows, cols), lambda m: (m, 0, 0, 0))
    plane = pl.BlockSpec((rows, cols), lambda m: (0, 0))
    north, south, east, west = rims
    row_rim = pl.BlockSpec((4, 1, levels, 1, cols), lambda m: (0, m, 0, 0, 0))
    col_rim = pl.BlockSpec((4, 1, levels, rows, 1), lambda m: (0, m, 0, 0, 0))
    surface = pl.BlockSpec((1, rows, cols), lambda m: (m, 0, 0))
    volume_shape = jax.ShapeDtypeStruct(temp.shape, jnp.float32)
    surface_shape = jax.ShapeDtypeStruct((members, rows, cols), jnp.float32)
    return pl.pallas_call(
        functools.partial(volume_kernel, lax.axis_size("gridy")),
        grid=(members,),
        in_specs=[field] * 4 + [plane, row_rim, row_rim, col_rim, col_rim],
        out_specs=[field] * 4 + [surface] * 2,
        out_shape=[volume_shape] * 4 + [surface_shape] * 2,
    )(temp, salt, uvel, vvel, land_mask, north, south, east, west)


def ring(axis):
    count = lax.axis_size(axis)
    forward = [(i, (i + 1) % count) for i in range(count)]
    backward = [((i + 1) % count, i) for i in range(count)]
    return forward, backward


def exchange(block, ydim, xdim, south_keep, north_keep):
    fwd_y, bwd_y = ring("gridy")
    fwd_x, bwd_x = ring("gridx")
    rows = block.shape[ydim]
    cols = block.shape[xdim]
    north = lax.ppermute(lax.slice_in_dim(block, 0, 1, axis=ydim), "gridy", bwd_y) * north_keep
    south = lax.ppermute(lax.slice_in_dim(block, rows - 1, rows, axis=ydim), "gridy", fwd_y) * south_keep
    east = lax.ppermute(lax.slice_in_dim(block, 0, 1, axis=xdim), "gridx", bwd_x)
    west = lax.ppermute(lax.slice_in_dim(block, cols - 1, cols, axis=xdim), "gridx", fwd_x)
    return (east, west, north, south)


def exchange_fields(fields, south_keep, north_keep):
    fwd_y, bwd_y = ring("gridy")
    fwd_x, bwd_x = ring("gridx")
    north = lax.ppermute(jnp.stack([f[..., :1, :] for f in fields]), "gridy", bwd_y)
    south = lax.ppermute(jnp.stack([f[..., -1:, :] for f in fields]), "gridy", fwd_y)
    east = lax.ppermute(jnp.stack([f[..., :, :1] for f in fields]), "gridx", bwd_x)
    west = lax.ppermute(jnp.stack([f[..., :, -1:] for f in fields]), "gridx", fwd_x)
    return (north, south, east, west)


def sides(field, rims, ydim, xdim):
    east, west, north, south = rims
    rows = field.shape[ydim]
    cols = field.shape[xdim]
    east_side = jnp.concatenate([lax.slice_in_dim(field, 1, cols, axis=xdim), east], axis=xdim)
    west_side = jnp.concatenate([west, lax.slice_in_dim(field, 0, cols - 1, axis=xdim)], axis=xdim)
    north_side = jnp.concatenate([lax.slice_in_dim(field, 1, rows, axis=ydim), north], axis=ydim)
    south_side = jnp.concatenate([south, lax.slice_in_dim(field, 0, rows - 1, axis=ydim)], axis=ydim)
    return (east_side, west_side, north_side, south_side)


def pressure(temp, salt):
    return PRESS_K * jnp.cumsum(BETA_S * salt - ALPHA_T * temp, axis=-3)


def surface_apply(field, rims):
    east_side, west_side, north_side, south_side = sides(field, rims, 1, 2)
    return (1.0 + 4.0 * SURF_C) * field - SURF_C * (east_side + west_side + north_side + south_side)


def member_total(values):
    return jnp.sum(values, axis=(1, 2))


def widen(values):
    return values[:, None, None]


def combine(a, fa, b, fb):
    def one(u, v):
        left = u if a is None else widen(a) * u
        return left + (v if b is None else widen(b) * v)

    return one(fa[0], fb[0]), tuple(one(u, v) for u, v in zip(fa[1], fb[1]))


def scaled(a, fa):
    return widen(a) * fa[0], tuple(widen(a) * u for u in fa[1])


def padded_2(block, sides_of, width):
    for axis, dim in sides_of:
        count = lax.axis_size(axis)
        forward = [(i, (i + 1) % count) for i in range(count)]
        backward = [((i + 1) % count, i) for i in range(count)]
        size = block.shape[dim]
        low = lax.ppermute(lax.slice_in_dim(block, size - width, size, axis=dim), axis, forward)
        high = lax.ppermute(lax.slice_in_dim(block, 0, width, axis=dim), axis, backward)
        block = jnp.concatenate([low, block, high], axis=dim)
    return block


def crop(field, by):
    if by == 0:
        return field
    return field[..., by:-by, by:-by]


def around(field):
    return (
        field[..., 1:-1, 1:-1],
        field[..., 1:-1, 2:],
        field[..., 1:-1, :-2],
        field[..., 2:, 1:-1],
        field[..., :-2, 1:-1],
    )


def rows_at(inside, full, want):
    cut = full - want
    return inside if cut == 0 else inside[cut:-cut]


def apply_wide(field, inside):
    centre, east, west, north, south = around(field)
    return ((1.0 + 4.0 * SURF_C) * centre - SURF_C * (east + west + north + south)) * inside


def surface_solve(rhs, inside, width, full):
    residual, wide_r = rhs, width
    gamma_prev = None
    alpha_prev = None
    for count in range(ITERS):
        image_res = apply_wide(residual, rows_at(inside, full, wide_r - 1))
        own_res = crop(residual, wide_r)
        own_img = crop(image_res, wide_r - 1)
        dots = grid_sum(jnp.stack([member_total(own_res * own_res), member_total(own_res * own_img)]))
        gamma, delta = dots[0], dots[1]
        if count == 0:
            alpha = gamma / delta
            direction, wide_p = residual, wide_r
            image_dir, wide_s = image_res, wide_r - 1
            solution, wide_x = widen(alpha) * direction, wide_r
        else:
            beta = gamma / gamma_prev
            alpha = gamma / (delta - beta * gamma / alpha_prev)
            direction = residual + widen(beta) * crop(direction, wide_p - wide_r)
            wide_p = wide_r
            image_dir = image_res + widen(beta) * crop(image_dir, wide_s - (wide_r - 1))
            wide_s = wide_r - 1
            solution = crop(solution, wide_x - wide_r) + widen(alpha) * direction
            wide_x = wide_r
        if count < ITERS - 1:
            residual = crop(residual, 1) - widen(alpha) * image_dir
            wide_r -= 1
        gamma_prev = gamma
        alpha_prev = alpha
    return solution


def shards(temp, salt, uvel, vvel, eta, land_mask, clone_source):
    levels = temp.shape[1]
    rows = temp.shape[2]
    cols = temp.shape[3]
    ocean = land_mask.astype(jnp.float32)
    tile_row = lax.axis_index("gridy")
    tile_count = lax.axis_size("gridy")
    total_rows = rows * tile_count
    total_cols = cols * lax.axis_size("gridx")
    south_keep = (tile_row > 0).astype(jnp.float32)
    north_keep = (tile_row < tile_count - 1).astype(jnp.float32)
    latitude = (tile_row * rows + jnp.arange(rows, dtype=jnp.int32)).astype(jnp.float32) + 0.5
    coriolis = (CORI_K * (2.0 * latitude / total_rows - 1.0))[:, None]
    cor_tile = jnp.broadcast_to(coriolis, (rows, cols))
    band = 8
    block = 128
    frame_rows = rows + 2 * band
    frame_cols = cols + 2 * block
    row_at = lax.broadcasted_iota(jnp.int32, (frame_rows, frame_cols), 0)
    col_at = lax.broadcasted_iota(jnp.int32, (frame_rows, frame_cols), 1)
    global_row = tile_row * rows + jnp.where(row_at < rows + band, row_at, row_at - frame_rows)
    wide_inside = ((global_row >= 0) & (global_row < total_rows)).astype(jnp.float32)
    own_mask = ((row_at < rows) & (col_at < cols)).astype(jnp.float32)
    for count in range(STEPS):
        fields = (temp, salt, uvel, vvel)
        rims = exchange_fields(fields, south_keep, north_keep)
        temp_next, salt_next, ustar, vstar, trans_u, trans_v = volume_step(
            temp, salt, uvel, vvel, land_mask, rims
        )
        solved = surface_kernel_solve(trans_u, trans_v, eta, wide_inside, own_mask)
        eta = solved[0]
        east_west = solved[1]
        north_south = solved[2]
        uvel = ocean * (ustar - GRAV_K * 0.5 * east_west[:, None])
        vvel = ocean * (vstar - GRAV_K * 0.5 * north_south[:, None])
        if count == STEPS - 1:
            tracers_other = lax.ppermute(jnp.stack((temp_next, salt_next)), "member", [(0, 1), (1, 0)])
        temp = temp_next
        salt = salt_next
    zonal_scale = 1.0 / jnp.sqrt(jnp.float32(total_cols))
    score_scale = 1.0 / jnp.sqrt(jnp.float32(levels * total_rows))
    lat_weight = latitude / total_rows
    members = temp.shape[0]
    zonal_local = jnp.sum(vvel, axis=3)
    depth_weight = (levels - jnp.arange(levels, dtype=jnp.int32)).astype(jnp.float32)
    score_local = jnp.sum(zonal_local * depth_weight[None, :, None] * lat_weight[None, None, :], axis=(1, 2))
    slot = lax.broadcasted_iota(jnp.int32, (tile_count, 1, 1, 1), 0) == tile_row
    zonal_slots = jnp.where(slot, zonal_local[None], 0.0).reshape(-1, 128)
    score_row = jnp.zeros((8, 128), jnp.float32).at[0, :members].set(score_local)
    summed = grid_sum(jnp.concatenate([zonal_slots, score_row], axis=0))
    zonal_whole = summed[: zonal_slots.shape[0]].reshape((tile_count,) + zonal_local.shape)
    zonal_whole = jnp.sum(jnp.where(slot, zonal_whole, 0.0), axis=0)
    overturn = jnp.cumsum(zonal_whole, axis=1) * zonal_scale
    score = summed[zonal_slots.shape[0], :members] * (zonal_scale * score_scale)
    swap = [(0, 1), (1, 0)]
    mine = lax.axis_index("member")
    score_slab = jnp.zeros((members, 1) + eta.shape[1:], jnp.float32).at[:, 0, 0, 0].set(score)
    flows = jnp.concatenate([uvel, vvel, eta[:, None], score_slab], axis=1)
    flows_other = lax.ppermute(flows, "member", swap)
    score_other = flows_other[:, 2 * levels + 1, 0, 0]
    every_score = jnp.where(
        mine == 0, jnp.concatenate([score, score_other]), jnp.concatenate([score_other, score])
    )
    here = (clone_source // members) == mine
    local_at = clone_source % members

    def pick(local, other):
        chosen = []
        for place in range(members):
            from_here = lax.dynamic_index_in_dim(local, local_at[place], 0, keepdims=False)
            from_other = lax.dynamic_index_in_dim(other, local_at[place], 0, keepdims=False)
            chosen.append(jnp.where(here[place], from_here, from_other))
        return jnp.stack(chosen)

    new_temp = pick(temp, tracers_other[0])
    new_salt = pick(salt, tracers_other[1])
    new_flows = pick(flows[:, : 2 * levels + 1], flows_other[:, : 2 * levels + 1])
    clone_weight = jnp.take(every_score, clone_source, axis=0) - jnp.mean(every_score)
    return (
        new_temp,
        new_salt,
        new_flows[:, :levels],
        new_flows[:, levels : 2 * levels],
        new_flows[:, 2 * levels],
        overturn,
        clone_weight,
    )


def solution(mesh):
    in_specs = (
        P("member", None, "gridy", "gridx"),
        P("member", None, "gridy", "gridx"),
        P("member", None, "gridy", "gridx"),
        P("member", None, "gridy", "gridx"),
        P("member", "gridy", "gridx"),
        P("gridy", "gridx"),
        P("member"),
    )
    out_specs = (
        P("member", None, "gridy", "gridx"),
        P("member", None, "gridy", "gridx"),
        P("member", None, "gridy", "gridx"),
        P("member", None, "gridy", "gridx"),
        P("member", "gridy", "gridx"),
        P("member", None, "gridy"),
        P("member"),
    )
    return jax.shard_map(shards, mesh=mesh, in_specs=in_specs, out_specs=out_specs, check_vma=False)
```

```python
import functools

import jax
import jax.numpy as jnp
from jax import lax
from jax.experimental import pallas as pl
from jax.experimental.pallas import tpu as pltpu
from jax.sharding import PartitionSpec as P

STEPS = 2
ITERS = 3


ALPHA_T = 0.8
BETA_S = 0.6
PRESS_K = 0.25
STEP_DT = 0.1
KAPPA = 0.1
VISCOSITY = 0.1
DRAG_K = 0.05
CORI_K = 1.0
SURF_C = 4.0
DIV_K = 0.5
GRAV_K = 0.5


def tree_sum(values, axes):
    for axis in axes:
        count = lax.axis_size(axis)
        step = 1
        while step < count:
            pairs = [(i, i ^ step) for i in range(count)]
            values = values + lax.ppermute(values, axis, pairs)
            step *= 2
    return values


def gather_sum_kernel(ny, nx, x_ref, o_ref, recv_y, recv_x, part, send_y, rsem_y, send_x, rsem_x):
    mesh_id = pl.DeviceIdType.MESH
    member = lax.axis_index("member")
    my = lax.axis_index("gridy")
    mx = lax.axis_index("gridx")
    barrier = pltpu.get_barrier_semaphore()
    for d in range(1, ny):
        pl.semaphore_signal(barrier, 1, device_id=(member, (my + d) % ny, mx), device_id_type=mesh_id)
    for d in range(1, nx):
        pl.semaphore_signal(barrier, 1, device_id=(member, my, (mx + d) % nx), device_id_type=mesh_id)
    pl.semaphore_wait(barrier, (ny - 1) + (nx - 1))

    def phase(src, recv, send_sem, recv_sem, count, me, device):
        recv[me] = src[...]
        sent = []
        for d in range(1, count):
            peer = (me + d) % count
            copy = pltpu.make_async_remote_copy(
                src_ref=src,
                dst_ref=recv.at[me],
                send_sem=send_sem.at[peer],
                recv_sem=recv_sem.at[me],
                device_id=device(peer),
                device_id_type=mesh_id,
            )
            copy.start()
            sent.append(copy)
        for d in range(1, count):
            peer = (me + d) % count
            pltpu.make_async_remote_copy(
                src_ref=src,
                dst_ref=recv.at[peer],
                send_sem=send_sem.at[peer],
                recv_sem=recv_sem.at[peer],
                device_id=device(peer),
                device_id_type=mesh_id,
            ).wait_recv()
        for copy in sent:
            copy.wait_send()
        total = recv[0]
        for j in range(1, count):
            total = total + recv[j]
        return total

    part[...] = phase(x_ref, recv_y, send_y, rsem_y, ny, my, lambda p: (member, p, mx))
    o_ref[...] = phase(part, recv_x, send_x, rsem_x, nx, mx, lambda p: (member, my, p))


def grid_sum(values):
    ny = lax.axis_size("gridy")
    nx = lax.axis_size("gridx")
    shape = values.shape
    return pl.pallas_call(
        functools.partial(gather_sum_kernel, ny, nx),
        out_shape=jax.ShapeDtypeStruct(shape, values.dtype),
        in_specs=[pl.BlockSpec(memory_space=pltpu.VMEM)],
        out_specs=pl.BlockSpec(memory_space=pltpu.VMEM),
        scratch_shapes=[
            pltpu.VMEM((ny,) + shape, values.dtype),
            pltpu.VMEM((nx,) + shape, values.dtype),
            pltpu.VMEM(shape, values.dtype),
            pltpu.SemaphoreType.DMA((ny,)),
            pltpu.SemaphoreType.DMA((ny,)),
            pltpu.SemaphoreType.DMA((nx,)),
            pltpu.SemaphoreType.DMA((nx,)),
        ],
        compiler_params=pltpu.CompilerParams(collective_id=0, has_side_effects=True),
    )(values)


def exchange_sum(k, vec, ny, nx, bufs, device_ids):
    send_y, recv_y, send_x, recv_x, sy, ry, sx, rx = bufs
    my, mx, along_y, along_x = device_ids
    mesh_id = pl.DeviceIdType.MESH

    def phase(value, send_buf, recv, send_sem, recv_sem, count, me, device):
        send_buf[k] = value
        recv[k, me] = value
        sent = []
        for d in range(1, count):
            peer = (me + d) % count
            copy = pltpu.make_async_remote_copy(
                src_ref=send_buf.at[k],
                dst_ref=recv.at[k, me],
                send_sem=send_sem.at[k, peer],
                recv_sem=recv_sem.at[k, me],
                device_id=device(peer),
                device_id_type=mesh_id,
            )
            copy.start()
            sent.append(copy)
        for d in range(1, count):
            peer = (me + d) % count
            pltpu.make_async_remote_copy(
                src_ref=send_buf.at[k],
                dst_ref=recv.at[k, peer],
                send_sem=send_sem.at[k, peer],
                recv_sem=recv_sem.at[k, peer],
                device_id=device(peer),
                device_id_type=mesh_id,
            ).wait_recv()
        for copy in sent:
            copy.wait_send()
        total = recv[k, 0]
        for j in range(1, count):
            total = total + recv[k, j]
        return total

    partial = phase(vec, send_y, recv_y, sy, ry, ny, my, along_y)
    return phase(partial, send_x, recv_x, sx, rx, nx, mx, along_x)


def solve_kernel(ny, nx, tu_ref, tv_ref, eta_ref, inside_ref, own_ref, out_ref, frame, hsend, hrecv, *bufs):
    mesh_id = pl.DeviceIdType.MESH
    member = lax.axis_index("member")
    my = lax.axis_index("gridy")
    mx = lax.axis_index("gridx")
    along_y = lambda p: (member, p, mx)
    along_x = lambda p: (member, my, p)
    barrier = pltpu.get_barrier_semaphore()
    for d in range(1, ny):
        pl.semaphore_signal(barrier, 1, device_id=along_y((my + d) % ny), device_id_type=mesh_id)
    for d in range(1, nx):
        pl.semaphore_signal(barrier, 1, device_id=along_x((mx + d) % nx), device_id_type=mesh_id)
    for dy in (1, ny - 1):
        for dx in (1, nx - 1):
            pl.semaphore_signal(
                barrier, 1, device_id=(member, (my + dy) % ny, (mx + dx) % nx), device_id_type=mesh_id
            )
    rows, cols = eta_ref.shape[1], eta_ref.shape[2]
    wide_rows, wide_cols = frame.shape[2], frame.shape[3]
    band = (wide_rows - rows) // 2
    block = (wide_cols - cols) // 2
    frame[0, :, 0:rows, 0:cols] = tu_ref[...]
    frame[1, :, 0:rows, 0:cols] = tv_ref[...]
    frame[2, :, 0:rows, 0:cols] = eta_ref[...]
    pl.semaphore_wait(barrier, (ny - 1) + (nx - 1) + 4)

    def halo_copies(first, moves):
        started = []
        for slot, (src, dst, device) in enumerate(moves, start=first):
            copy = pltpu.make_async_remote_copy(
                src_ref=src, dst_ref=dst, send_sem=hsend.at[slot], recv_sem=hrecv.at[slot],
                device_id=device, device_id_type=mesh_id,
            )
            copy.start()
            started.append(copy)
        for copy in started:
            copy.wait()

    up, down = (my + 1) % ny, (my + ny - 1) % ny
    right, left = (mx + 1) % nx, (mx + nx - 1) % nx
    top_rows = slice(0, band)
    low_rows = slice(rows - band, rows)
    own_rows = slice(0, rows)
    west_part = slice(0, block)
    east_part = slice(cols - block, cols)
    own_cols = slice(0, cols)
    north_halo = slice(rows, rows + band)
    south_halo = slice(rows + band, wide_rows)
    east_halo = slice(cols, cols + block)
    west_halo = slice(cols + block, wide_cols)
    halo_copies(0, [
        (frame.at[:, :, top_rows, own_cols], frame.at[:, :, north_halo, own_cols], (member, down, mx)),
        (frame.at[:, :, low_rows, own_cols], frame.at[:, :, south_halo, own_cols], (member, up, mx)),
        (frame.at[:, :, own_rows, west_part], frame.at[:, :, own_rows, east_halo], (member, my, left)),
        (frame.at[:, :, own_rows, east_part], frame.at[:, :, own_rows, west_halo], (member, my, right)),
        (frame.at[:, :, top_rows, west_part], frame.at[:, :, north_halo, east_halo], (member, down, left)),
        (frame.at[:, :, top_rows, east_part], frame.at[:, :, north_halo, west_halo], (member, down, right)),
        (frame.at[:, :, low_rows, west_part], frame.at[:, :, south_halo, east_halo], (member, up, left)),
        (frame.at[:, :, low_rows, east_part], frame.at[:, :, south_halo, west_halo], (member, up, right)),
    ])

    members = eta_ref.shape[0]
    inside = inside_ref[...]
    own = own_ref[...] > 0.5

    def east(f):
        return pltpu.roll(f, wide_cols - 1, 1)

    def west(f):
        return pltpu.roll(f, 1, 1)

    def north(f):
        return pltpu.roll(f, wide_rows - 1, 0)

    def south(f):
        return pltpu.roll(f, 1, 0)

    def apply(f):
        return ((1.0 + 4.0 * SURF_C) * f - SURF_C * (east(f) + west(f) + north(f) + south(f))) * inside

    def total(f):
        return jnp.sum(f[0:rows, 0:cols], axis=(0, 1), keepdims=True)

    residual = []
    for m in range(members):
        trans_u = frame[0, m] * inside
        trans_v = frame[1, m] * inside
        level = frame[2, m] * inside
        residual.append(
            (level - DIV_K * 0.5 * (east(trans_u) - west(trans_u) + (north(trans_v) - south(trans_v)))) * inside
        )
    lane = lax.broadcasted_iota(jnp.int32, (8, 128), 1)
    direction = [None] * members
    image_dir = [None] * members
    solution = [None] * members
    gamma_prev = [None] * members
    alpha_prev = [None] * members
    for count in range(ITERS):
        image_res = [apply(residual[m]) for m in range(members)]
        vec = jnp.zeros((8, 128), jnp.float32)
        for m in range(members):
            vec = jnp.where(lane == 2 * m, total(residual[m] * residual[m]), vec)
            vec = jnp.where(lane == 2 * m + 1, total(residual[m] * image_res[m]), vec)
        sums = exchange_sum(count, vec, ny, nx, bufs, (my, mx, along_y, along_x))
        for m in range(members):
            gamma = sums[0:1, 2 * m : 2 * m + 1]
            delta = sums[0:1, 2 * m + 1 : 2 * m + 2]
            if count == 0:
                alpha = gamma / delta
                direction[m] = residual[m]
                image_dir[m] = image_res[m]
                solution[m] = alpha * direction[m]
            else:
                beta = gamma / gamma_prev[m]
                alpha = gamma / (delta - beta * gamma / alpha_prev[m])
                direction[m] = residual[m] + beta * direction[m]
                image_dir[m] = image_res[m] + beta * image_dir[m]
                solution[m] = solution[m] + alpha * direction[m]
            if count < ITERS - 1:
                residual[m] = residual[m] - alpha * image_dir[m]
            gamma_prev[m] = gamma
            alpha_prev[m] = alpha
    for m in range(members):
        x = solution[m]
        out_ref[0, m] = x[0:rows, 0:cols]
        out_ref[1, m] = (east(x) - west(x))[0:rows, 0:cols]
        out_ref[2, m] = (north(x) - south(x))[0:rows, 0:cols]


def surface_kernel_solve(trans_u, trans_v, eta, inside, own):
    ny = lax.axis_size("gridy")
    nx = lax.axis_size("gridx")
    members, rows, cols = eta.shape
    fields = 3
    return pl.pallas_call(
        functools.partial(solve_kernel, ny, nx),
        out_shape=jax.ShapeDtypeStruct((3, members, rows, cols), jnp.float32),
        in_specs=[pl.BlockSpec(memory_space=pltpu.VMEM)] * 5,
        out_specs=pl.BlockSpec(memory_space=pltpu.VMEM),
        scratch_shapes=[
            pltpu.VMEM((fields, members) + inside.shape, jnp.float32),
            pltpu.SemaphoreType.DMA((8,)),
            pltpu.SemaphoreType.DMA((8,)),
            pltpu.VMEM((ITERS, 8, 128), jnp.float32),
            pltpu.VMEM((ITERS, ny, 8, 128), jnp.float32),
            pltpu.VMEM((ITERS, 8, 128), jnp.float32),
            pltpu.VMEM((ITERS, nx, 8, 128), jnp.float32),
            pltpu.SemaphoreType.DMA((ITERS, ny)),
            pltpu.SemaphoreType.DMA((ITERS, ny)),
            pltpu.SemaphoreType.DMA((ITERS, nx)),
            pltpu.SemaphoreType.DMA((ITERS, nx)),
        ],
        compiler_params=pltpu.CompilerParams(collective_id=1, has_side_effects=True),
    )(trans_u, trans_v, eta, inside, own)


def volume_kernel(ny, temp_ref, salt_ref, uvel_ref, vvel_ref, land_ref, n_ref, s_ref, e_ref, w_ref,
                  tn_ref, sn_ref, us_ref, vs_ref, tu_ref, tv_ref):
    levels, rows, cols = temp_ref.shape[1], temp_ref.shape[2], temp_ref.shape[3]
    row = lax.broadcasted_iota(jnp.int32, (rows, cols), 0)
    col = lax.broadcasted_iota(jnp.int32, (rows, cols), 1)
    tile_row = lax.axis_index("gridy")
    north_keep = jnp.where(tile_row < ny - 1, 1.0, 0.0)
    south_keep = jnp.where(tile_row > 0, 1.0, 0.0)
    latitude = (tile_row * rows + row).astype(jnp.float32) + 0.5
    top = row == rows - 1
    bottom = row == 0
    right = col == cols - 1
    left = col == 0
    ocean = land_ref[...].astype(jnp.float32)
    cor = CORI_K * (2.0 * latitude / (rows * ny) - 1.0)

    def around(f, rims):
        n, s, e, w = rims
        return (
            jnp.where(right, e, pltpu.roll(f, cols - 1, 1)),
            jnp.where(left, w, pltpu.roll(f, 1, 1)),
            jnp.where(top, n, pltpu.roll(f, rows - 1, 0)),
            jnp.where(bottom, s, pltpu.roll(f, 1, 0)),
        )

    def rims_of(k, l):
        return (n_ref[k, 0, l] * north_keep, s_ref[k, 0, l] * south_keep, e_ref[k, 0, l], w_ref[k, 0, l])

    running = None
    running_rims = None
    tu = None
    tv = None
    for l in range(levels):
        t = temp_ref[0, l]
        s = salt_ref[0, l]
        u = uvel_ref[0, l]
        v = vvel_ref[0, l]
        rt, rs, ru, rv = rims_of(0, l), rims_of(1, l), rims_of(2, l), rims_of(3, l)
        layer = BETA_S * s - ALPHA_T * t
        layer_rims = tuple(BETA_S * b - ALPHA_T * a for a, b in zip(rt, rs))
        if running is None:
            running, running_rims = layer, layer_rims
        else:
            running = running + layer
            running_rims = tuple(a + b for a, b in zip(running_rims, layer_rims))
        press = PRESS_K * running
        press_rims = tuple(PRESS_K * a for a in running_rims)
        te, tw, tn, ts = around(t, rt)
        se, sw, sn, ss = around(s, rs)
        ue, uw, un, us = around(u, ru)
        ve, vw, vn, vs = around(v, rv)
        pe, pw, pn, ps = around(press, press_rims)
        tn_ref[0, l] = ocean * (
            t - STEP_DT * 0.5 * (u * (te - tw) + v * (tn - ts)) + KAPPA * (te + tw + tn + ts - 4.0 * t)
        )
        sn_ref[0, l] = ocean * (
            s - STEP_DT * 0.5 * (u * (se - sw) + v * (sn - ss)) + KAPPA * (se + sw + sn + ss - 4.0 * s)
        )
        ustar = ocean * (
            u + STEP_DT * (cor * v - 0.5 * (pe - pw) - DRAG_K * u) + VISCOSITY * (ue + uw + un + us - 4.0 * u)
        )
        vstar = ocean * (
            v + STEP_DT * (-cor * u - 0.5 * (pn - ps) - DRAG_K * v) + VISCOSITY * (ve + vw + vn + vs - 4.0 * v)
        )
        us_ref[0, l] = ustar
        vs_ref[0, l] = vstar
        tu = ustar if tu is None else tu + ustar
        tv = vstar if tv is None else tv + vstar
    tu_ref[0] = tu
    tv_ref[0] = tv


def volume_step(temp, salt, uvel, vvel, land_mask, rims):
    members, levels, rows, cols = temp.shape
    field = pl.BlockSpec((1, levels, rows, cols), lambda m: (m, 0, 0, 0))
    plane = pl.BlockSpec((rows, cols), lambda m: (0, 0))
    north, south, east, west = rims
    row_rim = pl.BlockSpec((4, 1, levels, 1, cols), lambda m: (0, m, 0, 0, 0))
    col_rim = pl.BlockSpec((4, 1, levels, rows, 1), lambda m: (0, m, 0, 0, 0))
    surface = pl.BlockSpec((1, rows, cols), lambda m: (m, 0, 0))
    volume_shape = jax.ShapeDtypeStruct(temp.shape, jnp.float32)
    surface_shape = jax.ShapeDtypeStruct((members, rows, cols), jnp.float32)
    return pl.pallas_call(
        functools.partial(volume_kernel, lax.axis_size("gridy")),
        grid=(members,),
        in_specs=[field] * 4 + [plane, row_rim, row_rim, col_rim, col_rim],
        out_specs=[field] * 4 + [surface] * 2,
        out_shape=[volume_shape] * 4 + [surface_shape] * 2,
    )(temp, salt, uvel, vvel, land_mask, north, south, east, west)


def ring(axis):
    count = lax.axis_size(axis)
    forward = [(i, (i + 1) % count) for i in range(count)]
    backward = [((i + 1) % count, i) for i in range(count)]
    return forward, backward


def exchange(block, ydim, xdim, south_keep, north_keep):
    fwd_y, bwd_y = ring("gridy")
    fwd_x, bwd_x = ring("gridx")
    rows = block.shape[ydim]
    cols = block.shape[xdim]
    north = lax.ppermute(lax.slice_in_dim(block, 0, 1, axis=ydim), "gridy", bwd_y) * north_keep
    south = lax.ppermute(lax.slice_in_dim(block, rows - 1, rows, axis=ydim), "gridy", fwd_y) * south_keep
    east = lax.ppermute(lax.slice_in_dim(block, 0, 1, axis=xdim), "gridx", bwd_x)
    west = lax.ppermute(lax.slice_in_dim(block, cols - 1, cols, axis=xdim), "gridx", fwd_x)
    return (east, west, north, south)


def exchange_fields(fields, south_keep, north_keep):
    fwd_y, bwd_y = ring("gridy")
    fwd_x, bwd_x = ring("gridx")
    north = lax.ppermute(jnp.stack([f[..., :1, :] for f in fields]), "gridy", bwd_y)
    south = lax.ppermute(jnp.stack([f[..., -1:, :] for f in fields]), "gridy", fwd_y)
    east = lax.ppermute(jnp.stack([f[..., :, :1] for f in fields]), "gridx", bwd_x)
    west = lax.ppermute(jnp.stack([f[..., :, -1:] for f in fields]), "gridx", fwd_x)
    return (north, south, east, west)


def sides(field, rims, ydim, xdim):
    east, west, north, south = rims
    rows = field.shape[ydim]
    cols = field.shape[xdim]
    east_side = jnp.concatenate([lax.slice_in_dim(field, 1, cols, axis=xdim), east], axis=xdim)
    west_side = jnp.concatenate([west, lax.slice_in_dim(field, 0, cols - 1, axis=xdim)], axis=xdim)
    north_side = jnp.concatenate([lax.slice_in_dim(field, 1, rows, axis=ydim), north], axis=ydim)
    south_side = jnp.concatenate([south, lax.slice_in_dim(field, 0, rows - 1, axis=ydim)], axis=ydim)
    return (east_side, west_side, north_side, south_side)


def pressure(temp, salt):
    return PRESS_K * jnp.cumsum(BETA_S * salt - ALPHA_T * temp, axis=-3)


def surface_apply(field, rims):
    east_side, west_side, north_side, south_side = sides(field, rims, 1, 2)
    return (1.0 + 4.0 * SURF_C) * field - SURF_C * (east_side + west_side + north_side + south_side)


def member_total(values):
    return jnp.sum(values, axis=(1, 2))


def widen(values):
    return values[:, None, None]


def combine(a, fa, b, fb):
    def one(u, v):
        left = u if a is None else widen(a) * u
        return left + (v if b is None else widen(b) * v)

    return one(fa[0], fb[0]), tuple(one(u, v) for u, v in zip(fa[1], fb[1]))


def scaled(a, fa):
    return widen(a) * fa[0], tuple(widen(a) * u for u in fa[1])


def padded_2(block, sides_of, width):
    for axis, dim in sides_of:
        count = lax.axis_size(axis)
        forward = [(i, (i + 1) % count) for i in range(count)]
        backward = [((i + 1) % count, i) for i in range(count)]
        size = block.shape[dim]
        low = lax.ppermute(lax.slice_in_dim(block, size - width, size, axis=dim), axis, forward)
        high = lax.ppermute(lax.slice_in_dim(block, 0, width, axis=dim), axis, backward)
        block = jnp.concatenate([low, block, high], axis=dim)
    return block


def crop(field, by):
    if by == 0:
        return field
    return field[..., by:-by, by:-by]


def around(field):
    return (
        field[..., 1:-1, 1:-1],
        field[..., 1:-1, 2:],
        field[..., 1:-1, :-2],
        field[..., 2:, 1:-1],
        field[..., :-2, 1:-1],
    )


def rows_at(inside, full, want):
    cut = full - want
    return inside if cut == 0 else inside[cut:-cut]


def apply_wide(field, inside):
    centre, east, west, north, south = around(field)
    return ((1.0 + 4.0 * SURF_C) * centre - SURF_C * (east + west + north + south)) * inside


def surface_solve(rhs, inside, width, full):
    residual, wide_r = rhs, width
    gamma_prev = None
    alpha_prev = None
    for count in range(ITERS):
        image_res = apply_wide(residual, rows_at(inside, full, wide_r - 1))
        own_res = crop(residual, wide_r)
        own_img = crop(image_res, wide_r - 1)
        dots = grid_sum(jnp.stack([member_total(own_res * own_res), member_total(own_res * own_img)]))
        gamma, delta = dots[0], dots[1]
        if count == 0:
            alpha = gamma / delta
            direction, wide_p = residual, wide_r
            image_dir, wide_s = image_res, wide_r - 1
            solution, wide_x = widen(alpha) * direction, wide_r
        else:
            beta = gamma / gamma_prev
            alpha = gamma / (delta - beta * gamma / alpha_prev)
            direction = residual + widen(beta) * crop(direction, wide_p - wide_r)
            wide_p = wide_r
            image_dir = image_res + widen(beta) * crop(image_dir, wide_s - (wide_r - 1))
            wide_s = wide_r - 1
            solution = crop(solution, wide_x - wide_r) + widen(alpha) * direction
            wide_x = wide_r
        if count < ITERS - 1:
            residual = crop(residual, 1) - widen(alpha) * image_dir
            wide_r -= 1
        gamma_prev = gamma
        alpha_prev = alpha
    return solution


def shards(temp, salt, uvel, vvel, eta, land_mask, clone_source):
    levels = temp.shape[1]
    rows = temp.shape[2]
    cols = temp.shape[3]
    ocean = land_mask.astype(jnp.float32)
    tile_row = lax.axis_index("gridy")
    tile_count = lax.axis_size("gridy")
    total_rows = rows * tile_count
    total_cols = cols * lax.axis_size("gridx")
    south_keep = (tile_row > 0).astype(jnp.float32)
    north_keep = (tile_row < tile_count - 1).astype(jnp.float32)
    latitude = (tile_row * rows + jnp.arange(rows, dtype=jnp.int32)).astype(jnp.float32) + 0.5
    coriolis = (CORI_K * (2.0 * latitude / total_rows - 1.0))[:, None]
    cor_tile = jnp.broadcast_to(coriolis, (rows, cols))
    band = 8
    block = 128
    frame_rows = rows + 2 * band
    frame_cols = cols + 2 * block
    row_at = lax.broadcasted_iota(jnp.int32, (frame_rows, frame_cols), 0)
    col_at = lax.broadcasted_iota(jnp.int32, (frame_rows, frame_cols), 1)
    global_row = tile_row * rows + jnp.where(row_at < rows + band, row_at, row_at - frame_rows)
    wide_inside = ((global_row >= 0) & (global_row < total_rows)).astype(jnp.float32)
    own_mask = ((row_at < rows) & (col_at < cols)).astype(jnp.float32)
    for count in range(STEPS):
        fields = (temp, salt, uvel, vvel)
        rims = exchange_fields(fields, south_keep, north_keep)
        temp_next, salt_next, ustar, vstar, trans_u, trans_v = volume_step(
            temp, salt, uvel, vvel, land_mask, rims
        )
        solved = surface_kernel_solve(trans_u, trans_v, eta, wide_inside, own_mask)
        eta = solved[0]
        east_west = solved[1]
        north_south = solved[2]
        uvel = ocean * (ustar - GRAV_K * 0.5 * east_west[:, None])
        vvel = ocean * (vstar - GRAV_K * 0.5 * north_south[:, None])
        if count == STEPS - 1:
            tracers_other = lax.ppermute(jnp.stack((temp_next, salt_next)), "member", [(0, 1), (1, 0)])
        temp = temp_next
        salt = salt_next
    zonal_scale = 1.0 / jnp.sqrt(jnp.float32(total_cols))
    score_scale = 1.0 / jnp.sqrt(jnp.float32(levels * total_rows))
    lat_weight = latitude / total_rows
    members = temp.shape[0]
    zonal_local = jnp.sum(vvel, axis=3)
    depth_weight = (levels - jnp.arange(levels, dtype=jnp.int32)).astype(jnp.float32)
    score_local = jnp.sum(zonal_local * depth_weight[None, :, None] * lat_weight[None, None, :], axis=(1, 2))
    slot = lax.broadcasted_iota(jnp.int32, (tile_count, 1, 1, 1), 0) == tile_row
    zonal_slots = jnp.where(slot, zonal_local[None], 0.0).reshape(-1, 128)
    score_row = jnp.zeros((8, 128), jnp.float32).at[0, :members].set(score_local)
    summed = grid_sum(jnp.concatenate([zonal_slots, score_row], axis=0))
    zonal_whole = summed[: zonal_slots.shape[0]].reshape((tile_count,) + zonal_local.shape)
    zonal_whole = jnp.sum(jnp.where(slot, zonal_whole, 0.0), axis=0)
    overturn = jnp.cumsum(zonal_whole, axis=1) * zonal_scale
    score = summed[zonal_slots.shape[0], :members] * (zonal_scale * score_scale)
    swap = [(0, 1), (1, 0)]
    mine = lax.axis_index("member")
    after_score = eta + 0.0 * jnp.sum(score)
    flows = jnp.concatenate([uvel, vvel, after_score[:, None]], axis=1)
    flows_other = lax.ppermute(flows, "member", swap)
    score_other = lax.ppermute(score, "member", swap)
    every_score = jnp.where(
        mine == 0, jnp.concatenate([score, score_other]), jnp.concatenate([score_other, score])
    )
    here = (clone_source // members) == mine
    local_at = clone_source % members

    def pick(local, other):
        chosen = []
        for place in range(members):
            from_here = lax.dynamic_index_in_dim(local, local_at[place], 0, keepdims=False)
            from_other = lax.dynamic_index_in_dim(other, local_at[place], 0, keepdims=False)
            chosen.append(jnp.where(here[place], from_here, from_other))
        return jnp.stack(chosen)

    new_temp = pick(temp, tracers_other[0])
    new_salt = pick(salt, tracers_other[1])
    new_flows = pick(flows[:, : 2 * levels + 1], flows_other[:, : 2 * levels + 1])
    clone_weight = jnp.take(every_score, clone_source, axis=0) - jnp.mean(every_score)
    return (
        new_temp,
        new_salt,
        new_flows[:, :levels],
        new_flows[:, levels : 2 * levels],
        new_flows[:, 2 * levels],
        overturn,
        clone_weight,
    )


def solution(mesh):
    in_specs = (
        P("member", None, "gridy", "gridx"),
        P("member", None, "gridy", "gridx"),
        P("member", None, "gridy", "gridx"),
        P("member", None, "gridy", "gridx"),
        P("member", "gridy", "gridx"),
        P("gridy", "gridx"),
        P("member"),
    )
    out_specs = (
        P("member", None, "gridy", "gridx"),
        P("member", None, "gridy", "gridx"),
        P("member", None, "gridy", "gridx"),
        P("member", None, "gridy", "gridx"),
        P("member", "gridy", "gridx"),
        P("member", None, "gridy"),
        P("member"),
    )
    return jax.shard_map(shards, mesh=mesh, in_specs=in_specs, out_specs=out_specs, check_vma=False)
```

```python
import functools

import jax
import jax.numpy as jnp
from jax import lax
from jax.experimental import pallas as pl
from jax.experimental.pallas import tpu as pltpu
from jax.sharding import PartitionSpec as P

STEPS = 2
ITERS = 3


ALPHA_T = 0.8
BETA_S = 0.6
PRESS_K = 0.25
STEP_DT = 0.1
KAPPA = 0.1
VISCOSITY = 0.1
DRAG_K = 0.05
CORI_K = 1.0
SURF_C = 4.0
DIV_K = 0.5
GRAV_K = 0.5


def tree_sum(values, axes):
    for axis in axes:
        count = lax.axis_size(axis)
        step = 1
        while step < count:
            pairs = [(i, i ^ step) for i in range(count)]
            values = values + lax.ppermute(values, axis, pairs)
            step *= 2
    return values


def gather_sum_kernel(ny, nx, x_ref, o_ref, recv_y, recv_x, part, send_y, rsem_y, send_x, rsem_x):
    mesh_id = pl.DeviceIdType.MESH
    member = lax.axis_index("member")
    my = lax.axis_index("gridy")
    mx = lax.axis_index("gridx")
    barrier = pltpu.get_barrier_semaphore()
    for d in range(1, ny):
        pl.semaphore_signal(barrier, 1, device_id=(member, (my + d) % ny, mx), device_id_type=mesh_id)
    for d in range(1, nx):
        pl.semaphore_signal(barrier, 1, device_id=(member, my, (mx + d) % nx), device_id_type=mesh_id)
    pl.semaphore_wait(barrier, (ny - 1) + (nx - 1))

    def phase(src, recv, send_sem, recv_sem, count, me, device):
        recv[me] = src[...]
        sent = []
        for d in range(1, count):
            peer = (me + d) % count
            copy = pltpu.make_async_remote_copy(
                src_ref=src,
                dst_ref=recv.at[me],
                send_sem=send_sem.at[peer],
                recv_sem=recv_sem.at[me],
                device_id=device(peer),
                device_id_type=mesh_id,
            )
            copy.start()
            sent.append(copy)
        for d in range(1, count):
            peer = (me + d) % count
            pltpu.make_async_remote_copy(
                src_ref=src,
                dst_ref=recv.at[peer],
                send_sem=send_sem.at[peer],
                recv_sem=recv_sem.at[peer],
                device_id=device(peer),
                device_id_type=mesh_id,
            ).wait_recv()
        for copy in sent:
            copy.wait_send()
        total = recv[0]
        for j in range(1, count):
            total = total + recv[j]
        return total

    part[...] = phase(x_ref, recv_y, send_y, rsem_y, ny, my, lambda p: (member, p, mx))
    o_ref[...] = phase(part, recv_x, send_x, rsem_x, nx, mx, lambda p: (member, my, p))


def grid_sum(values):
    ny = lax.axis_size("gridy")
    nx = lax.axis_size("gridx")
    shape = values.shape
    return pl.pallas_call(
        functools.partial(gather_sum_kernel, ny, nx),
        out_shape=jax.ShapeDtypeStruct(shape, values.dtype),
        in_specs=[pl.BlockSpec(memory_space=pltpu.VMEM)],
        out_specs=pl.BlockSpec(memory_space=pltpu.VMEM),
        scratch_shapes=[
            pltpu.VMEM((ny,) + shape, values.dtype),
            pltpu.VMEM((nx,) + shape, values.dtype),
            pltpu.VMEM(shape, values.dtype),
            pltpu.SemaphoreType.DMA((ny,)),
            pltpu.SemaphoreType.DMA((ny,)),
            pltpu.SemaphoreType.DMA((nx,)),
            pltpu.SemaphoreType.DMA((nx,)),
        ],
        compiler_params=pltpu.CompilerParams(collective_id=0, has_side_effects=True),
    )(values)


def exchange_sum(k, vec, ny, nx, bufs, device_ids):
    send_y, recv_y, send_x, recv_x, sy, ry, sx, rx = bufs
    my, mx, along_y, along_x = device_ids
    mesh_id = pl.DeviceIdType.MESH

    def phase(value, send_buf, recv, send_sem, recv_sem, count, me, device):
        send_buf[k] = value
        recv[k, me] = value
        sent = []
        for d in range(1, count):
            peer = (me + d) % count
            copy = pltpu.make_async_remote_copy(
                src_ref=send_buf.at[k],
                dst_ref=recv.at[k, me],
                send_sem=send_sem.at[k, peer],
                recv_sem=recv_sem.at[k, me],
                device_id=device(peer),
                device_id_type=mesh_id,
            )
            copy.start()
            sent.append(copy)
        for d in range(1, count):
            peer = (me + d) % count
            pltpu.make_async_remote_copy(
                src_ref=send_buf.at[k],
                dst_ref=recv.at[k, peer],
                send_sem=send_sem.at[k, peer],
                recv_sem=recv_sem.at[k, peer],
                device_id=device(peer),
                device_id_type=mesh_id,
            ).wait_recv()
        for copy in sent:
            copy.wait_send()
        total = recv[k, 0]
        for j in range(1, count):
            total = total + recv[k, j]
        return total

    partial = phase(vec, send_y, recv_y, sy, ry, ny, my, along_y)
    return phase(partial, send_x, recv_x, sx, rx, nx, mx, along_x)


def solve_kernel(ny, nx, tu_ref, tv_ref, eta_ref, inside_ref, own_ref, out_ref, frame, hsend, hrecv, *bufs):
    mesh_id = pl.DeviceIdType.MESH
    member = lax.axis_index("member")
    my = lax.axis_index("gridy")
    mx = lax.axis_index("gridx")
    along_y = lambda p: (member, p, mx)
    along_x = lambda p: (member, my, p)
    barrier = pltpu.get_barrier_semaphore()
    for d in range(1, ny):
        pl.semaphore_signal(barrier, 1, device_id=along_y((my + d) % ny), device_id_type=mesh_id)
    for d in range(1, nx):
        pl.semaphore_signal(barrier, 1, device_id=along_x((mx + d) % nx), device_id_type=mesh_id)
    for dy in (1, ny - 1):
        for dx in (1, nx - 1):
            pl.semaphore_signal(
                barrier, 1, device_id=(member, (my + dy) % ny, (mx + dx) % nx), device_id_type=mesh_id
            )
    rows, cols = eta_ref.shape[1], eta_ref.shape[2]
    wide_rows, wide_cols = frame.shape[2], frame.shape[3]
    band = (wide_rows - rows) // 2
    block = (wide_cols - cols) // 2
    frame[0, :, 0:rows, 0:cols] = tu_ref[...]
    frame[1, :, 0:rows, 0:cols] = tv_ref[...]
    frame[2, :, 0:rows, 0:cols] = eta_ref[...]
    pl.semaphore_wait(barrier, (ny - 1) + (nx - 1) + 4)

    def halo_copies(first, moves):
        started = []
        for slot, (src, dst, device) in enumerate(moves, start=first):
            copy = pltpu.make_async_remote_copy(
                src_ref=src, dst_ref=dst, send_sem=hsend.at[slot], recv_sem=hrecv.at[slot],
                device_id=device, device_id_type=mesh_id,
            )
            copy.start()
            started.append(copy)
        for copy in started:
            copy.wait()

    up, down = (my + 1) % ny, (my + ny - 1) % ny
    right, left = (mx + 1) % nx, (mx + nx - 1) % nx
    top_rows = slice(0, band)
    low_rows = slice(rows - band, rows)
    own_rows = slice(0, rows)
    west_part = slice(0, block)
    east_part = slice(cols - block, cols)
    own_cols = slice(0, cols)
    north_halo = slice(rows, rows + band)
    south_halo = slice(rows + band, wide_rows)
    east_halo = slice(cols, cols + block)
    west_halo = slice(cols + block, wide_cols)
    halo_copies(0, [
        (frame.at[:, :, top_rows, own_cols], frame.at[:, :, north_halo, own_cols], (member, down, mx)),
        (frame.at[:, :, low_rows, own_cols], frame.at[:, :, south_halo, own_cols], (member, up, mx)),
        (frame.at[:, :, own_rows, west_part], frame.at[:, :, own_rows, east_halo], (member, my, left)),
        (frame.at[:, :, own_rows, east_part], frame.at[:, :, own_rows, west_halo], (member, my, right)),
        (frame.at[:, :, top_rows, west_part], frame.at[:, :, north_halo, east_halo], (member, down, left)),
        (frame.at[:, :, top_rows, east_part], frame.at[:, :, north_halo, west_halo], (member, down, right)),
        (frame.at[:, :, low_rows, west_part], frame.at[:, :, south_halo, east_halo], (member, up, left)),
        (frame.at[:, :, low_rows, east_part], frame.at[:, :, south_halo, west_halo], (member, up, right)),
    ])

    members = eta_ref.shape[0]
    inside = inside_ref[...]
    own = own_ref[...] > 0.5

    def east(f):
        return pltpu.roll(f, wide_cols - 1, 1)

    def west(f):
        return pltpu.roll(f, 1, 1)

    def north(f):
        return pltpu.roll(f, wide_rows - 1, 0)

    def south(f):
        return pltpu.roll(f, 1, 0)

    def apply(f):
        return ((1.0 + 4.0 * SURF_C) * f - SURF_C * (east(f) + west(f) + north(f) + south(f))) * inside

    def total(f):
        return jnp.sum(f[0:rows, 0:cols], axis=(0, 1), keepdims=True)

    residual = []
    for m in range(members):
        trans_u = frame[0, m] * inside
        trans_v = frame[1, m] * inside
        level = frame[2, m] * inside
        residual.append(
            (level - DIV_K * 0.5 * (east(trans_u) - west(trans_u) + (north(trans_v) - south(trans_v)))) * inside
        )
    lane = lax.broadcasted_iota(jnp.int32, (8, 128), 1)
    direction = [None] * members
    image_dir = [None] * members
    solution = [None] * members
    gamma_prev = [None] * members
    alpha_prev = [None] * members
    for count in range(ITERS):
        image_res = [apply(residual[m]) for m in range(members)]
        vec = jnp.zeros((8, 128), jnp.float32)
        for m in range(members):
            vec = jnp.where(lane == 2 * m, total(residual[m] * residual[m]), vec)
            vec = jnp.where(lane == 2 * m + 1, total(residual[m] * image_res[m]), vec)
        sums = exchange_sum(count, vec, ny, nx, bufs, (my, mx, along_y, along_x))
        for m in range(members):
            gamma = sums[0:1, 2 * m : 2 * m + 1]
            delta = sums[0:1, 2 * m + 1 : 2 * m + 2]
            if count == 0:
                alpha = gamma / delta
                direction[m] = residual[m]
                image_dir[m] = image_res[m]
                solution[m] = alpha * direction[m]
            else:
                beta = gamma / gamma_prev[m]
                alpha = gamma / (delta - beta * gamma / alpha_prev[m])
                direction[m] = residual[m] + beta * direction[m]
                image_dir[m] = image_res[m] + beta * image_dir[m]
                solution[m] = solution[m] + alpha * direction[m]
            if count < ITERS - 1:
                residual[m] = residual[m] - alpha * image_dir[m]
            gamma_prev[m] = gamma
            alpha_prev[m] = alpha
    for m in range(members):
        x = solution[m]
        out_ref[0, m] = x[0:rows, 0:cols]
        out_ref[1, m] = (east(x) - west(x))[0:rows, 0:cols]
        out_ref[2, m] = (north(x) - south(x))[0:rows, 0:cols]


def surface_kernel_solve(trans_u, trans_v, eta, inside, own):
    ny = lax.axis_size("gridy")
    nx = lax.axis_size("gridx")
    members, rows, cols = eta.shape
    fields = 3
    return pl.pallas_call(
        functools.partial(solve_kernel, ny, nx),
        out_shape=jax.ShapeDtypeStruct((3, members, rows, cols), jnp.float32),
        in_specs=[pl.BlockSpec(memory_space=pltpu.VMEM)] * 5,
        out_specs=pl.BlockSpec(memory_space=pltpu.VMEM),
        scratch_shapes=[
            pltpu.VMEM((fields, members) + inside.shape, jnp.float32),
            pltpu.SemaphoreType.DMA((8,)),
            pltpu.SemaphoreType.DMA((8,)),
            pltpu.VMEM((ITERS, 8, 128), jnp.float32),
            pltpu.VMEM((ITERS, ny, 8, 128), jnp.float32),
            pltpu.VMEM((ITERS, 8, 128), jnp.float32),
            pltpu.VMEM((ITERS, nx, 8, 128), jnp.float32),
            pltpu.SemaphoreType.DMA((ITERS, ny)),
            pltpu.SemaphoreType.DMA((ITERS, ny)),
            pltpu.SemaphoreType.DMA((ITERS, nx)),
            pltpu.SemaphoreType.DMA((ITERS, nx)),
        ],
        compiler_params=pltpu.CompilerParams(collective_id=1, has_side_effects=True),
    )(trans_u, trans_v, eta, inside, own)


def volume_kernel(ny, temp_ref, salt_ref, uvel_ref, vvel_ref, land_ref, n_ref, s_ref, e_ref, w_ref,
                  tn_ref, sn_ref, us_ref, vs_ref, tu_ref, tv_ref):
    levels, rows, cols = temp_ref.shape[1], temp_ref.shape[2], temp_ref.shape[3]
    row = lax.broadcasted_iota(jnp.int32, (rows, cols), 0)
    col = lax.broadcasted_iota(jnp.int32, (rows, cols), 1)
    tile_row = lax.axis_index("gridy")
    north_keep = jnp.where(tile_row < ny - 1, 1.0, 0.0)
    south_keep = jnp.where(tile_row > 0, 1.0, 0.0)
    latitude = (tile_row * rows + row).astype(jnp.float32) + 0.5
    top = row == rows - 1
    bottom = row == 0
    right = col == cols - 1
    left = col == 0
    ocean = land_ref[...].astype(jnp.float32)
    cor = CORI_K * (2.0 * latitude / (rows * ny) - 1.0)

    def around(f, rims):
        n, s, e, w = rims
        return (
            jnp.where(right, e, pltpu.roll(f, cols - 1, 1)),
            jnp.where(left, w, pltpu.roll(f, 1, 1)),
            jnp.where(top, n, pltpu.roll(f, rows - 1, 0)),
            jnp.where(bottom, s, pltpu.roll(f, 1, 0)),
        )

    east_cols = [e_ref[k, 0].T for k in range(4)]
    west_cols = [w_ref[k, 0].T for k in range(4)]

    def rims_of(k, l):
        return (
            n_ref[k, 0, l] * north_keep,
            s_ref[k, 0, l] * south_keep,
            east_cols[k][:, l : l + 1],
            west_cols[k][:, l : l + 1],
        )

    running = None
    running_rims = None
    tu = None
    tv = None
    for l in range(levels):
        t = temp_ref[0, l]
        s = salt_ref[0, l]
        u = uvel_ref[0, l]
        v = vvel_ref[0, l]
        rt, rs, ru, rv = rims_of(0, l), rims_of(1, l), rims_of(2, l), rims_of(3, l)
        layer = BETA_S * s - ALPHA_T * t
        layer_rims = tuple(BETA_S * b - ALPHA_T * a for a, b in zip(rt, rs))
        if running is None:
            running, running_rims = layer, layer_rims
        else:
            running = running + layer
            running_rims = tuple(a + b for a, b in zip(running_rims, layer_rims))
        press = PRESS_K * running
        press_rims = tuple(PRESS_K * a for a in running_rims)
        te, tw, tn, ts = around(t, rt)
        se, sw, sn, ss = around(s, rs)
        ue, uw, un, us = around(u, ru)
        ve, vw, vn, vs = around(v, rv)
        pe, pw, pn, ps = around(press, press_rims)
        tn_ref[0, l] = ocean * (
            t - STEP_DT * 0.5 * (u * (te - tw) + v * (tn - ts)) + KAPPA * (te + tw + tn + ts - 4.0 * t)
        )
        sn_ref[0, l] = ocean * (
            s - STEP_DT * 0.5 * (u * (se - sw) + v * (sn - ss)) + KAPPA * (se + sw + sn + ss - 4.0 * s)
        )
        ustar = ocean * (
            u + STEP_DT * (cor * v - 0.5 * (pe - pw) - DRAG_K * u) + VISCOSITY * (ue + uw + un + us - 4.0 * u)
        )
        vstar = ocean * (
            v + STEP_DT * (-cor * u - 0.5 * (pn - ps) - DRAG_K * v) + VISCOSITY * (ve + vw + vn + vs - 4.0 * v)
        )
        us_ref[0, l] = ustar
        vs_ref[0, l] = vstar
        tu = ustar if tu is None else tu + ustar
        tv = vstar if tv is None else tv + vstar
    tu_ref[0] = tu
    tv_ref[0] = tv


def volume_step(temp, salt, uvel, vvel, land_mask, rims):
    members, levels, rows, cols = temp.shape
    field = pl.BlockSpec((1, levels, rows, cols), lambda m: (m, 0, 0, 0))
    plane = pl.BlockSpec((rows, cols), lambda m: (0, 0))
    north, south, east, west = rims
    row_rim = pl.BlockSpec((4, 1, levels, 1, cols), lambda m: (0, m, 0, 0, 0))
    col_rim = pl.BlockSpec((4, 1, levels, rows), lambda m: (0, m, 0, 0))
    surface = pl.BlockSpec((1, rows, cols), lambda m: (m, 0, 0))
    volume_shape = jax.ShapeDtypeStruct(temp.shape, jnp.float32)
    surface_shape = jax.ShapeDtypeStruct((members, rows, cols), jnp.float32)
    return pl.pallas_call(
        functools.partial(volume_kernel, lax.axis_size("gridy")),
        grid=(members,),
        in_specs=[field] * 4 + [plane, row_rim, row_rim, col_rim, col_rim],
        out_specs=[field] * 4 + [surface] * 2,
        out_shape=[volume_shape] * 4 + [surface_shape] * 2,
    )(temp, salt, uvel, vvel, land_mask, north, south, east, west)


def ring(axis):
    count = lax.axis_size(axis)
    forward = [(i, (i + 1) % count) for i in range(count)]
    backward = [((i + 1) % count, i) for i in range(count)]
    return forward, backward


def exchange(block, ydim, xdim, south_keep, north_keep):
    fwd_y, bwd_y = ring("gridy")
    fwd_x, bwd_x = ring("gridx")
    rows = block.shape[ydim]
    cols = block.shape[xdim]
    north = lax.ppermute(lax.slice_in_dim(block, 0, 1, axis=ydim), "gridy", bwd_y) * north_keep
    south = lax.ppermute(lax.slice_in_dim(block, rows - 1, rows, axis=ydim), "gridy", fwd_y) * south_keep
    east = lax.ppermute(lax.slice_in_dim(block, 0, 1, axis=xdim), "gridx", bwd_x)
    west = lax.ppermute(lax.slice_in_dim(block, cols - 1, cols, axis=xdim), "gridx", fwd_x)
    return (east, west, north, south)


def exchange_fields(fields, south_keep, north_keep):
    fwd_y, bwd_y = ring("gridy")
    fwd_x, bwd_x = ring("gridx")
    north = lax.ppermute(jnp.stack([f[..., :1, :] for f in fields]), "gridy", bwd_y)
    south = lax.ppermute(jnp.stack([f[..., -1:, :] for f in fields]), "gridy", fwd_y)
    east = lax.ppermute(jnp.stack([f[..., :, 0] for f in fields]), "gridx", bwd_x)
    west = lax.ppermute(jnp.stack([f[..., :, -1] for f in fields]), "gridx", fwd_x)
    return (north, south, east, west)


def sides(field, rims, ydim, xdim):
    east, west, north, south = rims
    rows = field.shape[ydim]
    cols = field.shape[xdim]
    east_side = jnp.concatenate([lax.slice_in_dim(field, 1, cols, axis=xdim), east], axis=xdim)
    west_side = jnp.concatenate([west, lax.slice_in_dim(field, 0, cols - 1, axis=xdim)], axis=xdim)
    north_side = jnp.concatenate([lax.slice_in_dim(field, 1, rows, axis=ydim), north], axis=ydim)
    south_side = jnp.concatenate([south, lax.slice_in_dim(field, 0, rows - 1, axis=ydim)], axis=ydim)
    return (east_side, west_side, north_side, south_side)


def pressure(temp, salt):
    return PRESS_K * jnp.cumsum(BETA_S * salt - ALPHA_T * temp, axis=-3)


def surface_apply(field, rims):
    east_side, west_side, north_side, south_side = sides(field, rims, 1, 2)
    return (1.0 + 4.0 * SURF_C) * field - SURF_C * (east_side + west_side + north_side + south_side)


def member_total(values):
    return jnp.sum(values, axis=(1, 2))


def widen(values):
    return values[:, None, None]


def combine(a, fa, b, fb):
    def one(u, v):
        left = u if a is None else widen(a) * u
        return left + (v if b is None else widen(b) * v)

    return one(fa[0], fb[0]), tuple(one(u, v) for u, v in zip(fa[1], fb[1]))


def scaled(a, fa):
    return widen(a) * fa[0], tuple(widen(a) * u for u in fa[1])


def padded_2(block, sides_of, width):
    for axis, dim in sides_of:
        count = lax.axis_size(axis)
        forward = [(i, (i + 1) % count) for i in range(count)]
        backward = [((i + 1) % count, i) for i in range(count)]
        size = block.shape[dim]
        low = lax.ppermute(lax.slice_in_dim(block, size - width, size, axis=dim), axis, forward)
        high = lax.ppermute(lax.slice_in_dim(block, 0, width, axis=dim), axis, backward)
        block = jnp.concatenate([low, block, high], axis=dim)
    return block


def crop(field, by):
    if by == 0:
        return field
    return field[..., by:-by, by:-by]


def around(field):
    return (
        field[..., 1:-1, 1:-1],
        field[..., 1:-1, 2:],
        field[..., 1:-1, :-2],
        field[..., 2:, 1:-1],
        field[..., :-2, 1:-1],
    )


def rows_at(inside, full, want):
    cut = full - want
    return inside if cut == 0 else inside[cut:-cut]


def apply_wide(field, inside):
    centre, east, west, north, south = around(field)
    return ((1.0 + 4.0 * SURF_C) * centre - SURF_C * (east + west + north + south)) * inside


def surface_solve(rhs, inside, width, full):
    residual, wide_r = rhs, width
    gamma_prev = None
    alpha_prev = None
    for count in range(ITERS):
        image_res = apply_wide(residual, rows_at(inside, full, wide_r - 1))
        own_res = crop(residual, wide_r)
        own_img = crop(image_res, wide_r - 1)
        dots = grid_sum(jnp.stack([member_total(own_res * own_res), member_total(own_res * own_img)]))
        gamma, delta = dots[0], dots[1]
        if count == 0:
            alpha = gamma / delta
            direction, wide_p = residual, wide_r
            image_dir, wide_s = image_res, wide_r - 1
            solution, wide_x = widen(alpha) * direction, wide_r
        else:
            beta = gamma / gamma_prev
            alpha = gamma / (delta - beta * gamma / alpha_prev)
            direction = residual + widen(beta) * crop(direction, wide_p - wide_r)
            wide_p = wide_r
            image_dir = image_res + widen(beta) * crop(image_dir, wide_s - (wide_r - 1))
            wide_s = wide_r - 1
            solution = crop(solution, wide_x - wide_r) + widen(alpha) * direction
            wide_x = wide_r
        if count < ITERS - 1:
            residual = crop(residual, 1) - widen(alpha) * image_dir
            wide_r -= 1
        gamma_prev = gamma
        alpha_prev = alpha
    return solution


def shards(temp, salt, uvel, vvel, eta, land_mask, clone_source):
    levels = temp.shape[1]
    rows = temp.shape[2]
    cols = temp.shape[3]
    ocean = land_mask.astype(jnp.float32)
    tile_row = lax.axis_index("gridy")
    tile_count = lax.axis_size("gridy")
    total_rows = rows * tile_count
    total_cols = cols * lax.axis_size("gridx")
    south_keep = (tile_row > 0).astype(jnp.float32)
    north_keep = (tile_row < tile_count - 1).astype(jnp.float32)
    latitude = (tile_row * rows + jnp.arange(rows, dtype=jnp.int32)).astype(jnp.float32) + 0.5
    coriolis = (CORI_K * (2.0 * latitude / total_rows - 1.0))[:, None]
    cor_tile = jnp.broadcast_to(coriolis, (rows, cols))
    band = 8
    block = 128
    frame_rows = rows + 2 * band
    frame_cols = cols + 2 * block
    row_at = lax.broadcasted_iota(jnp.int32, (frame_rows, frame_cols), 0)
    col_at = lax.broadcasted_iota(jnp.int32, (frame_rows, frame_cols), 1)
    global_row = tile_row * rows + jnp.where(row_at < rows + band, row_at, row_at - frame_rows)
    wide_inside = ((global_row >= 0) & (global_row < total_rows)).astype(jnp.float32)
    own_mask = ((row_at < rows) & (col_at < cols)).astype(jnp.float32)
    for count in range(STEPS):
        fields = (temp, salt, uvel, vvel)
        rims = exchange_fields(fields, south_keep, north_keep)
        temp_next, salt_next, ustar, vstar, trans_u, trans_v = volume_step(
            temp, salt, uvel, vvel, land_mask, rims
        )
        solved = surface_kernel_solve(trans_u, trans_v, eta, wide_inside, own_mask)
        eta = solved[0]
        east_west = solved[1]
        north_south = solved[2]
        uvel = ocean * (ustar - GRAV_K * 0.5 * east_west[:, None])
        vvel = ocean * (vstar - GRAV_K * 0.5 * north_south[:, None])
        if count == STEPS - 1:
            tracers_other = lax.ppermute(jnp.stack((temp_next, salt_next)), "member", [(0, 1), (1, 0)])
        temp = temp_next
        salt = salt_next
    zonal_scale = 1.0 / jnp.sqrt(jnp.float32(total_cols))
    score_scale = 1.0 / jnp.sqrt(jnp.float32(levels * total_rows))
    lat_weight = latitude / total_rows
    members = temp.shape[0]
    zonal_local = jnp.sum(vvel, axis=3)
    depth_weight = (levels - jnp.arange(levels, dtype=jnp.int32)).astype(jnp.float32)
    score_local = jnp.sum(zonal_local * depth_weight[None, :, None] * lat_weight[None, None, :], axis=(1, 2))
    slot = lax.broadcasted_iota(jnp.int32, (tile_count, 1, 1, 1), 0) == tile_row
    zonal_slots = jnp.where(slot, zonal_local[None], 0.0).reshape(-1, 128)
    score_row = jnp.zeros((8, 128), jnp.float32).at[0, :members].set(score_local)
    summed = grid_sum(jnp.concatenate([zonal_slots, score_row], axis=0))
    zonal_whole = summed[: zonal_slots.shape[0]].reshape((tile_count,) + zonal_local.shape)
    zonal_whole = jnp.sum(jnp.where(slot, zonal_whole, 0.0), axis=0)
    overturn = jnp.cumsum(zonal_whole, axis=1) * zonal_scale
    score = summed[zonal_slots.shape[0], :members] * (zonal_scale * score_scale)
    swap = [(0, 1), (1, 0)]
    mine = lax.axis_index("member")
    score_slab = jnp.zeros((members, 1) + eta.shape[1:], jnp.float32).at[:, 0, 0, 0].set(score)
    flows = jnp.concatenate([uvel, vvel, eta[:, None], score_slab], axis=1)
    flows_other = lax.ppermute(flows, "member", swap)
    score_other = flows_other[:, 2 * levels + 1, 0, 0]
    every_score = jnp.where(
        mine == 0, jnp.concatenate([score, score_other]), jnp.concatenate([score_other, score])
    )
    here = (clone_source // members) == mine
    local_at = clone_source % members

    def pick(local, other):
        chosen = []
        for place in range(members):
            from_here = lax.dynamic_index_in_dim(local, local_at[place], 0, keepdims=False)
            from_other = lax.dynamic_index_in_dim(other, local_at[place], 0, keepdims=False)
            chosen.append(jnp.where(here[place], from_here, from_other))
        return jnp.stack(chosen)

    new_temp = pick(temp, tracers_other[0])
    new_salt = pick(salt, tracers_other[1])
    new_flows = pick(flows[:, : 2 * levels + 1], flows_other[:, : 2 * levels + 1])
    clone_weight = jnp.take(every_score, clone_source, axis=0) - jnp.mean(every_score)
    return (
        new_temp,
        new_salt,
        new_flows[:, :levels],
        new_flows[:, levels : 2 * levels],
        new_flows[:, 2 * levels],
        overturn,
        clone_weight,
    )


def solution(mesh):
    in_specs = (
        P("member", None, "gridy", "gridx"),
        P("member", None, "gridy", "gridx"),
        P("member", None, "gridy", "gridx"),
        P("member", None, "gridy", "gridx"),
        P("member", "gridy", "gridx"),
        P("gridy", "gridx"),
        P("member"),
    )
    out_specs = (
        P("member", None, "gridy", "gridx"),
        P("member", None, "gridy", "gridx"),
        P("member", None, "gridy", "gridx"),
        P("member", None, "gridy", "gridx"),
        P("member", "gridy", "gridx"),
        P("member", None, "gridy"),
        P("member"),
    )
    return jax.shard_map(shards, mesh=mesh, in_specs=in_specs, out_specs=out_specs, check_vma=False)
```

```python
import functools

import jax
import jax.numpy as jnp
from jax import lax
from jax.experimental import pallas as pl
from jax.experimental.pallas import tpu as pltpu
from jax.sharding import PartitionSpec as P

STEPS = 2
ITERS = 3


ALPHA_T = 0.8
BETA_S = 0.6
PRESS_K = 0.25
STEP_DT = 0.1
KAPPA = 0.1
VISCOSITY = 0.1
DRAG_K = 0.05
CORI_K = 1.0
SURF_C = 4.0
DIV_K = 0.5
GRAV_K = 0.5


def tree_sum(values, axes):
    for axis in axes:
        count = lax.axis_size(axis)
        step = 1
        while step < count:
            pairs = [(i, i ^ step) for i in range(count)]
            values = values + lax.ppermute(values, axis, pairs)
            step *= 2
    return values


def gather_sum_kernel(ny, nx, x_ref, o_ref, recv_y, recv_x, part, send_y, rsem_y, send_x, rsem_x):
    mesh_id = pl.DeviceIdType.MESH
    member = lax.axis_index("member")
    my = lax.axis_index("gridy")
    mx = lax.axis_index("gridx")
    barrier = pltpu.get_barrier_semaphore()
    for d in range(1, ny):
        pl.semaphore_signal(barrier, 1, device_id=(member, (my + d) % ny, mx), device_id_type=mesh_id)
    for d in range(1, nx):
        pl.semaphore_signal(barrier, 1, device_id=(member, my, (mx + d) % nx), device_id_type=mesh_id)
    pl.semaphore_wait(barrier, (ny - 1) + (nx - 1))

    def phase(src, recv, send_sem, recv_sem, count, me, device):
        recv[me] = src[...]
        sent = []
        for d in range(1, count):
            peer = (me + d) % count
            copy = pltpu.make_async_remote_copy(
                src_ref=src,
                dst_ref=recv.at[me],
                send_sem=send_sem.at[peer],
                recv_sem=recv_sem.at[me],
                device_id=device(peer),
                device_id_type=mesh_id,
            )
            copy.start()
            sent.append(copy)
        for d in range(1, count):
            peer = (me + d) % count
            pltpu.make_async_remote_copy(
                src_ref=src,
                dst_ref=recv.at[peer],
                send_sem=send_sem.at[peer],
                recv_sem=recv_sem.at[peer],
                device_id=device(peer),
                device_id_type=mesh_id,
            ).wait_recv()
        for copy in sent:
            copy.wait_send()
        total = recv[0]
        for j in range(1, count):
            total = total + recv[j]
        return total

    part[...] = phase(x_ref, recv_y, send_y, rsem_y, ny, my, lambda p: (member, p, mx))
    o_ref[...] = phase(part, recv_x, send_x, rsem_x, nx, mx, lambda p: (member, my, p))


def grid_sum(values):
    ny = lax.axis_size("gridy")
    nx = lax.axis_size("gridx")
    shape = values.shape
    return pl.pallas_call(
        functools.partial(gather_sum_kernel, ny, nx),
        out_shape=jax.ShapeDtypeStruct(shape, values.dtype),
        in_specs=[pl.BlockSpec(memory_space=pltpu.VMEM)],
        out_specs=pl.BlockSpec(memory_space=pltpu.VMEM),
        scratch_shapes=[
            pltpu.VMEM((ny,) + shape, values.dtype),
            pltpu.VMEM((nx,) + shape, values.dtype),
            pltpu.VMEM(shape, values.dtype),
            pltpu.SemaphoreType.DMA((ny,)),
            pltpu.SemaphoreType.DMA((ny,)),
            pltpu.SemaphoreType.DMA((nx,)),
            pltpu.SemaphoreType.DMA((nx,)),
        ],
        compiler_params=pltpu.CompilerParams(collective_id=0, has_side_effects=True),
    )(values)


def exchange_sum(k, vec, ny, nx, bufs, device_ids):
    send_y, recv_y, send_x, recv_x, sy, ry, sx, rx = bufs
    my, mx, along_y, along_x = device_ids
    mesh_id = pl.DeviceIdType.MESH

    def phase(value, send_buf, recv, send_sem, recv_sem, count, me, device):
        send_buf[k] = value
        recv[k, me] = value
        sent = []
        for d in range(1, count):
            peer = (me + d) % count
            copy = pltpu.make_async_remote_copy(
                src_ref=send_buf.at[k],
                dst_ref=recv.at[k, me],
                send_sem=send_sem.at[k, peer],
                recv_sem=recv_sem.at[k, me],
                device_id=device(peer),
                device_id_type=mesh_id,
            )
            copy.start()
            sent.append(copy)
        for d in range(1, count):
            peer = (me + d) % count
            pltpu.make_async_remote_copy(
                src_ref=send_buf.at[k],
                dst_ref=recv.at[k, peer],
                send_sem=send_sem.at[k, peer],
                recv_sem=recv_sem.at[k, peer],
                device_id=device(peer),
                device_id_type=mesh_id,
            ).wait_recv()
        for copy in sent:
            copy.wait_send()
        total = recv[k, 0]
        for j in range(1, count):
            total = total + recv[k, j]
        return total

    partial = phase(vec, send_y, recv_y, sy, ry, ny, my, along_y)
    return phase(partial, send_x, recv_x, sx, rx, nx, mx, along_x)


def solve_kernel(ny, nx, tu_ref, tv_ref, eta_ref, inside_ref, own_ref, out_ref, frame, hsend, hrecv, *bufs):
    mesh_id = pl.DeviceIdType.MESH
    member = lax.axis_index("member")
    my = lax.axis_index("gridy")
    mx = lax.axis_index("gridx")
    along_y = lambda p: (member, p, mx)
    along_x = lambda p: (member, my, p)
    barrier = pltpu.get_barrier_semaphore()
    for d in range(1, ny):
        pl.semaphore_signal(barrier, 1, device_id=along_y((my + d) % ny), device_id_type=mesh_id)
    for d in range(1, nx):
        pl.semaphore_signal(barrier, 1, device_id=along_x((mx + d) % nx), device_id_type=mesh_id)
    for dy in (1, ny - 1):
        for dx in (1, nx - 1):
            pl.semaphore_signal(
                barrier, 1, device_id=(member, (my + dy) % ny, (mx + dx) % nx), device_id_type=mesh_id
            )
    rows, cols = eta_ref.shape[1], eta_ref.shape[2]
    wide_rows, wide_cols = frame.shape[2], frame.shape[3]
    band = (wide_rows - rows) // 2
    block = (wide_cols - cols) // 2
    frame[0, :, 0:rows, 0:cols] = tu_ref[...]
    frame[1, :, 0:rows, 0:cols] = tv_ref[...]
    frame[2, :, 0:rows, 0:cols] = eta_ref[...]
    pl.semaphore_wait(barrier, (ny - 1) + (nx - 1) + 4)

    def halo_copies(first, moves):
        started = []
        for slot, (src, dst, device) in enumerate(moves, start=first):
            copy = pltpu.make_async_remote_copy(
                src_ref=src, dst_ref=dst, send_sem=hsend.at[slot], recv_sem=hrecv.at[slot],
                device_id=device, device_id_type=mesh_id,
            )
            copy.start()
            started.append(copy)
        for copy in started:
            copy.wait()

    up, down = (my + 1) % ny, (my + ny - 1) % ny
    right, left = (mx + 1) % nx, (mx + nx - 1) % nx
    top_rows = slice(0, band)
    low_rows = slice(rows - band, rows)
    own_rows = slice(0, rows)
    west_part = slice(0, block)
    east_part = slice(cols - block, cols)
    own_cols = slice(0, cols)
    north_halo = slice(rows, rows + band)
    south_halo = slice(rows + band, wide_rows)
    east_halo = slice(cols, cols + block)
    west_halo = slice(cols + block, wide_cols)
    halo_copies(0, [
        (frame.at[:, :, top_rows, own_cols], frame.at[:, :, north_halo, own_cols], (member, down, mx)),
        (frame.at[:, :, low_rows, own_cols], frame.at[:, :, south_halo, own_cols], (member, up, mx)),
        (frame.at[:, :, own_rows, west_part], frame.at[:, :, own_rows, east_halo], (member, my, left)),
        (frame.at[:, :, own_rows, east_part], frame.at[:, :, own_rows, west_halo], (member, my, right)),
        (frame.at[:, :, top_rows, west_part], frame.at[:, :, north_halo, east_halo], (member, down, left)),
        (frame.at[:, :, top_rows, east_part], frame.at[:, :, north_halo, west_halo], (member, down, right)),
        (frame.at[:, :, low_rows, west_part], frame.at[:, :, south_halo, east_halo], (member, up, left)),
        (frame.at[:, :, low_rows, east_part], frame.at[:, :, south_halo, west_halo], (member, up, right)),
    ])

    members = eta_ref.shape[0]
    inside = inside_ref[...]
    own = own_ref[...] > 0.5

    def east(f):
        return pltpu.roll(f, wide_cols - 1, 1)

    def west(f):
        return pltpu.roll(f, 1, 1)

    def north(f):
        return pltpu.roll(f, wide_rows - 1, 0)

    def south(f):
        return pltpu.roll(f, 1, 0)

    def apply(f):
        return ((1.0 + 4.0 * SURF_C) * f - SURF_C * (east(f) + west(f) + north(f) + south(f))) * inside

    def total(f):
        return jnp.sum(f[0:rows, 0:cols], axis=(0, 1), keepdims=True)

    residual = []
    for m in range(members):
        trans_u = frame[0, m] * inside
        trans_v = frame[1, m] * inside
        level = frame[2, m] * inside
        residual.append(
            (level - DIV_K * 0.5 * (east(trans_u) - west(trans_u) + (north(trans_v) - south(trans_v)))) * inside
        )
    lane = lax.broadcasted_iota(jnp.int32, (8, 128), 1)
    direction = [None] * members
    image_dir = [None] * members
    solution = [None] * members
    gamma_prev = [None] * members
    alpha_prev = [None] * members
    for count in range(ITERS):
        image_res = [apply(residual[m]) for m in range(members)]
        vec = jnp.zeros((8, 128), jnp.float32)
        for m in range(members):
            vec = jnp.where(lane == 2 * m, total(residual[m] * residual[m]), vec)
            vec = jnp.where(lane == 2 * m + 1, total(residual[m] * image_res[m]), vec)
        sums = exchange_sum(count, vec, ny, nx, bufs, (my, mx, along_y, along_x))
        for m in range(members):
            gamma = sums[0:1, 2 * m : 2 * m + 1]
            delta = sums[0:1, 2 * m + 1 : 2 * m + 2]
            if count == 0:
                alpha = gamma / delta
                direction[m] = residual[m]
                image_dir[m] = image_res[m]
                solution[m] = alpha * direction[m]
            else:
                beta = gamma / gamma_prev[m]
                alpha = gamma / (delta - beta * gamma / alpha_prev[m])
                direction[m] = residual[m] + beta * direction[m]
                image_dir[m] = image_res[m] + beta * image_dir[m]
                solution[m] = solution[m] + alpha * direction[m]
            if count < ITERS - 1:
                residual[m] = residual[m] - alpha * image_dir[m]
            gamma_prev[m] = gamma
            alpha_prev[m] = alpha
    for m in range(members):
        x = solution[m]
        out_ref[0, m] = x[0:rows, 0:cols]
        out_ref[1, m] = (east(x) - west(x))[0:rows, 0:cols]
        out_ref[2, m] = (north(x) - south(x))[0:rows, 0:cols]


def surface_kernel_solve(trans_u, trans_v, eta, inside, own):
    ny = lax.axis_size("gridy")
    nx = lax.axis_size("gridx")
    members, rows, cols = eta.shape
    fields = 3
    return pl.pallas_call(
        functools.partial(solve_kernel, ny, nx),
        out_shape=jax.ShapeDtypeStruct((3, members, rows, cols), jnp.float32),
        in_specs=[pl.BlockSpec(memory_space=pltpu.VMEM)] * 5,
        out_specs=pl.BlockSpec(memory_space=pltpu.VMEM),
        scratch_shapes=[
            pltpu.VMEM((fields, members) + inside.shape, jnp.float32),
            pltpu.SemaphoreType.DMA((8,)),
            pltpu.SemaphoreType.DMA((8,)),
            pltpu.VMEM((ITERS, 8, 128), jnp.float32),
            pltpu.VMEM((ITERS, ny, 8, 128), jnp.float32),
            pltpu.VMEM((ITERS, 8, 128), jnp.float32),
            pltpu.VMEM((ITERS, nx, 8, 128), jnp.float32),
            pltpu.SemaphoreType.DMA((ITERS, ny)),
            pltpu.SemaphoreType.DMA((ITERS, ny)),
            pltpu.SemaphoreType.DMA((ITERS, nx)),
            pltpu.SemaphoreType.DMA((ITERS, nx)),
        ],
        compiler_params=pltpu.CompilerParams(collective_id=1, has_side_effects=True),
    )(trans_u, trans_v, eta, inside, own)


def volume_kernel(ny, temp_ref, salt_ref, uvel_ref, vvel_ref, land_ref, n_ref, s_ref, e_ref, w_ref,
                  tn_ref, sn_ref, us_ref, vs_ref, tu_ref, tv_ref):
    levels, rows, cols = temp_ref.shape[1], temp_ref.shape[2], temp_ref.shape[3]
    row = lax.broadcasted_iota(jnp.int32, (rows, cols), 0)
    col = lax.broadcasted_iota(jnp.int32, (rows, cols), 1)
    tile_row = lax.axis_index("gridy")
    north_keep = jnp.where(tile_row < ny - 1, 1.0, 0.0)
    south_keep = jnp.where(tile_row > 0, 1.0, 0.0)
    latitude = (tile_row * rows + row).astype(jnp.float32) + 0.5
    top = row == rows - 1
    bottom = row == 0
    right = col == cols - 1
    left = col == 0
    ocean = land_ref[...].astype(jnp.float32)
    cor = CORI_K * (2.0 * latitude / (rows * ny) - 1.0)

    def around(f, rims):
        n, s, e, w = rims
        return (
            jnp.where(right, e, pltpu.roll(f, cols - 1, 1)),
            jnp.where(left, w, pltpu.roll(f, 1, 1)),
            jnp.where(top, n, pltpu.roll(f, rows - 1, 0)),
            jnp.where(bottom, s, pltpu.roll(f, 1, 0)),
        )

    def rims_of(k, l, m):
        return (n_ref[k, m, l] * north_keep, s_ref[k, m, l] * south_keep, e_ref[k, m, l], w_ref[k, m, l])

    for m in range(temp_ref.shape[0]):
        running = None
        running_rims = None
        tu = None
        tv = None
        for l in range(levels):
            t = temp_ref[m, l]
            s = salt_ref[m, l]
            u = uvel_ref[m, l]
            v = vvel_ref[m, l]
            rt, rs, ru, rv = rims_of(0, l, m), rims_of(1, l, m), rims_of(2, l, m), rims_of(3, l, m)
            layer = BETA_S * s - ALPHA_T * t
            layer_rims = tuple(BETA_S * b - ALPHA_T * a for a, b in zip(rt, rs))
            if running is None:
                running, running_rims = layer, layer_rims
            else:
                running = running + layer
                running_rims = tuple(a + b for a, b in zip(running_rims, layer_rims))
            press = PRESS_K * running
            press_rims = tuple(PRESS_K * a for a in running_rims)
            te, tw, tn, ts = around(t, rt)
            se, sw, sn, ss = around(s, rs)
            ue, uw, un, us = around(u, ru)
            ve, vw, vn, vs = around(v, rv)
            pe, pw, pn, ps = around(press, press_rims)
            tn_ref[m, l] = ocean * (
                t - STEP_DT * 0.5 * (u * (te - tw) + v * (tn - ts)) + KAPPA * (te + tw + tn + ts - 4.0 * t)
            )
            sn_ref[m, l] = ocean * (
                s - STEP_DT * 0.5 * (u * (se - sw) + v * (sn - ss)) + KAPPA * (se + sw + sn + ss - 4.0 * s)
            )
            ustar = ocean * (
                u + STEP_DT * (cor * v - 0.5 * (pe - pw) - DRAG_K * u) + VISCOSITY * (ue + uw + un + us - 4.0 * u)
            )
            vstar = ocean * (
                v + STEP_DT * (-cor * u - 0.5 * (pn - ps) - DRAG_K * v) + VISCOSITY * (ve + vw + vn + vs - 4.0 * v)
            )
            us_ref[m, l] = ustar
            vs_ref[m, l] = vstar
            tu = ustar if tu is None else tu + ustar
            tv = vstar if tv is None else tv + vstar
        tu_ref[m] = tu
        tv_ref[m] = tv


def volume_step(temp, salt, uvel, vvel, land_mask, rims):
    members, levels, rows, cols = temp.shape
    field = pl.BlockSpec((1, levels, rows, cols), lambda m: (m, 0, 0, 0))
    plane = pl.BlockSpec((rows, cols), lambda m: (0, 0))
    north, south, east, west = rims
    row_rim = pl.BlockSpec((4, 1, levels, 1, cols), lambda m: (0, m, 0, 0, 0))
    col_rim = pl.BlockSpec((4, 1, levels, rows, 1), lambda m: (0, m, 0, 0, 0))
    surface = pl.BlockSpec((1, rows, cols), lambda m: (m, 0, 0))
    volume_shape = jax.ShapeDtypeStruct(temp.shape, jnp.float32)
    surface_shape = jax.ShapeDtypeStruct((members, rows, cols), jnp.float32)
    vmem = pl.BlockSpec(memory_space=pltpu.VMEM)
    return pl.pallas_call(
        functools.partial(volume_kernel, lax.axis_size("gridy")),
        in_specs=[vmem] * 9,
        out_specs=[vmem] * 6,
        out_shape=[volume_shape] * 4 + [surface_shape] * 2,
    )(temp, salt, uvel, vvel, land_mask, north, south, east, west)


def ring(axis):
    count = lax.axis_size(axis)
    forward = [(i, (i + 1) % count) for i in range(count)]
    backward = [((i + 1) % count, i) for i in range(count)]
    return forward, backward


def exchange(block, ydim, xdim, south_keep, north_keep):
    fwd_y, bwd_y = ring("gridy")
    fwd_x, bwd_x = ring("gridx")
    rows = block.shape[ydim]
    cols = block.shape[xdim]
    north = lax.ppermute(lax.slice_in_dim(block, 0, 1, axis=ydim), "gridy", bwd_y) * north_keep
    south = lax.ppermute(lax.slice_in_dim(block, rows - 1, rows, axis=ydim), "gridy", fwd_y) * south_keep
    east = lax.ppermute(lax.slice_in_dim(block, 0, 1, axis=xdim), "gridx", bwd_x)
    west = lax.ppermute(lax.slice_in_dim(block, cols - 1, cols, axis=xdim), "gridx", fwd_x)
    return (east, west, north, south)


def exchange_fields(fields, south_keep, north_keep):
    fwd_y, bwd_y = ring("gridy")
    fwd_x, bwd_x = ring("gridx")
    north = lax.ppermute(jnp.stack([f[..., :1, :] for f in fields]), "gridy", bwd_y)
    south = lax.ppermute(jnp.stack([f[..., -1:, :] for f in fields]), "gridy", fwd_y)
    east = lax.ppermute(jnp.stack([f[..., :, :1] for f in fields]), "gridx", bwd_x)
    west = lax.ppermute(jnp.stack([f[..., :, -1:] for f in fields]), "gridx", fwd_x)
    return (north, south, east, west)


def sides(field, rims, ydim, xdim):
    east, west, north, south = rims
    rows = field.shape[ydim]
    cols = field.shape[xdim]
    east_side = jnp.concatenate([lax.slice_in_dim(field, 1, cols, axis=xdim), east], axis=xdim)
    west_side = jnp.concatenate([west, lax.slice_in_dim(field, 0, cols - 1, axis=xdim)], axis=xdim)
    north_side = jnp.concatenate([lax.slice_in_dim(field, 1, rows, axis=ydim), north], axis=ydim)
    south_side = jnp.concatenate([south, lax.slice_in_dim(field, 0, rows - 1, axis=ydim)], axis=ydim)
    return (east_side, west_side, north_side, south_side)


def pressure(temp, salt):
    return PRESS_K * jnp.cumsum(BETA_S * salt - ALPHA_T * temp, axis=-3)


def surface_apply(field, rims):
    east_side, west_side, north_side, south_side = sides(field, rims, 1, 2)
    return (1.0 + 4.0 * SURF_C) * field - SURF_C * (east_side + west_side + north_side + south_side)


def member_total(values):
    return jnp.sum(values, axis=(1, 2))


def widen(values):
    return values[:, None, None]


def combine(a, fa, b, fb):
    def one(u, v):
        left = u if a is None else widen(a) * u
        return left + (v if b is None else widen(b) * v)

    return one(fa[0], fb[0]), tuple(one(u, v) for u, v in zip(fa[1], fb[1]))


def scaled(a, fa):
    return widen(a) * fa[0], tuple(widen(a) * u for u in fa[1])


def padded_2(block, sides_of, width):
    for axis, dim in sides_of:
        count = lax.axis_size(axis)
        forward = [(i, (i + 1) % count) for i in range(count)]
        backward = [((i + 1) % count, i) for i in range(count)]
        size = block.shape[dim]
        low = lax.ppermute(lax.slice_in_dim(block, size - width, size, axis=dim), axis, forward)
        high = lax.ppermute(lax.slice_in_dim(block, 0, width, axis=dim), axis, backward)
        block = jnp.concatenate([low, block, high], axis=dim)
    return block


def crop(field, by):
    if by == 0:
        return field
    return field[..., by:-by, by:-by]


def around(field):
    return (
        field[..., 1:-1, 1:-1],
        field[..., 1:-1, 2:],
        field[..., 1:-1, :-2],
        field[..., 2:, 1:-1],
        field[..., :-2, 1:-1],
    )


def rows_at(inside, full, want):
    cut = full - want
    return inside if cut == 0 else inside[cut:-cut]


def apply_wide(field, inside):
    centre, east, west, north, south = around(field)
    return ((1.0 + 4.0 * SURF_C) * centre - SURF_C * (east + west + north + south)) * inside


def surface_solve(rhs, inside, width, full):
    residual, wide_r = rhs, width
    gamma_prev = None
    alpha_prev = None
    for count in range(ITERS):
        image_res = apply_wide(residual, rows_at(inside, full, wide_r - 1))
        own_res = crop(residual, wide_r)
        own_img = crop(image_res, wide_r - 1)
        dots = grid_sum(jnp.stack([member_total(own_res * own_res), member_total(own_res * own_img)]))
        gamma, delta = dots[0], dots[1]
        if count == 0:
            alpha = gamma / delta
            direction, wide_p = residual, wide_r
            image_dir, wide_s = image_res, wide_r - 1
            solution, wide_x = widen(alpha) * direction, wide_r
        else:
            beta = gamma / gamma_prev
            alpha = gamma / (delta - beta * gamma / alpha_prev)
            direction = residual + widen(beta) * crop(direction, wide_p - wide_r)
            wide_p = wide_r
            image_dir = image_res + widen(beta) * crop(image_dir, wide_s - (wide_r - 1))
            wide_s = wide_r - 1
            solution = crop(solution, wide_x - wide_r) + widen(alpha) * direction
            wide_x = wide_r
        if count < ITERS - 1:
            residual = crop(residual, 1) - widen(alpha) * image_dir
            wide_r -= 1
        gamma_prev = gamma
        alpha_prev = alpha
    return solution


def shards(temp, salt, uvel, vvel, eta, land_mask, clone_source):
    levels = temp.shape[1]
    rows = temp.shape[2]
    cols = temp.shape[3]
    ocean = land_mask.astype(jnp.float32)
    tile_row = lax.axis_index("gridy")
    tile_count = lax.axis_size("gridy")
    total_rows = rows * tile_count
    total_cols = cols * lax.axis_size("gridx")
    south_keep = (tile_row > 0).astype(jnp.float32)
    north_keep = (tile_row < tile_count - 1).astype(jnp.float32)
    latitude = (tile_row * rows + jnp.arange(rows, dtype=jnp.int32)).astype(jnp.float32) + 0.5
    coriolis = (CORI_K * (2.0 * latitude / total_rows - 1.0))[:, None]
    cor_tile = jnp.broadcast_to(coriolis, (rows, cols))
    band = 8
    block = 128
    frame_rows = rows + 2 * band
    frame_cols = cols + 2 * block
    row_at = lax.broadcasted_iota(jnp.int32, (frame_rows, frame_cols), 0)
    col_at = lax.broadcasted_iota(jnp.int32, (frame_rows, frame_cols), 1)
    global_row = tile_row * rows + jnp.where(row_at < rows + band, row_at, row_at - frame_rows)
    wide_inside = ((global_row >= 0) & (global_row < total_rows)).astype(jnp.float32)
    own_mask = ((row_at < rows) & (col_at < cols)).astype(jnp.float32)
    for count in range(STEPS):
        fields = (temp, salt, uvel, vvel)
        rims = exchange_fields(fields, south_keep, north_keep)
        temp_next, salt_next, ustar, vstar, trans_u, trans_v = volume_step(
            temp, salt, uvel, vvel, land_mask, rims
        )
        solved = surface_kernel_solve(trans_u, trans_v, eta, wide_inside, own_mask)
        eta = solved[0]
        east_west = solved[1]
        north_south = solved[2]
        uvel = ocean * (ustar - GRAV_K * 0.5 * east_west[:, None])
        vvel = ocean * (vstar - GRAV_K * 0.5 * north_south[:, None])
        if count == STEPS - 1:
            tracers_other = lax.ppermute(jnp.stack((temp_next, salt_next)), "member", [(0, 1), (1, 0)])
        temp = temp_next
        salt = salt_next
    zonal_scale = 1.0 / jnp.sqrt(jnp.float32(total_cols))
    score_scale = 1.0 / jnp.sqrt(jnp.float32(levels * total_rows))
    lat_weight = latitude / total_rows
    members = temp.shape[0]
    zonal_local = jnp.sum(vvel, axis=3)
    depth_weight = (levels - jnp.arange(levels, dtype=jnp.int32)).astype(jnp.float32)
    score_local = jnp.sum(zonal_local * depth_weight[None, :, None] * lat_weight[None, None, :], axis=(1, 2))
    slot = lax.broadcasted_iota(jnp.int32, (tile_count, 1, 1, 1), 0) == tile_row
    zonal_slots = jnp.where(slot, zonal_local[None], 0.0).reshape(-1, 128)
    score_row = jnp.zeros((8, 128), jnp.float32).at[0, :members].set(score_local)
    summed = grid_sum(jnp.concatenate([zonal_slots, score_row], axis=0))
    zonal_whole = summed[: zonal_slots.shape[0]].reshape((tile_count,) + zonal_local.shape)
    zonal_whole = jnp.sum(jnp.where(slot, zonal_whole, 0.0), axis=0)
    overturn = jnp.cumsum(zonal_whole, axis=1) * zonal_scale
    score = summed[zonal_slots.shape[0], :members] * (zonal_scale * score_scale)
    swap = [(0, 1), (1, 0)]
    mine = lax.axis_index("member")
    score_slab = jnp.zeros((members, 1) + eta.shape[1:], jnp.float32).at[:, 0, 0, 0].set(score)
    flows = jnp.concatenate([uvel, vvel, eta[:, None], score_slab], axis=1)
    flows_other = lax.ppermute(flows, "member", swap)
    score_other = flows_other[:, 2 * levels + 1, 0, 0]
    every_score = jnp.where(
        mine == 0, jnp.concatenate([score, score_other]), jnp.concatenate([score_other, score])
    )
    here = (clone_source // members) == mine
    local_at = clone_source % members

    def pick(local, other):
        chosen = []
        for place in range(members):
            from_here = lax.dynamic_index_in_dim(local, local_at[place], 0, keepdims=False)
            from_other = lax.dynamic_index_in_dim(other, local_at[place], 0, keepdims=False)
            chosen.append(jnp.where(here[place], from_here, from_other))
        return jnp.stack(chosen)

    new_temp = pick(temp, tracers_other[0])
    new_salt = pick(salt, tracers_other[1])
    new_flows = pick(flows[:, : 2 * levels + 1], flows_other[:, : 2 * levels + 1])
    clone_weight = jnp.take(every_score, clone_source, axis=0) - jnp.mean(every_score)
    return (
        new_temp,
        new_salt,
        new_flows[:, :levels],
        new_flows[:, levels : 2 * levels],
        new_flows[:, 2 * levels],
        overturn,
        clone_weight,
    )


def solution(mesh):
    in_specs = (
        P("member", None, "gridy", "gridx"),
        P("member", None, "gridy", "gridx"),
        P("member", None, "gridy", "gridx"),
        P("member", None, "gridy", "gridx"),
        P("member", "gridy", "gridx"),
        P("gridy", "gridx"),
        P("member"),
    )
    out_specs = (
        P("member", None, "gridy", "gridx"),
        P("member", None, "gridy", "gridx"),
        P("member", None, "gridy", "gridx"),
        P("member", None, "gridy", "gridx"),
        P("member", "gridy", "gridx"),
        P("member", None, "gridy"),
        P("member"),
    )
    return jax.shard_map(shards, mesh=mesh, in_specs=in_specs, out_specs=out_specs, check_vma=False)
```

```python
import functools

import jax
import jax.numpy as jnp
from jax import lax
from jax.experimental import pallas as pl
from jax.experimental.pallas import tpu as pltpu
from jax.sharding import PartitionSpec as P

STEPS = 2
ITERS = 3


ALPHA_T = 0.8
BETA_S = 0.6
PRESS_K = 0.25
STEP_DT = 0.1
KAPPA = 0.1
VISCOSITY = 0.1
DRAG_K = 0.05
CORI_K = 1.0
SURF_C = 4.0
DIV_K = 0.5
GRAV_K = 0.5


def tree_sum(values, axes):
    for axis in axes:
        count = lax.axis_size(axis)
        step = 1
        while step < count:
            pairs = [(i, i ^ step) for i in range(count)]
            values = values + lax.ppermute(values, axis, pairs)
            step *= 2
    return values


def gather_sum_kernel(ny, nx, x_ref, o_ref, recv_y, recv_x, part, send_y, rsem_y, send_x, rsem_x):
    mesh_id = pl.DeviceIdType.MESH
    member = lax.axis_index("member")
    my = lax.axis_index("gridy")
    mx = lax.axis_index("gridx")
    barrier = pltpu.get_barrier_semaphore()
    for d in range(1, ny):
        pl.semaphore_signal(barrier, 1, device_id=(member, (my + d) % ny, mx), device_id_type=mesh_id)
    for d in range(1, nx):
        pl.semaphore_signal(barrier, 1, device_id=(member, my, (mx + d) % nx), device_id_type=mesh_id)
    pl.semaphore_wait(barrier, (ny - 1) + (nx - 1))

    def phase(src, recv, send_sem, recv_sem, count, me, device):
        recv[me] = src[...]
        sent = []
        for d in range(1, count):
            peer = (me + d) % count
            copy = pltpu.make_async_remote_copy(
                src_ref=src,
                dst_ref=recv.at[me],
                send_sem=send_sem.at[peer],
                recv_sem=recv_sem.at[me],
                device_id=device(peer),
                device_id_type=mesh_id,
            )
            copy.start()
            sent.append(copy)
        for d in range(1, count):
            peer = (me + d) % count
            pltpu.make_async_remote_copy(
                src_ref=src,
                dst_ref=recv.at[peer],
                send_sem=send_sem.at[peer],
                recv_sem=recv_sem.at[peer],
                device_id=device(peer),
                device_id_type=mesh_id,
            ).wait_recv()
        for copy in sent:
            copy.wait_send()
        total = recv[0]
        for j in range(1, count):
            total = total + recv[j]
        return total

    part[...] = phase(x_ref, recv_y, send_y, rsem_y, ny, my, lambda p: (member, p, mx))
    o_ref[...] = phase(part, recv_x, send_x, rsem_x, nx, mx, lambda p: (member, my, p))


def grid_sum(values):
    ny = lax.axis_size("gridy")
    nx = lax.axis_size("gridx")
    shape = values.shape
    return pl.pallas_call(
        functools.partial(gather_sum_kernel, ny, nx),
        out_shape=jax.ShapeDtypeStruct(shape, values.dtype),
        in_specs=[pl.BlockSpec(memory_space=pltpu.VMEM)],
        out_specs=pl.BlockSpec(memory_space=pltpu.VMEM),
        scratch_shapes=[
            pltpu.VMEM((ny,) + shape, values.dtype),
            pltpu.VMEM((nx,) + shape, values.dtype),
            pltpu.VMEM(shape, values.dtype),
            pltpu.SemaphoreType.DMA((ny,)),
            pltpu.SemaphoreType.DMA((ny,)),
            pltpu.SemaphoreType.DMA((nx,)),
            pltpu.SemaphoreType.DMA((nx,)),
        ],
        compiler_params=pltpu.CompilerParams(collective_id=0, has_side_effects=True),
    )(values)


def exchange_sum(k, vec, ny, nx, bufs, device_ids):
    send_y, recv_y, send_x, recv_x, sy, ry, sx, rx = bufs
    my, mx, along_y, along_x = device_ids
    mesh_id = pl.DeviceIdType.MESH

    def phase(value, send_buf, recv, send_sem, recv_sem, count, me, device):
        send_buf[k] = value
        recv[k, me] = value
        sent = []
        for d in range(1, count):
            peer = (me + d) % count
            copy = pltpu.make_async_remote_copy(
                src_ref=send_buf.at[k],
                dst_ref=recv.at[k, me],
                send_sem=send_sem.at[k, peer],
                recv_sem=recv_sem.at[k, me],
                device_id=device(peer),
                device_id_type=mesh_id,
            )
            copy.start()
            sent.append(copy)
        for d in range(1, count):
            peer = (me + d) % count
            pltpu.make_async_remote_copy(
                src_ref=send_buf.at[k],
                dst_ref=recv.at[k, peer],
                send_sem=send_sem.at[k, peer],
                recv_sem=recv_sem.at[k, peer],
                device_id=device(peer),
                device_id_type=mesh_id,
            ).wait_recv()
        for copy in sent:
            copy.wait_send()
        total = recv[k, 0]
        for j in range(1, count):
            total = total + recv[k, j]
        return total

    partial = phase(vec, send_y, recv_y, sy, ry, ny, my, along_y)
    return phase(partial, send_x, recv_x, sx, rx, nx, mx, along_x)


def solve_kernel(ny, nx, tu_ref, tv_ref, eta_ref, inside_ref, out_ref, frame, hsend, hrecv, *bufs):
    mesh_id = pl.DeviceIdType.MESH
    member = lax.axis_index("member")
    my = lax.axis_index("gridy")
    mx = lax.axis_index("gridx")
    along_y = lambda p: (member, p, mx)
    along_x = lambda p: (member, my, p)
    barrier = pltpu.get_barrier_semaphore()
    for d in range(1, ny):
        pl.semaphore_signal(barrier, 1, device_id=along_y((my + d) % ny), device_id_type=mesh_id)
    for d in range(1, nx):
        pl.semaphore_signal(barrier, 1, device_id=along_x((mx + d) % nx), device_id_type=mesh_id)
    for dy in (1, ny - 1):
        for dx in (1, nx - 1):
            pl.semaphore_signal(
                barrier, 1, device_id=(member, (my + dy) % ny, (mx + dx) % nx), device_id_type=mesh_id
            )
    rows, cols = eta_ref.shape[1], eta_ref.shape[2]
    wide_rows, wide_cols = frame.shape[2], frame.shape[3]
    band = (wide_rows - rows) // 2
    block = (wide_cols - cols) // 2
    frame[0, :, 0:rows, 0:cols] = tu_ref[...]
    frame[1, :, 0:rows, 0:cols] = tv_ref[...]
    frame[2, :, 0:rows, 0:cols] = eta_ref[...]
    pl.semaphore_wait(barrier, (ny - 1) + (nx - 1) + 4)

    def halo_copies(first, moves):
        started = []
        for slot, (src, dst, device) in enumerate(moves, start=first):
            copy = pltpu.make_async_remote_copy(
                src_ref=src, dst_ref=dst, send_sem=hsend.at[slot], recv_sem=hrecv.at[slot],
                device_id=device, device_id_type=mesh_id,
            )
            copy.start()
            started.append(copy)
        for copy in started:
            copy.wait()

    up, down = (my + 1) % ny, (my + ny - 1) % ny
    right, left = (mx + 1) % nx, (mx + nx - 1) % nx
    top_rows = slice(0, band)
    low_rows = slice(rows - band, rows)
    own_rows = slice(0, rows)
    west_part = slice(0, block)
    east_part = slice(cols - block, cols)
    own_cols = slice(0, cols)
    north_halo = slice(rows, rows + band)
    south_halo = slice(rows + band, wide_rows)
    east_halo = slice(cols, cols + block)
    west_halo = slice(cols + block, wide_cols)
    halo_copies(0, [
        (frame.at[:, :, top_rows, own_cols], frame.at[:, :, north_halo, own_cols], (member, down, mx)),
        (frame.at[:, :, low_rows, own_cols], frame.at[:, :, south_halo, own_cols], (member, up, mx)),
        (frame.at[:, :, own_rows, west_part], frame.at[:, :, own_rows, east_halo], (member, my, left)),
        (frame.at[:, :, own_rows, east_part], frame.at[:, :, own_rows, west_halo], (member, my, right)),
        (frame.at[:, :, top_rows, west_part], frame.at[:, :, north_halo, east_halo], (member, down, left)),
        (frame.at[:, :, top_rows, east_part], frame.at[:, :, north_halo, west_halo], (member, down, right)),
        (frame.at[:, :, low_rows, west_part], frame.at[:, :, south_halo, east_halo], (member, up, left)),
        (frame.at[:, :, low_rows, east_part], frame.at[:, :, south_halo, west_halo], (member, up, right)),
    ])

    members = eta_ref.shape[0]
    inside = inside_ref[...]

    def east(f):
        return pltpu.roll(f, wide_cols - 1, 1)

    def west(f):
        return pltpu.roll(f, 1, 1)

    def north(f):
        return pltpu.roll(f, wide_rows - 1, 0)

    def south(f):
        return pltpu.roll(f, 1, 0)

    def apply(f):
        return ((1.0 + 4.0 * SURF_C) * f - SURF_C * (east(f) + west(f) + north(f) + south(f))) * inside

    def total(f):
        return jnp.sum(f[0:rows, 0:cols], axis=(0, 1), keepdims=True)

    residual = []
    for m in range(members):
        trans_u = frame[0, m] * inside
        trans_v = frame[1, m] * inside
        level = frame[2, m] * inside
        residual.append(
            (level - DIV_K * 0.5 * (east(trans_u) - west(trans_u) + (north(trans_v) - south(trans_v)))) * inside
        )
    lane = lax.broadcasted_iota(jnp.int32, (8, 128), 1)
    direction = [None] * members
    image_dir = [None] * members
    solution = [None] * members
    gamma_prev = [None] * members
    alpha_prev = [None] * members
    for count in range(ITERS):
        image_res = [apply(residual[m]) for m in range(members)]
        vec = jnp.zeros((8, 128), jnp.float32)
        for m in range(members):
            vec = jnp.where(lane == 2 * m, total(residual[m] * residual[m]), vec)
            vec = jnp.where(lane == 2 * m + 1, total(residual[m] * image_res[m]), vec)
        sums = exchange_sum(count, vec, ny, nx, bufs, (my, mx, along_y, along_x))
        for m in range(members):
            gamma = sums[0:1, 2 * m : 2 * m + 1]
            delta = sums[0:1, 2 * m + 1 : 2 * m + 2]
            if count == 0:
                alpha = gamma / delta
                direction[m] = residual[m]
                image_dir[m] = image_res[m]
                solution[m] = alpha * direction[m]
            else:
                beta = gamma / gamma_prev[m]
                alpha = gamma / (delta - beta * gamma / alpha_prev[m])
                direction[m] = residual[m] + beta * direction[m]
                image_dir[m] = image_res[m] + beta * image_dir[m]
                solution[m] = solution[m] + alpha * direction[m]
            if count < ITERS - 1:
                residual[m] = residual[m] - alpha * image_dir[m]
            gamma_prev[m] = gamma
            alpha_prev[m] = alpha
    for m in range(members):
        x = solution[m]
        out_ref[0, m] = x[0:rows, 0:cols]
        out_ref[1, m] = (east(x) - west(x))[0:rows, 0:cols]
        out_ref[2, m] = (north(x) - south(x))[0:rows, 0:cols]


def surface_kernel_solve(trans_u, trans_v, eta, inside):
    ny = lax.axis_size("gridy")
    nx = lax.axis_size("gridx")
    members, rows, cols = eta.shape
    fields = 3
    return pl.pallas_call(
        functools.partial(solve_kernel, ny, nx),
        out_shape=jax.ShapeDtypeStruct((3, members, rows, cols), jnp.float32),
        in_specs=[pl.BlockSpec(memory_space=pltpu.VMEM)] * 4,
        out_specs=pl.BlockSpec(memory_space=pltpu.VMEM),
        scratch_shapes=[
            pltpu.VMEM((fields, members) + inside.shape, jnp.float32),
            pltpu.SemaphoreType.DMA((8,)),
            pltpu.SemaphoreType.DMA((8,)),
            pltpu.VMEM((ITERS, 8, 128), jnp.float32),
            pltpu.VMEM((ITERS, ny, 8, 128), jnp.float32),
            pltpu.VMEM((ITERS, 8, 128), jnp.float32),
            pltpu.VMEM((ITERS, nx, 8, 128), jnp.float32),
            pltpu.SemaphoreType.DMA((ITERS, ny)),
            pltpu.SemaphoreType.DMA((ITERS, ny)),
            pltpu.SemaphoreType.DMA((ITERS, nx)),
            pltpu.SemaphoreType.DMA((ITERS, nx)),
        ],
        compiler_params=pltpu.CompilerParams(collective_id=1, has_side_effects=True),
    )(trans_u, trans_v, eta, inside)


def volume_kernel(ny, temp_ref, salt_ref, uvel_ref, vvel_ref, land_ref, n_ref, s_ref, e_ref, w_ref,
                  tn_ref, sn_ref, us_ref, vs_ref, tu_ref, tv_ref):
    levels, rows, cols = temp_ref.shape[1], temp_ref.shape[2], temp_ref.shape[3]
    row = lax.broadcasted_iota(jnp.int32, (rows, cols), 0)
    col = lax.broadcasted_iota(jnp.int32, (rows, cols), 1)
    tile_row = lax.axis_index("gridy")
    north_keep = jnp.where(tile_row < ny - 1, 1.0, 0.0)
    south_keep = jnp.where(tile_row > 0, 1.0, 0.0)
    latitude = (tile_row * rows + row).astype(jnp.float32) + 0.5
    top = row == rows - 1
    bottom = row == 0
    right = col == cols - 1
    left = col == 0
    ocean = land_ref[...].astype(jnp.float32)
    cor = CORI_K * (2.0 * latitude / (rows * ny) - 1.0)

    def around(f, rims):
        n, s, e, w = rims
        return (
            jnp.where(right, e, pltpu.roll(f, cols - 1, 1)),
            jnp.where(left, w, pltpu.roll(f, 1, 1)),
            jnp.where(top, n, pltpu.roll(f, rows - 1, 0)),
            jnp.where(bottom, s, pltpu.roll(f, 1, 0)),
        )

    def rims_of(k, l):
        return (n_ref[k, 0, l] * north_keep, s_ref[k, 0, l] * south_keep, e_ref[k, 0, l], w_ref[k, 0, l])

    running = None
    running_rims = None
    tu = None
    tv = None
    for l in range(levels):
        t = temp_ref[0, l]
        s = salt_ref[0, l]
        u = uvel_ref[0, l]
        v = vvel_ref[0, l]
        rt, rs, ru, rv = rims_of(0, l), rims_of(1, l), rims_of(2, l), rims_of(3, l)
        layer = BETA_S * s - ALPHA_T * t
        layer_rims = tuple(BETA_S * b - ALPHA_T * a for a, b in zip(rt, rs))
        if running is None:
            running, running_rims = layer, layer_rims
        else:
            running = running + layer
            running_rims = tuple(a + b for a, b in zip(running_rims, layer_rims))
        press = PRESS_K * running
        press_rims = tuple(PRESS_K * a for a in running_rims)
        te, tw, tn, ts = around(t, rt)
        se, sw, sn, ss = around(s, rs)
        ue, uw, un, us = around(u, ru)
        ve, vw, vn, vs = around(v, rv)
        pe, pw, pn, ps = around(press, press_rims)
        tn_ref[0, l] = ocean * (
            t - STEP_DT * 0.5 * (u * (te - tw) + v * (tn - ts)) + KAPPA * (te + tw + tn + ts - 4.0 * t)
        )
        sn_ref[0, l] = ocean * (
            s - STEP_DT * 0.5 * (u * (se - sw) + v * (sn - ss)) + KAPPA * (se + sw + sn + ss - 4.0 * s)
        )
        ustar = ocean * (
            u + STEP_DT * (cor * v - 0.5 * (pe - pw) - DRAG_K * u) + VISCOSITY * (ue + uw + un + us - 4.0 * u)
        )
        vstar = ocean * (
            v + STEP_DT * (-cor * u - 0.5 * (pn - ps) - DRAG_K * v) + VISCOSITY * (ve + vw + vn + vs - 4.0 * v)
        )
        us_ref[0, l] = ustar
        vs_ref[0, l] = vstar
        tu = ustar if tu is None else tu + ustar
        tv = vstar if tv is None else tv + vstar
    tu_ref[0] = tu
    tv_ref[0] = tv


def volume_step(temp, salt, uvel, vvel, land_mask, rims):
    members, levels, rows, cols = temp.shape
    field = pl.BlockSpec((1, levels, rows, cols), lambda m: (m, 0, 0, 0))
    plane = pl.BlockSpec((rows, cols), lambda m: (0, 0))
    north, south, east, west = rims
    row_rim = pl.BlockSpec((4, 1, levels, 1, cols), lambda m: (0, m, 0, 0, 0))
    col_rim = pl.BlockSpec((4, 1, levels, rows, 1), lambda m: (0, m, 0, 0, 0))
    surface = pl.BlockSpec((1, rows, cols), lambda m: (m, 0, 0))
    volume_shape = jax.ShapeDtypeStruct(temp.shape, jnp.float32)
    surface_shape = jax.ShapeDtypeStruct((members, rows, cols), jnp.float32)
    return pl.pallas_call(
        functools.partial(volume_kernel, lax.axis_size("gridy")),
        grid=(members,),
        in_specs=[field] * 4 + [plane, row_rim, row_rim, col_rim, col_rim],
        out_specs=[field] * 4 + [surface] * 2,
        out_shape=[volume_shape] * 4 + [surface_shape] * 2,
    )(temp, salt, uvel, vvel, land_mask, north, south, east, west)


def ring(axis):
    count = lax.axis_size(axis)
    forward = [(i, (i + 1) % count) for i in range(count)]
    backward = [((i + 1) % count, i) for i in range(count)]
    return forward, backward


def exchange(block, ydim, xdim, south_keep, north_keep):
    fwd_y, bwd_y = ring("gridy")
    fwd_x, bwd_x = ring("gridx")
    rows = block.shape[ydim]
    cols = block.shape[xdim]
    north = lax.ppermute(lax.slice_in_dim(block, 0, 1, axis=ydim), "gridy", bwd_y) * north_keep
    south = lax.ppermute(lax.slice_in_dim(block, rows - 1, rows, axis=ydim), "gridy", fwd_y) * south_keep
    east = lax.ppermute(lax.slice_in_dim(block, 0, 1, axis=xdim), "gridx", bwd_x)
    west = lax.ppermute(lax.slice_in_dim(block, cols - 1, cols, axis=xdim), "gridx", fwd_x)
    return (east, west, north, south)


def exchange_fields(fields, south_keep, north_keep):
    fwd_y, bwd_y = ring("gridy")
    fwd_x, bwd_x = ring("gridx")
    north = lax.ppermute(jnp.stack([f[..., :1, :] for f in fields]), "gridy", bwd_y)
    south = lax.ppermute(jnp.stack([f[..., -1:, :] for f in fields]), "gridy", fwd_y)
    east = lax.ppermute(jnp.stack([f[..., :, :1] for f in fields]), "gridx", bwd_x)
    west = lax.ppermute(jnp.stack([f[..., :, -1:] for f in fields]), "gridx", fwd_x)
    return (north, south, east, west)


def sides(field, rims, ydim, xdim):
    east, west, north, south = rims
    rows = field.shape[ydim]
    cols = field.shape[xdim]
    east_side = jnp.concatenate([lax.slice_in_dim(field, 1, cols, axis=xdim), east], axis=xdim)
    west_side = jnp.concatenate([west, lax.slice_in_dim(field, 0, cols - 1, axis=xdim)], axis=xdim)
    north_side = jnp.concatenate([lax.slice_in_dim(field, 1, rows, axis=ydim), north], axis=ydim)
    south_side = jnp.concatenate([south, lax.slice_in_dim(field, 0, rows - 1, axis=ydim)], axis=ydim)
    return (east_side, west_side, north_side, south_side)


def pressure(temp, salt):
    return PRESS_K * jnp.cumsum(BETA_S * salt - ALPHA_T * temp, axis=-3)


def surface_apply(field, rims):
    east_side, west_side, north_side, south_side = sides(field, rims, 1, 2)
    return (1.0 + 4.0 * SURF_C) * field - SURF_C * (east_side + west_side + north_side + south_side)


def member_total(values):
    return jnp.sum(values, axis=(1, 2))


def widen(values):
    return values[:, None, None]


def combine(a, fa, b, fb):
    def one(u, v):
        left = u if a is None else widen(a) * u
        return left + (v if b is None else widen(b) * v)

    return one(fa[0], fb[0]), tuple(one(u, v) for u, v in zip(fa[1], fb[1]))


def scaled(a, fa):
    return widen(a) * fa[0], tuple(widen(a) * u for u in fa[1])


def padded_2(block, sides_of, width):
    for axis, dim in sides_of:
        count = lax.axis_size(axis)
        forward = [(i, (i + 1) % count) for i in range(count)]
        backward = [((i + 1) % count, i) for i in range(count)]
        size = block.shape[dim]
        low = lax.ppermute(lax.slice_in_dim(block, size - width, size, axis=dim), axis, forward)
        high = lax.ppermute(lax.slice_in_dim(block, 0, width, axis=dim), axis, backward)
        block = jnp.concatenate([low, block, high], axis=dim)
    return block


def crop(field, by):
    if by == 0:
        return field
    return field[..., by:-by, by:-by]


def around(field):
    return (
        field[..., 1:-1, 1:-1],
        field[..., 1:-1, 2:],
        field[..., 1:-1, :-2],
        field[..., 2:, 1:-1],
        field[..., :-2, 1:-1],
    )


def rows_at(inside, full, want):
    cut = full - want
    return inside if cut == 0 else inside[cut:-cut]


def apply_wide(field, inside):
    centre, east, west, north, south = around(field)
    return ((1.0 + 4.0 * SURF_C) * centre - SURF_C * (east + west + north + south)) * inside


def surface_solve(rhs, inside, width, full):
    residual, wide_r = rhs, width
    gamma_prev = None
    alpha_prev = None
    for count in range(ITERS):
        image_res = apply_wide(residual, rows_at(inside, full, wide_r - 1))
        own_res = crop(residual, wide_r)
        own_img = crop(image_res, wide_r - 1)
        dots = grid_sum(jnp.stack([member_total(own_res * own_res), member_total(own_res * own_img)]))
        gamma, delta = dots[0], dots[1]
        if count == 0:
            alpha = gamma / delta
            direction, wide_p = residual, wide_r
            image_dir, wide_s = image_res, wide_r - 1
            solution, wide_x = widen(alpha) * direction, wide_r
        else:
            beta = gamma / gamma_prev
            alpha = gamma / (delta - beta * gamma / alpha_prev)
            direction = residual + widen(beta) * crop(direction, wide_p - wide_r)
            wide_p = wide_r
            image_dir = image_res + widen(beta) * crop(image_dir, wide_s - (wide_r - 1))
            wide_s = wide_r - 1
            solution = crop(solution, wide_x - wide_r) + widen(alpha) * direction
            wide_x = wide_r
        if count < ITERS - 1:
            residual = crop(residual, 1) - widen(alpha) * image_dir
            wide_r -= 1
        gamma_prev = gamma
        alpha_prev = alpha
    return solution


def shards(temp, salt, uvel, vvel, eta, land_mask, clone_source):
    levels = temp.shape[1]
    rows = temp.shape[2]
    cols = temp.shape[3]
    ocean = land_mask.astype(jnp.float32)
    tile_row = lax.axis_index("gridy")
    tile_count = lax.axis_size("gridy")
    total_rows = rows * tile_count
    total_cols = cols * lax.axis_size("gridx")
    south_keep = (tile_row > 0).astype(jnp.float32)
    north_keep = (tile_row < tile_count - 1).astype(jnp.float32)
    latitude = (tile_row * rows + jnp.arange(rows, dtype=jnp.int32)).astype(jnp.float32) + 0.5
    coriolis = (CORI_K * (2.0 * latitude / total_rows - 1.0))[:, None]
    cor_tile = jnp.broadcast_to(coriolis, (rows, cols))
    band = 8
    block = 128
    frame_rows = rows + 2 * band
    frame_cols = cols + 2 * block
    row_at = lax.broadcasted_iota(jnp.int32, (frame_rows, frame_cols), 0)
    col_at = lax.broadcasted_iota(jnp.int32, (frame_rows, frame_cols), 1)
    global_row = tile_row * rows + jnp.where(row_at < rows + band, row_at, row_at - frame_rows)
    wide_inside = ((global_row >= 0) & (global_row < total_rows)).astype(jnp.float32)
    own_mask = ((row_at < rows) & (col_at < cols)).astype(jnp.float32)
    for count in range(STEPS):
        fields = (temp, salt, uvel, vvel)
        rims = exchange_fields(fields, south_keep, north_keep)
        temp_next, salt_next, ustar, vstar, trans_u, trans_v = volume_step(
            temp, salt, uvel, vvel, land_mask, rims
        )
        solved = surface_kernel_solve(trans_u, trans_v, eta, wide_inside)
        eta = solved[0]
        east_west = solved[1]
        north_south = solved[2]
        uvel = ocean * (ustar - GRAV_K * 0.5 * east_west[:, None])
        vvel = ocean * (vstar - GRAV_K * 0.5 * north_south[:, None])
        if count == STEPS - 1:
            tracers_other = lax.ppermute(jnp.stack((temp_next, salt_next)), "member", [(0, 1), (1, 0)])
        temp = temp_next
        salt = salt_next
    zonal_scale = 1.0 / jnp.sqrt(jnp.float32(total_cols))
    score_scale = 1.0 / jnp.sqrt(jnp.float32(levels * total_rows))
    lat_weight = latitude / total_rows
    members = temp.shape[0]
    zonal_local = jnp.sum(vvel, axis=3)
    depth_weight = (levels - jnp.arange(levels, dtype=jnp.int32)).astype(jnp.float32)
    score_local = jnp.sum(zonal_local * depth_weight[None, :, None] * lat_weight[None, None, :], axis=(1, 2))
    slot = lax.broadcasted_iota(jnp.int32, (tile_count, 1, 1, 1), 0) == tile_row
    zonal_slots = jnp.where(slot, zonal_local[None], 0.0).reshape(-1, 128)
    score_row = jnp.zeros((8, 128), jnp.float32).at[0, :members].set(score_local)
    summed = grid_sum(jnp.concatenate([zonal_slots, score_row], axis=0))
    zonal_whole = summed[: zonal_slots.shape[0]].reshape((tile_count,) + zonal_local.shape)
    zonal_whole = jnp.sum(jnp.where(slot, zonal_whole, 0.0), axis=0)
    overturn = jnp.cumsum(zonal_whole, axis=1) * zonal_scale
    score = summed[zonal_slots.shape[0], :members] * (zonal_scale * score_scale)
    swap = [(0, 1), (1, 0)]
    mine = lax.axis_index("member")
    score_slab = jnp.zeros((members, 1) + eta.shape[1:], jnp.float32).at[:, 0, 0, 0].set(score)
    flows = jnp.concatenate([uvel, vvel, eta[:, None], score_slab], axis=1)
    flows_other = lax.ppermute(flows, "member", swap)
    score_other = flows_other[:, 2 * levels + 1, 0, 0]
    every_score = jnp.where(
        mine == 0, jnp.concatenate([score, score_other]), jnp.concatenate([score_other, score])
    )
    here = (clone_source // members) == mine
    local_at = clone_source % members

    def pick(local, other):
        chosen = []
        for place in range(members):
            from_here = lax.dynamic_index_in_dim(local, local_at[place], 0, keepdims=False)
            from_other = lax.dynamic_index_in_dim(other, local_at[place], 0, keepdims=False)
            chosen.append(jnp.where(here[place], from_here, from_other))
        return jnp.stack(chosen)

    new_temp = pick(temp, tracers_other[0])
    new_salt = pick(salt, tracers_other[1])
    new_flows = pick(flows[:, : 2 * levels + 1], flows_other[:, : 2 * levels + 1])
    clone_weight = jnp.take(every_score, clone_source, axis=0) - jnp.mean(every_score)
    return (
        new_temp,
        new_salt,
        new_flows[:, :levels],
        new_flows[:, levels : 2 * levels],
        new_flows[:, 2 * levels],
        overturn,
        clone_weight,
    )


def solution(mesh):
    in_specs = (
        P("member", None, "gridy", "gridx"),
        P("member", None, "gridy", "gridx"),
        P("member", None, "gridy", "gridx"),
        P("member", None, "gridy", "gridx"),
        P("member", "gridy", "gridx"),
        P("gridy", "gridx"),
        P("member"),
    )
    out_specs = (
        P("member", None, "gridy", "gridx"),
        P("member", None, "gridy", "gridx"),
        P("member", None, "gridy", "gridx"),
        P("member", None, "gridy", "gridx"),
        P("member", "gridy", "gridx"),
        P("member", None, "gridy"),
        P("member"),
    )
    return jax.shard_map(shards, mesh=mesh, in_specs=in_specs, out_specs=out_specs, check_vma=False)
```

```python
import functools

import jax
import jax.numpy as jnp
from jax import lax
from jax.experimental import pallas as pl
from jax.experimental.pallas import tpu as pltpu
from jax.sharding import PartitionSpec as P

STEPS = 2
ITERS = 3


ALPHA_T = 0.8
BETA_S = 0.6
PRESS_K = 0.25
STEP_DT = 0.1
KAPPA = 0.1
VISCOSITY = 0.1
DRAG_K = 0.05
CORI_K = 1.0
SURF_C = 4.0
DIV_K = 0.5
GRAV_K = 0.5


def tree_sum(values, axes):
    for axis in axes:
        count = lax.axis_size(axis)
        step = 1
        while step < count:
            pairs = [(i, i ^ step) for i in range(count)]
            values = values + lax.ppermute(values, axis, pairs)
            step *= 2
    return values


def gather_sum_kernel(ny, nx, x_ref, o_ref, recv_y, recv_x, part, send_y, rsem_y, send_x, rsem_x):
    mesh_id = pl.DeviceIdType.MESH
    member = lax.axis_index("member")
    my = lax.axis_index("gridy")
    mx = lax.axis_index("gridx")
    barrier = pltpu.get_barrier_semaphore()
    for d in range(1, ny):
        pl.semaphore_signal(barrier, 1, device_id=(member, (my + d) % ny, mx), device_id_type=mesh_id)
    for d in range(1, nx):
        pl.semaphore_signal(barrier, 1, device_id=(member, my, (mx + d) % nx), device_id_type=mesh_id)
    pl.semaphore_wait(barrier, (ny - 1) + (nx - 1))

    def phase(src, recv, send_sem, recv_sem, count, me, device):
        recv[me] = src[...]
        sent = []
        for d in range(1, count):
            peer = (me + d) % count
            copy = pltpu.make_async_remote_copy(
                src_ref=src,
                dst_ref=recv.at[me],
                send_sem=send_sem.at[peer],
                recv_sem=recv_sem.at[me],
                device_id=device(peer),
                device_id_type=mesh_id,
            )
            copy.start()
            sent.append(copy)
        for d in range(1, count):
            peer = (me + d) % count
            pltpu.make_async_remote_copy(
                src_ref=src,
                dst_ref=recv.at[peer],
                send_sem=send_sem.at[peer],
                recv_sem=recv_sem.at[peer],
                device_id=device(peer),
                device_id_type=mesh_id,
            ).wait_recv()
        for copy in sent:
            copy.wait_send()
        total = recv[0]
        for j in range(1, count):
            total = total + recv[j]
        return total

    part[...] = phase(x_ref, recv_y, send_y, rsem_y, ny, my, lambda p: (member, p, mx))
    o_ref[...] = phase(part, recv_x, send_x, rsem_x, nx, mx, lambda p: (member, my, p))


def grid_sum(values):
    ny = lax.axis_size("gridy")
    nx = lax.axis_size("gridx")
    shape = values.shape
    return pl.pallas_call(
        functools.partial(gather_sum_kernel, ny, nx),
        out_shape=jax.ShapeDtypeStruct(shape, values.dtype),
        in_specs=[pl.BlockSpec(memory_space=pltpu.VMEM)],
        out_specs=pl.BlockSpec(memory_space=pltpu.VMEM),
        scratch_shapes=[
            pltpu.VMEM((ny,) + shape, values.dtype),
            pltpu.VMEM((nx,) + shape, values.dtype),
            pltpu.VMEM(shape, values.dtype),
            pltpu.SemaphoreType.DMA((ny,)),
            pltpu.SemaphoreType.DMA((ny,)),
            pltpu.SemaphoreType.DMA((nx,)),
            pltpu.SemaphoreType.DMA((nx,)),
        ],
        compiler_params=pltpu.CompilerParams(collective_id=0, has_side_effects=True),
    )(values)


def exchange_sum(k, vec, ny, nx, bufs, device_ids):
    send_y, recv_y, send_x, recv_x, sy, ry, sx, rx = bufs
    my, mx, along_y, along_x = device_ids
    mesh_id = pl.DeviceIdType.MESH

    def phase(value, send_buf, recv, send_sem, recv_sem, count, me, device):
        send_buf[k] = value
        recv[k, me] = value
        sent = []
        for d in range(1, count):
            peer = (me + d) % count
            copy = pltpu.make_async_remote_copy(
                src_ref=send_buf.at[k],
                dst_ref=recv.at[k, me],
                send_sem=send_sem.at[k, peer],
                recv_sem=recv_sem.at[k, me],
                device_id=device(peer),
                device_id_type=mesh_id,
            )
            copy.start()
            sent.append(copy)
        for d in range(1, count):
            peer = (me + d) % count
            pltpu.make_async_remote_copy(
                src_ref=send_buf.at[k],
                dst_ref=recv.at[k, peer],
                send_sem=send_sem.at[k, peer],
                recv_sem=recv_sem.at[k, peer],
                device_id=device(peer),
                device_id_type=mesh_id,
            ).wait_recv()
        for copy in sent:
            copy.wait_send()
        total = recv[k, 0]
        for j in range(1, count):
            total = total + recv[k, j]
        return total

    partial = phase(vec, send_y, recv_y, sy, ry, ny, my, along_y)
    return phase(partial, send_x, recv_x, sx, rx, nx, mx, along_x)


def solve_kernel(ny, nx, tu_ref, tv_ref, eta_ref, out_ref, frame, hsend, hrecv, *bufs):
    mesh_id = pl.DeviceIdType.MESH
    member = lax.axis_index("member")
    my = lax.axis_index("gridy")
    mx = lax.axis_index("gridx")
    along_y = lambda p: (member, p, mx)
    along_x = lambda p: (member, my, p)
    barrier = pltpu.get_barrier_semaphore()
    for d in range(1, ny):
        pl.semaphore_signal(barrier, 1, device_id=along_y((my + d) % ny), device_id_type=mesh_id)
    for d in range(1, nx):
        pl.semaphore_signal(barrier, 1, device_id=along_x((mx + d) % nx), device_id_type=mesh_id)
    for dy in (1, ny - 1):
        for dx in (1, nx - 1):
            pl.semaphore_signal(
                barrier, 1, device_id=(member, (my + dy) % ny, (mx + dx) % nx), device_id_type=mesh_id
            )
    rows, cols = eta_ref.shape[1], eta_ref.shape[2]
    wide_rows, wide_cols = frame.shape[2], frame.shape[3]
    band = (wide_rows - rows) // 2
    block = (wide_cols - cols) // 2
    frame[0, :, 0:rows, 0:cols] = tu_ref[...]
    frame[1, :, 0:rows, 0:cols] = tv_ref[...]
    frame[2, :, 0:rows, 0:cols] = eta_ref[...]
    pl.semaphore_wait(barrier, (ny - 1) + (nx - 1) + 4)

    def halo_copies(first, moves):
        started = []
        for slot, (src, dst, device) in enumerate(moves, start=first):
            copy = pltpu.make_async_remote_copy(
                src_ref=src, dst_ref=dst, send_sem=hsend.at[slot], recv_sem=hrecv.at[slot],
                device_id=device, device_id_type=mesh_id,
            )
            copy.start()
            started.append(copy)
        for copy in started:
            copy.wait()

    up, down = (my + 1) % ny, (my + ny - 1) % ny
    right, left = (mx + 1) % nx, (mx + nx - 1) % nx
    top_rows = slice(0, band)
    low_rows = slice(rows - band, rows)
    own_rows = slice(0, rows)
    west_part = slice(0, block)
    east_part = slice(cols - block, cols)
    own_cols = slice(0, cols)
    north_halo = slice(rows, rows + band)
    south_halo = slice(rows + band, wide_rows)
    east_halo = slice(cols, cols + block)
    west_halo = slice(cols + block, wide_cols)
    halo_copies(0, [
        (frame.at[:, :, top_rows, own_cols], frame.at[:, :, north_halo, own_cols], (member, down, mx)),
        (frame.at[:, :, low_rows, own_cols], frame.at[:, :, south_halo, own_cols], (member, up, mx)),
        (frame.at[:, :, own_rows, west_part], frame.at[:, :, own_rows, east_halo], (member, my, left)),
        (frame.at[:, :, own_rows, east_part], frame.at[:, :, own_rows, west_halo], (member, my, right)),
        (frame.at[:, :, top_rows, west_part], frame.at[:, :, north_halo, east_halo], (member, down, left)),
        (frame.at[:, :, top_rows, east_part], frame.at[:, :, north_halo, west_halo], (member, down, right)),
        (frame.at[:, :, low_rows, west_part], frame.at[:, :, south_halo, east_halo], (member, up, left)),
        (frame.at[:, :, low_rows, east_part], frame.at[:, :, south_halo, west_halo], (member, up, right)),
    ])

    members = eta_ref.shape[0]
    frame_row = lax.broadcasted_iota(jnp.int32, (wide_rows, wide_cols), 0)
    global_row = my * rows + jnp.where(frame_row < rows + band, frame_row, frame_row - wide_rows)
    inside = ((global_row >= 0) & (global_row < rows * ny)).astype(jnp.float32)

    def east(f):
        return pltpu.roll(f, wide_cols - 1, 1)

    def west(f):
        return pltpu.roll(f, 1, 1)

    def north(f):
        return pltpu.roll(f, wide_rows - 1, 0)

    def south(f):
        return pltpu.roll(f, 1, 0)

    def apply(f):
        return ((1.0 + 4.0 * SURF_C) * f - SURF_C * (east(f) + west(f) + north(f) + south(f))) * inside

    def total(f):
        return jnp.sum(f[0:rows, 0:cols], axis=(0, 1), keepdims=True)

    residual = []
    for m in range(members):
        trans_u = frame[0, m] * inside
        trans_v = frame[1, m] * inside
        level = frame[2, m] * inside
        residual.append(
            (level - DIV_K * 0.5 * (east(trans_u) - west(trans_u) + (north(trans_v) - south(trans_v)))) * inside
        )
    lane = lax.broadcasted_iota(jnp.int32, (8, 128), 1)
    direction = [None] * members
    image_dir = [None] * members
    solution = [None] * members
    gamma_prev = [None] * members
    alpha_prev = [None] * members
    for count in range(ITERS):
        image_res = [apply(residual[m]) for m in range(members)]
        vec = jnp.zeros((8, 128), jnp.float32)
        for m in range(members):
            vec = jnp.where(lane == 2 * m, total(residual[m] * residual[m]), vec)
            vec = jnp.where(lane == 2 * m + 1, total(residual[m] * image_res[m]), vec)
        sums = exchange_sum(count, vec, ny, nx, bufs, (my, mx, along_y, along_x))
        for m in range(members):
            gamma = sums[0:1, 2 * m : 2 * m + 1]
            delta = sums[0:1, 2 * m + 1 : 2 * m + 2]
            if count == 0:
                alpha = gamma / delta
                direction[m] = residual[m]
                image_dir[m] = image_res[m]
                solution[m] = alpha * direction[m]
            else:
                beta = gamma / gamma_prev[m]
                alpha = gamma / (delta - beta * gamma / alpha_prev[m])
                direction[m] = residual[m] + beta * direction[m]
                image_dir[m] = image_res[m] + beta * image_dir[m]
                solution[m] = solution[m] + alpha * direction[m]
            if count < ITERS - 1:
                residual[m] = residual[m] - alpha * image_dir[m]
            gamma_prev[m] = gamma
            alpha_prev[m] = alpha
    for m in range(members):
        x = solution[m]
        out_ref[0, m] = x[0:rows, 0:cols]
        out_ref[1, m] = (east(x) - west(x))[0:rows, 0:cols]
        out_ref[2, m] = (north(x) - south(x))[0:rows, 0:cols]


def surface_kernel_solve(trans_u, trans_v, eta, inside_shape):
    ny = lax.axis_size("gridy")
    nx = lax.axis_size("gridx")
    members, rows, cols = eta.shape
    fields = 3
    return pl.pallas_call(
        functools.partial(solve_kernel, ny, nx),
        out_shape=jax.ShapeDtypeStruct((3, members, rows, cols), jnp.float32),
        in_specs=[pl.BlockSpec(memory_space=pltpu.VMEM)] * 3,
        out_specs=pl.BlockSpec(memory_space=pltpu.VMEM),
        scratch_shapes=[
            pltpu.VMEM((fields, members) + inside_shape, jnp.float32),
            pltpu.SemaphoreType.DMA((8,)),
            pltpu.SemaphoreType.DMA((8,)),
            pltpu.VMEM((ITERS, 8, 128), jnp.float32),
            pltpu.VMEM((ITERS, ny, 8, 128), jnp.float32),
            pltpu.VMEM((ITERS, 8, 128), jnp.float32),
            pltpu.VMEM((ITERS, nx, 8, 128), jnp.float32),
            pltpu.SemaphoreType.DMA((ITERS, ny)),
            pltpu.SemaphoreType.DMA((ITERS, ny)),
            pltpu.SemaphoreType.DMA((ITERS, nx)),
            pltpu.SemaphoreType.DMA((ITERS, nx)),
        ],
        compiler_params=pltpu.CompilerParams(collective_id=1, has_side_effects=True),
    )(trans_u, trans_v, eta)


def volume_kernel(ny, temp_ref, salt_ref, uvel_ref, vvel_ref, land_ref, n_ref, s_ref, e_ref, w_ref,
                  tn_ref, sn_ref, us_ref, vs_ref, tu_ref, tv_ref):
    levels, rows, cols = temp_ref.shape[1], temp_ref.shape[2], temp_ref.shape[3]
    row = lax.broadcasted_iota(jnp.int32, (rows, cols), 0)
    col = lax.broadcasted_iota(jnp.int32, (rows, cols), 1)
    tile_row = lax.axis_index("gridy")
    north_keep = jnp.where(tile_row < ny - 1, 1.0, 0.0)
    south_keep = jnp.where(tile_row > 0, 1.0, 0.0)
    latitude = (tile_row * rows + row).astype(jnp.float32) + 0.5
    top = row == rows - 1
    bottom = row == 0
    right = col == cols - 1
    left = col == 0
    ocean = land_ref[...].astype(jnp.float32)
    cor = CORI_K * (2.0 * latitude / (rows * ny) - 1.0)

    def around(f, rims):
        n, s, e, w = rims
        return (
            jnp.where(right, e, pltpu.roll(f, cols - 1, 1)),
            jnp.where(left, w, pltpu.roll(f, 1, 1)),
            jnp.where(top, n, pltpu.roll(f, rows - 1, 0)),
            jnp.where(bottom, s, pltpu.roll(f, 1, 0)),
        )

    def rims_of(k, l):
        return (n_ref[k, 0, l] * north_keep, s_ref[k, 0, l] * south_keep, e_ref[k, 0, l], w_ref[k, 0, l])

    running = None
    running_rims = None
    tu = None
    tv = None
    for l in range(levels):
        t = temp_ref[0, l]
        s = salt_ref[0, l]
        u = uvel_ref[0, l]
        v = vvel_ref[0, l]
        rt, rs, ru, rv = rims_of(0, l), rims_of(1, l), rims_of(2, l), rims_of(3, l)
        layer = BETA_S * s - ALPHA_T * t
        layer_rims = tuple(BETA_S * b - ALPHA_T * a for a, b in zip(rt, rs))
        if running is None:
            running, running_rims = layer, layer_rims
        else:
            running = running + layer
            running_rims = tuple(a + b for a, b in zip(running_rims, layer_rims))
        press = PRESS_K * running
        press_rims = tuple(PRESS_K * a for a in running_rims)
        te, tw, tn, ts = around(t, rt)
        se, sw, sn, ss = around(s, rs)
        ue, uw, un, us = around(u, ru)
        ve, vw, vn, vs = around(v, rv)
        pe, pw, pn, ps = around(press, press_rims)
        tn_ref[0, l] = ocean * (
            t - STEP_DT * 0.5 * (u * (te - tw) + v * (tn - ts)) + KAPPA * (te + tw + tn + ts - 4.0 * t)
        )
        sn_ref[0, l] = ocean * (
            s - STEP_DT * 0.5 * (u * (se - sw) + v * (sn - ss)) + KAPPA * (se + sw + sn + ss - 4.0 * s)
        )
        ustar = ocean * (
            u + STEP_DT * (cor * v - 0.5 * (pe - pw) - DRAG_K * u) + VISCOSITY * (ue + uw + un + us - 4.0 * u)
        )
        vstar = ocean * (
            v + STEP_DT * (-cor * u - 0.5 * (pn - ps) - DRAG_K * v) + VISCOSITY * (ve + vw + vn + vs - 4.0 * v)
        )
        us_ref[0, l] = ustar
        vs_ref[0, l] = vstar
        tu = ustar if tu is None else tu + ustar
        tv = vstar if tv is None else tv + vstar
    tu_ref[0] = tu
    tv_ref[0] = tv


def volume_step(temp, salt, uvel, vvel, land_mask, rims):
    members, levels, rows, cols = temp.shape
    field = pl.BlockSpec((1, levels, rows, cols), lambda m: (m, 0, 0, 0))
    plane = pl.BlockSpec((rows, cols), lambda m: (0, 0))
    north, south, east, west = rims
    row_rim = pl.BlockSpec((4, 1, levels, 1, cols), lambda m: (0, m, 0, 0, 0))
    col_rim = pl.BlockSpec((4, 1, levels, rows, 1), lambda m: (0, m, 0, 0, 0))
    surface = pl.BlockSpec((1, rows, cols), lambda m: (m, 0, 0))
    volume_shape = jax.ShapeDtypeStruct(temp.shape, jnp.float32)
    surface_shape = jax.ShapeDtypeStruct((members, rows, cols), jnp.float32)
    return pl.pallas_call(
        functools.partial(volume_kernel, lax.axis_size("gridy")),
        grid=(members,),
        in_specs=[field] * 4 + [plane, row_rim, row_rim, col_rim, col_rim],
        out_specs=[field] * 4 + [surface] * 2,
        out_shape=[volume_shape] * 4 + [surface_shape] * 2,
    )(temp, salt, uvel, vvel, land_mask, north, south, east, west)


def ring(axis):
    count = lax.axis_size(axis)
    forward = [(i, (i + 1) % count) for i in range(count)]
    backward = [((i + 1) % count, i) for i in range(count)]
    return forward, backward


def exchange(block, ydim, xdim, south_keep, north_keep):
    fwd_y, bwd_y = ring("gridy")
    fwd_x, bwd_x = ring("gridx")
    rows = block.shape[ydim]
    cols = block.shape[xdim]
    north = lax.ppermute(lax.slice_in_dim(block, 0, 1, axis=ydim), "gridy", bwd_y) * north_keep
    south = lax.ppermute(lax.slice_in_dim(block, rows - 1, rows, axis=ydim), "gridy", fwd_y) * south_keep
    east = lax.ppermute(lax.slice_in_dim(block, 0, 1, axis=xdim), "gridx", bwd_x)
    west = lax.ppermute(lax.slice_in_dim(block, cols - 1, cols, axis=xdim), "gridx", fwd_x)
    return (east, west, north, south)


def exchange_fields(fields, south_keep, north_keep):
    fwd_y, bwd_y = ring("gridy")
    fwd_x, bwd_x = ring("gridx")
    north = lax.ppermute(jnp.stack([f[..., :1, :] for f in fields]), "gridy", bwd_y)
    south = lax.ppermute(jnp.stack([f[..., -1:, :] for f in fields]), "gridy", fwd_y)
    east = lax.ppermute(jnp.stack([f[..., :, :1] for f in fields]), "gridx", bwd_x)
    west = lax.ppermute(jnp.stack([f[..., :, -1:] for f in fields]), "gridx", fwd_x)
    return (north, south, east, west)


def sides(field, rims, ydim, xdim):
    east, west, north, south = rims
    rows = field.shape[ydim]
    cols = field.shape[xdim]
    east_side = jnp.concatenate([lax.slice_in_dim(field, 1, cols, axis=xdim), east], axis=xdim)
    west_side = jnp.concatenate([west, lax.slice_in_dim(field, 0, cols - 1, axis=xdim)], axis=xdim)
    north_side = jnp.concatenate([lax.slice_in_dim(field, 1, rows, axis=ydim), north], axis=ydim)
    south_side = jnp.concatenate([south, lax.slice_in_dim(field, 0, rows - 1, axis=ydim)], axis=ydim)
    return (east_side, west_side, north_side, south_side)


def pressure(temp, salt):
    return PRESS_K * jnp.cumsum(BETA_S * salt - ALPHA_T * temp, axis=-3)


def surface_apply(field, rims):
    east_side, west_side, north_side, south_side = sides(field, rims, 1, 2)
    return (1.0 + 4.0 * SURF_C) * field - SURF_C * (east_side + west_side + north_side + south_side)


def member_total(values):
    return jnp.sum(values, axis=(1, 2))


def widen(values):
    return values[:, None, None]


def combine(a, fa, b, fb):
    def one(u, v):
        left = u if a is None else widen(a) * u
        return left + (v if b is None else widen(b) * v)

    return one(fa[0], fb[0]), tuple(one(u, v) for u, v in zip(fa[1], fb[1]))


def scaled(a, fa):
    return widen(a) * fa[0], tuple(widen(a) * u for u in fa[1])


def padded_2(block, sides_of, width):
    for axis, dim in sides_of:
        count = lax.axis_size(axis)
        forward = [(i, (i + 1) % count) for i in range(count)]
        backward = [((i + 1) % count, i) for i in range(count)]
        size = block.shape[dim]
        low = lax.ppermute(lax.slice_in_dim(block, size - width, size, axis=dim), axis, forward)
        high = lax.ppermute(lax.slice_in_dim(block, 0, width, axis=dim), axis, backward)
        block = jnp.concatenate([low, block, high], axis=dim)
    return block


def crop(field, by):
    if by == 0:
        return field
    return field[..., by:-by, by:-by]


def around(field):
    return (
        field[..., 1:-1, 1:-1],
        field[..., 1:-1, 2:],
        field[..., 1:-1, :-2],
        field[..., 2:, 1:-1],
        field[..., :-2, 1:-1],
    )


def rows_at(inside, full, want):
    cut = full - want
    return inside if cut == 0 else inside[cut:-cut]


def apply_wide(field, inside):
    centre, east, west, north, south = around(field)
    return ((1.0 + 4.0 * SURF_C) * centre - SURF_C * (east + west + north + south)) * inside


def surface_solve(rhs, inside, width, full):
    residual, wide_r = rhs, width
    gamma_prev = None
    alpha_prev = None
    for count in range(ITERS):
        image_res = apply_wide(residual, rows_at(inside, full, wide_r - 1))
        own_res = crop(residual, wide_r)
        own_img = crop(image_res, wide_r - 1)
        dots = grid_sum(jnp.stack([member_total(own_res * own_res), member_total(own_res * own_img)]))
        gamma, delta = dots[0], dots[1]
        if count == 0:
            alpha = gamma / delta
            direction, wide_p = residual, wide_r
            image_dir, wide_s = image_res, wide_r - 1
            solution, wide_x = widen(alpha) * direction, wide_r
        else:
            beta = gamma / gamma_prev
            alpha = gamma / (delta - beta * gamma / alpha_prev)
            direction = residual + widen(beta) * crop(direction, wide_p - wide_r)
            wide_p = wide_r
            image_dir = image_res + widen(beta) * crop(image_dir, wide_s - (wide_r - 1))
            wide_s = wide_r - 1
            solution = crop(solution, wide_x - wide_r) + widen(alpha) * direction
            wide_x = wide_r
        if count < ITERS - 1:
            residual = crop(residual, 1) - widen(alpha) * image_dir
            wide_r -= 1
        gamma_prev = gamma
        alpha_prev = alpha
    return solution


def shards(temp, salt, uvel, vvel, eta, land_mask, clone_source):
    levels = temp.shape[1]
    rows = temp.shape[2]
    cols = temp.shape[3]
    ocean = land_mask.astype(jnp.float32)
    tile_row = lax.axis_index("gridy")
    tile_count = lax.axis_size("gridy")
    total_rows = rows * tile_count
    total_cols = cols * lax.axis_size("gridx")
    south_keep = (tile_row > 0).astype(jnp.float32)
    north_keep = (tile_row < tile_count - 1).astype(jnp.float32)
    latitude = (tile_row * rows + jnp.arange(rows, dtype=jnp.int32)).astype(jnp.float32) + 0.5
    coriolis = (CORI_K * (2.0 * latitude / total_rows - 1.0))[:, None]
    cor_tile = jnp.broadcast_to(coriolis, (rows, cols))
    band = 8
    block = 128
    frame_rows = rows + 2 * band
    frame_cols = cols + 2 * block
    row_at = lax.broadcasted_iota(jnp.int32, (frame_rows, frame_cols), 0)
    col_at = lax.broadcasted_iota(jnp.int32, (frame_rows, frame_cols), 1)
    global_row = tile_row * rows + jnp.where(row_at < rows + band, row_at, row_at - frame_rows)
    wide_inside = ((global_row >= 0) & (global_row < total_rows)).astype(jnp.float32)
    own_mask = ((row_at < rows) & (col_at < cols)).astype(jnp.float32)
    for count in range(STEPS):
        fields = (temp, salt, uvel, vvel)
        rims = exchange_fields(fields, south_keep, north_keep)
        temp_next, salt_next, ustar, vstar, trans_u, trans_v = volume_step(
            temp, salt, uvel, vvel, land_mask, rims
        )
        solved = surface_kernel_solve(trans_u, trans_v, eta, wide_inside.shape)
        eta = solved[0]
        east_west = solved[1]
        north_south = solved[2]
        uvel = ocean * (ustar - GRAV_K * 0.5 * east_west[:, None])
        vvel = ocean * (vstar - GRAV_K * 0.5 * north_south[:, None])
        if count == STEPS - 1:
            tracers_other = lax.ppermute(jnp.stack((temp_next, salt_next)), "member", [(0, 1), (1, 0)])
        temp = temp_next
        salt = salt_next
    zonal_scale = 1.0 / jnp.sqrt(jnp.float32(total_cols))
    score_scale = 1.0 / jnp.sqrt(jnp.float32(levels * total_rows))
    lat_weight = latitude / total_rows
    members = temp.shape[0]
    zonal_local = jnp.sum(vvel, axis=3)
    depth_weight = (levels - jnp.arange(levels, dtype=jnp.int32)).astype(jnp.float32)
    score_local = jnp.sum(zonal_local * depth_weight[None, :, None] * lat_weight[None, None, :], axis=(1, 2))
    slot = lax.broadcasted_iota(jnp.int32, (tile_count, 1, 1, 1), 0) == tile_row
    zonal_slots = jnp.where(slot, zonal_local[None], 0.0).reshape(-1, 128)
    score_row = jnp.zeros((8, 128), jnp.float32).at[0, :members].set(score_local)
    summed = grid_sum(jnp.concatenate([zonal_slots, score_row], axis=0))
    zonal_whole = summed[: zonal_slots.shape[0]].reshape((tile_count,) + zonal_local.shape)
    zonal_whole = jnp.sum(jnp.where(slot, zonal_whole, 0.0), axis=0)
    overturn = jnp.cumsum(zonal_whole, axis=1) * zonal_scale
    score = summed[zonal_slots.shape[0], :members] * (zonal_scale * score_scale)
    swap = [(0, 1), (1, 0)]
    mine = lax.axis_index("member")
    score_slab = jnp.zeros((members, 1) + eta.shape[1:], jnp.float32).at[:, 0, 0, 0].set(score)
    flows = jnp.concatenate([uvel, vvel, eta[:, None], score_slab], axis=1)
    flows_other = lax.ppermute(flows, "member", swap)
    score_other = flows_other[:, 2 * levels + 1, 0, 0]
    every_score = jnp.where(
        mine == 0, jnp.concatenate([score, score_other]), jnp.concatenate([score_other, score])
    )
    here = (clone_source // members) == mine
    local_at = clone_source % members

    def pick(local, other):
        chosen = []
        for place in range(members):
            from_here = lax.dynamic_index_in_dim(local, local_at[place], 0, keepdims=False)
            from_other = lax.dynamic_index_in_dim(other, local_at[place], 0, keepdims=False)
            chosen.append(jnp.where(here[place], from_here, from_other))
        return jnp.stack(chosen)

    new_temp = pick(temp, tracers_other[0])
    new_salt = pick(salt, tracers_other[1])
    new_flows = pick(flows[:, : 2 * levels + 1], flows_other[:, : 2 * levels + 1])
    clone_weight = jnp.take(every_score, clone_source, axis=0) - jnp.mean(every_score)
    return (
        new_temp,
        new_salt,
        new_flows[:, :levels],
        new_flows[:, levels : 2 * levels],
        new_flows[:, 2 * levels],
        overturn,
        clone_weight,
    )


def solution(mesh):
    in_specs = (
        P("member", None, "gridy", "gridx"),
        P("member", None, "gridy", "gridx"),
        P("member", None, "gridy", "gridx"),
        P("member", None, "gridy", "gridx"),
        P("member", "gridy", "gridx"),
        P("gridy", "gridx"),
        P("member"),
    )
    out_specs = (
        P("member", None, "gridy", "gridx"),
        P("member", None, "gridy", "gridx"),
        P("member", None, "gridy", "gridx"),
        P("member", None, "gridy", "gridx"),
        P("member", "gridy", "gridx"),
        P("member", None, "gridy"),
        P("member"),
    )
    return jax.shard_map(shards, mesh=mesh, in_specs=in_specs, out_specs=out_specs, check_vma=False)
```
